32 devices in a mesh: rows: 2 (over y), seq: 16 (over z, x, core).
Axes of the slice: x: 2, y: 2, z: 4, core: 2. Of those that a mesh axis runs over, the one named last changes fastest.
Arguments:
- frames: bfloat16 [2, 2048, 768], P('rows', 'seq'), may hold values from -6 to 6
- segment_ids: int32 [2, 2048], P('rows', 'seq'), may hold values from 0 to 7, never falling along the last dimension, each value on 1 to 1024 neighbouring positions
- qkv_weight: bfloat16 [768, 2304], replicated, may hold values from -0.21875 to 0.21875
- query_bias: float32 [768], replicated, may hold values from -3 to 3
- value_bias: float32 [768], replicated, may hold values from -0.3125 to 0.3125
- out_weight: bfloat16 [768, 768], replicated, may hold values from -3.5 to 3.5
- out_bias: float32 [768], replicated, may hold values from -3 to 3
- norm1_gain: float32 [768], replicated, may hold values from 0.5 to 1.5
- norm1_shift: float32 [768], replicated, may hold values from -3 to 3
- up_weight: bfloat16 [768, 3072], replicated, may hold values from -0.21875 to 0.21875
- up_bias: float32 [3072], replicated, may hold values from -3 to 3
- down_weight: bfloat16 [3072, 768], replicated, may hold values from -0.109375 to 0.109375
- down_bias: float32 [768], replicated, may hold values from -3 to 3
- norm2_gain: float32 [768], replicated, may hold values from 0.5 to 1.5
- norm2_shift: float32 [768], replicated, may hold values from -3 to 3
- cotangent: bfloat16 [2, 2048, 768], P('rows', 'seq'), may hold values from -6 to 6
Outputs:
- layer_out: bfloat16 [2, 2048, 768], P('rows', 'seq')
- input_grad: float32 [2, 2048, 768], P('rows', 'seq')
- qkv_gradient: float32 [768, 2304], P(('rows', 'seq'))
- querybias_gradient: float32 [768], P(('rows', 'seq'))
- valuebias_gradient: float32 [768], P(('rows', 'seq'))
- out_gradient: float32 [768, 768], P(('rows', 'seq'))
- outbias_gradient: float32 [768], P(('rows', 'seq'))
- gain1_gradient: float32 [768], P(('rows', 'seq'))
- shift1_gradient: float32 [768], P(('rows', 'seq'))
- up_gradient: float32 [768, 3072], P(('rows', 'seq'))
- upbias_gradient: float32 [3072], P(('rows', 'seq'))
- down_gradient: float32 [3072, 768], P(('rows', 'seq'))
- downbias_gradient: float32 [768], P(('rows', 'seq'))
- gain2_gradient: float32 [768], P(('rows', 'seq'))
- shift2_gradient: float32 [768], P(('rows', 'seq'))
The draws below stay inside these ranges and needn't reach their ends.
Inputs may be any that keep to these rules, and one draw needn't show every extreme that they name: `segment_ids`: along each row the ids never fall; each clip has 1 to 1024 frames and one has exactly 1024.
All inputs are finite; a program needn't handle non-finite values.
Results may differ from the reference program's by a relative error of at most 0.02.
Values may be sent and summed in bfloat16 or wider, within the bound.
A program may use at most 192 MiB of HBM per device.

```python
import math
import jax
import jax.numpy as jnp
import numpy as np
from jax import lax

D = 768
HEADS = 12
HEAD_DIM = 64
FF = 3072
TOK_DEV = 128
CLIPS = 8
ROWS = 2
FRAMES = 2048
CLIP_MOST = 1024
N_SEQ = 16


def strengthened(values, key, source, target, parts, factor):
    owner, partner = [(jnp.arange(values.shape[position]) // (values.shape[position] // parts)).reshape([-1 if axis == position else 1 for axis in range(values.ndim)]) for position in (source, target)]
    chosen = jax.random.permutation(key, parts)[partner]
    strong = (owner == chosen) | (owner == (partner + parts // 2) % parts)
    return jnp.where(strong, factor * values, values)


def steps_of(rng, dims, split, low, top_value):
    def one(position, parts):
        draws = jax.random.uniform(jax.random.fold_in(jax.random.fold_in(rng, 6), position), (parts,), jnp.float32, low / len(split), top_value / len(split))
        return jnp.repeat(jnp.exp(draws), dims[position] // parts).reshape((-1,) + (1,) * (len(dims) - position - 1))

    factor_of = one(*split[0])
    for cut in split[1:]:
        factor_of = factor_of * one(*cut)
    return factor_of


def split_up(number_of, total, most, skew):
    loads = [(1 << 20) // math.isqrt(standing ** skew) + 1 for standing in range(2, number_of + 1)]
    rest, holding = total - most - (number_of - 1), [1] * (number_of - 1)
    while rest > 0:
        movable = [i for i in range(number_of - 1) if holding[i] < most]
        pool, remaining = sum([loads[i] for i in movable]), rest
        for i in movable:
            extra = min(most - holding[i], max(1, remaining * loads[i] // pool), rest)
            holding[i] = holding[i] + extra
            rest = rest - extra
    return np.array([most] + holding)


def ragged_sizes(own_key, number_of, total, bound, lean):
    if number_of == 2:
        one = jax.random.randint(own_key, (), max(1, total - bound), min(bound, total - 1) + 1)
        return jnp.stack([one, total - one])
    sizes = jnp.asarray(split_up(number_of, total, bound, lean), jnp.int32)
    pairs = (number_of - 1) // 2
    source_of, receiver = sizes[1:1 + 2 * pairs:2], sizes[2:2 + 2 * pairs:2]
    slack = jnp.minimum(source_of - 1, bound - receiver)
    moved = jax.random.randint(jax.random.fold_in(own_key, 1), (pairs,), 0, 1 << 20) % (slack + 1)
    sizes = sizes.at[1:1 + 2 * pairs:2].set(source_of - moved).at[2:2 + 2 * pairs:2].set(receiver + moved)
    return sizes[jax.random.permutation(jax.random.fold_in(own_key, 2), number_of)]


def scatter_about(rng, extent, width, reach, split=(), kind=jnp.bfloat16):
    level = steps_of(rng, extent, split, -0.22, 0.18) if split else 1.0
    array = jax.random.normal(rng, extent, jnp.float32) * width * level
    return jnp.minimum(jnp.maximum(array, -reach), reach).astype(kind)


def heavy_noise(own_key, dims, scale, most, shards, heavy, dtype=jnp.bfloat16):
    values = scale * jax.random.normal(own_key, dims, jnp.float32)
    if shards:
        values = values * steps_of(own_key, dims, shards, -0.22, 0.18)
    return jnp.clip(strengthened(values, jax.random.fold_in(own_key, 3), *heavy), -most, most).astype(dtype)


def setup_inputs(seed: int = 0) -> dict:
    seeds = jax.random.split(jax.random.key(seed), 17)
    frames = heavy_noise(seeds[0], (ROWS, FRAMES, D), 1.0, 6.0, ((0, 2), (1, 16)), (1, 2, 16, 2.0))
    segment_ids = jax.vmap(lambda own: jnp.searchsorted(jnp.cumsum(ragged_sizes(own, CLIPS, FRAMES, CLIP_MOST, 2)), jnp.arange(FRAMES), side="right"))(jax.random.split(seeds[1], ROWS)).reshape((ROWS, FRAMES)).astype(jnp.int32)
    qkv_weight = scatter_about(seeds[2], (D, 3 * D), D ** -0.5, 0.21875)
    query_bias = scatter_about(seeds[3], (D,), 0.5, 3.0, (), jnp.float32)
    value_bias = scatter_about(seeds[4], (D,), 0.05, 0.3125, (), jnp.float32)
    out_weight = scatter_about(seeds[5], (D, D), (max(1, D * 8 // (TOK_DEV * N_SEQ))) ** -0.5, 3.5)
    out_bias = scatter_about(seeds[6], (D,), 0.5, 3.0, (), jnp.float32)
    norm1_gain = jnp.clip(1.0 + 0.1 * jax.random.normal(seeds[7], (D,), jnp.float32), 0.5, 1.5)
    norm1_shift = scatter_about(seeds[8], (D,), 0.5, 3.0, (), jnp.float32)
    up_weight = scatter_about(seeds[9], (D, FF), D ** -0.5, 0.21875)
    up_bias = scatter_about(seeds[10], (FF,), 0.5, 3.0, (), jnp.float32)
    down_weight = scatter_about(seeds[11], (FF, D), FF ** -0.5, 0.109375)
    down_bias = scatter_about(seeds[12], (D,), 0.5, 3.0, (), jnp.float32)
    norm2_gain = jnp.clip(1.0 + 0.1 * jax.random.normal(seeds[13], (D,), jnp.float32), 0.5, 1.5)
    norm2_shift = scatter_about(seeds[14], (D,), 0.5, 3.0, (), jnp.float32)
    cotangent = scatter_about(seeds[15], (ROWS, FRAMES, D), 1.0, 6.0, ((0, 2), (1, 16)))
    return {"frames": frames, "segment_ids": segment_ids, "qkv_weight": qkv_weight, "query_bias": query_bias, "value_bias": value_bias, "out_weight": out_weight, "out_bias": out_bias, "norm1_gain": norm1_gain, "norm1_shift": norm1_shift, "up_weight": up_weight, "up_bias": up_bias, "down_weight": down_weight, "down_bias": down_bias, "norm2_gain": norm2_gain, "norm2_shift": norm2_shift, "cotangent": cotangent}


@jax.custom_vjp
def low(v):
    return lax.optimization_barrier(v.astype(jnp.bfloat16)).astype(jnp.float32)

@jax.custom_vjp
def low_back(v):
    return v

def low_keep(v):
    return (low(v), None)

def low_pass(kept, grad):
    return (grad,)

def back_keep(v):
    return (v, None)

def back_low(kept, grad):
    return (low(grad),)
low.defvjp(low_keep, low_pass)
low_back.defvjp(back_keep, back_low)
norm_eps = 1e-05
mask_fill = -1e+30
highest = lax.Precision.HIGHEST

def layer_norm(resid, gain, shift):
    centred = resid - lax.optimization_barrier(jnp.mean(resid, axis=-1, keepdims=True))
    variance = lax.optimization_barrier(jnp.mean(centred * centred, axis=-1, keepdims=True))
    return centred * lax.rsqrt(variance + norm_eps) * gain + shift

def block_attend(query_block, ids_block, keys, values, key_ids):
    scores = jnp.einsum('qhe,khe->hqk', query_block, keys, precision=highest)
    scores = low_back(scores) * HEAD_DIM ** (-0.5)
    same_clip = ids_block[:, None] == key_ids[None, :]
    scores = jnp.where(same_clip[None], scores, mask_fill)
    peak = lax.optimization_barrier(jnp.max(scores, axis=-1, keepdims=True))
    log_total = peak + jnp.log(lax.optimization_barrier(jnp.sum(jnp.exp(scores - peak), axis=-1, keepdims=True)))
    probs = low(jnp.exp(scores - log_total))
    return jnp.einsum('hqk,khe->qhe', probs, values, precision=highest)

def row_attend(queries, keys, values, row_ids):
    block_rows = math.gcd(FRAMES, 128)
    block_count = FRAMES // block_rows
    query_blocks = queries.reshape(block_count, block_rows, HEADS, HEAD_DIM)
    id_blocks = row_ids.reshape(block_count, block_rows)

    def one_block(block_pair):
        return block_attend(block_pair[0], block_pair[1], keys, values, row_ids)
    attended = lax.map(jax.checkpoint(one_block), (query_blocks, id_blocks))
    return attended.reshape(FRAMES, D)

def forward(params, segment_ids):
    frames, qkv_weight, query_bias, value_bias, out_weight, out_bias, norm1_gain, norm1_shift, up_weight, up_bias, down_weight, down_bias, norm2_gain, norm2_shift = params
    flat = frames.reshape(ROWS * FRAMES, D)
    projected = jnp.dot(flat, qkv_weight, precision=highest)
    queries = low(low_back(projected[:, :D] + query_bias))
    keys = low(low_back(projected[:, D:2 * D]))
    values = low(low_back(projected[:, 2 * D:] + value_bias))
    pieces = []
    for row_index in range(ROWS):
        lower = row_index * FRAMES
        upper = lower + FRAMES
        pieces.append(row_attend(queries[lower:upper].reshape(FRAMES, HEADS, HEAD_DIM), keys[lower:upper].reshape(FRAMES, HEADS, HEAD_DIM), values[lower:upper].reshape(FRAMES, HEADS, HEAD_DIM), segment_ids[row_index]))
    context = low(low_back(jnp.concatenate(pieces, axis=0)))
    resid_one = flat + low_back(jnp.dot(context, out_weight, precision=highest)) + out_bias
    hidden = layer_norm(resid_one, norm1_gain, norm1_shift)
    pre_act = low_back(jnp.dot(low(hidden), up_weight, precision=highest)) + up_bias
    act = low(jax.nn.gelu(pre_act, approximate=False))
    resid_two = hidden + low_back(jnp.dot(act, down_weight, precision=highest)) + down_bias
    return layer_norm(resid_two, norm2_gain, norm2_shift).reshape(ROWS, FRAMES, D)

def reference(frames, segment_ids, qkv_weight, query_bias, value_bias, out_weight, out_bias, norm1_gain, norm1_shift, up_weight, up_bias, down_weight, down_bias, norm2_gain, norm2_shift, cotangent):
    params = (frames.astype(jnp.float32), qkv_weight.astype(jnp.float32), query_bias.astype(jnp.float32), value_bias.astype(jnp.float32), out_weight.astype(jnp.float32), out_bias.astype(jnp.float32), norm1_gain.astype(jnp.float32), norm1_shift.astype(jnp.float32), up_weight.astype(jnp.float32), up_bias.astype(jnp.float32), down_weight.astype(jnp.float32), down_bias.astype(jnp.float32), norm2_gain.astype(jnp.float32), norm2_shift.astype(jnp.float32))

    def wrapped(all_params):
        return forward(all_params, segment_ids)
    result, pullback = jax.vjp(wrapped, params)
    grads = pullback(cotangent.astype(jnp.float32))[0]
    return (result.astype(jnp.bfloat16), grads[0], grads[1], grads[2], grads[3], grads[4], grads[5], grads[6], grads[7], grads[8], grads[9], grads[10], grads[11], grads[12], grads[13])
```

```python
import functools
import math

import jax
import jax.numpy as jnp
from jax import lax
from jax.experimental import pallas as pl
from jax.experimental.pallas import tpu as pltpu
from jax.sharding import PartitionSpec as P

HEADS = 12
HEAD_DIM = 64


norm_eps = 1e-05
mask_fill = -1e30


def shortened(shard):

    def short(part):
        return part.astype(jnp.bfloat16) if part.dtype == jnp.float32 else part

    return jax.tree.map(short, shard)


def passed_along(value, axis, steps):
    count = lax.axis_size(axis)
    pairs = [(source, (source + steps) % count) for source in range(count)]
    return lax.ppermute(value, axis, pairs)


def layer_norm(resid, gain, shift):
    centred = resid - jnp.mean(resid, axis=-1, keepdims=True)
    inv_std = lax.rsqrt(jnp.mean(centred * centred, axis=-1, keepdims=True) + norm_eps)
    normed = centred * inv_std
    return (normed * gain + shift, normed, inv_std)


def norm_back(upstream, normed, inv_std, gain):
    scaled = upstream * gain
    first_mean = jnp.mean(scaled, axis=-1, keepdims=True)
    second_mean = jnp.mean(scaled * normed, axis=-1, keepdims=True)
    grad_in = inv_std * (scaled - first_mean - normed * second_mean)
    return (grad_in, jnp.sum(upstream * normed, axis=0), jnp.sum(upstream, axis=0))


def gelu_slope(pre_act):
    normal_cdf = 0.5 * (1.0 + lax.erf(pre_act * 0.5**0.5))
    normal_pdf = jnp.exp(-0.5 * pre_act * pre_act) * (2.0 * math.pi) ** (-0.5)
    return normal_cdf + pre_act * normal_pdf


def head_groups(head_count):
    return [(0, head_count, 1)]


def pass_keys(blocks):
    return jax.tree.map(
        lambda part, own: part.astype(own.dtype), passed_along(shortened(blocks), "seq", 1), blocks
    )


def pass_again(blocks):
    return jax.tree.map(
        lambda part, own: part.astype(own.dtype), passed_along(shortened(blocks), "seq", 1), blocks
    )


def pass_grads(blocks):
    return (
        passed_along(blocks[0].astype(jnp.bfloat16), "seq", 1).astype(jnp.float32),
        passed_along(blocks[1].astype(jnp.bfloat16), "seq", 1).astype(jnp.float32),
    )


def block_scores(query_part, key_part, query_ids, key_ids):
    scores = jnp.einsum(
        "qhe,khe->hqk", query_part, key_part, preferred_element_type=jnp.float32
    ) * HEAD_DIM ** (-0.5)
    return jnp.where((query_ids[:, None] == key_ids[None, :])[None], scores, mask_fill)


def attend_block(carried, query_part, key_part, value_part, query_ids, key_ids):
    run_max, run_total, run_acc = carried
    scores = block_scores(query_part, key_part, query_ids, key_ids)
    new_max = jnp.maximum(run_max, jnp.max(scores, axis=-1))
    weights = jnp.exp(scores - new_max[:, :, None])
    factor = jnp.exp(run_max - new_max)
    new_total = run_total * factor + jnp.sum(weights, axis=-1)
    update = jnp.einsum(
        "hqk,khe->qhe", weights.astype(jnp.bfloat16), value_part, preferred_element_type=jnp.float32
    )
    return (new_max, new_total, run_acc * factor.T[:, :, None] + update)


def grad_block(
    carried,
    query_part,
    key_part,
    value_part,
    query_ids,
    key_ids,
    context_part,
    log_part,
    delta_part,
):
    query_acc, key_acc, value_acc = carried
    scores = block_scores(query_part, key_part, query_ids, key_ids)
    probs = jnp.exp(scores - log_part[:, :, None])
    prob_grad = jnp.einsum(
        "qhe,khe->hqk", context_part, value_part, preferred_element_type=jnp.float32
    )
    score_grad = (probs * (prob_grad - delta_part[:, :, None])).astype(jnp.bfloat16)
    scale = HEAD_DIM ** (-0.5)
    query_acc = query_acc + scale * jnp.einsum(
        "hqk,khe->qhe", score_grad, key_part, preferred_element_type=jnp.float32
    )
    key_acc = key_acc + scale * jnp.einsum(
        "hqk,qhe->khe", score_grad, query_part, preferred_element_type=jnp.float32
    )
    value_acc = value_acc + jnp.einsum(
        "hqk,qhe->khe", probs.astype(jnp.bfloat16), context_part, preferred_element_type=jnp.float32
    )
    return (query_acc, key_acc, value_acc)


def forward_cycle(
    query_heads, key_heads, value_heads, local_ids, every_id, cycle_place, cycle_size
):
    frame_count, head_count, head_width = query_heads.shape
    grouping = head_groups(head_count)
    states = []
    blocks = []
    for head_first, head_last, direction in grouping:
        head_span = head_last - head_first
        initial = (
            jnp.full((head_span, frame_count), mask_fill, jnp.float32),
            jnp.zeros((head_span, frame_count), jnp.float32),
            jnp.zeros((frame_count, head_span, head_width), jnp.float32),
        )
        states.append(
            attend_block(initial, query_heads, key_heads, value_heads, local_ids, local_ids)
        )
        blocks.append((key_heads, value_heads))

    def forward_cycle_turn(turn_index, cycle_carry):
        old_states, old_blocks = cycle_carry
        new_states = []
        new_blocks = []
        for group_info, part_state, part_block in zip(grouping, old_states, old_blocks):
            head_first, head_last, direction = group_info
            part_block = pass_keys(part_block)
            source_index = (cycle_place - direction * turn_index) % cycle_size
            key_ids = lax.dynamic_slice_in_dim(every_id, source_index * frame_count, frame_count)
            new_states.append(
                attend_block(
                    part_state, query_heads, part_block[0], part_block[1], local_ids, key_ids
                )
            )
            new_blocks.append(part_block)
        return (new_states, new_blocks)

    states, blocks = lax.fori_loop(1, cycle_size, forward_cycle_turn, (states, blocks))
    maxima = jnp.concatenate([part_state[0] for part_state in states], axis=0)
    totals = jnp.concatenate([part_state[1] for part_state in states], axis=0)
    sums_all = jnp.concatenate([part_state[2] for part_state in states], axis=1)
    attended = sums_all / totals.T[:, :, None]
    return (attended, maxima + jnp.log(totals))


def backward_cycle(
    query_heads,
    key_heads,
    value_heads,
    local_ids,
    every_id,
    context_heads,
    log_total,
    row_delta,
    cycle_place,
    cycle_size,
):
    frame_count, head_count, head_width = query_heads.shape
    grouping = head_groups(head_count)
    initial = []
    for head_first, head_last, direction in grouping:
        zero_part = jnp.zeros((frame_count, head_last - head_first, head_width), jnp.float32)
        initial.append((zero_part, (key_heads, value_heads), (zero_part, zero_part)))

    def backward_cycle_turn(turn_index, cycle_carry):
        new_carry = []
        for group_info, part_carry in zip(grouping, cycle_carry):
            head_first, head_last, direction = group_info
            query_acc, part_block, part_grads = part_carry
            source_index = (cycle_place - direction * turn_index) % cycle_size
            key_ids = lax.dynamic_slice_in_dim(every_id, source_index * frame_count, frame_count)
            query_acc, key_acc, value_acc = grad_block(
                (query_acc, part_grads[0], part_grads[1]),
                query_heads,
                part_block[0],
                part_block[1],
                local_ids,
                key_ids,
                context_heads,
                log_total,
                row_delta,
            )
            part_grads = pass_grads((key_acc, value_acc))
            part_block = pass_again(part_block)
            new_carry.append((query_acc, part_block, part_grads))
        return new_carry

    final = lax.fori_loop(0, cycle_size, backward_cycle_turn, initial)
    query_grad = jnp.concatenate([part_carry[0] for part_carry in final], axis=1)
    key_grad = jnp.concatenate([part_carry[2][0] for part_carry in final], axis=1)
    value_grad = jnp.concatenate([part_carry[2][1] for part_carry in final], axis=1)
    return (query_grad, key_grad, value_grad)


def shards(
    frames,
    segment_ids,
    qkv_weight,
    query_bias,
    value_bias,
    out_weight,
    out_bias,
    norm1_gain,
    norm1_shift,
    up_weight,
    up_bias,
    down_weight,
    down_bias,
    norm2_gain,
    norm2_shift,
    cotangent,
):
    inputs = frames[0]
    local_ids = segment_ids[0]
    frame_count, model_width = inputs.shape
    cycle_size = lax.axis_size("seq")
    cycle_place = lax.axis_index("seq")
    every_id = lax.all_gather(segment_ids, "seq", axis=1, tiled=True)[0]
    head_shape = (frame_count, HEADS, HEAD_DIM)
    projected = jnp.dot(inputs, qkv_weight, preferred_element_type=jnp.float32)
    query_heads = (projected[:, :model_width] + query_bias).astype(jnp.bfloat16).reshape(head_shape)
    key_heads = projected[:, model_width : 2 * model_width].astype(jnp.bfloat16).reshape(head_shape)
    value_heads = (
        (projected[:, 2 * model_width :] + value_bias).astype(jnp.bfloat16).reshape(head_shape)
    )
    attended, log_total = forward_cycle(
        query_heads, key_heads, value_heads, local_ids, every_id, cycle_place, cycle_size
    )
    context = attended.astype(jnp.bfloat16).reshape(frame_count, model_width)
    resid_one = (
        inputs.astype(jnp.float32)
        + jnp.dot(context, out_weight, preferred_element_type=jnp.float32)
        + out_bias
    )
    hidden, normed_one, inverse_one = layer_norm(resid_one, norm1_gain, norm1_shift)
    hidden_low = hidden.astype(jnp.bfloat16)
    pre_act = jnp.dot(hidden_low, up_weight, preferred_element_type=jnp.float32) + up_bias
    act_low = jax.nn.gelu(pre_act, approximate=False).astype(jnp.bfloat16)
    resid_two = (
        hidden + jnp.dot(act_low, down_weight, preferred_element_type=jnp.float32) + down_bias
    )
    output, normed_two, inverse_two = layer_norm(resid_two, norm2_gain, norm2_shift)
    upstream = cotangent[0].astype(jnp.float32)
    second_grad, gain_two_grad, shift_two_grad = norm_back(
        upstream, normed_two, inverse_two, norm2_gain
    )
    second_low = second_grad.astype(jnp.bfloat16)
    down_grad = jnp.einsum("tf,td->fd", act_low, second_low, preferred_element_type=jnp.float32)
    pre_grad = jnp.einsum(
        "td,fd->tf", second_low, down_weight, preferred_element_type=jnp.float32
    ) * gelu_slope(pre_act)
    pre_low = pre_grad.astype(jnp.bfloat16)
    up_grad = jnp.einsum("td,tf->df", hidden_low, pre_low, preferred_element_type=jnp.float32)
    hidden_grad = second_grad + jnp.einsum(
        "tf,df->td", pre_low, up_weight, preferred_element_type=jnp.float32
    )
    first_grad, gain_one_grad, shift_one_grad = norm_back(
        hidden_grad, normed_one, inverse_one, norm1_gain
    )
    first_low = first_grad.astype(jnp.bfloat16)
    out_grad = jnp.einsum("td,te->de", context, first_low, preferred_element_type=jnp.float32)
    context_grad = (
        jnp.einsum("te,de->td", first_low, out_weight, preferred_element_type=jnp.float32)
        .astype(jnp.bfloat16)
        .reshape(head_shape)
    )
    row_delta = jnp.einsum("qhe,qhe->hq", context_grad.astype(jnp.float32), attended)
    query_grad, key_grad, value_grad = backward_cycle(
        query_heads,
        key_heads,
        value_heads,
        local_ids,
        every_id,
        context_grad,
        log_total,
        row_delta,
        cycle_place,
        cycle_size,
    )
    query_low = query_grad.astype(jnp.bfloat16).reshape(frame_count, model_width)
    key_low = key_grad.astype(jnp.bfloat16).reshape(frame_count, model_width)
    value_low = value_grad.astype(jnp.bfloat16).reshape(frame_count, model_width)
    proj_grad = jnp.concatenate([query_low, key_low, value_low], axis=1)
    qkv_grad = jnp.einsum("td,te->de", inputs, proj_grad, preferred_element_type=jnp.float32)
    input_grad = (
        jnp.einsum("te,de->td", proj_grad, qkv_weight, preferred_element_type=jnp.float32)
        + first_grad
    )
    summed = (
        lax.psum_scatter(qkv_grad, ("rows", "seq"), scatter_dimension=0, tiled=True),
        lax.psum_scatter(
            jnp.sum(query_low.astype(jnp.float32), axis=0),
            ("rows", "seq"),
            scatter_dimension=0,
            tiled=True,
        ),
        lax.psum_scatter(
            jnp.sum(value_low.astype(jnp.float32), axis=0),
            ("rows", "seq"),
            scatter_dimension=0,
            tiled=True,
        ),
        lax.psum_scatter(out_grad, ("rows", "seq"), scatter_dimension=0, tiled=True),
        lax.psum_scatter(
            jnp.sum(first_grad, axis=0), ("rows", "seq"), scatter_dimension=0, tiled=True
        ),
        lax.psum_scatter(gain_one_grad, ("rows", "seq"), scatter_dimension=0, tiled=True),
        lax.psum_scatter(shift_one_grad, ("rows", "seq"), scatter_dimension=0, tiled=True),
        lax.psum_scatter(up_grad, ("rows", "seq"), scatter_dimension=0, tiled=True),
        lax.psum_scatter(
            jnp.sum(pre_grad, axis=0), ("rows", "seq"), scatter_dimension=0, tiled=True
        ),
        lax.psum_scatter(down_grad, ("rows", "seq"), scatter_dimension=0, tiled=True),
        lax.psum_scatter(
            jnp.sum(second_grad, axis=0), ("rows", "seq"), scatter_dimension=0, tiled=True
        ),
        lax.psum_scatter(gain_two_grad, ("rows", "seq"), scatter_dimension=0, tiled=True),
        lax.psum_scatter(shift_two_grad, ("rows", "seq"), scatter_dimension=0, tiled=True),
    )
    return (
        output.astype(jnp.bfloat16)[None],
        input_grad[None],
        summed[0],
        summed[1],
        summed[2],
        summed[3],
        summed[4],
        summed[5],
        summed[6],
        summed[7],
        summed[8],
        summed[9],
        summed[10],
        summed[11],
        summed[12],
    )


HALF = HEAD_DIM
PAIRS = HEADS // 2
CONTRACT_LAST = (((1,), (1,)), ((), ()))
CONTRACT_INNER = (((1,), (0,)), ((), ()))
CONTRACT_FIRST = (((0,), (0,)), ((), ()))
IN_VMEM = pl.BlockSpec(memory_space=pltpu.VMEM)
IN_PLACE = pl.BlockSpec(memory_space=pl.ANY)
MESH_ID = pl.DeviceIdType.MESH
VMEM_BYTES = 58 << 20
BLOCKS = 16
PLANES = 4


def product(left, right, dims):
    return lax.dot_general(left, right, dims, preferred_element_type=jnp.float32)


def where_am_i():
    row = lax.axis_index("rows")
    place = lax.axis_index("seq")
    return row, place // 4, place // 2 % 2, place % 2


def meet(partners, count):
    barrier = pltpu.get_barrier_semaphore()
    for present, target in partners:

        def signal(target=target):
            pl.semaphore_signal(barrier, inc=1, device_id=target, device_id_type=MESH_ID)

        if present is None:
            signal()
        else:
            pl.when(present)(signal)
    pl.semaphore_wait(barrier, count)


class RowGather:
    UP, DOWN, ACROSS, BESIDE = range(4)

    def __init__(self, parts, send_sem, recv_sem):
        self.parts = parts
        self.send_sem = send_sem
        self.recv_sem = recv_sem
        self.row, self.z, self.x, self.c = where_am_i()
        self.sent = []

    def device(self, z, x, c):
        return (self.row, z * 4 + x * 2 + c)

    def targets(self):
        return (
            self.device(self.z + 1, self.x, self.c),
            self.device(self.z - 1, self.x, self.c),
            self.device(self.z, 1 - self.x, self.c),
            self.device(self.z, self.x, 1 - self.c),
        )

    def meet(self):
        up, down, across, beside = self.targets()
        has_up = self.z < PLANES - 1
        has_down = self.z > 0
        meet(
            [(has_up, up), (has_down, down), (None, across), (None, beside)],
            2 + has_up.astype(jnp.int32) + has_down.astype(jnp.int32),
        )

    def copy(self, part, block, way):
        ref, first, rows = self.parts[part]
        piece = ref.at[block, pl.ds(first, rows)]
        return pltpu.make_async_remote_copy(
            src_ref=piece,
            dst_ref=piece,
            send_sem=self.send_sem.at[part, way, block],
            recv_sem=self.recv_sem.at[part, block],
            device_id=self.targets()[way],
            device_id_type=MESH_ID,
        )

    def send(self, part, block, way, present=None):
        self.sent.append((part, block, way, present))
        if present is None:
            self.copy(part, block, way).start()
        else:
            pl.when(present)(lambda: self.copy(part, block, way).start())

    def arrived(self, part, block):
        self.copy(part, block, self.BESIDE).wait_recv()

    def finish(self):
        for part, block, way, present in self.sent:
            if present is None:
                self.copy(part, block, way).wait_send()
            else:
                pl.when(present)(
                    lambda part=part, block=block, way=way: self.copy(part, block, way).wait_send()
                )

    def relay(self, part, z, x, ways, present):
        block = z * 4 + x * 2 + self.c

        def wait():
            self.arrived(part, block)

        if present is None:
            wait()
        else:
            pl.when(present)(wait)
        for way, also in ways:
            both = present if also is None else (also if present is None else present & also)
            self.send(part, block, way, both)

    def own(self, across_first, line_parts):
        z, x, c = self.z, self.x, self.c
        mine = z * 4 + x * 2 + c
        has_up, has_down = z < PLANES - 1, z > 0
        for part in across_first:
            self.send(part, mine, self.ACROSS)
        for part in list(line_parts) + list(across_first):
            self.send(part, mine, self.UP, has_up)
            self.send(part, mine, self.DOWN, has_down)
        for part in line_parts:
            self.send(part, mine, self.ACROSS)
        for part in list(across_first) + list(line_parts):
            self.send(part, mine, self.BESIDE)

    def first_round(self, across_first, line_parts):
        z, x = self.z, self.x
        has_up, has_down = z < PLANES - 1, z > 0
        up, down, across, beside = (
            (self.UP, has_up),
            (self.DOWN, has_down),
            (self.ACROSS, None),
            (self.BESIDE, None),
        )
        for part in across_first:
            self.relay(part, z, 1 - x, [up, down, beside], None)
        for part in line_parts:
            self.relay(part, z - 1, x, [up, across, beside], has_down)
            self.relay(part, z + 1, x, [down, across, beside], has_up)
        for part in across_first:
            self.relay(part, z - 1, x, [up, beside], has_down)
            self.relay(part, z + 1, x, [down, beside], has_up)
        for part in line_parts:
            self.relay(part, z, 1 - x, [beside], None)

    def plane_done(self, z, parts, present=None):
        def wait():
            for x in range(2):
                for part in parts:
                    self.arrived(part, z * 4 + x * 2 + 1 - self.c)

        if present is None:
            wait()
        else:
            pl.when(present)(wait)

    def second_round(self, across_first, line_parts):
        z, x = self.z, self.x
        has_up, has_down = z < PLANES - 1, z > 0
        up, down, beside = (self.UP, has_up), (self.DOWN, has_down), (self.BESIDE, None)
        for part in across_first:
            self.relay(part, z - 1, 1 - x, [up, beside], has_down)
            self.relay(part, z + 1, 1 - x, [down, beside], has_up)
        for part in line_parts:
            self.relay(part, z - 1, 1 - x, [beside], has_down)
            self.relay(part, z + 1, 1 - x, [beside], has_up)

    def far_plane(self):
        return (self.z + 2) % PLANES

    def third_round(self, across_first, line_parts):
        far, x = self.far_plane(), self.x
        across, beside = (self.ACROSS, None), (self.BESIDE, None)
        for part in line_parts:
            self.relay(part, far, x, [across, beside], None)
        for part in across_first:
            self.relay(part, far, x, [beside], None)
            self.relay(part, far, 1 - x, [beside], None)
        for part in line_parts:
            self.relay(part, far, 1 - x, [beside], None)


def attend_kernel(
    frames_ref,
    ids_row_ref,
    ids_column_ref,
    weight_ref,
    query_bias_ref,
    value_bias_ref,
    attended_ref,
    log_ref,
    every_ids_ref,
    projected_hbm,
    block_ref,
    projected_ref,
    bias_ref,
    send_sem,
    recv_sem,
    store_sem,
):
    frame_count, width = frames_ref.shape
    padded = block_ref.shape[1]
    first_rows = 80
    link = RowGather(
        [(block_ref, 0, first_rows), (block_ref, first_rows, padded - first_rows)],
        send_sem,
        recv_sem,
    )
    z, x, c = link.z, link.x, link.c
    mine = z * 4 + x * 2 + c
    has_up, has_down = z < PLANES - 1, z > 0
    line, crossing = (0,), (1,)
    link.meet()
    block_ref[mine, pl.ds(0, frame_count), :] = frames_ref[...]
    block_ref[mine, pl.ds(frame_count, padded - frame_count), pl.ds(0, frame_count)] = (
        jnp.broadcast_to(ids_row_ref[...], (padded - frame_count, frame_count))
        .astype(jnp.float32)
        .astype(jnp.bfloat16)
    )
    link.own(crossing, line)

    def store(plane):
        return pltpu.make_async_copy(
            projected_ref.at[pl.ds(plane * 4, 4)],
            projected_hbm.at[pl.ds(plane * 4, 4)],
            store_sem.at[plane],
        )

    def project(plane):
        rows = jnp.concatenate(
            [block_ref[plane * 4 + i, pl.ds(0, frame_count), :] for i in range(4)], axis=0
        )
        for third in range(3):
            columns = pl.ds(third * width, width)
            part = product(rows, weight_ref[:, columns], CONTRACT_INNER)
            if third == 0:
                part = (part + query_bias_ref[...]).astype(jnp.bfloat16) * HEAD_DIM**-0.5
            elif third == 2:
                part = part + value_bias_ref[...]
            part = part.astype(jnp.bfloat16)
            for i in range(4):
                projected_ref[plane * 4 + i, :, columns] = part[
                    i * frame_count : (i + 1) * frame_count
                ]
        store(plane).start()

    link.first_round(crossing, line)
    link.plane_done(z, (0, 1))
    project(z)
    link.second_round(crossing, line)

    @pl.when(has_down)
    def _():
        link.plane_done(z - 1, (0, 1))
        project(z - 1)

    link.third_round(crossing, line)

    @pl.when(has_up)
    def _():
        link.plane_done(z + 1, (0, 1))
        project(z + 1)

    link.plane_done(link.far_plane(), (0, 1))
    project(link.far_plane())

    @pl.when(jnp.logical_not(has_up & has_down))
    def _():
        lost = PLANES - 1 - z
        for i in range(4):
            projected_ref[lost * 4 + i] = jnp.zeros_like(projected_ref[0])
            block_ref[lost * 4 + i, pl.ds(frame_count, padded - frame_count), :] = jnp.full(
                (padded - frame_count, width), -1.0, jnp.bfloat16
            )
        store(lost).start()

    every = jnp.concatenate(
        [
            block_ref[b, pl.ds(frame_count, 8), pl.ds(0, frame_count)].astype(jnp.float32)
            for b in range(BLOCKS)
        ],
        axis=1,
    )
    every_ids_ref[...] = every
    bias_ref[...] = jnp.where(
        every[:1] == ids_column_ref[...].astype(jnp.float32), 0.0, mask_fill
    )
    lane = lax.broadcasted_iota(jnp.int32, (frame_count, 2 * HALF), 1)
    total = BLOCKS * frame_count

    def pair(j, logs):
        query = projected_ref[mine, :, pl.ds(pl.multiple_of(j * 128, 128), 128)]
        keys = projected_ref[:, :, pl.ds(pl.multiple_of(width + j * 128, 128), 128)].reshape(
            total, 128
        )
        values = projected_ref[
            :, :, pl.ds(pl.multiple_of(2 * width + j * 128, 128), 128)
        ].reshape(total, 128)
        outs = []
        for h in range(2):
            chosen = (lane < HALF) == (h == 0)
            scores = (
                product(jnp.where(chosen, query, jnp.zeros_like(query)), keys, CONTRACT_LAST)
                + bias_ref[...]
            )
            peak = jnp.max(scores, axis=1, keepdims=True)
            weights = jnp.exp(scores - peak)
            whole = jnp.sum(weights, axis=1, keepdims=True)
            outs.append(
                product(weights.astype(jnp.bfloat16), values, CONTRACT_INNER) / whole
            )
            logs = jnp.where(lane == 2 * j + h, peak + jnp.log(whole), logs)
        attended_ref[:, pl.ds(pl.multiple_of(j * 128, 128), 128)] = jnp.where(
            lane < HALF, outs[0], outs[1]
        )
        return logs

    log_ref[...] = lax.fori_loop(
        0, PAIRS, pair, jnp.zeros((frame_count, 2 * HALF), jnp.float32)
    )
    for plane in range(PLANES):
        store(plane).wait()
    link.finish()


def attend_back_kernel(
    context_grad_ref,
    attended_ref,
    log_ref,
    every_ids_ref,
    ids_column_ref,
    projected_ref,
    grad_ref,
    block_ref,
    stats_ref,
    bias_ref,
    delta_ref,
    send_sem,
    recv_sem,
):
    frame_count, width = context_grad_ref.shape
    first_rows = 80
    link = RowGather(
        [
            (block_ref, 0, first_rows),
            (block_ref, first_rows, frame_count - first_rows),
            (stats_ref, 0, 32),
        ],
        send_sem,
        recv_sem,
    )
    z, x, c = link.z, link.x, link.c
    mine = z * 4 + x * 2 + c
    has_up, has_down = z < PLANES - 1, z > 0
    line, crossing = (2, 0), (1,)
    lane = lax.broadcasted_iota(jnp.int32, (frame_count, 2 * HALF), 1)
    total = BLOCKS * frame_count
    link.meet()
    block_ref[mine] = context_grad_ref[...]
    delta = jnp.zeros((frame_count, 2 * HALF), jnp.float32)
    for j in range(PAIRS):
        columns = pl.ds(j * 128, 128)
        both = context_grad_ref[:, columns].astype(jnp.float32) * attended_ref[:, columns]
        for h in range(2):
            one = jnp.sum(
                jnp.where((lane < HALF) == (h == 0), both, 0.0), axis=1, keepdims=True
            )
            delta = jnp.where(lane == 2 * j + h, one, delta)
    delta_ref[...] = delta
    stats_ref[mine, pl.ds(0, 16), :] = log_ref[...].T[:16]
    stats_ref[mine, pl.ds(16, 16), :] = delta.T[:16]
    link.own(crossing, line)

    bias_ref[...] = jnp.where(
        every_ids_ref[:1] == ids_column_ref[...].astype(jnp.float32), 0.0, mask_fill
    )

    def columns_of(third, j):
        return pl.ds(pl.multiple_of(third * width + j * 128, 128), 128)

    def query_pair(j):
        query = projected_ref[mine, :, columns_of(0, j)]
        upstream = context_grad_ref[:, columns_of(0, j)]
        keys = projected_ref[:, :, columns_of(1, j)].reshape(total, 128)
        values = projected_ref[:, :, columns_of(2, j)].reshape(total, 128)
        outs = []
        for h in range(2):
            chosen = (lane < HALF) == (h == 0)
            nothing = jnp.zeros_like(query)
            logs = jnp.sum(
                jnp.where(lane == 2 * j + h, log_ref[...], 0.0), axis=1, keepdims=True
            )
            shift = jnp.sum(
                jnp.where(lane == 2 * j + h, delta_ref[...], 0.0), axis=1, keepdims=True
            )
            scores = product(jnp.where(chosen, query, nothing), keys, CONTRACT_LAST)
            probs = jnp.exp(scores + bias_ref[...] - logs)
            prob_grad = product(jnp.where(chosen, upstream, nothing), values, CONTRACT_LAST)
            score_grad = (probs * (prob_grad - shift)).astype(jnp.bfloat16)
            outs.append(product(score_grad, keys, CONTRACT_INNER))
        grad_ref[:, columns_of(0, j)] = (
            jnp.where(lane < HALF, outs[0], outs[1]) * HEAD_DIM**-0.5
        ).astype(jnp.bfloat16)

    def query_pairs(first, last):
        def one(j, carry):
            query_pair(j)
            return carry

        lax.fori_loop(first, last, one, 0)

    query_pairs(0, 2)
    link.first_round(crossing, line)
    query_pairs(2, 4)
    link.second_round(crossing, line)
    query_pairs(4, 5)
    link.third_round(crossing, line)
    query_pairs(5, 6)
    link.plane_done(z, (0, 1, 2))
    link.plane_done(z - 1, (0, 1, 2), has_down)
    link.plane_done(z + 1, (0, 1, 2), has_up)
    link.plane_done(link.far_plane(), (0, 1, 2))

    @pl.when(jnp.logical_not(has_up & has_down))
    def _():
        lost = PLANES - 1 - z
        for i in range(4):
            block_ref[lost * 4 + i] = jnp.zeros_like(block_ref[0])
            stats_ref[lost * 4 + i] = jnp.zeros_like(stats_ref[0])

    def key_pair(j, carry):
        key = projected_ref[mine, :, columns_of(1, j)]
        value = projected_ref[mine, :, columns_of(2, j)]
        queries = projected_ref[:, :, columns_of(0, j)].reshape(total, 128)
        upstream = block_ref[:, :, columns_of(0, j)].reshape(total, 128)
        key_outs = []
        value_outs = []
        for h in range(2):
            chosen = (lane < HALF) == (h == 0)
            nothing = jnp.zeros_like(key)
            logs = jnp.concatenate(
                [stats_ref[b, pl.ds(2 * j + h, 1), :] for b in range(BLOCKS)], axis=1
            )
            shift = jnp.concatenate(
                [stats_ref[b, pl.ds(16 + 2 * j + h, 1), :] for b in range(BLOCKS)], axis=1
            )
            scores = product(jnp.where(chosen, key, nothing), queries, CONTRACT_LAST)
            probs = jnp.exp(scores + bias_ref[...] - logs)
            prob_grad = product(jnp.where(chosen, value, nothing), upstream, CONTRACT_LAST)
            score_grad = (probs * (prob_grad - shift)).astype(jnp.bfloat16)
            key_outs.append(product(score_grad, queries, CONTRACT_INNER))
            value_outs.append(product(probs.astype(jnp.bfloat16), upstream, CONTRACT_INNER))
        grad_ref[:, columns_of(1, j)] = jnp.where(
            lane < HALF, key_outs[0], key_outs[1]
        ).astype(jnp.bfloat16)
        grad_ref[:, columns_of(2, j)] = jnp.where(
            lane < HALF, value_outs[0], value_outs[1]
        ).astype(jnp.bfloat16)
        return carry

    lax.fori_loop(0, PAIRS, key_pair, 0)
    link.finish()


class QuadSum:
    def __init__(self, left, right, buffers, sems):
        self.left, self.right = left, right
        self.lefts, self.rights, self.whole, self.x_in, self.halved, self.z_in, self.last, self.side = (
            buffers
        )
        self.send, self.recv_left, self.recv_right, self.x_sems, self.z_send, self.z_recv, self.side_sems = (
            sems
        )
        self.y, self.z, self.x, self.c = where_am_i()
        self.quad = self.y * 2 + self.c
        self.left_half = self.lefts.shape[2]
        self.right_half = self.rights.shape[2]
        self.flying = []

    def device(self, y, z, x, c):
        return (y, z * 4 + x * 2 + c)

    def fly(self, source, target, send_sem, recv_sem, device):
        copy = pltpu.make_async_remote_copy(
            src_ref=source,
            dst_ref=target,
            send_sem=send_sem,
            recv_sem=recv_sem,
            device_id=device,
            device_id_type=MESH_ID,
        )
        copy.start()
        self.flying.append(copy)

    def left_of(self, y):
        return self.left.at[:, pl.ds(pl.multiple_of(y * self.left_half, 128), self.left_half)]

    def right_of(self, c):
        return self.right.at[:, pl.ds(pl.multiple_of(c * self.right_half, 128), self.right_half)]

    def share_left(self):
        y, z, x, c, quad = self.y, self.z, self.x, self.c, self.quad
        self.fly(
            self.left_of(1 - y), self.lefts.at[quad], self.send.at[0], self.recv_left.at[quad],
            self.device(1 - y, z, x, c),
        )
        self.fly(
            self.left_of(y), self.lefts.at[quad], self.send.at[1], self.recv_left.at[quad],
            self.device(y, z, x, 1 - c),
        )

    def share_right(self):
        y, z, x, c, quad = self.y, self.z, self.x, self.c, self.quad
        self.fly(
            self.right_of(c), self.rights.at[quad], self.send.at[2], self.recv_right.at[quad],
            self.device(1 - y, z, x, c),
        )
        self.fly(
            self.right_of(1 - c), self.rights.at[quad], self.send.at[3], self.recv_right.at[quad],
            self.device(1 - y, z, x, 1 - c),
        )
        self.fly(
            self.right_of(1 - c), self.rights.at[quad], self.send.at[4], self.recv_right.at[quad],
            self.device(y, z, x, 1 - c),
        )

    def landed(self, ref, sem):
        pltpu.make_async_remote_copy(
            src_ref=ref,
            dst_ref=ref,
            send_sem=self.send.at[0],
            recv_sem=sem,
            device_id=self.device(self.y, self.z, self.x, 1 - self.c),
            device_id_type=MESH_ID,
        ).wait_recv()

    def relay_left(self):
        peer = (1 - self.y) * 2 + self.c
        self.landed(self.lefts.at[peer], self.recv_left.at[peer])
        self.fly(
            self.lefts.at[peer], self.lefts.at[peer], self.send.at[5], self.recv_left.at[peer],
            self.device(self.y, self.z, self.x, 1 - self.c),
        )

    def multiply(self):
        y, c = self.y, self.c
        self.lefts[self.quad] = self.left_of(y)[...]
        self.rights[self.quad] = self.right_of(c)[...]
        for other in (y * 2 + 1 - c, (1 - y) * 2 + 1 - c):
            self.landed(self.lefts.at[other], self.recv_left.at[other])
        for other in (y * 2 + 1 - c, (1 - y) * 2 + c, (1 - y) * 2 + 1 - c):
            self.landed(self.rights.at[other], self.recv_right.at[other])
        tokens = self.lefts.shape[0] * self.lefts.shape[1]
        planes, _, rows, _ = self.whole.shape
        step = 384
        if self.left_half > step:
            right = self.rights[...].reshape(tokens, self.right_half)

            def one(i, carry):
                left = self.lefts[:, :, pl.ds(pl.multiple_of(i * step, 128), step)]
                part = product(left.reshape(tokens, step), right, CONTRACT_FIRST)
                self.whole[i] = part.astype(jnp.bfloat16).reshape(2, rows, self.right_half)
                return carry

            lax.fori_loop(0, self.left_half // step, one, 0)
        else:
            left = self.lefts[...].reshape(tokens, self.left_half)

            def one(i, carry):
                columns = pl.ds(pl.multiple_of(i * step, 128), step)
                part = product(
                    left, self.rights[:, :, columns].reshape(tokens, step), CONTRACT_FIRST
                )
                self.whole[:, :, :, columns] = part.astype(jnp.bfloat16).reshape(
                    planes, 2, rows, step
                )
                return carry

            lax.fori_loop(0, self.right_half // step, one, 0)

    def halve(self):
        self.fly(
            self.whole.at[:, 1 - self.x], self.x_in, self.x_sems.at[0], self.x_sems.at[1],
            self.device(self.y, self.z, 1 - self.x, self.c),
        )

    def spread(self):
        self.landed(self.x_in, self.x_sems.at[1])
        self.halved[...] = (
            self.whole[:, self.x].astype(jnp.float32) + self.x_in[...].astype(jnp.float32)
        ).astype(jnp.bfloat16)
        for step in range(1, PLANES):
            target = (self.z + step) % PLANES
            self.fly(
                self.halved.at[target], self.z_in.at[self.z], self.z_send.at[step],
                self.z_recv.at[self.z], self.device(self.y, target, self.x, self.c),
            )

    def collect(self):
        total = self.halved[self.z].astype(jnp.float32)
        for step in range(1, PLANES):
            source = (self.z + step) % PLANES
            self.landed(self.z_in.at[source], self.z_recv.at[source])
            total = total + self.z_in[source].astype(jnp.float32)
        self.last[...] = total
        rows = self.last.shape[0] // 2
        self.fly(
            self.last.at[pl.ds(pl.multiple_of((1 - self.c) * rows, 8), rows)], self.side,
            self.side_sems.at[0], self.side_sems.at[1],
            self.device(self.y, self.z, self.x, 1 - self.c),
        )

    def deliver(self, out_ref):
        rows = self.last.shape[0] // 2
        width = self.right_half
        out_ref[:, pl.ds(pl.multiple_of(self.c * width, 128), width)] = self.last[
            pl.ds(pl.multiple_of(self.c * rows, 8), rows), :
        ]
        self.landed(self.side, self.side_sems.at[1])
        out_ref[:, pl.ds(pl.multiple_of((1 - self.c) * width, 128), width)] = self.side[...]

    def finish(self):
        for copy in self.flying:
            copy.wait_send()


QUAD_REFS = 15


def quad_scratch(frame_count, left_width, right_width):
    left_half, right_half = left_width // 2, right_width // 2
    rows = left_half // (2 * PLANES)
    low, wide = jnp.bfloat16, jnp.float32
    return [
        pltpu.VMEM((4, frame_count, left_half), low),
        pltpu.VMEM((4, frame_count, right_half), low),
        pltpu.VMEM((PLANES, 2, rows, right_half), low),
        pltpu.VMEM((PLANES, rows, right_half), low),
        pltpu.VMEM((PLANES, rows, right_half), low),
        pltpu.VMEM((PLANES, rows, right_half), low),
        pltpu.VMEM((rows, right_half), wide),
        pltpu.VMEM((rows // 2, right_half), wide),
        pltpu.SemaphoreType.DMA((6,)),
        pltpu.SemaphoreType.DMA((4,)),
        pltpu.SemaphoreType.DMA((4,)),
        pltpu.SemaphoreType.DMA((2,)),
        pltpu.SemaphoreType.DMA((PLANES,)),
        pltpu.SemaphoreType.DMA((PLANES,)),
        pltpu.SemaphoreType.DMA((2,)),
    ]


class VectorSum:
    def __init__(self, ref, partial, arrived, send_sem, recv_sem):
        self.ref, self.partial, self.arrived = ref, partial, arrived
        self.send_sem, self.recv_sem = send_sem, recv_sem
        self.y, self.z, self.x, self.c = where_am_i()
        self.flying = []

    def device(self, y, z, x, c):
        return (y, z * 4 + x * 2 + c)

    def copy(self, source, slot, device):
        return pltpu.make_async_remote_copy(
            src_ref=source,
            dst_ref=self.arrived.at[slot],
            send_sem=self.send_sem.at[slot],
            recv_sem=self.recv_sem.at[slot],
            device_id=device,
            device_id_type=MESH_ID,
        )

    def start(self, stage):
        y, z, x, c = self.y, self.z, self.x, self.c
        source = self.ref if stage == 0 else self.partial.at[stage - 1]
        if stage < 3:
            device = (
                self.device(y, z, x, 1 - c),
                self.device(1 - y, z, x, c),
                self.device(y, z, 1 - x, c),
            )[stage]
            copy = self.copy(source, stage, device)
            copy.start()
            self.flying.append(copy)
        else:
            for step in range(1, PLANES):
                copy = self.copy(
                    source, 2 + step, self.device(y, (z + step) % PLANES, x, c)
                )
                copy.start()
                self.flying.append(copy)

    def take(self, stage):
        y, z, x, c = self.y, self.z, self.x, self.c
        total = self.ref[...] if stage == 0 else self.partial[stage - 1]
        for slot in (stage,) if stage < 3 else (3, 4, 5):
            self.copy(self.ref, slot, self.device(y, z, x, 1 - c)).wait_recv()
            total = total + self.arrived[slot]
        self.partial[stage] = total

    def finish(self):
        for copy in self.flying:
            copy.wait_send()

    def own_share(self, rows, share):
        width = self.ref.shape[1]
        place = self.y * 16 + self.z * 4 + self.x * 2 + self.c
        per_row = width // share
        offset = place % per_row * share
        row_index = lax.broadcasted_iota(jnp.int32, (width, 128), 0)
        column_index = lax.broadcasted_iota(jnp.int32, (width, 128), 1)
        picked = jnp.where(
            (row_index == column_index + offset) & (column_index < share), 1.0, 0.0
        ).astype(jnp.bfloat16)
        rest = rows
        total = jnp.zeros((rows.shape[0], 128), jnp.float32)
        for _ in range(3):
            piece = rest.astype(jnp.bfloat16)
            total = total + product(piece, picked, CONTRACT_INNER)
            rest = rest - piece.astype(jnp.float32)
        return total, place // per_row


def gradient_kernel(count, *refs):
    operands = refs[: 2 * count]
    vector_ref = refs[2 * count]
    out_refs = refs[2 * count + 1 : 3 * count + 1]
    share_ref, up_share_ref = refs[3 * count + 1 : 3 * count + 3]
    scratch = refs[3 * count + 3 :]
    sums = []
    for w in range(count):
        held = scratch[w * QUAD_REFS : (w + 1) * QUAD_REFS]
        sums.append(QuadSum(operands[2 * w], operands[2 * w + 1], held[:8], held[8:]))
    vector = VectorSum(vector_ref, *scratch[count * QUAD_REFS :])
    one = sums[0]
    y, z, x, c = one.y, one.z, one.x, one.c
    partners = [
        (None, one.device(y, z, x, 1 - c)),
        (None, one.device(1 - y, z, x, c)),
        (None, one.device(1 - y, z, x, 1 - c)),
        (None, one.device(y, z, 1 - x, c)),
    ]
    partners += [(None, one.device(y, (z + step) % PLANES, x, c)) for step in range(1, PLANES)]
    meet(partners, len(partners))
    vector.start(0)
    for each in sums:
        each.share_left()
        each.share_right()
    stage = 0
    for each in sums:
        each.relay_left()
        each.multiply()
        each.halve()
        vector.take(stage)
        stage += 1
        if stage < 4:
            vector.start(stage)
    for each in sums:
        each.spread()
    for each in sums:
        each.collect()
    for each, out_ref in zip(sums, out_refs):
        each.deliver(out_ref)
    total = vector.partial[3]
    shares, _ = vector.own_share(total[:8], out_refs[0].shape[0] // 4)
    share_ref[...] = shares
    up_shares, row = vector.own_share(total[8:16], out_refs[0].shape[0])
    keep = lax.broadcasted_iota(jnp.int32, up_shares.shape, 0) == row
    up_share_ref[...] = jnp.sum(jnp.where(keep, up_shares, 0.0), axis=0, keepdims=True)
    for each in sums:
        each.finish()
    vector.finish()


def weight_gradients(pairs, vectors):
    frame_count = pairs[0][0].shape[0]
    operands, outs, scratch = [], [], []
    for left, right in pairs:
        operands += [left, right]
        outs.append(jax.ShapeDtypeStruct((left.shape[1] // 32, right.shape[1]), jnp.float32))
        scratch += quad_scratch(frame_count, left.shape[1], right.shape[1])
    outs += [
        jax.ShapeDtypeStruct((8, 128), jnp.float32),
        jax.ShapeDtypeStruct((1, 128), jnp.float32),
    ]
    scratch += [
        pltpu.VMEM((4,) + vectors.shape, jnp.float32),
        pltpu.VMEM((6,) + vectors.shape, jnp.float32),
        pltpu.SemaphoreType.DMA((6,)),
        pltpu.SemaphoreType.DMA((6,)),
    ]
    return pl.pallas_call(
        functools.partial(gradient_kernel, len(pairs)),
        out_shape=tuple(outs),
        in_specs=[IN_VMEM] * (len(operands) + 1),
        out_specs=(IN_VMEM,) * len(outs),
        scratch_shapes=scratch,
        compiler_params=pltpu.CompilerParams(
            collective_id=2, has_side_effects=True, vmem_limit_bytes=VMEM_BYTES
        ),
    )(*operands, vectors)


def layer_step(
    frames,
    segment_ids,
    qkv_weight,
    query_bias,
    value_bias,
    out_weight,
    out_bias,
    norm1_gain,
    norm1_shift,
    up_weight,
    up_bias,
    down_weight,
    down_bias,
    norm2_gain,
    norm2_shift,
    cotangent,
):
    inputs = frames[0]
    frame_count, width = inputs.shape
    low, wide = jnp.bfloat16, jnp.float32
    ids_column = segment_ids.reshape(frame_count, 1)
    attended, log_total, every_ids, projected = pl.pallas_call(
        attend_kernel,
        out_shape=(
            jax.ShapeDtypeStruct((frame_count, width), wide),
            jax.ShapeDtypeStruct((frame_count, 2 * HALF), wide),
            jax.ShapeDtypeStruct((8, BLOCKS * frame_count), wide),
            jax.ShapeDtypeStruct((BLOCKS, frame_count, 3 * width), low),
        ),
        in_specs=[IN_VMEM] * 6,
        out_specs=(IN_VMEM, IN_VMEM, IN_VMEM, IN_PLACE),
        scratch_shapes=[
            pltpu.VMEM((BLOCKS, frame_count + 16, width), low),
            pltpu.VMEM((BLOCKS, frame_count, 3 * width), low),
            pltpu.VMEM((frame_count, BLOCKS * frame_count), wide),
            pltpu.SemaphoreType.DMA((2, 4, BLOCKS)),
            pltpu.SemaphoreType.DMA((2, BLOCKS)),
            pltpu.SemaphoreType.DMA((PLANES,)),
        ],
        compiler_params=pltpu.CompilerParams(
            collective_id=0, has_side_effects=True, vmem_limit_bytes=VMEM_BYTES
        ),
    )(inputs, segment_ids, ids_column, qkv_weight, query_bias[None], value_bias[None])
    context = attended.astype(low)
    resid_one = (
        inputs.astype(wide) + jnp.dot(context, out_weight, preferred_element_type=wide) + out_bias
    )
    hidden, normed_one, inverse_one = layer_norm(resid_one, norm1_gain, norm1_shift)
    hidden_low = hidden.astype(low)
    pre_act = jnp.dot(hidden_low, up_weight, preferred_element_type=wide) + up_bias
    act_low = jax.nn.gelu(pre_act, approximate=False).astype(low)
    resid_two = hidden + jnp.dot(act_low, down_weight, preferred_element_type=wide) + down_bias
    output, normed_two, inverse_two = layer_norm(resid_two, norm2_gain, norm2_shift)
    upstream = cotangent[0].astype(wide)
    second_grad, gain_two_grad, shift_two_grad = norm_back(
        upstream, normed_two, inverse_two, norm2_gain
    )
    second_low = second_grad.astype(low)
    pre_grad = jnp.einsum(
        "td,fd->tf", second_low, down_weight, preferred_element_type=wide
    ) * gelu_slope(pre_act)
    pre_low = pre_grad.astype(low)
    hidden_grad = second_grad + jnp.einsum(
        "tf,df->td", pre_low, up_weight, preferred_element_type=wide
    )
    first_grad, gain_one_grad, shift_one_grad = norm_back(
        hidden_grad, normed_one, inverse_one, norm1_gain
    )
    first_low = first_grad.astype(low)
    context_grad = jnp.einsum("te,de->td", first_low, out_weight, preferred_element_type=wide).astype(
        low
    )
    proj_grad = pl.pallas_call(
        attend_back_kernel,
        out_shape=jax.ShapeDtypeStruct((frame_count, 3 * width), low),
        in_specs=[IN_VMEM] * 6,
        out_specs=IN_VMEM,
        scratch_shapes=[
            pltpu.VMEM((BLOCKS, frame_count, width), low),
            pltpu.VMEM((BLOCKS, 32, frame_count), wide),
            pltpu.VMEM((frame_count, BLOCKS * frame_count), wide),
            pltpu.VMEM((frame_count, 2 * HALF), wide),
            pltpu.SemaphoreType.DMA((3, 4, BLOCKS)),
            pltpu.SemaphoreType.DMA((3, BLOCKS)),
        ],
        compiler_params=pltpu.CompilerParams(
            collective_id=1, has_side_effects=True, vmem_limit_bytes=VMEM_BYTES
        ),
    )(context_grad, attended, log_total, every_ids, ids_column, projected)
    input_grad = (
        jnp.einsum("te,de->td", proj_grad, qkv_weight, preferred_element_type=wide) + first_grad
    )
    proj_sums = jnp.sum(proj_grad.astype(wide), axis=0)
    vectors = jnp.concatenate(
        [
            jnp.stack(
                [
                    proj_sums[:width],
                    proj_sums[2 * width :],
                    jnp.sum(first_grad, axis=0),
                    gain_one_grad,
                    shift_one_grad,
                    jnp.sum(second_grad, axis=0),
                    gain_two_grad,
                    shift_two_grad,
                ]
            ),
            jnp.sum(pre_grad, axis=0).reshape(4, width),
            jnp.zeros((4, width), wide),
        ],
        axis=0,
    )
    down_grad, up_grad, out_grad, qkv_grad, shares, up_share = weight_gradients(
        [
            (act_low, second_low),
            (hidden_low, pre_low),
            (context, first_low),
            (inputs, proj_grad),
        ],
        vectors,
    )
    share = down_grad.shape[0] // 4
    return (
        output.astype(low)[None],
        input_grad[None],
        qkv_grad,
        shares[0, :share],
        shares[1, :share],
        out_grad,
        shares[2, :share],
        shares[3, :share],
        shares[4, :share],
        up_grad,
        up_share[0, : 4 * share],
        down_grad,
        shares[5, :share],
        shares[6, :share],
        shares[7, :share],
    )


def solution(mesh):
    chosen = layer_step if dict(mesh.shape) == {"rows": 2, "seq": 16} else shards
    in_specs = (
        P("rows", "seq", None),
        P("rows", "seq"),
        P(),
        P(),
        P(),
        P(),
        P(),
        P(),
        P(),
        P(),
        P(),
        P(),
        P(),
        P(),
        P(),
        P("rows", "seq", None),
    )
    out_specs = (
        P("rows", "seq", None),
        P("rows", "seq", None),
        P(("rows", "seq"), None),
        P(("rows", "seq")),
        P(("rows", "seq")),
        P(("rows", "seq"), None),
        P(("rows", "seq")),
        P(("rows", "seq")),
        P(("rows", "seq")),
        P(("rows", "seq"), None),
        P(("rows", "seq")),
        P(("rows", "seq"), None),
        P(("rows", "seq")),
        P(("rows", "seq")),
        P(("rows", "seq")),
    )
    return jax.shard_map(chosen, mesh=mesh, in_specs=in_specs, out_specs=out_specs, check_vma=False)
```

```python
import functools
import math
import typing

import jax
import jax.numpy as jnp
from jax import lax
from jax.experimental import pallas as pl
from jax.experimental.pallas import tpu as pltpu
from jax.sharding import PartitionSpec as P

HEADS = 12
HEAD_DIM = 64


norm_eps = 1e-05
mask_fill = -1e30


def shortened(shard):

    def short(part):
        return part.astype(jnp.bfloat16) if part.dtype == jnp.float32 else part

    return jax.tree.map(short, shard)


def passed_along(value, axis, steps):
    count = lax.axis_size(axis)
    pairs = [(source, (source + steps) % count) for source in range(count)]
    return lax.ppermute(value, axis, pairs)


def layer_norm(resid, gain, shift):
    centred = resid - jnp.mean(resid, axis=-1, keepdims=True)
    inv_std = lax.rsqrt(jnp.mean(centred * centred, axis=-1, keepdims=True) + norm_eps)
    normed = centred * inv_std
    return (normed * gain + shift, normed, inv_std)


def norm_back(upstream, normed, inv_std, gain):
    scaled = upstream * gain
    first_mean = jnp.mean(scaled, axis=-1, keepdims=True)
    second_mean = jnp.mean(scaled * normed, axis=-1, keepdims=True)
    grad_in = inv_std * (scaled - first_mean - normed * second_mean)
    return (grad_in, jnp.sum(upstream * normed, axis=0), jnp.sum(upstream, axis=0))


def gelu_slope(pre_act):
    normal_cdf = 0.5 * (1.0 + lax.erf(pre_act * 0.5**0.5))
    normal_pdf = jnp.exp(-0.5 * pre_act * pre_act) * (2.0 * math.pi) ** (-0.5)
    return normal_cdf + pre_act * normal_pdf


def head_groups(head_count):
    return [(0, head_count, 1)]


def pass_keys(blocks):
    return jax.tree.map(
        lambda part, own: part.astype(own.dtype), passed_along(shortened(blocks), "seq", 1), blocks
    )


def pass_again(blocks):
    return jax.tree.map(
        lambda part, own: part.astype(own.dtype), passed_along(shortened(blocks), "seq", 1), blocks
    )


def pass_grads(blocks):
    return (
        passed_along(blocks[0].astype(jnp.bfloat16), "seq", 1).astype(jnp.float32),
        passed_along(blocks[1].astype(jnp.bfloat16), "seq", 1).astype(jnp.float32),
    )


def block_scores(query_part, key_part, query_ids, key_ids):
    scores = jnp.einsum(
        "qhe,khe->hqk", query_part, key_part, preferred_element_type=jnp.float32
    ) * HEAD_DIM ** (-0.5)
    return jnp.where((query_ids[:, None] == key_ids[None, :])[None], scores, mask_fill)


def attend_block(carried, query_part, key_part, value_part, query_ids, key_ids):
    run_max, run_total, run_acc = carried
    scores = block_scores(query_part, key_part, query_ids, key_ids)
    new_max = jnp.maximum(run_max, jnp.max(scores, axis=-1))
    weights = jnp.exp(scores - new_max[:, :, None])
    factor = jnp.exp(run_max - new_max)
    new_total = run_total * factor + jnp.sum(weights, axis=-1)
    update = jnp.einsum(
        "hqk,khe->qhe", weights.astype(jnp.bfloat16), value_part, preferred_element_type=jnp.float32
    )
    return (new_max, new_total, run_acc * factor.T[:, :, None] + update)


def grad_block(
    carried,
    query_part,
    key_part,
    value_part,
    query_ids,
    key_ids,
    context_part,
    log_part,
    delta_part,
):
    query_acc, key_acc, value_acc = carried
    scores = block_scores(query_part, key_part, query_ids, key_ids)
    probs = jnp.exp(scores - log_part[:, :, None])
    prob_grad = jnp.einsum(
        "qhe,khe->hqk", context_part, value_part, preferred_element_type=jnp.float32
    )
    score_grad = (probs * (prob_grad - delta_part[:, :, None])).astype(jnp.bfloat16)
    scale = HEAD_DIM ** (-0.5)
    query_acc = query_acc + scale * jnp.einsum(
        "hqk,khe->qhe", score_grad, key_part, preferred_element_type=jnp.float32
    )
    key_acc = key_acc + scale * jnp.einsum(
        "hqk,qhe->khe", score_grad, query_part, preferred_element_type=jnp.float32
    )
    value_acc = value_acc + jnp.einsum(
        "hqk,qhe->khe", probs.astype(jnp.bfloat16), context_part, preferred_element_type=jnp.float32
    )
    return (query_acc, key_acc, value_acc)


def forward_cycle(
    query_heads, key_heads, value_heads, local_ids, every_id, cycle_place, cycle_size
):
    frame_count, head_count, head_width = query_heads.shape
    grouping = head_groups(head_count)
    states = []
    blocks = []
    for head_first, head_last, direction in grouping:
        head_span = head_last - head_first
        initial = (
            jnp.full((head_span, frame_count), mask_fill, jnp.float32),
            jnp.zeros((head_span, frame_count), jnp.float32),
            jnp.zeros((frame_count, head_span, head_width), jnp.float32),
        )
        states.append(
            attend_block(initial, query_heads, key_heads, value_heads, local_ids, local_ids)
        )
        blocks.append((key_heads, value_heads))

    def forward_cycle_turn(turn_index, cycle_carry):
        old_states, old_blocks = cycle_carry
        new_states = []
        new_blocks = []
        for group_info, part_state, part_block in zip(grouping, old_states, old_blocks):
            head_first, head_last, direction = group_info
            part_block = pass_keys(part_block)
            source_index = (cycle_place - direction * turn_index) % cycle_size
            key_ids = lax.dynamic_slice_in_dim(every_id, source_index * frame_count, frame_count)
            new_states.append(
                attend_block(
                    part_state, query_heads, part_block[0], part_block[1], local_ids, key_ids
                )
            )
            new_blocks.append(part_block)
        return (new_states, new_blocks)

    states, blocks = lax.fori_loop(1, cycle_size, forward_cycle_turn, (states, blocks))
    maxima = jnp.concatenate([part_state[0] for part_state in states], axis=0)
    totals = jnp.concatenate([part_state[1] for part_state in states], axis=0)
    sums_all = jnp.concatenate([part_state[2] for part_state in states], axis=1)
    attended = sums_all / totals.T[:, :, None]
    return (attended, maxima + jnp.log(totals))


def backward_cycle(
    query_heads,
    key_heads,
    value_heads,
    local_ids,
    every_id,
    context_heads,
    log_total,
    row_delta,
    cycle_place,
    cycle_size,
):
    frame_count, head_count, head_width = query_heads.shape
    grouping = head_groups(head_count)
    initial = []
    for head_first, head_last, direction in grouping:
        zero_part = jnp.zeros((frame_count, head_last - head_first, head_width), jnp.float32)
        initial.append((zero_part, (key_heads, value_heads), (zero_part, zero_part)))

    def backward_cycle_turn(turn_index, cycle_carry):
        new_carry = []
        for group_info, part_carry in zip(grouping, cycle_carry):
            head_first, head_last, direction = group_info
            query_acc, part_block, part_grads = part_carry
            source_index = (cycle_place - direction * turn_index) % cycle_size
            key_ids = lax.dynamic_slice_in_dim(every_id, source_index * frame_count, frame_count)
            query_acc, key_acc, value_acc = grad_block(
                (query_acc, part_grads[0], part_grads[1]),
                query_heads,
                part_block[0],
                part_block[1],
                local_ids,
                key_ids,
                context_heads,
                log_total,
                row_delta,
            )
            part_grads = pass_grads((key_acc, value_acc))
            part_block = pass_again(part_block)
            new_carry.append((query_acc, part_block, part_grads))
        return new_carry

    final = lax.fori_loop(0, cycle_size, backward_cycle_turn, initial)
    query_grad = jnp.concatenate([part_carry[0] for part_carry in final], axis=1)
    key_grad = jnp.concatenate([part_carry[2][0] for part_carry in final], axis=1)
    value_grad = jnp.concatenate([part_carry[2][1] for part_carry in final], axis=1)
    return (query_grad, key_grad, value_grad)


def shards(
    frames,
    segment_ids,
    qkv_weight,
    query_bias,
    value_bias,
    out_weight,
    out_bias,
    norm1_gain,
    norm1_shift,
    up_weight,
    up_bias,
    down_weight,
    down_bias,
    norm2_gain,
    norm2_shift,
    cotangent,
):
    inputs = frames[0]
    local_ids = segment_ids[0]
    frame_count, model_width = inputs.shape
    cycle_size = lax.axis_size("seq")
    cycle_place = lax.axis_index("seq")
    every_id = lax.all_gather(segment_ids, "seq", axis=1, tiled=True)[0]
    head_shape = (frame_count, HEADS, HEAD_DIM)
    projected = jnp.dot(inputs, qkv_weight, preferred_element_type=jnp.float32)
    query_heads = (projected[:, :model_width] + query_bias).astype(jnp.bfloat16).reshape(head_shape)
    key_heads = projected[:, model_width : 2 * model_width].astype(jnp.bfloat16).reshape(head_shape)
    value_heads = (
        (projected[:, 2 * model_width :] + value_bias).astype(jnp.bfloat16).reshape(head_shape)
    )
    attended, log_total = forward_cycle(
        query_heads, key_heads, value_heads, local_ids, every_id, cycle_place, cycle_size
    )
    context = attended.astype(jnp.bfloat16).reshape(frame_count, model_width)
    resid_one = (
        inputs.astype(jnp.float32)
        + jnp.dot(context, out_weight, preferred_element_type=jnp.float32)
        + out_bias
    )
    hidden, normed_one, inverse_one = layer_norm(resid_one, norm1_gain, norm1_shift)
    hidden_low = hidden.astype(jnp.bfloat16)
    pre_act = jnp.dot(hidden_low, up_weight, preferred_element_type=jnp.float32) + up_bias
    act_low = jax.nn.gelu(pre_act, approximate=False).astype(jnp.bfloat16)
    resid_two = (
        hidden + jnp.dot(act_low, down_weight, preferred_element_type=jnp.float32) + down_bias
    )
    output, normed_two, inverse_two = layer_norm(resid_two, norm2_gain, norm2_shift)
    upstream = cotangent[0].astype(jnp.float32)
    second_grad, gain_two_grad, shift_two_grad = norm_back(
        upstream, normed_two, inverse_two, norm2_gain
    )
    second_low = second_grad.astype(jnp.bfloat16)
    down_grad = jnp.einsum("tf,td->fd", act_low, second_low, preferred_element_type=jnp.float32)
    pre_grad = jnp.einsum(
        "td,fd->tf", second_low, down_weight, preferred_element_type=jnp.float32
    ) * gelu_slope(pre_act)
    pre_low = pre_grad.astype(jnp.bfloat16)
    up_grad = jnp.einsum("td,tf->df", hidden_low, pre_low, preferred_element_type=jnp.float32)
    hidden_grad = second_grad + jnp.einsum(
        "tf,df->td", pre_low, up_weight, preferred_element_type=jnp.float32
    )
    first_grad, gain_one_grad, shift_one_grad = norm_back(
        hidden_grad, normed_one, inverse_one, norm1_gain
    )
    first_low = first_grad.astype(jnp.bfloat16)
    out_grad = jnp.einsum("td,te->de", context, first_low, preferred_element_type=jnp.float32)
    context_grad = (
        jnp.einsum("te,de->td", first_low, out_weight, preferred_element_type=jnp.float32)
        .astype(jnp.bfloat16)
        .reshape(head_shape)
    )
    row_delta = jnp.einsum("qhe,qhe->hq", context_grad.astype(jnp.float32), attended)
    query_grad, key_grad, value_grad = backward_cycle(
        query_heads,
        key_heads,
        value_heads,
        local_ids,
        every_id,
        context_grad,
        log_total,
        row_delta,
        cycle_place,
        cycle_size,
    )
    query_low = query_grad.astype(jnp.bfloat16).reshape(frame_count, model_width)
    key_low = key_grad.astype(jnp.bfloat16).reshape(frame_count, model_width)
    value_low = value_grad.astype(jnp.bfloat16).reshape(frame_count, model_width)
    proj_grad = jnp.concatenate([query_low, key_low, value_low], axis=1)
    qkv_grad = jnp.einsum("td,te->de", inputs, proj_grad, preferred_element_type=jnp.float32)
    input_grad = (
        jnp.einsum("te,de->td", proj_grad, qkv_weight, preferred_element_type=jnp.float32)
        + first_grad
    )
    summed = (
        lax.psum_scatter(qkv_grad, ("rows", "seq"), scatter_dimension=0, tiled=True),
        lax.psum_scatter(
            jnp.sum(query_low.astype(jnp.float32), axis=0),
            ("rows", "seq"),
            scatter_dimension=0,
            tiled=True,
        ),
        lax.psum_scatter(
            jnp.sum(value_low.astype(jnp.float32), axis=0),
            ("rows", "seq"),
            scatter_dimension=0,
            tiled=True,
        ),
        lax.psum_scatter(out_grad, ("rows", "seq"), scatter_dimension=0, tiled=True),
        lax.psum_scatter(
            jnp.sum(first_grad, axis=0), ("rows", "seq"), scatter_dimension=0, tiled=True
        ),
        lax.psum_scatter(gain_one_grad, ("rows", "seq"), scatter_dimension=0, tiled=True),
        lax.psum_scatter(shift_one_grad, ("rows", "seq"), scatter_dimension=0, tiled=True),
        lax.psum_scatter(up_grad, ("rows", "seq"), scatter_dimension=0, tiled=True),
        lax.psum_scatter(
            jnp.sum(pre_grad, axis=0), ("rows", "seq"), scatter_dimension=0, tiled=True
        ),
        lax.psum_scatter(down_grad, ("rows", "seq"), scatter_dimension=0, tiled=True),
        lax.psum_scatter(
            jnp.sum(second_grad, axis=0), ("rows", "seq"), scatter_dimension=0, tiled=True
        ),
        lax.psum_scatter(gain_two_grad, ("rows", "seq"), scatter_dimension=0, tiled=True),
        lax.psum_scatter(shift_two_grad, ("rows", "seq"), scatter_dimension=0, tiled=True),
    )
    return (
        output.astype(jnp.bfloat16)[None],
        input_grad[None],
        summed[0],
        summed[1],
        summed[2],
        summed[3],
        summed[4],
        summed[5],
        summed[6],
        summed[7],
        summed[8],
        summed[9],
        summed[10],
        summed[11],
        summed[12],
    )


HALF = HEAD_DIM
PAIRS = HEADS // 2
CONTRACT_LAST = (((1,), (1,)), ((), ()))
CONTRACT_INNER = (((1,), (0,)), ((), ()))
CONTRACT_FIRST = (((0,), (0,)), ((), ()))
IN_VMEM = pl.BlockSpec(memory_space=pltpu.VMEM)
IN_PLACE = pl.BlockSpec(memory_space=pl.ANY)
MESH_ID = pl.DeviceIdType.MESH
VMEM_BYTES = 60 << 20
BLOCKS = 16
PLANES = 4


def product(left, right, dims):
    return lax.dot_general(left, right, dims, preferred_element_type=jnp.float32)


def where_am_i():
    row = lax.axis_index("rows")
    place = lax.axis_index("seq")
    return row, place // 4, place // 2 % 2, place % 2


def meet(partners, count):
    barrier = pltpu.get_barrier_semaphore()
    for present, target in partners:

        def signal(target=target):
            pl.semaphore_signal(barrier, inc=1, device_id=target, device_id_type=MESH_ID)

        if present is None:
            signal()
        else:
            pl.when(present)(signal)
    pl.semaphore_wait(barrier, count)


class RowGather:
    UP, DOWN, ACROSS, BESIDE = range(4)

    def __init__(self, parts, send_sem, recv_sem):
        self.parts = parts
        self.send_sem = send_sem
        self.recv_sem = recv_sem
        self.row, self.z, self.x, self.c = where_am_i()
        self.sent = []

    def device(self, z, x, c):
        return (self.row, z * 4 + x * 2 + c)

    def targets(self):
        return (
            self.device(self.z + 1, self.x, self.c),
            self.device(self.z - 1, self.x, self.c),
            self.device(self.z, 1 - self.x, self.c),
            self.device(self.z, self.x, 1 - self.c),
        )

    def meet(self):
        up, down, across, beside = self.targets()
        has_up = self.z < PLANES - 1
        has_down = self.z > 0
        meet(
            [(has_up, up), (has_down, down), (None, across), (None, beside)],
            2 + has_up.astype(jnp.int32) + has_down.astype(jnp.int32),
        )

    def copy(self, part, block, way):
        ref, first, rows = self.parts[part]
        piece = ref.at[block, pl.ds(first, rows)]
        return pltpu.make_async_remote_copy(
            src_ref=piece,
            dst_ref=piece,
            send_sem=self.send_sem.at[part, way, block],
            recv_sem=self.recv_sem.at[part, block],
            device_id=self.targets()[way],
            device_id_type=MESH_ID,
        )

    def send(self, part, block, way, present=None):
        self.sent.append((part, block, way, present))
        if present is None:
            self.copy(part, block, way).start()
        else:
            pl.when(present)(lambda: self.copy(part, block, way).start())

    def arrived(self, part, block):
        self.copy(part, block, self.BESIDE).wait_recv()

    def finish(self):
        for part, block, way, present in self.sent:
            if present is None:
                self.copy(part, block, way).wait_send()
            else:
                pl.when(present)(
                    lambda part=part, block=block, way=way: self.copy(part, block, way).wait_send()
                )

    def relay(self, part, z, x, ways, present):
        block = z * 4 + x * 2 + self.c

        def wait():
            self.arrived(part, block)

        if present is None:
            wait()
        else:
            pl.when(present)(wait)
        for way, also in ways:
            both = present if also is None else (also if present is None else present & also)
            self.send(part, block, way, both)

    def own(self, across_first, line_parts):
        z, x, c = self.z, self.x, self.c
        mine = z * 4 + x * 2 + c
        has_up, has_down = z < PLANES - 1, z > 0
        for part in across_first:
            self.send(part, mine, self.ACROSS)
        for part in list(line_parts) + list(across_first):
            self.send(part, mine, self.UP, has_up)
            self.send(part, mine, self.DOWN, has_down)
        for part in line_parts:
            self.send(part, mine, self.ACROSS)
        for part in list(across_first) + list(line_parts):
            self.send(part, mine, self.BESIDE)

    def first_round(self, across_first, line_parts):
        z, x = self.z, self.x
        has_up, has_down = z < PLANES - 1, z > 0
        up, down, across, beside = (
            (self.UP, has_up),
            (self.DOWN, has_down),
            (self.ACROSS, None),
            (self.BESIDE, None),
        )
        for part in across_first:
            self.relay(part, z, 1 - x, [up, down, beside], None)
        for part in line_parts:
            self.relay(part, z - 1, x, [up, across, beside], has_down)
            self.relay(part, z + 1, x, [down, across, beside], has_up)
        for part in across_first:
            self.relay(part, z - 1, x, [up, beside], has_down)
            self.relay(part, z + 1, x, [down, beside], has_up)
        for part in line_parts:
            self.relay(part, z, 1 - x, [beside], None)

    def plane_done(self, z, parts, present=None):
        def wait():
            for x in range(2):
                for part in parts:
                    self.arrived(part, z * 4 + x * 2 + 1 - self.c)

        if present is None:
            wait()
        else:
            pl.when(present)(wait)

    def second_round(self, across_first, line_parts):
        z, x = self.z, self.x
        has_up, has_down = z < PLANES - 1, z > 0
        up, down, beside = (self.UP, has_up), (self.DOWN, has_down), (self.BESIDE, None)
        for part in across_first:
            self.relay(part, z - 1, 1 - x, [up, beside], has_down)
            self.relay(part, z + 1, 1 - x, [down, beside], has_up)
        for part in line_parts:
            self.relay(part, z - 1, 1 - x, [beside], has_down)
            self.relay(part, z + 1, 1 - x, [beside], has_up)

    def far_plane(self):
        return (self.z + 2) % PLANES

    def third_round(self, across_first, line_parts):
        far, x = self.far_plane(), self.x
        across, beside = (self.ACROSS, None), (self.BESIDE, None)
        for part in line_parts:
            self.relay(part, far, x, [across, beside], None)
        for part in across_first:
            self.relay(part, far, x, [beside], None)
            self.relay(part, far, 1 - x, [beside], None)
        for part in line_parts:
            self.relay(part, far, 1 - x, [beside], None)


class VectorSum:
    def __init__(self, ref, partial, arrived, send_sem, recv_sem):
        self.ref, self.partial, self.arrived = ref, partial, arrived
        self.send_sem, self.recv_sem = send_sem, recv_sem
        self.y, self.z, self.x, self.c = where_am_i()
        self.flying = []

    def device(self, y, z, x, c):
        return (y, z * 4 + x * 2 + c)

    def copy(self, source, slot, device):
        return pltpu.make_async_remote_copy(
            src_ref=source,
            dst_ref=self.arrived.at[slot],
            send_sem=self.send_sem.at[slot],
            recv_sem=self.recv_sem.at[slot],
            device_id=device,
            device_id_type=MESH_ID,
        )

    def start(self, stage):
        y, z, x, c = self.y, self.z, self.x, self.c
        source = self.ref if stage == 0 else self.partial.at[stage - 1]
        if stage < 3:
            device = (
                self.device(y, z, x, 1 - c),
                self.device(1 - y, z, x, c),
                self.device(y, z, 1 - x, c),
            )[stage]
            copy = self.copy(source, stage, device)
            copy.start()
            self.flying.append(copy)
        else:
            for step in range(1, PLANES):
                copy = self.copy(
                    source, 2 + step, self.device(y, (z + step) % PLANES, x, c)
                )
                copy.start()
                self.flying.append(copy)

    def take(self, stage):
        y, z, x, c = self.y, self.z, self.x, self.c
        total = self.ref[...] if stage == 0 else self.partial[stage - 1]
        for slot in (stage,) if stage < 3 else (3, 4, 5):
            self.copy(self.ref, slot, self.device(y, z, x, 1 - c)).wait_recv()
            total = total + self.arrived[slot]
        self.partial[stage] = total

    def finish(self):
        for copy in self.flying:
            copy.wait_send()

    def own_share(self, rows, share):
        width = self.ref.shape[1]
        place = self.y * 16 + self.z * 4 + self.x * 2 + self.c
        per_row = width // share
        offset = place % per_row * share
        row_index = lax.broadcasted_iota(jnp.int32, (width, 128), 0)
        column_index = lax.broadcasted_iota(jnp.int32, (width, 128), 1)
        picked = jnp.where(
            (row_index == column_index + offset) & (column_index < share), 1.0, 0.0
        ).astype(jnp.bfloat16)
        rest = rows
        total = jnp.zeros((rows.shape[0], 128), jnp.float32)
        for _ in range(3):
            piece = rest.astype(jnp.bfloat16)
            total = total + product(piece, picked, CONTRACT_INNER)
            rest = rest - piece.astype(jnp.float32)
        return total, place // per_row


STEP = 384


class Shared:
    def __init__(self, left, held, send_sem, recv_sem):
        self.left, self.held = left, held
        self.send_sem, self.recv_sem = send_sem, recv_sem
        self.y, self.z, self.x, self.c = where_am_i()
        self.quad = self.y * 2 + self.c
        self.peer = (1 - self.y) * 2 + self.c
        self.half = held.shape[2]
        self.flying = []

    def part(self, y):
        return self.left.at[:, pl.ds(pl.multiple_of(y * self.half, 128), self.half)]

    def fly(self, source, slot, which, device):
        copy = pltpu.make_async_remote_copy(
            src_ref=source,
            dst_ref=self.held.at[slot],
            send_sem=self.send_sem.at[which],
            recv_sem=self.recv_sem.at[slot],
            device_id=device,
            device_id_type=MESH_ID,
        )
        copy.start()
        self.flying.append(copy)

    def beside(self):
        return (self.y, self.z * 4 + self.x * 2 + 1 - self.c)

    def share(self):
        y, z, x, c = self.y, self.z, self.x, self.c
        self.fly(self.part(1 - y), self.quad, 0, (1 - y, z * 4 + x * 2 + c))
        self.fly(self.part(y), self.quad, 1, self.beside())
        self.held[self.quad] = self.part(y)[...]

    def landed(self, slot):
        pltpu.make_async_remote_copy(
            src_ref=self.held.at[slot],
            dst_ref=self.held.at[slot],
            send_sem=self.send_sem.at[0],
            recv_sem=self.recv_sem.at[slot],
            device_id=self.beside(),
            device_id_type=MESH_ID,
        ).wait_recv()

    def relay(self):
        self.landed(self.peer)
        self.fly(self.held.at[self.peer], self.peer, 2, self.beside())

    def complete(self):
        self.landed(self.y * 2 + 1 - self.c)
        self.landed((1 - self.y) * 2 + 1 - self.c)


class Piece:
    def __init__(self, shared, right, base, stride, out, buffers):
        self.shared, self.right, self.base, self.stride, self.out = shared, right, base, stride, out
        (
            self.rights, self.whole, self.x_in, self.z_in, self.last,
            self.send_sem, self.recv_sem, self.x_sem, self.z_send, self.z_recv, self.side_sem,
        ) = buffers
        self.y, self.z, self.x, self.c = where_am_i()
        self.quad = self.y * 2 + self.c
        self.flying = []

    def device(self, y, z, x, c):
        return (y, z * 4 + x * 2 + c)

    def columns(self, c):
        return pl.ds(pl.multiple_of(self.base + c * self.stride, 128), STEP)

    def fly(self, source, target, send_sem, recv_sem, device):
        copy = pltpu.make_async_remote_copy(
            src_ref=source,
            dst_ref=target,
            send_sem=send_sem,
            recv_sem=recv_sem,
            device_id=device,
            device_id_type=MESH_ID,
        )
        copy.start()
        self.flying.append(copy)

    def landed(self, ref, sem):
        pltpu.make_async_remote_copy(
            src_ref=ref,
            dst_ref=ref,
            send_sem=self.send_sem.at[0],
            recv_sem=sem,
            device_id=self.device(self.y, self.z, self.x, 1 - self.c),
            device_id_type=MESH_ID,
        ).wait_recv()

    def share(self):
        y, z, x, c, quad = self.y, self.z, self.x, self.c, self.quad
        mine, other = self.right.at[:, self.columns(c)], self.right.at[:, self.columns(1 - c)]
        target, arrival = self.rights.at[quad], self.recv_sem.at[quad]
        self.fly(mine, target, self.send_sem.at[0], arrival, self.device(1 - y, z, x, c))
        self.fly(other, target, self.send_sem.at[1], arrival, self.device(1 - y, z, x, 1 - c))
        self.fly(other, target, self.send_sem.at[2], arrival, self.device(y, z, x, 1 - c))
        self.rights[quad] = mine[...]

    def multiply(self):
        y, c = self.y, self.c
        for other in (y * 2 + 1 - c, (1 - y) * 2 + c, (1 - y) * 2 + 1 - c):
            self.landed(self.rights.at[other], self.recv_sem.at[other])
        held = self.shared.held
        tokens = held.shape[0] * held.shape[1]
        planes, _, rows, _ = self.whole.shape
        right = self.rights[...].reshape(tokens, STEP)
        if self.shared.half > STEP:

            def one(i, carry):
                left = held[:, :, pl.ds(pl.multiple_of(i * STEP, 128), STEP)]
                part = product(left.reshape(tokens, STEP), right, CONTRACT_FIRST)
                self.whole[i] = part.astype(jnp.bfloat16).reshape(2, rows, STEP)
                return carry

            lax.fori_loop(0, self.shared.half // STEP, one, 0)
        else:
            part = product(held[...].reshape(tokens, STEP), right, CONTRACT_FIRST)
            self.whole[...] = part.astype(jnp.bfloat16).reshape(planes, 2, rows, STEP)
        self.fly(
            self.whole.at[:, 1 - self.x], self.x_in, self.x_sem.at[0], self.x_sem.at[1],
            self.device(self.y, self.z, 1 - self.x, self.c),
        )

    def spread(self):
        self.landed(self.x_in, self.x_sem.at[1])
        self.whole[:, self.x] = (
            self.whole[:, self.x].astype(jnp.float32) + self.x_in[...].astype(jnp.float32)
        ).astype(jnp.bfloat16)
        for step in range(1, PLANES):
            target = (self.z + step) % PLANES
            self.fly(
                self.whole.at[target, self.x], self.z_in.at[self.z], self.z_send.at[step],
                self.z_recv.at[self.z], self.device(self.y, target, self.x, self.c),
            )

    def collect(self):
        total = self.whole[self.z, self.x].astype(jnp.float32)
        for step in range(1, PLANES):
            source = (self.z + step) % PLANES
            self.landed(self.z_in.at[source], self.z_recv.at[source])
            total = total + self.z_in[source].astype(jnp.float32)
        self.last[...] = total
        rows = self.last.shape[0] // 2
        self.fly(
            self.last.at[pl.ds(pl.multiple_of((1 - self.c) * rows, 8), rows)],
            self.out.at[:, self.columns(self.c)],
            self.side_sem.at[0], self.side_sem.at[1],
            self.device(self.y, self.z, self.x, 1 - self.c),
        )
        self.out[:, self.columns(self.c)] = self.last[
            pl.ds(pl.multiple_of(self.c * rows, 8), rows), :
        ]

    def delivered(self):
        self.landed(self.out.at[:, self.columns(1 - self.c)], self.side_sem.at[1])


def shared_scratch(frame_count, left_width):
    return [
        pltpu.VMEM((4, frame_count, left_width // 2), jnp.bfloat16),
        pltpu.SemaphoreType.DMA((3,)),
        pltpu.SemaphoreType.DMA((4,)),
    ]


def piece_scratch(frame_count, left_width):
    rows = left_width // 2 // (2 * PLANES)
    low = jnp.bfloat16
    return [
        pltpu.VMEM((4, frame_count, STEP), low),
        pltpu.VMEM((PLANES, 2, rows, STEP), low),
        pltpu.VMEM((PLANES, rows, STEP), low),
        pltpu.VMEM((PLANES, rows, STEP), low),
        pltpu.VMEM((rows, STEP), jnp.float32),
        pltpu.SemaphoreType.DMA((3,)),
        pltpu.SemaphoreType.DMA((4,)),
        pltpu.SemaphoreType.DMA((2,)),
        pltpu.SemaphoreType.DMA((PLANES,)),
        pltpu.SemaphoreType.DMA((PLANES,)),
        pltpu.SemaphoreType.DMA((2,)),
    ]


def layer_scratch(frame_count, width, inner):
    low, wide = jnp.bfloat16, jnp.float32
    dma = pltpu.SemaphoreType.DMA
    return dict(
        qkv_held=pltpu.VMEM((width, 3 * width), low),
        out_held=pltpu.VMEM((width, width), low),
        up_held=pltpu.VMEM((width, inner), low),
        down_held=pltpu.VMEM((inner, width), low),
        weight_sem=dma((4,)),
        block=pltpu.VMEM((BLOCKS, frame_count + 16, width), low),
        block_send=dma((2, 4, BLOCKS)),
        block_recv=dma((2, BLOCKS)),
        grad_block=pltpu.VMEM((BLOCKS, frame_count, width), low),
        stats=pltpu.VMEM((BLOCKS, 32, frame_count), wide),
        grad_send=dma((3, 4, BLOCKS)),
        grad_recv=dma((3, BLOCKS)),
        projected=pltpu.VMEM((BLOCKS, frame_count, 3 * width), low),
        mask=pltpu.VMEM((frame_count, BLOCKS * frame_count), wide),
        attended=pltpu.VMEM((frame_count, width), wide),
        slope=pltpu.VMEM((frame_count, inner), wide),
        logs=pltpu.VMEM((frame_count, 128), wide),
        delta=pltpu.VMEM((frame_count, 128), wide),
        inner_bias=pltpu.VMEM((1, inner), wide),
        act=pltpu.VMEM((frame_count, inner), low),
        pre_low=pltpu.VMEM((frame_count, inner), low),
        context=pltpu.VMEM((frame_count, width), low),
        hidden_low=pltpu.VMEM((frame_count, width), low),
        second_low=pltpu.VMEM((frame_count, width), low),
        first_low=pltpu.VMEM((frame_count, width), low),
        normed=pltpu.VMEM((frame_count, width), wide),
        running=pltpu.VMEM((frame_count, width), wide),
        first_grad=pltpu.VMEM((frame_count, width), wide),
        proj_grad=pltpu.VMEM((frame_count, 3 * width), low),
        vector=pltpu.VMEM((16, width), wide),
        vector_partial=pltpu.VMEM((4, 16, width), wide),
        vector_arrived=pltpu.VMEM((6, 16, width), wide),
        vector_send=dma((6,)),
        vector_recv=dma((6,)),
        down_left=shared_scratch(frame_count, inner),
        up_left=shared_scratch(frame_count, width),
        out_left=shared_scratch(frame_count, width),
        qkv_left=shared_scratch(frame_count, width),
        down_piece=piece_scratch(frame_count, inner),
        up_pieces=[piece_scratch(frame_count, width) for _ in range(4)],
        out_piece=piece_scratch(frame_count, width),
        qkv_pieces=[piece_scratch(frame_count, width) for _ in range(3)],
    )


class Inputs(typing.NamedTuple):
    frames: typing.Any
    segment_ids: typing.Any
    qkv_weight: typing.Any
    query_bias: typing.Any
    value_bias: typing.Any
    out_weight: typing.Any
    out_bias: typing.Any
    norm1_gain: typing.Any
    norm1_shift: typing.Any
    up_weight: typing.Any
    up_bias: typing.Any
    down_weight: typing.Any
    down_bias: typing.Any
    norm2_gain: typing.Any
    norm2_shift: typing.Any
    cotangent: typing.Any


class Outputs(typing.NamedTuple):
    layer_out: typing.Any
    input_grad: typing.Any
    qkv_g: typing.Any
    query_g: typing.Any
    value_g: typing.Any
    out_g: typing.Any
    outbias_g: typing.Any
    gain1_g: typing.Any
    shift1_g: typing.Any
    up_g: typing.Any
    upbias_g: typing.Any
    down_g: typing.Any
    downbias_g: typing.Any
    gain2_g: typing.Any
    shift2_g: typing.Any


class Refs:
    def __init__(self, *groups):
        for group in groups:
            for name, ref in group.items():
                setattr(self, name, ref)


def layer_kernel(held, *refs):
    inputs, outputs = len(Inputs._fields), len(Outputs._fields)
    scratch = jax.tree.unflatten(held, refs[inputs + outputs :])
    k = Refs(dict(zip(Inputs._fields + Outputs._fields, refs)), scratch)
    frame_count, width = k.frames.shape
    inner = k.inner_bias.shape[1]
    low, wide = jnp.bfloat16, jnp.float32
    total = BLOCKS * frame_count
    row, z, x, c = where_am_i()
    mine = z * 4 + x * 2 + c
    has_up, has_down = z < PLANES - 1, z > 0
    edge = jnp.logical_not(has_up & has_down)
    far = (z + 2) % PLANES
    lost = PLANES - 1 - z
    lane = lax.broadcasted_iota(jnp.int32, (frame_count, 128), 1)

    def fetch(i):
        source, target = (
            (k.qkv_weight, k.qkv_held),
            (k.out_weight, k.out_held),
            (k.up_weight, k.up_held),
            (k.down_weight, k.down_held),
        )[i]
        return pltpu.make_async_copy(source, target, k.weight_sem.at[i])

    for i in range(4):
        fetch(i).start()

    link = RowGather(
        [(k.block, 0, 64), (k.block, 64, frame_count - 48)], k.block_send, k.block_recv
    )
    back = RowGather(
        [(k.grad_block, 0, 64), (k.grad_block, 64, frame_count - 64), (k.stats, 0, 32)],
        k.grad_send,
        k.grad_recv,
    )
    down_left = Shared(k.act, *k.down_left)
    up_left = Shared(k.hidden_low, *k.up_left)
    out_left = Shared(k.context, *k.out_left)
    qkv_left = Shared(k.frames, *k.qkv_left)
    half_inner, half_width = inner // 2, width // 2
    down = Piece(down_left, k.second_low, 0, half_width, k.down_g, k.down_piece)
    ups = [
        Piece(up_left, k.pre_low, p * STEP, half_inner, k.up_g, k.up_pieces[p])
        for p in range(4)
    ]
    out = Piece(out_left, k.first_low, 0, half_width, k.out_g, k.out_piece)
    qkvs = [
        Piece(qkv_left, k.proj_grad, p * width, half_width, k.qkv_g, k.qkv_pieces[p])
        for p in range(3)
    ]
    vector = VectorSum(
        k.vector, k.vector_partial, k.vector_arrived, k.vector_send, k.vector_recv
    )

    partners = [
        (None, down.device(row, z, x, 1 - c)),
        (None, down.device(1 - row, z, x, c)),
        (None, down.device(1 - row, z, x, 1 - c)),
        (None, down.device(row, z, 1 - x, c)),
    ]
    partners += [(None, down.device(row, (z + step) % PLANES, x, c)) for step in range(1, PLANES)]
    meet(partners, len(partners))

    line, crossing = (0,), (1,)
    k.block[mine, pl.ds(0, frame_count), :] = k.frames[...]
    own_ids = jnp.broadcast_to(k.segment_ids[...], (frame_count, frame_count)).astype(wide)
    k.block[mine, pl.ds(frame_count, 16), pl.ds(0, frame_count)] = own_ids[:16].astype(low)
    link.own(crossing, line)
    qkv_left.share()
    ids_column = own_ids.T
    k.inner_bias[...] = k.up_bias[...].reshape(1, inner)
    query_bias = k.query_bias[...].reshape(1, width)
    value_bias = k.value_bias[...].reshape(1, width)

    def plane_rows(plane):
        return jnp.concatenate(
            [k.block[plane * 4 + i, pl.ds(0, frame_count), :] for i in range(4)], axis=0
        )

    def store_rows(plane, third, part):
        for i in range(4):
            k.projected[plane * 4 + i, :, pl.ds(third * width, width)] = part[
                i * frame_count : (i + 1) * frame_count
            ]

    def as_query(part):
        return (part + query_bias).astype(low) * HEAD_DIM**-0.5

    def project(plane):
        rows = plane_rows(plane)
        keys = product(rows, k.qkv_held[:, pl.ds(width, width)], CONTRACT_INNER)
        store_rows(plane, 1, keys.astype(low))
        values = product(rows, k.qkv_held[:, pl.ds(2 * width, width)], CONTRACT_INNER)
        store_rows(plane, 2, (values + value_bias).astype(low))
        for i in range(4):
            ids = k.block[plane * 4 + i, pl.ds(frame_count, 8), pl.ds(0, frame_count)]
            same = jnp.broadcast_to(ids.astype(wide)[:1], own_ids.shape) == ids_column
            at = pl.multiple_of((plane * 4 + i) * frame_count, 128)
            k.mask[:, pl.ds(at, frame_count)] = jnp.where(same, 0.0, mask_fill)

    def project_queries(plane):
        queries = product(plane_rows(plane), k.qkv_held[:, pl.ds(0, width)], CONTRACT_INNER)
        store_rows(plane, 0, as_query(queries))

    def columns_of(third, j):
        return pl.ds(pl.multiple_of(third * width + j * 128, 128), 128)

    def head_state(h):
        return pl.ds(pl.multiple_of(h * 128, 128), 128)

    def attend(plane, first):
        at = pl.multiple_of(plane * 4 * frame_count, 128)

        def pair(j, carry):
            query = k.projected[mine, :, columns_of(0, j)]
            keys = k.projected[pl.ds(plane * 4, 4), :, columns_of(1, j)].reshape(-1, 128)
            values = k.projected[pl.ds(plane * 4, 4), :, columns_of(2, j)].reshape(-1, 128)
            outs, factors = [], []
            for h in range(2):
                chosen = (lane < HALF) == (h == 0)
                scores = product(
                    jnp.where(chosen, query, jnp.zeros_like(query)), keys, CONTRACT_LAST
                )
                scores = scores + k.mask[:, pl.ds(at, 4 * frame_count)]
                peak = jnp.broadcast_to(jnp.max(scores, axis=1, keepdims=True), lane.shape)
                if not first:
                    old = k.slope[:, head_state(2 * j + h)]
                    peak = jnp.maximum(peak, old)
                    factors.append(jnp.exp(old - peak))
                weights = jnp.exp(scores - jnp.concatenate([peak] * 4, axis=1))
                whole = jnp.broadcast_to(jnp.sum(weights, axis=1, keepdims=True), lane.shape)
                if not first:
                    whole = whole + k.slope[:, head_state(HEADS + 2 * j + h)] * factors[h]
                k.slope[:, head_state(2 * j + h)] = peak
                k.slope[:, head_state(HEADS + 2 * j + h)] = whole
                outs.append(product(weights.astype(low), values, CONTRACT_INNER))
            both = jnp.where(lane < HALF, outs[0], outs[1])
            if not first:
                both = both + k.attended[:, columns_of(0, j)] * jnp.where(
                    lane < HALF, factors[0], factors[1]
                )
            k.attended[:, columns_of(0, j)] = both
            return carry

        lax.fori_loop(0, PAIRS, pair, 0)

    fetch(0).wait()
    own_query = product(k.frames[...], k.qkv_held[:, pl.ds(0, width)], CONTRACT_INNER)
    k.projected[mine, :, pl.ds(0, width)] = as_query(own_query)
    link.first_round(crossing, line)
    link.plane_done(z, (0, 1))
    project(z)
    link.second_round(crossing, line)
    attend(z, True)

    @pl.when(has_down)
    def _():
        link.plane_done(z - 1, (0, 1))
        project(z - 1)

    link.third_round(crossing, line)

    @pl.when(has_down)
    def _():
        attend(z - 1, False)

    @pl.when(has_up)
    def _():
        link.plane_done(z + 1, (0, 1))
        project(z + 1)
        attend(z + 1, False)

    link.plane_done(far, (0, 1))
    project(far)
    attend(far, False)
    logs = jnp.zeros(lane.shape, wide)
    for j in range(PAIRS):
        parts = []
        for h in range(2):
            whole = k.slope[:, head_state(HEADS + 2 * j + h)]
            logs = jnp.where(
                lane == 2 * j + h, k.slope[:, head_state(2 * j + h)] + jnp.log(whole), logs
            )
            parts.append(whole)
        done = k.attended[:, columns_of(0, j)] / jnp.where(lane < HALF, parts[0], parts[1])
        k.attended[:, columns_of(0, j)] = done
        k.context[:, columns_of(0, j)] = done.astype(low)
    k.logs[...] = logs
    out_left.share()

    def normalize(resid):
        centred = resid - jnp.mean(resid, axis=-1, keepdims=True)
        inverse = lax.rsqrt(jnp.mean(centred * centred, axis=-1, keepdims=True) + norm_eps)
        return centred * inverse, inverse

    def normalize_back(upstream, normed, inverse, gain):
        scaled = upstream * gain
        first_mean = jnp.mean(scaled, axis=-1, keepdims=True)
        second_mean = jnp.mean(scaled * normed, axis=-1, keepdims=True)
        return inverse * (scaled - first_mean - normed * second_mean)

    def note(index, values):
        k.vector[pl.ds(index, 1), :] = jnp.sum(values, axis=0, keepdims=True)

    def flat(ref):
        return ref[...].reshape(1, width)

    k.vector[pl.ds(8, 8), :] = jnp.zeros((8, width), wide)
    fetch(1).wait()
    resid_one = (
        k.frames[...].astype(wide)
        + product(k.context[...], k.out_held[...], CONTRACT_INNER)
        + flat(k.out_bias)
    )
    normed_one, inverse_one = normalize(resid_one)
    k.normed[...] = normed_one
    hidden = normed_one * flat(k.norm1_gain) + flat(k.norm1_shift)
    k.hidden_low[...] = hidden.astype(low)
    up_left.share()
    k.running[...] = hidden + flat(k.down_bias)
    fetch(2).wait()
    fetch(3).wait()

    def forward(f, carry):
        columns = pl.ds(pl.multiple_of(f * width, 128), width)
        pre_act = (
            product(k.hidden_low[...], k.up_held[:, columns], CONTRACT_INNER)
            + k.inner_bias[:, columns]
        )
        normal_cdf = 0.5 * (1.0 + lax.erf(pre_act * 0.5**0.5))
        normal_pdf = jnp.exp(-0.5 * pre_act * pre_act) * (2.0 * math.pi) ** (-0.5)
        act = (pre_act * normal_cdf).astype(low)
        k.act[:, columns] = act
        k.slope[:, columns] = normal_cdf + pre_act * normal_pdf
        k.running[...] += product(
            act, k.down_held[pl.ds(pl.multiple_of(f * width, 128), width), :], CONTRACT_INNER
        )
        return carry

    lax.fori_loop(0, inner // width, forward, 0)
    down_left.share()
    normed_two, inverse_two = normalize(k.running[...])
    k.layer_out[...] = (normed_two * flat(k.norm2_gain) + flat(k.norm2_shift)).astype(low)
    upstream = k.cotangent[...].astype(wide)
    second_grad = normalize_back(upstream, normed_two, inverse_two, flat(k.norm2_gain))
    k.second_low[...] = second_grad.astype(low)
    down.share()
    note(5, second_grad)
    note(6, upstream * normed_two)
    note(7, upstream)
    k.running[...] = second_grad
    for p in range(4):
        for side in range(2):
            first = side * half_inner + p * STEP
            columns = pl.ds(first, STEP)
            pre_grad = (
                product(k.second_low[...], k.down_held[columns, :], CONTRACT_LAST)
                * k.slope[:, columns]
            )
            k.vector[pl.ds(8 + first // width, 1), pl.ds(first % width, STEP)] = jnp.sum(
                pre_grad, axis=0, keepdims=True
            )
            k.pre_low[:, columns] = pre_grad.astype(low)
            k.running[...] += product(
                k.pre_low[:, columns], k.up_held[:, columns], CONTRACT_LAST
            )
        ups[p].share()
        if p == 1:
            out_left.relay()
            up_left.relay()
            qkv_left.relay()
    hidden_grad = k.running[...]
    normed_one = k.normed[...]
    first_grad = normalize_back(hidden_grad, normed_one, inverse_one, flat(k.norm1_gain))
    k.first_grad[...] = first_grad
    k.first_low[...] = first_grad.astype(low)
    out.share()
    context_grad = product(k.first_low[...], k.out_held[...], CONTRACT_LAST).astype(low)
    k.grad_block[mine] = context_grad
    delta = jnp.zeros(lane.shape, wide)
    for j in range(PAIRS):
        columns = slice(j * 128, (j + 1) * 128)
        both = context_grad[:, columns].astype(wide) * k.attended[:, columns]
        for h in range(2):
            one = jnp.sum(
                jnp.where((lane < HALF) == (h == 0), both, 0.0), axis=1, keepdims=True
            )
            delta = jnp.where(lane == 2 * j + h, one, delta)
    k.delta[...] = delta
    k.stats[mine, pl.ds(0, 16), :] = k.logs[...].T[:16]
    k.stats[mine, pl.ds(16, 16), :] = delta.T[:16]
    back_line, back_crossing = (2, 0), (1,)
    back.own(back_crossing, back_line)
    note(2, first_grad)
    note(3, hidden_grad * normed_one)
    note(4, hidden_grad)

    @pl.when(edge)
    def _():
        for i in range(4):
            k.projected[lost * 4 + i] = jnp.zeros((frame_count, 3 * width), low)
            k.grad_block[lost * 4 + i] = jnp.zeros((frame_count, width), low)
            k.stats[lost * 4 + i] = jnp.zeros((32, frame_count), wide)
            at = pl.multiple_of((lost * 4 + i) * frame_count, 128)
            k.mask[:, pl.ds(at, frame_count)] = jnp.full(lane.shape, mask_fill, wide)

    def query_pair(j):
        query = k.projected[mine, :, columns_of(0, j)]
        upstream = k.grad_block[mine, :, columns_of(0, j)]
        keys = k.projected[:, :, columns_of(1, j)].reshape(total, 128)
        values = k.projected[:, :, columns_of(2, j)].reshape(total, 128)
        outs = []
        for h in range(2):
            chosen = (lane < HALF) == (h == 0)
            nothing = jnp.zeros_like(query)
            logs = jnp.sum(
                jnp.where(lane == 2 * j + h, k.logs[...], 0.0), axis=1, keepdims=True
            )
            shift = jnp.sum(
                jnp.where(lane == 2 * j + h, k.delta[...], 0.0), axis=1, keepdims=True
            )
            scores = product(jnp.where(chosen, query, nothing), keys, CONTRACT_LAST)
            probs = jnp.exp(scores + k.mask[...] - logs)
            prob_grad = product(jnp.where(chosen, upstream, nothing), values, CONTRACT_LAST)
            score_grad = (probs * (prob_grad - shift)).astype(low)
            outs.append(product(score_grad, keys, CONTRACT_INNER))
        k.proj_grad[:, columns_of(0, j)] = (
            jnp.where(lane < HALF, outs[0], outs[1]) * HEAD_DIM**-0.5
        ).astype(low)

    def key_pair(j):
        key = k.projected[mine, :, columns_of(1, j)]
        value = k.projected[mine, :, columns_of(2, j)]
        queries = k.projected[:, :, columns_of(0, j)].reshape(total, 128)
        upstream = k.grad_block[:, :, columns_of(0, j)].reshape(total, 128)
        key_outs, value_outs = [], []
        for h in range(2):
            chosen = (lane < HALF) == (h == 0)
            nothing = jnp.zeros_like(key)
            logs = jnp.concatenate(
                [k.stats[b, pl.ds(2 * j + h, 1), :] for b in range(BLOCKS)], axis=1
            )
            shift = jnp.concatenate(
                [k.stats[b, pl.ds(16 + 2 * j + h, 1), :] for b in range(BLOCKS)], axis=1
            )
            scores = product(jnp.where(chosen, key, nothing), queries, CONTRACT_LAST)
            probs = jnp.exp(scores + k.mask[...] - logs)
            prob_grad = product(jnp.where(chosen, value, nothing), upstream, CONTRACT_LAST)
            score_grad = (probs * (prob_grad - shift)).astype(low)
            key_outs.append(product(score_grad, queries, CONTRACT_INNER))
            value_outs.append(product(probs.astype(low), upstream, CONTRACT_INNER))
        k.proj_grad[:, columns_of(1, j)] = jnp.where(
            lane < HALF, key_outs[0], key_outs[1]
        ).astype(low)
        k.proj_grad[:, columns_of(2, j)] = jnp.where(
            lane < HALF, value_outs[0], value_outs[1]
        ).astype(low)

    def pairs(one, first, last):
        def body(j, carry):
            one(j)
            return carry

        lax.fori_loop(first, last, body, 0)

    pairs(query_pair, 0, 2)
    back.first_round(back_crossing, back_line)
    down_left.relay()
    pairs(query_pair, 2, 4)
    back.second_round(back_crossing, back_line)
    pairs(query_pair, 4, 6)
    back.third_round(back_crossing, back_line)
    qkvs[0].share()
    down_left.complete()
    down.multiply()
    up_left.complete()
    project_queries(z)
    project_queries(far)
    ups[0].multiply()

    @pl.when(has_down)
    def _():
        project_queries(z - 1)

    @pl.when(has_up)
    def _():
        project_queries(z + 1)

    back.plane_done(z, (0, 1, 2))
    back.plane_done(z - 1, (0, 1, 2), has_down)
    back.plane_done(z + 1, (0, 1, 2), has_up)
    back.plane_done(far, (0, 1, 2))
    pairs(key_pair, 0, 2)
    ups[1].multiply()
    down.spread()
    pairs(key_pair, 2, 4)
    ups[2].multiply()
    ups[0].spread()
    pairs(key_pair, 4, 6)
    qkvs[1].share()
    qkvs[2].share()
    note(0, k.proj_grad[:, pl.ds(0, width)].astype(wide))
    note(1, k.proj_grad[:, pl.ds(2 * width, width)].astype(wide))
    vector.start(0)
    ups[3].multiply()
    down.collect()
    ups[1].spread()
    k.input_grad[...] = k.first_grad[...] + product(
        k.proj_grad[...], k.qkv_held[...], CONTRACT_LAST
    )
    vector.take(0)
    vector.start(1)
    out_left.complete()
    out.multiply()
    ups[2].spread()
    qkv_left.complete()
    qkvs[0].multiply()
    ups[0].collect()
    ups[3].spread()
    vector.take(1)
    vector.start(2)
    qkvs[1].multiply()
    ups[1].collect()
    out.spread()
    qkvs[2].multiply()
    ups[2].collect()
    qkvs[0].spread()
    vector.take(2)
    vector.start(3)
    ups[3].collect()
    qkvs[1].spread()
    out.collect()
    qkvs[2].spread()
    vector.take(3)
    summed = k.vector_partial[3]
    share = k.query_g.shape[0]
    shares, _ = vector.own_share(summed[:8], share)
    for i, ref in enumerate(
        (k.query_g, k.value_g, k.outbias_g, k.gain1_g, k.shift1_g, k.downbias_g, k.gain2_g, k.shift2_g)
    ):
        ref[...] = shares[i, :share]
    up_shares, at = vector.own_share(summed[8:], 4 * share)
    keep = lax.broadcasted_iota(jnp.int32, up_shares.shape, 0) == at
    picked = jnp.sum(jnp.where(keep, up_shares, 0.0), axis=0, keepdims=True)
    k.upbias_g[...] = picked[0, : 4 * share]
    qkvs[0].collect()
    qkvs[1].collect()
    qkvs[2].collect()
    pieces = [down] + ups + [out] + qkvs
    for each in pieces:
        each.delivered()
    link.finish()
    back.finish()
    for each in [down_left, up_left, out_left, qkv_left] + pieces:
        for copy in each.flying:
            copy.wait_send()
    vector.finish()


def layer_step(*args):
    frames = args[0]
    frame_count, width = frames.shape[1:]
    inner = args[9].shape[1]
    low, wide = jnp.bfloat16, jnp.float32
    scratch, held = jax.tree.flatten(layer_scratch(frame_count, width, inner))
    operands = [frames[0]] + list(args[1:-1]) + [args[-1][0]]
    share = width // 32
    shapes = [
        ((frame_count, width), low),
        ((frame_count, width), wide),
        ((share, 3 * width), wide),
        ((share,), wide),
        ((share,), wide),
        ((share, width), wide),
        ((share,), wide),
        ((share,), wide),
        ((share,), wide),
        ((share, inner), wide),
        ((4 * share,), wide),
        ((4 * share, width), wide),
        ((share,), wide),
        ((share,), wide),
        ((share,), wide),
    ]
    results = pl.pallas_call(
        functools.partial(layer_kernel, held),
        out_shape=tuple(jax.ShapeDtypeStruct(shape, kind) for shape, kind in shapes),
        in_specs=[IN_PLACE if each.ndim == 2 and each.shape[0] >= width else IN_VMEM for each in operands],
        out_specs=(IN_VMEM,) * len(shapes),
        scratch_shapes=scratch,
        compiler_params=pltpu.CompilerParams(
            collective_id=0, has_side_effects=True, vmem_limit_bytes=VMEM_BYTES
        ),
    )(*operands)
    return (results[0][None], results[1][None]) + tuple(results[2:])


def solution(mesh):
    chosen = layer_step if dict(mesh.shape) == {"rows": 2, "seq": 16} else shards
    in_specs = (
        P("rows", "seq", None),
        P("rows", "seq"),
        P(),
        P(),
        P(),
        P(),
        P(),
        P(),
        P(),
        P(),
        P(),
        P(),
        P(),
        P(),
        P(),
        P("rows", "seq", None),
    )
    out_specs = (
        P("rows", "seq", None),
        P("rows", "seq", None),
        P(("rows", "seq"), None),
        P(("rows", "seq")),
        P(("rows", "seq")),
        P(("rows", "seq"), None),
        P(("rows", "seq")),
        P(("rows", "seq")),
        P(("rows", "seq")),
        P(("rows", "seq"), None),
        P(("rows", "seq")),
        P(("rows", "seq"), None),
        P(("rows", "seq")),
        P(("rows", "seq")),
        P(("rows", "seq")),
    )
    return jax.shard_map(chosen, mesh=mesh, in_specs=in_specs, out_specs=out_specs, check_vma=False)
```

```python
import functools
import math
import typing

import jax
import jax.numpy as jnp
from jax import lax
from jax.experimental import pallas as pl
from jax.experimental.pallas import tpu as pltpu
from jax.sharding import PartitionSpec as P

HEADS = 12
HEAD_DIM = 64


norm_eps = 1e-05
mask_fill = -1e30


def shortened(shard):

    def short(part):
        return part.astype(jnp.bfloat16) if part.dtype == jnp.float32 else part

    return jax.tree.map(short, shard)


def passed_along(value, axis, steps):
    count = lax.axis_size(axis)
    pairs = [(source, (source + steps) % count) for source in range(count)]
    return lax.ppermute(value, axis, pairs)


def layer_norm(resid, gain, shift):
    centred = resid - jnp.mean(resid, axis=-1, keepdims=True)
    inv_std = lax.rsqrt(jnp.mean(centred * centred, axis=-1, keepdims=True) + norm_eps)
    normed = centred * inv_std
    return (normed * gain + shift, normed, inv_std)


def norm_back(upstream, normed, inv_std, gain):
    scaled = upstream * gain
    first_mean = jnp.mean(scaled, axis=-1, keepdims=True)
    second_mean = jnp.mean(scaled * normed, axis=-1, keepdims=True)
    grad_in = inv_std * (scaled - first_mean - normed * second_mean)
    return (grad_in, jnp.sum(upstream * normed, axis=0), jnp.sum(upstream, axis=0))


def gelu_slope(pre_act):
    normal_cdf = 0.5 * (1.0 + lax.erf(pre_act * 0.5**0.5))
    normal_pdf = jnp.exp(-0.5 * pre_act * pre_act) * (2.0 * math.pi) ** (-0.5)
    return normal_cdf + pre_act * normal_pdf


def head_groups(head_count):
    return [(0, head_count, 1)]


def pass_keys(blocks):
    return jax.tree.map(
        lambda part, own: part.astype(own.dtype), passed_along(shortened(blocks), "seq", 1), blocks
    )


def pass_again(blocks):
    return jax.tree.map(
        lambda part, own: part.astype(own.dtype), passed_along(shortened(blocks), "seq", 1), blocks
    )


def pass_grads(blocks):
    return (
        passed_along(blocks[0].astype(jnp.bfloat16), "seq", 1).astype(jnp.float32),
        passed_along(blocks[1].astype(jnp.bfloat16), "seq", 1).astype(jnp.float32),
    )


def block_scores(query_part, key_part, query_ids, key_ids):
    scores = jnp.einsum(
        "qhe,khe->hqk", query_part, key_part, preferred_element_type=jnp.float32
    ) * HEAD_DIM ** (-0.5)
    return jnp.where((query_ids[:, None] == key_ids[None, :])[None], scores, mask_fill)


def attend_block(carried, query_part, key_part, value_part, query_ids, key_ids):
    run_max, run_total, run_acc = carried
    scores = block_scores(query_part, key_part, query_ids, key_ids)
    new_max = jnp.maximum(run_max, jnp.max(scores, axis=-1))
    weights = jnp.exp(scores - new_max[:, :, None])
    factor = jnp.exp(run_max - new_max)
    new_total = run_total * factor + jnp.sum(weights, axis=-1)
    update = jnp.einsum(
        "hqk,khe->qhe", weights.astype(jnp.bfloat16), value_part, preferred_element_type=jnp.float32
    )
    return (new_max, new_total, run_acc * factor.T[:, :, None] + update)


def grad_block(
    carried,
    query_part,
    key_part,
    value_part,
    query_ids,
    key_ids,
    context_part,
    log_part,
    delta_part,
):
    query_acc, key_acc, value_acc = carried
    scores = block_scores(query_part, key_part, query_ids, key_ids)
    probs = jnp.exp(scores - log_part[:, :, None])
    prob_grad = jnp.einsum(
        "qhe,khe->hqk", context_part, value_part, preferred_element_type=jnp.float32
    )
    score_grad = (probs * (prob_grad - delta_part[:, :, None])).astype(jnp.bfloat16)
    scale = HEAD_DIM ** (-0.5)
    query_acc = query_acc + scale * jnp.einsum(
        "hqk,khe->qhe", score_grad, key_part, preferred_element_type=jnp.float32
    )
    key_acc = key_acc + scale * jnp.einsum(
        "hqk,qhe->khe", score_grad, query_part, preferred_element_type=jnp.float32
    )
    value_acc = value_acc + jnp.einsum(
        "hqk,qhe->khe", probs.astype(jnp.bfloat16), context_part, preferred_element_type=jnp.float32
    )
    return (query_acc, key_acc, value_acc)


def forward_cycle(
    query_heads, key_heads, value_heads, local_ids, every_id, cycle_place, cycle_size
):
    frame_count, head_count, head_width = query_heads.shape
    grouping = head_groups(head_count)
    states = []
    blocks = []
    for head_first, head_last, direction in grouping:
        head_span = head_last - head_first
        initial = (
            jnp.full((head_span, frame_count), mask_fill, jnp.float32),
            jnp.zeros((head_span, frame_count), jnp.float32),
            jnp.zeros((frame_count, head_span, head_width), jnp.float32),
        )
        states.append(
            attend_block(initial, query_heads, key_heads, value_heads, local_ids, local_ids)
        )
        blocks.append((key_heads, value_heads))

    def forward_cycle_turn(turn_index, cycle_carry):
        old_states, old_blocks = cycle_carry
        new_states = []
        new_blocks = []
        for group_info, part_state, part_block in zip(grouping, old_states, old_blocks):
            head_first, head_last, direction = group_info
            part_block = pass_keys(part_block)
            source_index = (cycle_place - direction * turn_index) % cycle_size
            key_ids = lax.dynamic_slice_in_dim(every_id, source_index * frame_count, frame_count)
            new_states.append(
                attend_block(
                    part_state, query_heads, part_block[0], part_block[1], local_ids, key_ids
                )
            )
            new_blocks.append(part_block)
        return (new_states, new_blocks)

    states, blocks = lax.fori_loop(1, cycle_size, forward_cycle_turn, (states, blocks))
    maxima = jnp.concatenate([part_state[0] for part_state in states], axis=0)
    totals = jnp.concatenate([part_state[1] for part_state in states], axis=0)
    sums_all = jnp.concatenate([part_state[2] for part_state in states], axis=1)
    attended = sums_all / totals.T[:, :, None]
    return (attended, maxima + jnp.log(totals))


def backward_cycle(
    query_heads,
    key_heads,
    value_heads,
    local_ids,
    every_id,
    context_heads,
    log_total,
    row_delta,
    cycle_place,
    cycle_size,
):
    frame_count, head_count, head_width = query_heads.shape
    grouping = head_groups(head_count)
    initial = []
    for head_first, head_last, direction in grouping:
        zero_part = jnp.zeros((frame_count, head_last - head_first, head_width), jnp.float32)
        initial.append((zero_part, (key_heads, value_heads), (zero_part, zero_part)))

    def backward_cycle_turn(turn_index, cycle_carry):
        new_carry = []
        for group_info, part_carry in zip(grouping, cycle_carry):
            head_first, head_last, direction = group_info
            query_acc, part_block, part_grads = part_carry
            source_index = (cycle_place - direction * turn_index) % cycle_size
            key_ids = lax.dynamic_slice_in_dim(every_id, source_index * frame_count, frame_count)
            query_acc, key_acc, value_acc = grad_block(
                (query_acc, part_grads[0], part_grads[1]),
                query_heads,
                part_block[0],
                part_block[1],
                local_ids,
                key_ids,
                context_heads,
                log_total,
                row_delta,
            )
            part_grads = pass_grads((key_acc, value_acc))
            part_block = pass_again(part_block)
            new_carry.append((query_acc, part_block, part_grads))
        return new_carry

    final = lax.fori_loop(0, cycle_size, backward_cycle_turn, initial)
    query_grad = jnp.concatenate([part_carry[0] for part_carry in final], axis=1)
    key_grad = jnp.concatenate([part_carry[2][0] for part_carry in final], axis=1)
    value_grad = jnp.concatenate([part_carry[2][1] for part_carry in final], axis=1)
    return (query_grad, key_grad, value_grad)


def shards(
    frames,
    segment_ids,
    qkv_weight,
    query_bias,
    value_bias,
    out_weight,
    out_bias,
    norm1_gain,
    norm1_shift,
    up_weight,
    up_bias,
    down_weight,
    down_bias,
    norm2_gain,
    norm2_shift,
    cotangent,
):
    inputs = frames[0]
    local_ids = segment_ids[0]
    frame_count, model_width = inputs.shape
    cycle_size = lax.axis_size("seq")
    cycle_place = lax.axis_index("seq")
    every_id = lax.all_gather(segment_ids, "seq", axis=1, tiled=True)[0]
    head_shape = (frame_count, HEADS, HEAD_DIM)
    projected = jnp.dot(inputs, qkv_weight, preferred_element_type=jnp.float32)
    query_heads = (projected[:, :model_width] + query_bias).astype(jnp.bfloat16).reshape(head_shape)
    key_heads = projected[:, model_width : 2 * model_width].astype(jnp.bfloat16).reshape(head_shape)
    value_heads = (
        (projected[:, 2 * model_width :] + value_bias).astype(jnp.bfloat16).reshape(head_shape)
    )
    attended, log_total = forward_cycle(
        query_heads, key_heads, value_heads, local_ids, every_id, cycle_place, cycle_size
    )
    context = attended.astype(jnp.bfloat16).reshape(frame_count, model_width)
    resid_one = (
        inputs.astype(jnp.float32)
        + jnp.dot(context, out_weight, preferred_element_type=jnp.float32)
        + out_bias
    )
    hidden, normed_one, inverse_one = layer_norm(resid_one, norm1_gain, norm1_shift)
    hidden_low = hidden.astype(jnp.bfloat16)
    pre_act = jnp.dot(hidden_low, up_weight, preferred_element_type=jnp.float32) + up_bias
    act_low = jax.nn.gelu(pre_act, approximate=False).astype(jnp.bfloat16)
    resid_two = (
        hidden + jnp.dot(act_low, down_weight, preferred_element_type=jnp.float32) + down_bias
    )
    output, normed_two, inverse_two = layer_norm(resid_two, norm2_gain, norm2_shift)
    upstream = cotangent[0].astype(jnp.float32)
    second_grad, gain_two_grad, shift_two_grad = norm_back(
        upstream, normed_two, inverse_two, norm2_gain
    )
    second_low = second_grad.astype(jnp.bfloat16)
    down_grad = jnp.einsum("tf,td->fd", act_low, second_low, preferred_element_type=jnp.float32)
    pre_grad = jnp.einsum(
        "td,fd->tf", second_low, down_weight, preferred_element_type=jnp.float32
    ) * gelu_slope(pre_act)
    pre_low = pre_grad.astype(jnp.bfloat16)
    up_grad = jnp.einsum("td,tf->df", hidden_low, pre_low, preferred_element_type=jnp.float32)
    hidden_grad = second_grad + jnp.einsum(
        "tf,df->td", pre_low, up_weight, preferred_element_type=jnp.float32
    )
    first_grad, gain_one_grad, shift_one_grad = norm_back(
        hidden_grad, normed_one, inverse_one, norm1_gain
    )
    first_low = first_grad.astype(jnp.bfloat16)
    out_grad = jnp.einsum("td,te->de", context, first_low, preferred_element_type=jnp.float32)
    context_grad = (
        jnp.einsum("te,de->td", first_low, out_weight, preferred_element_type=jnp.float32)
        .astype(jnp.bfloat16)
        .reshape(head_shape)
    )
    row_delta = jnp.einsum("qhe,qhe->hq", context_grad.astype(jnp.float32), attended)
    query_grad, key_grad, value_grad = backward_cycle(
        query_heads,
        key_heads,
        value_heads,
        local_ids,
        every_id,
        context_grad,
        log_total,
        row_delta,
        cycle_place,
        cycle_size,
    )
    query_low = query_grad.astype(jnp.bfloat16).reshape(frame_count, model_width)
    key_low = key_grad.astype(jnp.bfloat16).reshape(frame_count, model_width)
    value_low = value_grad.astype(jnp.bfloat16).reshape(frame_count, model_width)
    proj_grad = jnp.concatenate([query_low, key_low, value_low], axis=1)
    qkv_grad = jnp.einsum("td,te->de", inputs, proj_grad, preferred_element_type=jnp.float32)
    input_grad = (
        jnp.einsum("te,de->td", proj_grad, qkv_weight, preferred_element_type=jnp.float32)
        + first_grad
    )
    summed = (
        lax.psum_scatter(qkv_grad, ("rows", "seq"), scatter_dimension=0, tiled=True),
        lax.psum_scatter(
            jnp.sum(query_low.astype(jnp.float32), axis=0),
            ("rows", "seq"),
            scatter_dimension=0,
            tiled=True,
        ),
        lax.psum_scatter(
            jnp.sum(value_low.astype(jnp.float32), axis=0),
            ("rows", "seq"),
            scatter_dimension=0,
            tiled=True,
        ),
        lax.psum_scatter(out_grad, ("rows", "seq"), scatter_dimension=0, tiled=True),
        lax.psum_scatter(
            jnp.sum(first_grad, axis=0), ("rows", "seq"), scatter_dimension=0, tiled=True
        ),
        lax.psum_scatter(gain_one_grad, ("rows", "seq"), scatter_dimension=0, tiled=True),
        lax.psum_scatter(shift_one_grad, ("rows", "seq"), scatter_dimension=0, tiled=True),
        lax.psum_scatter(up_grad, ("rows", "seq"), scatter_dimension=0, tiled=True),
        lax.psum_scatter(
            jnp.sum(pre_grad, axis=0), ("rows", "seq"), scatter_dimension=0, tiled=True
        ),
        lax.psum_scatter(down_grad, ("rows", "seq"), scatter_dimension=0, tiled=True),
        lax.psum_scatter(
            jnp.sum(second_grad, axis=0), ("rows", "seq"), scatter_dimension=0, tiled=True
        ),
        lax.psum_scatter(gain_two_grad, ("rows", "seq"), scatter_dimension=0, tiled=True),
        lax.psum_scatter(shift_two_grad, ("rows", "seq"), scatter_dimension=0, tiled=True),
    )
    return (
        output.astype(jnp.bfloat16)[None],
        input_grad[None],
        summed[0],
        summed[1],
        summed[2],
        summed[3],
        summed[4],
        summed[5],
        summed[6],
        summed[7],
        summed[8],
        summed[9],
        summed[10],
        summed[11],
        summed[12],
    )


HALF = HEAD_DIM
PAIRS = HEADS // 2
CONTRACT_LAST = (((1,), (1,)), ((), ()))
CONTRACT_INNER = (((1,), (0,)), ((), ()))
CONTRACT_FIRST = (((0,), (0,)), ((), ()))
IN_VMEM = pl.BlockSpec(memory_space=pltpu.VMEM)
IN_PLACE = pl.BlockSpec(memory_space=pl.ANY)
MESH_ID = pl.DeviceIdType.MESH
VMEM_BYTES = 60 << 20
BLOCKS = 16
PLANES = 4


def product(left, right, dims):
    return lax.dot_general(left, right, dims, preferred_element_type=jnp.float32)


def where_am_i():
    row = lax.axis_index("rows")
    place = lax.axis_index("seq")
    return row, place // 4, place // 2 % 2, place % 2


def meet(partners, count):
    barrier = pltpu.get_barrier_semaphore()
    for present, target in partners:

        def signal(target=target):
            pl.semaphore_signal(barrier, inc=1, device_id=target, device_id_type=MESH_ID)

        if present is None:
            signal()
        else:
            pl.when(present)(signal)
    pl.semaphore_wait(barrier, count)


class RowGather:
    UP, DOWN, ACROSS, BESIDE = range(4)

    def __init__(self, parts, line, crossing, sems):
        self.parts, self.line, self.crossing = parts, line, crossing
        self.recv_sem, self.beside_sem, self.line_sem, self.out_sem = sems
        self.row, self.z, self.x, self.c = where_am_i()
        self.has_up, self.has_down = self.z < PLANES - 1, self.z > 0
        self.far = (self.z + 2) % PLANES
        self.buffers = []
        for ref, _, _ in parts:
            if not any(ref is known for known in self.buffers):
                self.buffers.append(ref)

    def group(self, part):
        return [self.parts[part][0] is ref for ref in self.buffers].index(True)

    def device(self, z, x, c):
        return (self.row, z * 4 + x * 2 + c)

    def target(self, way):
        return (
            self.device(self.z + 1, self.x, self.c),
            self.device(self.z - 1, self.x, self.c),
            self.device(self.z, 1 - self.x, self.c),
            self.device(self.z, self.x, 1 - self.c),
        )[way]

    def copy(self, part, z, x, way):
        ref, first, rows = self.parts[part]
        piece = ref.at[z * 4 + x * 2 + self.c, pl.ds(first, rows)]
        beside = way == self.BESIDE
        return pltpu.make_async_remote_copy(
            src_ref=piece,
            dst_ref=piece,
            send_sem=self.out_sem.at[self.group(part)] if beside else self.line_sem.at[part, way],
            recv_sem=(
                self.beside_sem.at[self.group(part), z]
                if beside
                else self.recv_sem.at[part, z * 2 + x]
            ),
            device_id=self.target(way),
            device_id_type=MESH_ID,
        )

    def send(self, part, z, x, way):
        present = {self.UP: self.has_up, self.DOWN: self.has_down}.get(way)
        if present is None:
            self.copy(part, z, x, way).start()
        else:
            pl.when(present)(lambda: self.copy(part, z, x, way).start())

    def relay(self, part, z, x, ways, present=None):
        def both():
            self.copy(part, z, x, self.ACROSS).wait_recv()
            for way in ways:
                self.send(part, z, x, way)

        if present is None:
            both()
        else:
            pl.when(present)(both)

    def own(self):
        z, x = self.z, self.x
        for part in self.crossing:
            self.send(part, z, x, self.ACROSS)
        for part in self.line + self.crossing:
            self.send(part, z, x, self.UP)
            self.send(part, z, x, self.DOWN)
        for part in self.line:
            self.send(part, z, x, self.ACROSS)
        for part in self.crossing + self.line:
            self.send(part, z, x, self.BESIDE)

    def near_first(self):
        z, x = self.z, self.x
        for part in self.line:
            self.relay(part, z - 1, x, (self.UP, self.ACROSS, self.BESIDE), self.has_down)
            self.relay(part, z + 1, x, (self.DOWN, self.ACROSS, self.BESIDE), self.has_up)
        for part in self.crossing:
            self.relay(part, z, 1 - x, (self.UP, self.DOWN, self.BESIDE))
        for part in self.crossing:
            self.relay(part, z - 1, x, (self.UP, self.BESIDE), self.has_down)
            self.relay(part, z + 1, x, (self.DOWN, self.BESIDE), self.has_up)
        for part in self.line:
            self.relay(part, z, 1 - x, (self.BESIDE,))

    def near_second(self):
        z, x = self.z, self.x
        for part in self.crossing:
            self.relay(part, z - 1, 1 - x, (self.UP, self.BESIDE), self.has_down)
            self.relay(part, z + 1, 1 - x, (self.DOWN, self.BESIDE), self.has_up)
        for part in self.line:
            self.relay(part, z - 1, 1 - x, (self.BESIDE,), self.has_down)
            self.relay(part, z + 1, 1 - x, (self.BESIDE,), self.has_up)

    def far_line(self):
        for part in self.line:
            self.relay(part, self.far, self.x, (self.ACROSS, self.BESIDE))

    def far_rest(self):
        for part in self.crossing:
            self.relay(part, self.far, self.x, (self.BESIDE,))
        for part in self.line:
            self.relay(part, self.far, 1 - self.x, (self.BESIDE,))
        for part in self.crossing:
            self.relay(part, self.far, 1 - self.x, (self.BESIDE,))

    def plane_done(self, z, present=None):
        def wait():
            for i, ref in enumerate(self.buffers):
                both = ref.at[pl.ds(0, 2)]
                pltpu.make_async_remote_copy(
                    src_ref=both,
                    dst_ref=both,
                    send_sem=self.out_sem.at[i],
                    recv_sem=self.beside_sem.at[i, z],
                    device_id=self.target(self.BESIDE),
                    device_id_type=MESH_ID,
                ).wait_recv()

        if present is None:
            wait()
        else:
            pl.when(present)(wait)

    def left(self, sem, ref, count, first, rows):
        sent = ref.at[pl.ds(0, count), pl.ds(first, rows)]
        pltpu.make_async_remote_copy(
            src_ref=sent,
            dst_ref=sent,
            send_sem=sem,
            recv_sem=self.beside_sem.at[0, 0],
            device_id=self.target(self.BESIDE),
            device_id_type=MESH_ID,
        ).wait_send()

    def finish(self):
        def settle(ways, hops, planes):
            for part, (ref, first, rows) in enumerate(self.parts):
                wide = 1 if part in self.line else 2
                for way in ways:
                    self.left(self.line_sem.at[part, way], ref, wide * hops, first, rows)
                across = planes if part in self.line else 1
                self.left(self.line_sem.at[part, self.ACROSS], ref, across, first, rows)
            for i, ref in enumerate(self.buffers):
                self.left(self.out_sem.at[i], ref, 2 * planes, 0, ref.shape[1])

        pl.when(self.has_up & self.has_down)(lambda: settle((self.UP, self.DOWN), 2, 4))
        pl.when(jnp.logical_not(self.has_down))(lambda: settle((self.UP,), 1, 3))
        pl.when(jnp.logical_not(self.has_up))(lambda: settle((self.DOWN,), 1, 3))


def gather_sems(parts, groups):
    dma = pltpu.SemaphoreType.DMA
    return [dma((parts, 2 * PLANES)), dma((groups, PLANES)), dma((parts, 3)), dma((groups,))]


class VectorSum:
    def __init__(self, ref, partial, arrived, send_sem, recv_sem):
        self.ref, self.partial, self.arrived = ref, partial, arrived
        self.send_sem, self.recv_sem = send_sem, recv_sem
        self.y, self.z, self.x, self.c = where_am_i()

    def device(self, y, z, x, c):
        return (y, z * 4 + x * 2 + c)

    def copy(self, source, slot, device):
        stage = min(slot, 3)
        return pltpu.make_async_remote_copy(
            src_ref=source,
            dst_ref=self.arrived.at[slot],
            send_sem=self.send_sem.at[stage],
            recv_sem=self.recv_sem.at[stage],
            device_id=device,
            device_id_type=MESH_ID,
        )

    def start(self, stage):
        y, z, x, c = self.y, self.z, self.x, self.c
        source = self.ref if stage == 0 else self.partial.at[stage - 1]
        if stage < 3:
            device = (
                self.device(y, z, x, 1 - c),
                self.device(1 - y, z, x, c),
                self.device(y, z, 1 - x, c),
            )[stage]
            self.copy(source, stage, device).start()
        else:
            for step in range(1, PLANES):
                self.copy(
                    source, 2 + step, self.device(y, (z + step) % PLANES, x, c)
                ).start()

    def counted(self, stage):
        both = self.arrived.at[pl.ds(0, 1 if stage < 3 else 3)]
        return pltpu.make_async_remote_copy(
            src_ref=both,
            dst_ref=both,
            send_sem=self.send_sem.at[stage],
            recv_sem=self.recv_sem.at[stage],
            device_id=self.device(self.y, self.z, self.x, 1 - self.c),
            device_id_type=MESH_ID,
        )

    def take(self, stage):
        total = self.ref[...] if stage == 0 else self.partial[stage - 1]
        self.counted(stage).wait_recv()
        for slot in (stage,) if stage < 3 else (3, 4, 5):
            total = total + self.arrived[slot]
        self.partial[stage] = total

    def finish(self):
        for stage in range(4):
            self.counted(stage).wait_send()

    def own_share(self, rows, share):
        width = self.ref.shape[1]
        place = self.y * 16 + self.z * 4 + self.x * 2 + self.c
        per_row = width // share
        offset = place % per_row * share
        row_index = lax.broadcasted_iota(jnp.int32, (width, 128), 0)
        column_index = lax.broadcasted_iota(jnp.int32, (width, 128), 1)
        picked = jnp.where(
            (row_index == column_index + offset) & (column_index < share), 1.0, 0.0
        ).astype(jnp.bfloat16)
        rest = rows
        total = jnp.zeros((rows.shape[0], 128), jnp.float32)
        for _ in range(3):
            piece = rest.astype(jnp.bfloat16)
            total = total + product(piece, picked, CONTRACT_INNER)
            rest = rest - piece.astype(jnp.float32)
        return total, place // per_row


STEP = 384
UNROLL = 6


class Quad:
    def __init__(self, by_x):
        self.by_x = by_x
        self.y, self.z, self.x, self.c = where_am_i()
        self.a, self.b = (self.x, self.y) if by_x else (self.y, self.x)
        self.mine = self.a * 2 + self.c
        self.peer = (1 - self.a) * 2 + self.c
        self.beside = self.a * 2 + 1 - self.c
        self.corner = (1 - self.a) * 2 + 1 - self.c

    def device(self, a, b, z, c):
        y, x = (b, a) if self.by_x else (a, b)
        return (y, z * 4 + x * 2 + c)

    def at_peer(self):
        return self.device(1 - self.a, self.b, self.z, self.c)

    def at_beside(self):
        return self.device(self.a, self.b, self.z, 1 - self.c)

    def at_corner(self):
        return self.device(1 - self.a, self.b, self.z, 1 - self.c)

    def link(self, source, target, send_sem, recv_sem, device):
        return pltpu.make_async_remote_copy(
            src_ref=source,
            dst_ref=target,
            send_sem=send_sem,
            recv_sem=recv_sem,
            device_id=device,
            device_id_type=MESH_ID,
        )

    def count(self, ref, send_sem, recv_sem):
        return self.link(ref, ref, send_sem, recv_sem, self.at_beside())


class Shared:
    def __init__(self, left, by_x, buffers):
        self.left = left
        self.held, self.send_sem, self.recv_sem = buffers
        self.quad = Quad(by_x)
        self.width = self.held.shape[2]

    def part(self, a):
        if self.quad.by_x:
            return self.left
        return self.left.at[:, pl.ds(pl.multiple_of(a * self.width, 128), self.width)]

    def share(self):
        q = self.quad
        slot = self.held.at[q.mine]
        send = self.send_sem.at[0]
        q.link(self.part(1 - q.a), slot, send, self.recv_sem.at[0], q.at_peer()).start()
        q.link(self.part(q.a), slot, send, self.recv_sem.at[1], q.at_beside()).start()
        self.held[q.mine] = self.part(q.a)[...]

    def relay(self):
        q = self.quad
        slot = self.held.at[q.peer]
        q.count(slot, self.send_sem.at[0], self.recv_sem.at[0]).wait_recv()
        q.link(slot, slot, self.send_sem.at[0], self.recv_sem.at[1], q.at_beside()).start()

    def complete(self):
        two = self.held.at[pl.ds(0, 2)]
        self.quad.count(two, self.send_sem.at[0], self.recv_sem.at[1]).wait_recv()

    def finish(self):
        three = self.held.at[pl.ds(0, 3)]
        self.quad.count(three, self.send_sem.at[0], self.recv_sem.at[1]).wait_send()


class Piece:
    def __init__(self, shared, right, base, stride, out, buffers):
        self.shared, self.right, self.base, self.stride, self.out = shared, right, base, stride, out
        self.rights, self.whole, self.b_in, self.z_in, self.last, self.send_sem, self.recv_sem = buffers
        self.quad = shared.quad
        self.share_rows = out.shape[0]

    def columns(self, member):
        place = member if self.quad.by_x else member % 2
        return pl.ds(pl.multiple_of(self.base + place * self.stride, 128), STEP)

    def give(self, member, device):
        self.quad.link(
            self.right.at[:, self.columns(member)], self.rights.at[self.quad.mine],
            self.send_sem.at[0], self.recv_sem.at[0], device,
        ).start()

    def share(self):
        q = self.quad
        self.give(q.peer, q.at_peer())
        self.give(q.corner, q.at_corner())
        self.give(q.beside, q.at_beside())
        self.rights[q.mine] = self.right[:, self.columns(q.mine)]

    def share_early(self):
        q = self.quad

        @pl.when(q.c == 0)
        def _():
            self.give(q.peer, q.at_peer())

        @pl.when(q.c == 1)
        def _():
            self.give(q.corner, q.at_corner())
            self.give(q.beside, q.at_beside())

    def share_late(self):
        q = self.quad

        @pl.when(q.c == 1)
        def _():
            self.give(q.peer, q.at_peer())

        @pl.when(q.c == 0)
        def _():
            self.give(q.corner, q.at_corner())
            self.give(q.beside, q.at_beside())

        self.rights[q.mine] = self.right[:, self.columns(q.mine)]

    def slab(self, b):
        return self.whole.at[b] if self.quad.by_x else self.whole.at[:, b]

    def cell(self, z):
        b = self.quad.b
        return self.whole.at[b, z] if self.quad.by_x else self.whole.at[z, b]

    def multiply(self):
        q = self.quad
        three = self.rights.at[pl.ds(0, 3)]
        q.count(three, self.send_sem.at[0], self.recv_sem.at[0]).wait_recv()
        held = self.shared.held
        tokens = held.shape[0] * held.shape[1]
        right = self.rights[...].reshape(tokens, STEP)
        if self.shared.width > STEP:

            def one(i, carry):
                left = held[:, :, pl.ds(pl.multiple_of(i * STEP, 128), STEP)]
                part = product(left.reshape(tokens, STEP), right, CONTRACT_FIRST)
                self.whole[i] = part.astype(jnp.bfloat16).reshape(self.whole.shape[1:])
                return carry

            lax.fori_loop(0, self.shared.width // STEP, one, 0)
        else:
            part = product(held[...].reshape(tokens, STEP), right, CONTRACT_FIRST)
            self.whole[...] = part.astype(jnp.bfloat16).reshape(self.whole.shape)
        q.link(
            self.slab(1 - q.b), self.b_in, self.send_sem.at[1], self.recv_sem.at[1],
            q.device(q.a, 1 - q.b, q.z, q.c),
        ).start()

    def spread(self):
        q = self.quad
        q.count(self.b_in, self.send_sem.at[1], self.recv_sem.at[1]).wait_recv()
        slab = self.slab(q.b)
        slab[...] = (slab[...].astype(jnp.float32) + self.b_in[...].astype(jnp.float32)).astype(
            jnp.bfloat16
        )
        q.count(self.rights.at[pl.ds(0, 3)], self.send_sem.at[0], self.recv_sem.at[0]).wait_send()
        for step in range(1, PLANES):
            target = (q.z + step) % PLANES
            q.link(
                self.cell(target), self.z_in.at[q.z], self.send_sem.at[0], self.recv_sem.at[2],
                q.device(q.a, q.b, target, q.c),
            ).start()

    def rows_of(self, member):
        place = member if self.quad.by_x else member % 2
        return self.last.at[pl.ds(pl.multiple_of(place * self.share_rows, 8), self.share_rows)]

    def collect(self):
        q = self.quad
        three = self.z_in.at[pl.ds(0, 3)]
        q.count(three, self.send_sem.at[0], self.recv_sem.at[2]).wait_recv()
        total = self.cell(q.z)[...].astype(jnp.float32)
        for step in range(1, PLANES):
            total = total + self.z_in[(q.z + step) % PLANES].astype(jnp.float32)
        self.last[...] = total
        q.count(self.b_in, self.send_sem.at[1], self.recv_sem.at[1]).wait_send()
        columns = self.out.at[:, self.columns(q.mine)]
        partners = [(q.beside, q.at_beside())]
        if q.by_x:
            partners = [(q.peer, q.at_peer()), (q.corner, q.at_corner())] + partners
        for member, device in partners:
            q.link(
                self.rows_of(member), columns, self.send_sem.at[1], self.recv_sem.at[3], device
            ).start()
        columns[...] = self.rows_of(q.mine)[...]

    def finish(self):
        q = self.quad
        others = self.last.at[pl.ds(0, (3 if q.by_x else 1) * self.share_rows)]
        q.count(others, self.send_sem.at[1], self.recv_sem.at[3]).wait()
        three = self.z_in.at[pl.ds(0, 3)]
        q.count(three, self.send_sem.at[0], self.recv_sem.at[2]).wait_send()


def shared_scratch(frame_count, left_width, by_x):
    return [
        pltpu.VMEM((4, frame_count, left_width if by_x else left_width // 2), jnp.bfloat16),
        pltpu.SemaphoreType.DMA((1,)),
        pltpu.SemaphoreType.DMA((2,)),
    ]


def piece_scratch(frame_count, left_width, by_x):
    rows = left_width // (2 * PLANES) if by_x else left_width // (4 * PLANES)
    low = jnp.bfloat16
    return [
        pltpu.VMEM((4, frame_count, STEP), low),
        pltpu.VMEM((2, PLANES, rows, STEP) if by_x else (PLANES, 2, rows, STEP), low),
        pltpu.VMEM((PLANES, rows, STEP), low),
        pltpu.VMEM((PLANES, rows, STEP), low),
        pltpu.VMEM((rows, STEP), jnp.float32),
        pltpu.SemaphoreType.DMA((2,)),
        pltpu.SemaphoreType.DMA((4,)),
    ]


def layer_scratch(frame_count, width, inner):
    low, wide = jnp.bfloat16, jnp.float32
    dma = pltpu.SemaphoreType.DMA
    return dict(
        qkv_held=pltpu.VMEM((width, 3 * width), low),
        out_held=pltpu.VMEM((width, width), low),
        up_held=pltpu.VMEM((width, inner), low),
        down_held=pltpu.VMEM((inner, width), low),
        weight_sem=dma((4,)),
        block=pltpu.VMEM((BLOCKS, frame_count + 16, width), low),
        block_sems=gather_sems(2, 1),
        grad_block=pltpu.VMEM((BLOCKS, frame_count, width), low),
        stats=pltpu.VMEM((BLOCKS, 32, frame_count), wide),
        grad_sems=gather_sems(3, 2),
        projected=pltpu.VMEM((BLOCKS, frame_count, 3 * width), low),
        mask=pltpu.VMEM((frame_count, BLOCKS * frame_count), wide),
        attended=pltpu.VMEM((frame_count, width), wide),
        slope=pltpu.VMEM((frame_count, inner), wide),
        logs=pltpu.VMEM((frame_count, 128), wide),
        delta=pltpu.VMEM((frame_count, 128), wide),
        inner_bias=pltpu.VMEM((1, inner), wide),
        act=pltpu.VMEM((frame_count, inner), low),
        pre_low=pltpu.VMEM((frame_count, inner), low),
        context=pltpu.VMEM((frame_count, width), low),
        hidden_low=pltpu.VMEM((frame_count, width), low),
        second_low=pltpu.VMEM((frame_count, width), low),
        first_low=pltpu.VMEM((frame_count, width), low),
        normed=pltpu.VMEM((frame_count, width), wide),
        running=pltpu.VMEM((frame_count, width), wide),
        first_grad=pltpu.VMEM((frame_count, width), wide),
        proj_grad=pltpu.VMEM((frame_count, 3 * width), low),
        vector=pltpu.VMEM((16, width), wide),
        vector_partial=pltpu.VMEM((4, 16, width), wide),
        vector_arrived=pltpu.VMEM((6, 16, width), wide),
        vector_send=dma((4,)),
        vector_recv=dma((4,)),
        down_left=shared_scratch(frame_count, inner, False),
        up_left=shared_scratch(frame_count, width, True),
        out_left=shared_scratch(frame_count, width, False),
        qkv_left=shared_scratch(frame_count, width, False),
        down_piece=piece_scratch(frame_count, inner, False),
        up_pieces=[piece_scratch(frame_count, width, True) for _ in range(2)],
        out_piece=piece_scratch(frame_count, width, False),
        qkv_pieces=[piece_scratch(frame_count, width, False) for _ in range(3)],
    )


class Inputs(typing.NamedTuple):
    frames: typing.Any
    segment_ids: typing.Any
    qkv_weight: typing.Any
    query_bias: typing.Any
    value_bias: typing.Any
    out_weight: typing.Any
    out_bias: typing.Any
    norm1_gain: typing.Any
    norm1_shift: typing.Any
    up_weight: typing.Any
    up_bias: typing.Any
    down_weight: typing.Any
    down_bias: typing.Any
    norm2_gain: typing.Any
    norm2_shift: typing.Any
    cotangent: typing.Any


class Outputs(typing.NamedTuple):
    layer_out: typing.Any
    input_grad: typing.Any
    qkv_g: typing.Any
    query_g: typing.Any
    value_g: typing.Any
    out_g: typing.Any
    outbias_g: typing.Any
    gain1_g: typing.Any
    shift1_g: typing.Any
    up_g: typing.Any
    upbias_g: typing.Any
    down_g: typing.Any
    downbias_g: typing.Any
    gain2_g: typing.Any
    shift2_g: typing.Any


class Refs:
    def __init__(self, *groups):
        for group in groups:
            for name, ref in group.items():
                setattr(self, name, ref)


def layer_kernel(held, *refs):
    inputs, outputs = len(Inputs._fields), len(Outputs._fields)
    scratch = jax.tree.unflatten(held, refs[inputs + outputs :])
    k = Refs(dict(zip(Inputs._fields + Outputs._fields, refs)), scratch)
    frame_count, width = k.frames.shape
    inner = k.inner_bias.shape[1]
    low, wide = jnp.bfloat16, jnp.float32
    total = BLOCKS * frame_count
    row, z, x, c = where_am_i()
    mine = z * 4 + x * 2 + c
    has_up, has_down = z < PLANES - 1, z > 0
    edge = jnp.logical_not(has_up & has_down)
    far = (z + 2) % PLANES
    lost = PLANES - 1 - z
    lane = lax.broadcasted_iota(jnp.int32, (frame_count, 128), 1)

    def fetch(i):
        source, target = (
            (k.qkv_weight, k.qkv_held),
            (k.out_weight, k.out_held),
            (k.up_weight, k.up_held),
            (k.down_weight, k.down_held),
        )[i]
        return pltpu.make_async_copy(source, target, k.weight_sem.at[i])

    for i in range(4):
        fetch(i).start()

    line_rows = frame_count // 2
    link = RowGather(
        [
            (k.block, 0, line_rows),
            (k.block, line_rows, k.block.shape[1] - line_rows),
        ],
        (0,),
        (1,),
        k.block_sems,
    )
    back = RowGather(
        [
            (k.grad_block, 0, line_rows),
            (k.grad_block, line_rows, frame_count - line_rows),
            (k.stats, 0, 32),
        ],
        (2, 0),
        (1,),
        k.grad_sems,
    )
    down_left = Shared(k.act, False, k.down_left)
    up_left = Shared(k.hidden_low, True, k.up_left)
    out_left = Shared(k.context, False, k.out_left)
    qkv_left = Shared(k.frames, False, k.qkv_left)
    half_width = width // 2
    down = Piece(down_left, k.second_low, 0, half_width, k.down_g, k.down_piece)
    ups = [
        Piece(up_left, k.pre_low, p * STEP, width, k.up_g, k.up_pieces[p]) for p in range(2)
    ]
    out = Piece(out_left, k.first_low, 0, half_width, k.out_g, k.out_piece)
    qkvs = [
        Piece(qkv_left, k.proj_grad, p * width, half_width, k.qkv_g, k.qkv_pieces[p])
        for p in range(3)
    ]
    vector = VectorSum(
        k.vector, k.vector_partial, k.vector_arrived, k.vector_send, k.vector_recv
    )

    places = [(row, z, x, 1 - c), (1 - row, z, x, c), (1 - row, z, x, 1 - c)]
    places += [(row, z, 1 - x, c), (row, z, 1 - x, 1 - c)]
    places += [(row, (z + step) % PLANES, x, c) for step in range(1, PLANES)]
    partners = [(None, (y, at * 4 + across * 2 + core)) for y, at, across, core in places]
    meet(partners, len(partners))

    k.block[mine, pl.ds(0, frame_count), :] = k.frames[...]
    own_ids = jnp.broadcast_to(k.segment_ids[...], (frame_count, frame_count)).astype(wide)
    k.block[mine, pl.ds(frame_count, 16), pl.ds(0, frame_count)] = own_ids[:16].astype(low)
    link.own()
    qkv_left.share()
    ids_column = own_ids.T
    k.inner_bias[...] = k.up_bias[...].reshape(1, inner)
    query_bias = k.query_bias[...].reshape(1, width)
    value_bias = k.value_bias[...].reshape(1, width)

    def plane_rows(plane):
        return jnp.concatenate(
            [k.block[plane * 4 + i, pl.ds(0, frame_count), :] for i in range(4)], axis=0
        )

    def store_rows(plane, third, part):
        for i in range(4):
            k.projected[plane * 4 + i, :, pl.ds(third * width, width)] = part[
                i * frame_count : (i + 1) * frame_count
            ]

    def as_query(part):
        return (part + query_bias).astype(low) * HEAD_DIM**-0.5

    def project(plane):
        rows = plane_rows(plane)
        keys = product(rows, k.qkv_held[:, pl.ds(width, width)], CONTRACT_INNER)
        store_rows(plane, 1, keys.astype(low))
        values = product(rows, k.qkv_held[:, pl.ds(2 * width, width)], CONTRACT_INNER)
        store_rows(plane, 2, (values + value_bias).astype(low))
        for i in range(4):
            ids = k.block[plane * 4 + i, pl.ds(frame_count, 8), pl.ds(0, frame_count)]
            same = jnp.broadcast_to(ids.astype(wide)[:1], own_ids.shape) == ids_column
            at = pl.multiple_of((plane * 4 + i) * frame_count, 128)
            k.mask[:, pl.ds(at, frame_count)] = jnp.where(same, 0.0, mask_fill)

    def project_queries(plane):
        queries = product(plane_rows(plane), k.qkv_held[:, pl.ds(0, width)], CONTRACT_INNER)
        store_rows(plane, 0, as_query(queries))

    def columns_of(third, j):
        return pl.ds(pl.multiple_of(third * width + j * 128, 128), 128)

    def head_state(h):
        return pl.ds(pl.multiple_of(h * 128, 128), 128)

    def both_heads(values):
        nothing = jnp.zeros_like(values)
        return jnp.concatenate(
            [jnp.where(lane < HALF, values, nothing), jnp.where(lane < HALF, nothing, values)],
            axis=0,
        )

    def own_halves(values):
        return jnp.where(lane < HALF, values[:frame_count], values[frame_count:])

    def attend(plane, first):
        at = pl.multiple_of(plane * 4 * frame_count, 128)

        def state(kind, j):
            return k.slope.at[:, pl.ds(pl.multiple_of((kind * HEADS + 2 * j) * 128, 128), 256)]

        def read(kind, j):
            pair_state = state(kind, j)[...]
            return jnp.concatenate([pair_state[:, :128], pair_state[:, 128:]], axis=0)

        def write(kind, j, values):
            state(kind, j)[...] = jnp.concatenate(
                [values[:frame_count], values[frame_count:]], axis=1
            )

        def pair(j, carry):
            query = both_heads(k.projected[mine, :, columns_of(0, j)])
            keys = k.projected[pl.ds(plane * 4, 4), :, columns_of(1, j)].reshape(-1, 128)
            values = k.projected[pl.ds(plane * 4, 4), :, columns_of(2, j)].reshape(-1, 128)
            mask = k.mask[:, pl.ds(at, 4 * frame_count)]
            scores = product(query, keys, CONTRACT_LAST) + jnp.concatenate([mask, mask], axis=0)
            tile = (2 * frame_count, 128)
            peak = jnp.broadcast_to(jnp.max(scores, axis=1, keepdims=True), tile)
            if not first:
                old = read(0, j)
                peak = jnp.maximum(peak, old)
                factor = jnp.exp(old - peak)
            weights = jnp.exp(scores - jnp.concatenate([peak] * 4, axis=1))
            whole = jnp.broadcast_to(jnp.sum(weights, axis=1, keepdims=True), tile)
            if not first:
                whole = whole + read(1, j) * factor
            write(0, j, peak)
            write(1, j, whole)
            both = own_halves(product(weights.astype(low), values, CONTRACT_INNER))
            if not first:
                both = both + k.attended[:, columns_of(0, j)] * own_halves(factor)
            k.attended[:, columns_of(0, j)] = both
            return carry

        lax.fori_loop(0, PAIRS, pair, 0, unroll=UNROLL)

    fetch(0).wait()
    own_query = product(k.frames[...], k.qkv_held[:, pl.ds(0, width)], CONTRACT_INNER)
    k.projected[mine, :, pl.ds(0, width)] = as_query(own_query)
    link.near_first()
    link.plane_done(z)
    project(z)
    link.near_second()
    attend(z, True)
    link.far_line()

    @pl.when(has_down)
    def _():
        link.plane_done(z - 1)
        project(z - 1)
        attend(z - 1, False)

    @pl.when(has_up)
    def _():
        link.plane_done(z + 1)
        project(z + 1)

    link.far_rest()

    @pl.when(has_up)
    def _():
        attend(z + 1, False)

    link.plane_done(far)
    project(far)
    attend(far, False)
    logs = jnp.zeros(lane.shape, wide)
    for j in range(PAIRS):
        parts = []
        for h in range(2):
            whole = k.slope[:, head_state(HEADS + 2 * j + h)]
            logs = jnp.where(
                lane == 2 * j + h, k.slope[:, head_state(2 * j + h)] + jnp.log(whole), logs
            )
            parts.append(whole)
        done = k.attended[:, columns_of(0, j)] / jnp.where(lane < HALF, parts[0], parts[1])
        k.attended[:, columns_of(0, j)] = done
        k.context[:, columns_of(0, j)] = done.astype(low)
    k.logs[...] = logs
    out_left.share()

    def normalize(resid):
        centred = resid - jnp.mean(resid, axis=-1, keepdims=True)
        inverse = lax.rsqrt(jnp.mean(centred * centred, axis=-1, keepdims=True) + norm_eps)
        return centred * inverse, inverse

    def normalize_back(upstream, normed, inverse, gain):
        scaled = upstream * gain
        first_mean = jnp.mean(scaled, axis=-1, keepdims=True)
        second_mean = jnp.mean(scaled * normed, axis=-1, keepdims=True)
        return inverse * (scaled - first_mean - normed * second_mean)

    def note(index, values):
        k.vector[pl.ds(index, 1), :] = jnp.sum(values, axis=0, keepdims=True)

    def flat(ref):
        return ref[...].reshape(1, width)

    k.vector[pl.ds(8, 8), :] = jnp.zeros((8, width), wide)
    fetch(1).wait()
    resid_one = (
        k.frames[...].astype(wide)
        + product(k.context[...], k.out_held[...], CONTRACT_INNER)
        + flat(k.out_bias)
    )
    normed_one, inverse_one = normalize(resid_one)
    k.normed[...] = normed_one
    hidden = normed_one * flat(k.norm1_gain) + flat(k.norm1_shift)
    k.hidden_low[...] = hidden.astype(low)
    up_left.share()
    k.running[...] = hidden + flat(k.down_bias)
    fetch(2).wait()
    fetch(3).wait()

    def forward(f, carry):
        columns = pl.ds(pl.multiple_of(f * width, 128), width)
        pre_act = (
            product(k.hidden_low[...], k.up_held[:, columns], CONTRACT_INNER)
            + k.inner_bias[:, columns]
        )
        normal_cdf = 0.5 * (1.0 + lax.erf(pre_act * 0.5**0.5))
        normal_pdf = jnp.exp(-0.5 * pre_act * pre_act) * (2.0 * math.pi) ** (-0.5)
        act = (pre_act * normal_cdf).astype(low)
        k.act[:, columns] = act
        k.slope[:, columns] = normal_cdf + pre_act * normal_pdf
        k.running[...] += product(
            act, k.down_held[pl.ds(pl.multiple_of(f * width, 128), width), :], CONTRACT_INNER
        )
        return carry

    lax.fori_loop(0, inner // width, forward, 0)
    down_left.share()
    normed_two, inverse_two = normalize(k.running[...])
    k.layer_out[...] = (normed_two * flat(k.norm2_gain) + flat(k.norm2_shift)).astype(low)
    upstream = k.cotangent[...].astype(wide)
    second_grad = normalize_back(upstream, normed_two, inverse_two, flat(k.norm2_gain))
    k.second_low[...] = second_grad.astype(low)
    down.share()
    note(5, second_grad)
    note(6, upstream * normed_two)
    note(7, upstream)
    k.running[...] = second_grad
    for p in range(2):
        for member in range(4):
            first = member * width + p * STEP
            columns = pl.ds(first, STEP)
            pre_grad = (
                product(k.second_low[...], k.down_held[columns, :], CONTRACT_LAST)
                * k.slope[:, columns]
            )
            k.vector[pl.ds(8 + first // width, 1), pl.ds(first % width, STEP)] = jnp.sum(
                pre_grad, axis=0, keepdims=True
            )
            k.pre_low[:, columns] = pre_grad.astype(low)
            k.running[...] += product(
                k.pre_low[:, columns], k.up_held[:, columns], CONTRACT_LAST
            )
        ups[p].share()
        if p == 0:
            up_left.relay()
    hidden_grad = k.running[...]
    normed_one = k.normed[...]
    first_grad = normalize_back(hidden_grad, normed_one, inverse_one, flat(k.norm1_gain))
    k.first_grad[...] = first_grad
    k.first_low[...] = first_grad.astype(low)
    out.share()
    context_grad = product(k.first_low[...], k.out_held[...], CONTRACT_LAST).astype(low)
    k.grad_block[mine] = context_grad
    delta = jnp.zeros(lane.shape, wide)
    for j in range(PAIRS):
        columns = slice(j * 128, (j + 1) * 128)
        both = context_grad[:, columns].astype(wide) * k.attended[:, columns]
        for h in range(2):
            one = jnp.sum(
                jnp.where((lane < HALF) == (h == 0), both, 0.0), axis=1, keepdims=True
            )
            delta = jnp.where(lane == 2 * j + h, one, delta)
    k.delta[...] = delta
    k.stats[mine, pl.ds(0, 16), :] = k.logs[...].T[:16]
    k.stats[mine, pl.ds(16, 16), :] = delta.T[:16]
    back.own()
    note(2, first_grad)
    note(3, hidden_grad * normed_one)
    note(4, hidden_grad)

    @pl.when(edge)
    def _():
        for i in range(4):
            k.projected[lost * 4 + i] = jnp.zeros((frame_count, 3 * width), low)
            k.grad_block[lost * 4 + i] = jnp.zeros((frame_count, width), low)
            k.stats[lost * 4 + i] = jnp.zeros((32, frame_count), wide)
            at = pl.multiple_of((lost * 4 + i) * frame_count, 128)
            k.mask[:, pl.ds(at, frame_count)] = jnp.full(lane.shape, mask_fill, wide)

    def query_pair(j):
        query = k.projected[mine, :, columns_of(0, j)]
        upstream = k.grad_block[mine, :, columns_of(0, j)]
        keys = k.projected[:, :, columns_of(1, j)].reshape(total, 128)
        values = k.projected[:, :, columns_of(2, j)].reshape(total, 128)
        outs = []
        for h in range(2):
            chosen = (lane < HALF) == (h == 0)
            nothing = jnp.zeros_like(query)
            logs = jnp.sum(
                jnp.where(lane == 2 * j + h, k.logs[...], 0.0), axis=1, keepdims=True
            )
            shift = jnp.sum(
                jnp.where(lane == 2 * j + h, k.delta[...], 0.0), axis=1, keepdims=True
            )
            scores = product(jnp.where(chosen, query, nothing), keys, CONTRACT_LAST)
            probs = jnp.exp(scores + k.mask[...] - logs)
            prob_grad = product(jnp.where(chosen, upstream, nothing), values, CONTRACT_LAST)
            score_grad = (probs * (prob_grad - shift)).astype(low)
            outs.append(product(score_grad, keys, CONTRACT_INNER))
        k.proj_grad[:, columns_of(0, j)] = (
            jnp.where(lane < HALF, outs[0], outs[1]) * HEAD_DIM**-0.5
        ).astype(low)

    def key_pair(j):
        key = k.projected[mine, :, columns_of(1, j)]
        value = k.projected[mine, :, columns_of(2, j)]
        queries = k.projected[:, :, columns_of(0, j)].reshape(total, 128)
        upstream = k.grad_block[:, :, columns_of(0, j)].reshape(total, 128)
        key_outs, value_outs = [], []
        for h in range(2):
            chosen = (lane < HALF) == (h == 0)
            nothing = jnp.zeros_like(key)
            logs = jnp.concatenate(
                [k.stats[b, pl.ds(2 * j + h, 1), :] for b in range(BLOCKS)], axis=1
            )
            shift = jnp.concatenate(
                [k.stats[b, pl.ds(16 + 2 * j + h, 1), :] for b in range(BLOCKS)], axis=1
            )
            scores = product(jnp.where(chosen, key, nothing), queries, CONTRACT_LAST)
            probs = jnp.exp(scores + k.mask[...] - logs)
            prob_grad = product(jnp.where(chosen, value, nothing), upstream, CONTRACT_LAST)
            score_grad = (probs * (prob_grad - shift)).astype(low)
            key_outs.append(product(score_grad, queries, CONTRACT_INNER))
            value_outs.append(product(probs.astype(low), upstream, CONTRACT_INNER))
        k.proj_grad[:, columns_of(1, j)] = jnp.where(
            lane < HALF, key_outs[0], key_outs[1]
        ).astype(low)
        k.proj_grad[:, columns_of(2, j)] = jnp.where(
            lane < HALF, value_outs[0], value_outs[1]
        ).astype(low)

    def pairs(one, first, last):
        def body(j, carry):
            one(j)
            return carry

        lax.fori_loop(first, last, body, 0)

    qkv_left.relay()
    pairs(query_pair, 0, 2)
    back.near_first()
    up_left.complete()
    pairs(query_pair, 2, 3)
    ups[0].multiply()
    back.near_second()
    pairs(query_pair, 3, 5)
    back.far_line()
    down_left.relay()
    ups[1].multiply()
    pairs(query_pair, 5, 6)
    qkvs[0].share()
    back.far_rest()
    project_queries(z)
    project_queries(far)
    down_left.complete()
    down.multiply()

    @pl.when(has_down)
    def _():
        project_queries(z - 1)

    @pl.when(has_up)
    def _():
        project_queries(z + 1)

    out_left.relay()
    ups[0].spread()
    back.plane_done(z)
    back.plane_done(z - 1, has_down)
    back.plane_done(z + 1, has_up)
    back.plane_done(far)
    pairs(key_pair, 0, 2)
    ups[1].spread()
    out_left.complete()
    out.multiply()
    pairs(key_pair, 2, 3)
    qkvs[1].share_early()
    qkvs[2].share_early()
    qkv_left.complete()
    qkvs[0].multiply()
    pairs(key_pair, 3, 4)
    down.spread()
    ups[0].collect()
    pairs(key_pair, 4, 5)
    out.spread()
    ups[1].collect()
    pairs(key_pair, 5, 6)
    qkvs[1].share_late()
    qkvs[2].share_late()
    note(0, k.proj_grad[:, pl.ds(0, width)].astype(wide))
    note(1, k.proj_grad[:, pl.ds(2 * width, width)].astype(wide))
    vector.start(0)
    qkvs[0].spread()
    k.input_grad[...] = k.first_grad[...] + product(
        k.proj_grad[...], k.qkv_held[...], CONTRACT_LAST
    )
    vector.take(0)
    vector.start(1)
    down.collect()
    out.collect()
    qkvs[1].multiply()
    vector.take(1)
    vector.start(2)
    qkvs[2].multiply()
    qkvs[0].collect()
    qkvs[1].spread()
    vector.take(2)
    vector.start(3)
    qkvs[2].spread()
    vector.take(3)
    summed = k.vector_partial[3]
    share = k.query_g.shape[0]
    shares, _ = vector.own_share(summed[:8], share)
    for i, ref in enumerate(
        (k.query_g, k.value_g, k.outbias_g, k.gain1_g, k.shift1_g, k.downbias_g, k.gain2_g, k.shift2_g)
    ):
        ref[...] = shares[i, :share]
    up_shares, at = vector.own_share(summed[8:], 4 * share)
    keep = lax.broadcasted_iota(jnp.int32, up_shares.shape, 0) == at
    picked = jnp.sum(jnp.where(keep, up_shares, 0.0), axis=0, keepdims=True)
    k.upbias_g[...] = picked[0, : 4 * share]
    qkvs[1].collect()
    qkvs[2].collect()
    for each in [down_left, up_left, out_left, qkv_left, down, out] + ups + qkvs:
        each.finish()
    back.finish()
    link.finish()
    vector.finish()


def copy_kernel(*refs):
    count = len(refs) // 2
    for source, target in zip(refs[:count], refs[count:]):
        target[...] = source[...]


def hand_over(results):
    return pl.pallas_call(
        copy_kernel,
        out_shape=tuple(jax.ShapeDtypeStruct(each.shape, each.dtype) for each in results),
        in_specs=[IN_VMEM] * len(results),
        out_specs=(IN_VMEM,) * len(results),
    )(*results)


def layer_step(*args):
    frames = args[0]
    frame_count, width = frames.shape[1:]
    inner = args[9].shape[1]
    low, wide = jnp.bfloat16, jnp.float32
    scratch, held = jax.tree.flatten(layer_scratch(frame_count, width, inner))
    operands = [frames[0]] + list(args[1:-1]) + [args[-1][0]]
    share = width // 32
    shapes = [
        ((frame_count, width), low),
        ((frame_count, width), wide),
        ((share, 3 * width), wide),
        ((share,), wide),
        ((share,), wide),
        ((share, width), wide),
        ((share,), wide),
        ((share,), wide),
        ((share,), wide),
        ((share, inner), wide),
        ((4 * share,), wide),
        ((4 * share, width), wide),
        ((share,), wide),
        ((share,), wide),
        ((share,), wide),
    ]
    results = pl.pallas_call(
        functools.partial(layer_kernel, held),
        out_shape=tuple(jax.ShapeDtypeStruct(shape, kind) for shape, kind in shapes),
        in_specs=[IN_PLACE if each.ndim == 2 and each.shape[0] >= width else IN_VMEM for each in operands],
        out_specs=(IN_VMEM,) * len(shapes),
        scratch_shapes=scratch,
        compiler_params=pltpu.CompilerParams(
            collective_id=0, has_side_effects=True, vmem_limit_bytes=VMEM_BYTES
        ),
    )(*operands)
    results = hand_over(results)
    return (results[0][None], results[1][None]) + tuple(results[2:])


def solution(mesh):
    chosen = layer_step if dict(mesh.shape) == {"rows": 2, "seq": 16} else shards
    in_specs = (
        P("rows", "seq", None),
        P("rows", "seq"),
        P(),
        P(),
        P(),
        P(),
        P(),
        P(),
        P(),
        P(),
        P(),
        P(),
        P(),
        P(),
        P(),
        P("rows", "seq", None),
    )
    out_specs = (
        P("rows", "seq", None),
        P("rows", "seq", None),
        P(("rows", "seq"), None),
        P(("rows", "seq")),
        P(("rows", "seq")),
        P(("rows", "seq"), None),
        P(("rows", "seq")),
        P(("rows", "seq")),
        P(("rows", "seq")),
        P(("rows", "seq"), None),
        P(("rows", "seq")),
        P(("rows", "seq"), None),
        P(("rows", "seq")),
        P(("rows", "seq")),
        P(("rows", "seq")),
    )
    return jax.shard_map(chosen, mesh=mesh, in_specs=in_specs, out_specs=out_specs, check_vma=False)
```

```python
import functools
import math
import typing

import jax
import jax.numpy as jnp
from jax import lax
from jax.experimental import pallas as pl
from jax.experimental.pallas import tpu as pltpu
from jax.sharding import PartitionSpec as P

HEADS = 12
HEAD_DIM = 64


norm_eps = 1e-05
mask_fill = -1e30


def shortened(shard):

    def short(part):
        return part.astype(jnp.bfloat16) if part.dtype == jnp.float32 else part

    return jax.tree.map(short, shard)


def passed_along(value, axis, steps):
    count = lax.axis_size(axis)
    pairs = [(source, (source + steps) % count) for source in range(count)]
    return lax.ppermute(value, axis, pairs)


def layer_norm(resid, gain, shift):
    centred = resid - jnp.mean(resid, axis=-1, keepdims=True)
    inv_std = lax.rsqrt(jnp.mean(centred * centred, axis=-1, keepdims=True) + norm_eps)
    normed = centred * inv_std
    return (normed * gain + shift, normed, inv_std)


def norm_back(upstream, normed, inv_std, gain):
    scaled = upstream * gain
    first_mean = jnp.mean(scaled, axis=-1, keepdims=True)
    second_mean = jnp.mean(scaled * normed, axis=-1, keepdims=True)
    grad_in = inv_std * (scaled - first_mean - normed * second_mean)
    return (grad_in, jnp.sum(upstream * normed, axis=0), jnp.sum(upstream, axis=0))


def gelu_slope(pre_act):
    normal_cdf = 0.5 * (1.0 + lax.erf(pre_act * 0.5**0.5))
    normal_pdf = jnp.exp(-0.5 * pre_act * pre_act) * (2.0 * math.pi) ** (-0.5)
    return normal_cdf + pre_act * normal_pdf


def head_groups(head_count):
    return [(0, head_count, 1)]


def pass_keys(blocks):
    return jax.tree.map(
        lambda part, own: part.astype(own.dtype), passed_along(shortened(blocks), "seq", 1), blocks
    )


def pass_again(blocks):
    return jax.tree.map(
        lambda part, own: part.astype(own.dtype), passed_along(shortened(blocks), "seq", 1), blocks
    )


def pass_grads(blocks):
    return (
        passed_along(blocks[0].astype(jnp.bfloat16), "seq", 1).astype(jnp.float32),
        passed_along(blocks[1].astype(jnp.bfloat16), "seq", 1).astype(jnp.float32),
    )


def block_scores(query_part, key_part, query_ids, key_ids):
    scores = jnp.einsum(
        "qhe,khe->hqk", query_part, key_part, preferred_element_type=jnp.float32
    ) * HEAD_DIM ** (-0.5)
    return jnp.where((query_ids[:, None] == key_ids[None, :])[None], scores, mask_fill)


def attend_block(carried, query_part, key_part, value_part, query_ids, key_ids):
    run_max, run_total, run_acc = carried
    scores = block_scores(query_part, key_part, query_ids, key_ids)
    new_max = jnp.maximum(run_max, jnp.max(scores, axis=-1))
    weights = jnp.exp(scores - new_max[:, :, None])
    factor = jnp.exp(run_max - new_max)
    new_total = run_total * factor + jnp.sum(weights, axis=-1)
    update = jnp.einsum(
        "hqk,khe->qhe", weights.astype(jnp.bfloat16), value_part, preferred_element_type=jnp.float32
    )
    return (new_max, new_total, run_acc * factor.T[:, :, None] + update)


def grad_block(
    carried,
    query_part,
    key_part,
    value_part,
    query_ids,
    key_ids,
    context_part,
    log_part,
    delta_part,
):
    query_acc, key_acc, value_acc = carried
    scores = block_scores(query_part, key_part, query_ids, key_ids)
    probs = jnp.exp(scores - log_part[:, :, None])
    prob_grad = jnp.einsum(
        "qhe,khe->hqk", context_part, value_part, preferred_element_type=jnp.float32
    )
    score_grad = (probs * (prob_grad - delta_part[:, :, None])).astype(jnp.bfloat16)
    scale = HEAD_DIM ** (-0.5)
    query_acc = query_acc + scale * jnp.einsum(
        "hqk,khe->qhe", score_grad, key_part, preferred_element_type=jnp.float32
    )
    key_acc = key_acc + scale * jnp.einsum(
        "hqk,qhe->khe", score_grad, query_part, preferred_element_type=jnp.float32
    )
    value_acc = value_acc + jnp.einsum(
        "hqk,qhe->khe", probs.astype(jnp.bfloat16), context_part, preferred_element_type=jnp.float32
    )
    return (query_acc, key_acc, value_acc)


def forward_cycle(
    query_heads, key_heads, value_heads, local_ids, every_id, cycle_place, cycle_size
):
    frame_count, head_count, head_width = query_heads.shape
    grouping = head_groups(head_count)
    states = []
    blocks = []
    for head_first, head_last, direction in grouping:
        head_span = head_last - head_first
        initial = (
            jnp.full((head_span, frame_count), mask_fill, jnp.float32),
            jnp.zeros((head_span, frame_count), jnp.float32),
            jnp.zeros((frame_count, head_span, head_width), jnp.float32),
        )
        states.append(
            attend_block(initial, query_heads, key_heads, value_heads, local_ids, local_ids)
        )
        blocks.append((key_heads, value_heads))

    def forward_cycle_turn(turn_index, cycle_carry):
        old_states, old_blocks = cycle_carry
        new_states = []
        new_blocks = []
        for group_info, part_state, part_block in zip(grouping, old_states, old_blocks):
            head_first, head_last, direction = group_info
            part_block = pass_keys(part_block)
            source_index = (cycle_place - direction * turn_index) % cycle_size
            key_ids = lax.dynamic_slice_in_dim(every_id, source_index * frame_count, frame_count)
            new_states.append(
                attend_block(
                    part_state, query_heads, part_block[0], part_block[1], local_ids, key_ids
                )
            )
            new_blocks.append(part_block)
        return (new_states, new_blocks)

    states, blocks = lax.fori_loop(1, cycle_size, forward_cycle_turn, (states, blocks))
    maxima = jnp.concatenate([part_state[0] for part_state in states], axis=0)
    totals = jnp.concatenate([part_state[1] for part_state in states], axis=0)
    sums_all = jnp.concatenate([part_state[2] for part_state in states], axis=1)
    attended = sums_all / totals.T[:, :, None]
    return (attended, maxima + jnp.log(totals))


def backward_cycle(
    query_heads,
    key_heads,
    value_heads,
    local_ids,
    every_id,
    context_heads,
    log_total,
    row_delta,
    cycle_place,
    cycle_size,
):
    frame_count, head_count, head_width = query_heads.shape
    grouping = head_groups(head_count)
    initial = []
    for head_first, head_last, direction in grouping:
        zero_part = jnp.zeros((frame_count, head_last - head_first, head_width), jnp.float32)
        initial.append((zero_part, (key_heads, value_heads), (zero_part, zero_part)))

    def backward_cycle_turn(turn_index, cycle_carry):
        new_carry = []
        for group_info, part_carry in zip(grouping, cycle_carry):
            head_first, head_last, direction = group_info
            query_acc, part_block, part_grads = part_carry
            source_index = (cycle_place - direction * turn_index) % cycle_size
            key_ids = lax.dynamic_slice_in_dim(every_id, source_index * frame_count, frame_count)
            query_acc, key_acc, value_acc = grad_block(
                (query_acc, part_grads[0], part_grads[1]),
                query_heads,
                part_block[0],
                part_block[1],
                local_ids,
                key_ids,
                context_heads,
                log_total,
                row_delta,
            )
            part_grads = pass_grads((key_acc, value_acc))
            part_block = pass_again(part_block)
            new_carry.append((query_acc, part_block, part_grads))
        return new_carry

    final = lax.fori_loop(0, cycle_size, backward_cycle_turn, initial)
    query_grad = jnp.concatenate([part_carry[0] for part_carry in final], axis=1)
    key_grad = jnp.concatenate([part_carry[2][0] for part_carry in final], axis=1)
    value_grad = jnp.concatenate([part_carry[2][1] for part_carry in final], axis=1)
    return (query_grad, key_grad, value_grad)


def shards(
    frames,
    segment_ids,
    qkv_weight,
    query_bias,
    value_bias,
    out_weight,
    out_bias,
    norm1_gain,
    norm1_shift,
    up_weight,
    up_bias,
    down_weight,
    down_bias,
    norm2_gain,
    norm2_shift,
    cotangent,
):
    inputs = frames[0]
    local_ids = segment_ids[0]
    frame_count, model_width = inputs.shape
    cycle_size = lax.axis_size("seq")
    cycle_place = lax.axis_index("seq")
    every_id = lax.all_gather(segment_ids, "seq", axis=1, tiled=True)[0]
    head_shape = (frame_count, HEADS, HEAD_DIM)
    projected = jnp.dot(inputs, qkv_weight, preferred_element_type=jnp.float32)
    query_heads = (projected[:, :model_width] + query_bias).astype(jnp.bfloat16).reshape(head_shape)
    key_heads = projected[:, model_width : 2 * model_width].astype(jnp.bfloat16).reshape(head_shape)
    value_heads = (
        (projected[:, 2 * model_width :] + value_bias).astype(jnp.bfloat16).reshape(head_shape)
    )
    attended, log_total = forward_cycle(
        query_heads, key_heads, value_heads, local_ids, every_id, cycle_place, cycle_size
    )
    context = attended.astype(jnp.bfloat16).reshape(frame_count, model_width)
    resid_one = (
        inputs.astype(jnp.float32)
        + jnp.dot(context, out_weight, preferred_element_type=jnp.float32)
        + out_bias
    )
    hidden, normed_one, inverse_one = layer_norm(resid_one, norm1_gain, norm1_shift)
    hidden_low = hidden.astype(jnp.bfloat16)
    pre_act = jnp.dot(hidden_low, up_weight, preferred_element_type=jnp.float32) + up_bias
    act_low = jax.nn.gelu(pre_act, approximate=False).astype(jnp.bfloat16)
    resid_two = (
        hidden + jnp.dot(act_low, down_weight, preferred_element_type=jnp.float32) + down_bias
    )
    output, normed_two, inverse_two = layer_norm(resid_two, norm2_gain, norm2_shift)
    upstream = cotangent[0].astype(jnp.float32)
    second_grad, gain_two_grad, shift_two_grad = norm_back(
        upstream, normed_two, inverse_two, norm2_gain
    )
    second_low = second_grad.astype(jnp.bfloat16)
    down_grad = jnp.einsum("tf,td->fd", act_low, second_low, preferred_element_type=jnp.float32)
    pre_grad = jnp.einsum(
        "td,fd->tf", second_low, down_weight, preferred_element_type=jnp.float32
    ) * gelu_slope(pre_act)
    pre_low = pre_grad.astype(jnp.bfloat16)
    up_grad = jnp.einsum("td,tf->df", hidden_low, pre_low, preferred_element_type=jnp.float32)
    hidden_grad = second_grad + jnp.einsum(
        "tf,df->td", pre_low, up_weight, preferred_element_type=jnp.float32
    )
    first_grad, gain_one_grad, shift_one_grad = norm_back(
        hidden_grad, normed_one, inverse_one, norm1_gain
    )
    first_low = first_grad.astype(jnp.bfloat16)
    out_grad = jnp.einsum("td,te->de", context, first_low, preferred_element_type=jnp.float32)
    context_grad = (
        jnp.einsum("te,de->td", first_low, out_weight, preferred_element_type=jnp.float32)
        .astype(jnp.bfloat16)
        .reshape(head_shape)
    )
    row_delta = jnp.einsum("qhe,qhe->hq", context_grad.astype(jnp.float32), attended)
    query_grad, key_grad, value_grad = backward_cycle(
        query_heads,
        key_heads,
        value_heads,
        local_ids,
        every_id,
        context_grad,
        log_total,
        row_delta,
        cycle_place,
        cycle_size,
    )
    query_low = query_grad.astype(jnp.bfloat16).reshape(frame_count, model_width)
    key_low = key_grad.astype(jnp.bfloat16).reshape(frame_count, model_width)
    value_low = value_grad.astype(jnp.bfloat16).reshape(frame_count, model_width)
    proj_grad = jnp.concatenate([query_low, key_low, value_low], axis=1)
    qkv_grad = jnp.einsum("td,te->de", inputs, proj_grad, preferred_element_type=jnp.float32)
    input_grad = (
        jnp.einsum("te,de->td", proj_grad, qkv_weight, preferred_element_type=jnp.float32)
        + first_grad
    )
    summed = (
        lax.psum_scatter(qkv_grad, ("rows", "seq"), scatter_dimension=0, tiled=True),
        lax.psum_scatter(
            jnp.sum(query_low.astype(jnp.float32), axis=0),
            ("rows", "seq"),
            scatter_dimension=0,
            tiled=True,
        ),
        lax.psum_scatter(
            jnp.sum(value_low.astype(jnp.float32), axis=0),
            ("rows", "seq"),
            scatter_dimension=0,
            tiled=True,
        ),
        lax.psum_scatter(out_grad, ("rows", "seq"), scatter_dimension=0, tiled=True),
        lax.psum_scatter(
            jnp.sum(first_grad, axis=0), ("rows", "seq"), scatter_dimension=0, tiled=True
        ),
        lax.psum_scatter(gain_one_grad, ("rows", "seq"), scatter_dimension=0, tiled=True),
        lax.psum_scatter(shift_one_grad, ("rows", "seq"), scatter_dimension=0, tiled=True),
        lax.psum_scatter(up_grad, ("rows", "seq"), scatter_dimension=0, tiled=True),
        lax.psum_scatter(
            jnp.sum(pre_grad, axis=0), ("rows", "seq"), scatter_dimension=0, tiled=True
        ),
        lax.psum_scatter(down_grad, ("rows", "seq"), scatter_dimension=0, tiled=True),
        lax.psum_scatter(
            jnp.sum(second_grad, axis=0), ("rows", "seq"), scatter_dimension=0, tiled=True
        ),
        lax.psum_scatter(gain_two_grad, ("rows", "seq"), scatter_dimension=0, tiled=True),
        lax.psum_scatter(shift_two_grad, ("rows", "seq"), scatter_dimension=0, tiled=True),
    )
    return (
        output.astype(jnp.bfloat16)[None],
        input_grad[None],
        summed[0],
        summed[1],
        summed[2],
        summed[3],
        summed[4],
        summed[5],
        summed[6],
        summed[7],
        summed[8],
        summed[9],
        summed[10],
        summed[11],
        summed[12],
    )


HALF = HEAD_DIM
PAIRS = HEADS // 2
CONTRACT_LAST = (((1,), (1,)), ((), ()))
CONTRACT_INNER = (((1,), (0,)), ((), ()))
CONTRACT_FIRST = (((0,), (0,)), ((), ()))
IN_VMEM = pl.BlockSpec(memory_space=pltpu.VMEM)
IN_PLACE = pl.BlockSpec(memory_space=pl.ANY)
MESH_ID = pl.DeviceIdType.MESH
VMEM_BYTES = 60 << 20
BLOCKS = 16
PLANES = 4


def product(left, right, dims):
    return lax.dot_general(left, right, dims, preferred_element_type=jnp.float32)


def where_am_i():
    row = lax.axis_index("rows")
    place = lax.axis_index("seq")
    return row, place // 4, place // 2 % 2, place % 2


def meet(partners, count):
    barrier = pltpu.get_barrier_semaphore()
    for present, target in partners:

        def signal(target=target):
            pl.semaphore_signal(barrier, inc=1, device_id=target, device_id_type=MESH_ID)

        if present is None:
            signal()
        else:
            pl.when(present)(signal)
    pl.semaphore_wait(barrier, count)


class RowGather:
    UP, DOWN, ACROSS, BESIDE = range(4)

    def __init__(self, parts, line, crossing, sems):
        self.parts, self.line, self.crossing = parts, line, crossing
        self.recv_sem, self.beside_sem, self.line_sem, self.out_sem = sems
        self.row, self.z, self.x, self.c = where_am_i()
        self.has_up, self.has_down = self.z < PLANES - 1, self.z > 0
        self.far = (self.z + 2) % PLANES
        self.buffers = []
        for ref, _, _ in parts:
            if not any(ref is known for known in self.buffers):
                self.buffers.append(ref)

    def group(self, part):
        return [self.parts[part][0] is ref for ref in self.buffers].index(True)

    def device(self, z, x, c):
        return (self.row, z * 4 + x * 2 + c)

    def target(self, way):
        return (
            self.device(self.z + 1, self.x, self.c),
            self.device(self.z - 1, self.x, self.c),
            self.device(self.z, 1 - self.x, self.c),
            self.device(self.z, self.x, 1 - self.c),
        )[way]

    def copy(self, part, z, x, way):
        ref, first, rows = self.parts[part]
        piece = ref.at[z * 4 + x * 2 + self.c, pl.ds(first, rows)]
        beside = way == self.BESIDE
        return pltpu.make_async_remote_copy(
            src_ref=piece,
            dst_ref=piece,
            send_sem=self.out_sem.at[self.group(part)] if beside else self.line_sem.at[part, way],
            recv_sem=(
                self.beside_sem.at[self.group(part), z]
                if beside
                else self.recv_sem.at[part, z * 2 + x]
            ),
            device_id=self.target(way),
            device_id_type=MESH_ID,
        )

    def send(self, part, z, x, way):
        present = {self.UP: self.has_up, self.DOWN: self.has_down}.get(way)
        if present is None:
            self.copy(part, z, x, way).start()
        else:
            pl.when(present)(lambda: self.copy(part, z, x, way).start())

    def relay(self, part, z, x, ways, present=None):
        def both():
            self.copy(part, z, x, self.ACROSS).wait_recv()
            for way in ways:
                self.send(part, z, x, way)

        if present is None:
            both()
        else:
            pl.when(present)(both)

    def own(self):
        z, x = self.z, self.x
        for part in self.crossing:
            self.send(part, z, x, self.ACROSS)
        for part in self.line + self.crossing:
            self.send(part, z, x, self.UP)
            self.send(part, z, x, self.DOWN)
        for part in self.line:
            self.send(part, z, x, self.ACROSS)
        for part in self.crossing + self.line:
            self.send(part, z, x, self.BESIDE)

    def line_near(self):
        for part in self.line:
            self.relay(part, self.z - 1, self.x, (self.UP, self.ACROSS, self.BESIDE), self.has_down)
            self.relay(part, self.z + 1, self.x, (self.DOWN, self.ACROSS, self.BESIDE), self.has_up)

    def cross_over(self):
        for part in self.crossing:
            self.relay(part, self.z, 1 - self.x, (self.UP, self.DOWN, self.BESIDE))

    def cross_from(self, x):
        for part in self.crossing:
            self.relay(part, self.z - 1, x, (self.UP, self.BESIDE), self.has_down)
            self.relay(part, self.z + 1, x, (self.DOWN, self.BESIDE), self.has_up)

    def cross_near(self):
        self.cross_from(self.x)

    def cross_near_over(self):
        self.cross_from(1 - self.x)

    def line_over(self):
        for part in self.line:
            self.relay(part, self.z, 1 - self.x, (self.BESIDE,))

    def line_near_over(self):
        for part in self.line:
            self.relay(part, self.z - 1, 1 - self.x, (self.BESIDE,), self.has_down)
            self.relay(part, self.z + 1, 1 - self.x, (self.BESIDE,), self.has_up)

    def line_far(self):
        for part in self.line:
            self.relay(part, self.far, self.x, (self.ACROSS, self.BESIDE))

    def cross_far(self):
        for part in self.crossing:
            self.relay(part, self.far, self.x, (self.BESIDE,))

    def line_far_over(self):
        for part in self.line:
            self.relay(part, self.far, 1 - self.x, (self.BESIDE,))

    def cross_far_over(self):
        for part in self.crossing:
            self.relay(part, self.far, 1 - self.x, (self.BESIDE,))

    def plane_done(self, z, present=None):
        def wait():
            for i, ref in enumerate(self.buffers):
                both = ref.at[pl.ds(0, 2)]
                pltpu.make_async_remote_copy(
                    src_ref=both,
                    dst_ref=both,
                    send_sem=self.out_sem.at[i],
                    recv_sem=self.beside_sem.at[i, z],
                    device_id=self.target(self.BESIDE),
                    device_id_type=MESH_ID,
                ).wait_recv()

        if present is None:
            wait()
        else:
            pl.when(present)(wait)

    def left(self, sem, ref, count, first, rows):
        sent = ref.at[pl.ds(0, count), pl.ds(first, rows)]
        pltpu.make_async_remote_copy(
            src_ref=sent,
            dst_ref=sent,
            send_sem=sem,
            recv_sem=self.beside_sem.at[0, 0],
            device_id=self.target(self.BESIDE),
            device_id_type=MESH_ID,
        ).wait_send()

    def finish(self):
        def settle(ways, hops, planes):
            for part, (ref, first, rows) in enumerate(self.parts):
                wide = 1 if part in self.line else 2
                for way in ways:
                    self.left(self.line_sem.at[part, way], ref, wide * hops, first, rows)
                across = planes if part in self.line else 1
                self.left(self.line_sem.at[part, self.ACROSS], ref, across, first, rows)
            for i, ref in enumerate(self.buffers):
                self.left(self.out_sem.at[i], ref, 2 * planes, 0, ref.shape[1])

        pl.when(self.has_up & self.has_down)(lambda: settle((self.UP, self.DOWN), 2, 4))
        pl.when(jnp.logical_not(self.has_down))(lambda: settle((self.UP,), 1, 3))
        pl.when(jnp.logical_not(self.has_up))(lambda: settle((self.DOWN,), 1, 3))


def gather_sems(parts, groups):
    dma = pltpu.SemaphoreType.DMA
    return [dma((parts, 2 * PLANES)), dma((groups, PLANES)), dma((parts, 3)), dma((groups,))]


class VectorSum:
    STAGES = 5

    def __init__(self, ref, partial, arrived, send_sem, recv_sem):
        self.ref, self.partial, self.arrived = ref, partial, arrived
        self.send_sem, self.recv_sem = send_sem, recv_sem
        self.y, self.z, self.x, self.c = where_am_i()

    def copy(self, stage):
        y, z, x, c = self.y, self.z, self.x, self.c
        core, row, across, near, far = (
            (y, z, x, 1 - c),
            (1 - y, z, x, c),
            (y, z, 1 - x, c),
            (y, z + 1 - 2 * (z % 2), x, c),
            (y, (z + 2) % PLANES, x, c),
        )
        y, z, x, c = (core, row, across, near, far)[stage]
        return pltpu.make_async_remote_copy(
            src_ref=self.ref if stage == 0 else self.partial.at[stage - 1],
            dst_ref=self.arrived.at[stage],
            send_sem=self.send_sem.at[stage],
            recv_sem=self.recv_sem.at[stage],
            device_id=(y, z * 4 + x * 2 + c),
            device_id_type=MESH_ID,
        )

    def step(self, stage):
        if stage > 0:
            self.copy(stage - 1).wait_recv()
            before = self.ref[...] if stage == 1 else self.partial[stage - 2]
            self.partial[stage - 1] = before + self.arrived[stage - 1]
        if stage < self.STAGES:
            self.copy(stage).start()

    def finish(self):
        for stage in range(self.STAGES):
            self.copy(stage).wait_send()

    def own_share(self, rows, share):
        width = self.ref.shape[1]
        place = self.y * 16 + self.z * 4 + self.x * 2 + self.c
        per_row = width // share
        offset = place % per_row * share
        row_index = lax.broadcasted_iota(jnp.int32, (width, 128), 0)
        column_index = lax.broadcasted_iota(jnp.int32, (width, 128), 1)
        picked = jnp.where(
            (row_index == column_index + offset) & (column_index < share), 1.0, 0.0
        ).astype(jnp.bfloat16)
        rest = rows
        total = jnp.zeros((rows.shape[0], 128), jnp.float32)
        for _ in range(3):
            piece = rest.astype(jnp.bfloat16)
            total = total + product(piece, picked, CONTRACT_INNER)
            rest = rest - piece.astype(jnp.float32)
        return total, place // per_row


STEP = 384
KEY_STEP = 384
UNROLL = 6


class Quad:
    def __init__(self, by_x):
        self.by_x = by_x
        self.y, self.z, self.x, self.c = where_am_i()
        self.a, self.b = (self.x, self.y) if by_x else (self.y, self.x)
        self.mine = self.a * 2 + self.c
        self.peer = (1 - self.a) * 2 + self.c
        self.beside = self.a * 2 + 1 - self.c
        self.corner = (1 - self.a) * 2 + 1 - self.c

    def device(self, a, b, z, c):
        y, x = (b, a) if self.by_x else (a, b)
        return (y, z * 4 + x * 2 + c)

    def at_peer(self):
        return self.device(1 - self.a, self.b, self.z, self.c)

    def at_beside(self):
        return self.device(self.a, self.b, self.z, 1 - self.c)

    def at_corner(self):
        return self.device(1 - self.a, self.b, self.z, 1 - self.c)

    def link(self, source, target, send_sem, recv_sem, device):
        return pltpu.make_async_remote_copy(
            src_ref=source,
            dst_ref=target,
            send_sem=send_sem,
            recv_sem=recv_sem,
            device_id=device,
            device_id_type=MESH_ID,
        )

    def count(self, ref, send_sem, recv_sem):
        return self.link(ref, ref, send_sem, recv_sem, self.at_beside())


class Shared:
    def __init__(self, left, by_x, buffers):
        self.left = left
        self.held, self.send_sem, self.recv_sem = buffers
        self.quad = Quad(by_x)
        self.width = self.held.shape[2]

    def part(self, a):
        if self.quad.by_x:
            return self.left
        return self.left.at[:, pl.ds(pl.multiple_of(a * self.width, 128), self.width)]

    def share(self):
        q = self.quad
        slot = self.held.at[q.mine]
        send = self.send_sem.at[0]
        q.link(self.part(1 - q.a), slot, send, self.recv_sem.at[0], q.at_peer()).start()
        q.link(self.part(q.a), slot, send, self.recv_sem.at[1], q.at_beside()).start()
        self.held[q.mine] = self.part(q.a)[...]

    def relay(self):
        q = self.quad
        slot = self.held.at[q.peer]
        q.count(slot, self.send_sem.at[0], self.recv_sem.at[0]).wait_recv()
        q.link(slot, slot, self.send_sem.at[0], self.recv_sem.at[1], q.at_beside()).start()

    def complete(self):
        two = self.held.at[pl.ds(0, 2)]
        self.quad.count(two, self.send_sem.at[0], self.recv_sem.at[1]).wait_recv()

    def finish(self):
        three = self.held.at[pl.ds(0, 3)]
        self.quad.count(three, self.send_sem.at[0], self.recv_sem.at[1]).wait_send()


class Piece:
    def __init__(self, shared, right, base, stride, out, buffers):
        self.shared, self.right, self.base, self.stride, self.out = shared, right, base, stride, out
        self.rights, self.whole, self.b_in, self.z_in, self.last, self.send_sem, self.recv_sem = buffers
        self.wide = self.rights.shape[2]
        self.quad = shared.quad
        self.share_rows = out.shape[0]

    def columns(self, member):
        place = member if self.quad.by_x else member % 2
        return pl.ds(pl.multiple_of(self.base + place * self.stride, 128), self.wide)

    def give(self, member, device):
        self.quad.link(
            self.right.at[:, self.columns(member)], self.rights.at[self.quad.mine],
            self.send_sem.at[0], self.recv_sem.at[0], device,
        ).start()

    def share(self):
        q = self.quad
        self.give(q.peer, q.at_peer())
        self.give(q.corner, q.at_corner())
        self.give(q.beside, q.at_beside())
        self.rights[q.mine] = self.right[:, self.columns(q.mine)]

    def slab(self, b):
        return self.whole.at[b] if self.quad.by_x else self.whole.at[:, b]

    def cell(self, z):
        b = self.quad.b
        return self.whole.at[b, z] if self.quad.by_x else self.whole.at[z, b]

    def multiply(self):
        q = self.quad
        three = self.rights.at[pl.ds(0, 3)]
        q.count(three, self.send_sem.at[0], self.recv_sem.at[0]).wait_recv()
        held = self.shared.held
        tokens = held.shape[0] * held.shape[1]
        right = self.rights[...].reshape(tokens, self.wide)
        if self.shared.width > STEP:

            def one(i, carry):
                left = held[:, :, pl.ds(pl.multiple_of(i * STEP, 128), STEP)]
                part = product(left.reshape(tokens, STEP), right, CONTRACT_FIRST)
                self.whole[i] = part.astype(jnp.bfloat16).reshape(self.whole.shape[1:])
                return carry

            lax.fori_loop(0, self.shared.width // STEP, one, 0)
        else:
            part = product(held[...].reshape(tokens, STEP), right, CONTRACT_FIRST)
            self.whole[...] = part.astype(jnp.bfloat16).reshape(self.whole.shape)
        q.link(
            self.slab(1 - q.b), self.b_in, self.send_sem.at[1], self.recv_sem.at[1],
            q.device(q.a, 1 - q.b, q.z, q.c),
        ).start()

    def spread(self):
        q = self.quad
        q.count(self.b_in, self.send_sem.at[1], self.recv_sem.at[1]).wait_recv()
        slab = self.slab(q.b)
        slab[...] = (slab[...].astype(jnp.float32) + self.b_in[...].astype(jnp.float32)).astype(
            jnp.bfloat16
        )
        q.count(self.rights.at[pl.ds(0, 3)], self.send_sem.at[0], self.recv_sem.at[0]).wait_send()
        inner = self.inner()

        @pl.when(inner)
        def _():
            self.to_plane(self.cell(self.end()), 0, 1, self.end())

        @pl.when(jnp.logical_not(inner))
        def _():
            first = 1 - q.z // (PLANES - 1)
            three = pl.ds(first, 3)
            cells = self.whole.at[q.b, three] if q.by_x else self.whole.at[three, q.b]
            self.to_plane(cells, pl.ds(0, 3), 0, 1 + q.z // 2)

    def inner(self):
        return (self.quad.z > 0) & (self.quad.z < PLANES - 1)

    def end(self):
        return self.quad.z // 2 * (PLANES - 1)

    def to_plane(self, source, slot, which, z):
        q = self.quad
        q.link(
            source, self.z_in.at[slot], self.send_sem.at[0], self.recv_sem.at[2 + which],
            q.device(q.a, q.b, z, q.c),
        ).start()

    def fold(self):
        q = self.quad

        @pl.when(self.inner())
        def _():
            three = self.z_in.at[pl.ds(0, 3)]
            q.count(three, self.send_sem.at[0], self.recv_sem.at[2]).wait_recv()
            first = 2 - q.z
            for target in (PLANES - 1 - self.end(), PLANES - 1 - q.z):
                cell = self.cell(target)
                cell[...] = (
                    cell[...].astype(jnp.float32) + self.z_in[target - first].astype(jnp.float32)
                ).astype(jnp.bfloat16)
                self.to_plane(cell, 3, 1, target)

    def rows_of(self, member):
        place = member if self.quad.by_x else member % 2
        return self.last.at[pl.ds(pl.multiple_of(place * self.share_rows, 8), self.share_rows)]

    def collect(self):
        q = self.quad
        inner = self.inner()

        def arrived(count):
            some = self.z_in.at[pl.ds(0, count)]
            q.count(some, self.send_sem.at[0], self.recv_sem.at[3]).wait_recv()

        pl.when(inner)(lambda: arrived(1))
        pl.when(jnp.logical_not(inner))(lambda: arrived(2))
        beside = q.z // 2 * 2 * (1 - q.z // (PLANES - 1))
        self.last[...] = (
            self.cell(q.z)[...].astype(jnp.float32)
            + self.z_in[beside].astype(jnp.float32)
            + self.z_in[3].astype(jnp.float32)
        )
        q.count(self.b_in, self.send_sem.at[1], self.recv_sem.at[1]).wait_send()
        columns = self.out.at[:, self.columns(q.mine)]
        partners = [(q.beside, q.at_beside())]
        if q.by_x:
            partners = [(q.peer, q.at_peer()), (q.corner, q.at_corner())] + partners
        for member, device in partners:
            q.link(
                self.rows_of(member), columns, self.send_sem.at[1], self.recv_sem.at[4], device
            ).start()
        columns[...] = self.rows_of(q.mine)[...]

    def finish(self):
        q = self.quad
        others = self.last.at[pl.ds(0, (3 if q.by_x else 1) * self.share_rows)]
        q.count(others, self.send_sem.at[1], self.recv_sem.at[4]).wait()
        three = self.z_in.at[pl.ds(0, 3)]
        q.count(three, self.send_sem.at[0], self.recv_sem.at[2]).wait_send()


def shared_scratch(frame_count, left_width, by_x):
    return [
        pltpu.VMEM((4, frame_count, left_width if by_x else left_width // 2), jnp.bfloat16),
        pltpu.SemaphoreType.DMA((1,)),
        pltpu.SemaphoreType.DMA((2,)),
    ]


def piece_scratch(frame_count, left_width, by_x, wide=STEP):
    rows = left_width // (2 * PLANES) if by_x else left_width // (4 * PLANES)
    low = jnp.bfloat16
    return [
        pltpu.VMEM((4, frame_count, wide), low),
        pltpu.VMEM((2, PLANES, rows, wide) if by_x else (PLANES, 2, rows, wide), low),
        pltpu.VMEM((PLANES, rows, wide), low),
        pltpu.VMEM((PLANES, rows, wide), low),
        pltpu.VMEM((rows, wide), jnp.float32),
        pltpu.SemaphoreType.DMA((2,)),
        pltpu.SemaphoreType.DMA((5,)),
    ]


def vector_scratch(rows, width):
    wide = jnp.float32
    return [
        pltpu.VMEM((rows, width), wide),
        pltpu.VMEM((VectorSum.STAGES, rows, width), wide),
        pltpu.VMEM((VectorSum.STAGES, rows, width), wide),
        pltpu.SemaphoreType.DMA((VectorSum.STAGES,)),
        pltpu.SemaphoreType.DMA((VectorSum.STAGES,)),
    ]


def layer_scratch(frame_count, width, inner):
    low, wide = jnp.bfloat16, jnp.float32
    dma = pltpu.SemaphoreType.DMA
    return dict(
        qkv_held=pltpu.VMEM((width, 3 * width), low),
        out_held=pltpu.VMEM((width, width), low),
        up_held=pltpu.VMEM((width, inner), low),
        down_held=pltpu.VMEM((inner, width), low),
        weight_sem=dma((4,)),
        block=pltpu.VMEM((BLOCKS, frame_count + 16, width), low),
        block_sems=gather_sems(2, 1),
        grad_block=pltpu.VMEM((BLOCKS, frame_count, width), low),
        stats=pltpu.VMEM((BLOCKS, 32, frame_count), wide),
        grad_sems=gather_sems(3, 2),
        projected=pltpu.VMEM((BLOCKS, frame_count, 3 * width), low),
        mask=pltpu.VMEM((frame_count, BLOCKS * frame_count), wide),
        attended=pltpu.VMEM((frame_count, width), wide),
        slope=pltpu.VMEM((frame_count, inner), wide),
        logs=pltpu.VMEM((frame_count, 128), wide),
        delta=pltpu.VMEM((frame_count, 128), wide),
        inner_bias=pltpu.VMEM((1, inner), wide),
        act=pltpu.VMEM((frame_count, inner), low),
        pre_low=pltpu.VMEM((frame_count, inner), low),
        context=pltpu.VMEM((frame_count, width), low),
        hidden_low=pltpu.VMEM((frame_count, width), low),
        second_low=pltpu.VMEM((frame_count, width), low),
        first_low=pltpu.VMEM((frame_count, width), low),
        normed=pltpu.VMEM((frame_count, width), wide),
        running=pltpu.VMEM((frame_count, width), wide),
        first_grad=pltpu.VMEM((frame_count, width), wide),
        proj_grad=pltpu.VMEM((frame_count, 3 * width), low),
        early=vector_scratch(16, width),
        late=vector_scratch(8, width),
        down_left=shared_scratch(frame_count, inner, False),
        up_left=shared_scratch(frame_count, width, True),
        out_left=shared_scratch(frame_count, width, False),
        qkv_left=shared_scratch(frame_count, width, False),
        down_piece=piece_scratch(frame_count, inner, False),
        up_pieces=[piece_scratch(frame_count, width, True) for _ in range(2)],
        out_piece=piece_scratch(frame_count, width, False),
        query_piece=piece_scratch(frame_count, width, False),
        key_pieces=[
            piece_scratch(frame_count, width, False, KEY_STEP) for _ in range(width // KEY_STEP)
        ],
    )


class Inputs(typing.NamedTuple):
    frames: typing.Any
    segment_ids: typing.Any
    qkv_weight: typing.Any
    query_bias: typing.Any
    value_bias: typing.Any
    out_weight: typing.Any
    out_bias: typing.Any
    norm1_gain: typing.Any
    norm1_shift: typing.Any
    up_weight: typing.Any
    up_bias: typing.Any
    down_weight: typing.Any
    down_bias: typing.Any
    norm2_gain: typing.Any
    norm2_shift: typing.Any
    cotangent: typing.Any


class Outputs(typing.NamedTuple):
    layer_out: typing.Any
    input_grad: typing.Any
    qkv_g: typing.Any
    query_g: typing.Any
    value_g: typing.Any
    out_g: typing.Any
    outbias_g: typing.Any
    gain1_g: typing.Any
    shift1_g: typing.Any
    up_g: typing.Any
    upbias_g: typing.Any
    down_g: typing.Any
    downbias_g: typing.Any
    gain2_g: typing.Any
    shift2_g: typing.Any


class Refs:
    def __init__(self, *groups):
        for group in groups:
            for name, ref in group.items():
                setattr(self, name, ref)


def layer_kernel(held, *refs):
    inputs, outputs = len(Inputs._fields), len(Outputs._fields)
    scratch = jax.tree.unflatten(held, refs[inputs + outputs :])
    k = Refs(dict(zip(Inputs._fields + Outputs._fields, refs)), scratch)
    frame_count, width = k.frames.shape
    inner = k.inner_bias.shape[1]
    low, wide = jnp.bfloat16, jnp.float32
    total = BLOCKS * frame_count
    row, z, x, c = where_am_i()
    mine = z * 4 + x * 2 + c
    has_up, has_down = z < PLANES - 1, z > 0
    far = (z + 2) % PLANES
    lost = PLANES - 1 - z
    lane = lax.broadcasted_iota(jnp.int32, (frame_count, 128), 1)

    def fetch(i):
        source, target = (
            (k.qkv_weight, k.qkv_held),
            (k.out_weight, k.out_held),
            (k.up_weight, k.up_held),
            (k.down_weight, k.down_held),
        )[i]
        return pltpu.make_async_copy(source, target, k.weight_sem.at[i])

    for i in range(4):
        fetch(i).start()

    line_rows = frame_count * 64 // 128
    back_rows = frame_count * 32 // 128
    link = RowGather(
        [
            (k.block, 0, line_rows),
            (k.block, line_rows, k.block.shape[1] - line_rows),
        ],
        (0,),
        (1,),
        k.block_sems,
    )
    back = RowGather(
        [
            (k.grad_block, 0, back_rows),
            (k.grad_block, back_rows, frame_count - back_rows),
            (k.stats, 0, 32),
        ],
        (2, 0),
        (1,),
        k.grad_sems,
    )
    down_left = Shared(k.act, False, k.down_left)
    up_left = Shared(k.hidden_low, True, k.up_left)
    out_left = Shared(k.context, False, k.out_left)
    qkv_left = Shared(k.frames, False, k.qkv_left)
    half_width = width // 2
    down = Piece(down_left, k.second_low, 0, half_width, k.down_g, k.down_piece)
    ups = [
        Piece(up_left, k.pre_low, p * STEP, width, k.up_g, k.up_pieces[p]) for p in range(2)
    ]
    out = Piece(out_left, k.first_low, 0, half_width, k.out_g, k.out_piece)
    query = Piece(qkv_left, k.proj_grad, 0, half_width, k.qkv_g, k.query_piece)
    keys = [
        Piece(qkv_left, k.proj_grad, width + i * KEY_STEP, width, k.qkv_g, buffers)
        for i, buffers in enumerate(k.key_pieces)
    ]
    early, late = VectorSum(*k.early), VectorSum(*k.late)

    places = [(row, z, x, 1 - c), (1 - row, z, x, c), (1 - row, z, x, 1 - c)]
    places += [(row, z, 1 - x, c), (row, z, 1 - x, 1 - c)]
    places += [(row, (z + 2) % PLANES, x, c), (row, z + 1 - 2 * (z % 2), x, c)]
    partners = [(None, (y, at * 4 + across * 2 + core)) for y, at, across, core in places]
    middle = has_up & has_down
    partners.append((middle, (row, (PLANES - 1 - z) * 4 + x * 2 + c)))
    meet(partners, len(places) + middle.astype(jnp.int32))

    own_ids = jnp.broadcast_to(k.segment_ids[...], (frame_count, frame_count)).astype(wide)
    ids_column = own_ids.T
    k.block[mine, pl.ds(0, frame_count), :] = k.frames[...]
    k.block[mine, pl.ds(frame_count, 16), pl.ds(0, frame_count)] = own_ids[:16].astype(low)
    link.own()
    link.cross_over()
    link.line_near()
    k.inner_bias[...] = k.up_bias[...].reshape(1, inner)
    query_bias = k.query_bias[...].reshape(1, width)
    value_bias = k.value_bias[...].reshape(1, width)

    def plane_rows(plane):
        return jnp.concatenate(
            [k.block[plane * 4 + i, pl.ds(0, frame_count), :] for i in range(4)], axis=0
        )

    def store_rows(plane, third, part):
        for i in range(4):
            k.projected[plane * 4 + i, :, pl.ds(third * width, width)] = part[
                i * frame_count : (i + 1) * frame_count
            ]

    def as_query(part):
        return (part + query_bias).astype(low) * HEAD_DIM**-0.5

    def project(plane):
        rows = plane_rows(plane)
        keys = product(rows, k.qkv_held[:, pl.ds(width, width)], CONTRACT_INNER)
        store_rows(plane, 1, keys.astype(low))
        values = product(rows, k.qkv_held[:, pl.ds(2 * width, width)], CONTRACT_INNER)
        store_rows(plane, 2, (values + value_bias).astype(low))
        for i in range(4):
            ids = k.block[plane * 4 + i, pl.ds(frame_count, 8), pl.ds(0, frame_count)]
            same = jnp.broadcast_to(ids.astype(wide)[:1], own_ids.shape) == ids_column
            at = pl.multiple_of((plane * 4 + i) * frame_count, 128)
            k.mask[:, pl.ds(at, frame_count)] = jnp.where(same, 0.0, mask_fill)

    def project_queries(plane):
        queries = product(plane_rows(plane), k.qkv_held[:, pl.ds(0, width)], CONTRACT_INNER)
        store_rows(plane, 0, as_query(queries))

    def queries_own_far():
        project_queries(z)
        project_queries(far)

    def queries_near():
        pl.when(has_down)(lambda: project_queries(z - 1))
        pl.when(has_up)(lambda: project_queries(z + 1))

    def planes_done():
        back.plane_done(z)
        back.plane_done(z - 1, has_down)
        back.plane_done(z + 1, has_up)
        back.plane_done(far)

    def input_gradient():
        k.input_grad[...] = k.first_grad[...] + product(
            k.proj_grad[...], k.qkv_held[...], CONTRACT_LAST
        )

    def late_notes():
        note(late, 0, k.proj_grad[:, pl.ds(0, width)].astype(wide))
        note(late, 1, k.proj_grad[:, pl.ds(2 * width, width)].astype(wide))

    def small_shares():
        share = k.query_g.shape[0]
        first = early.partial[VectorSum.STAGES - 1]
        shares, _ = early.own_share(first[:8], share)
        last, _ = late.own_share(late.partial[VectorSum.STAGES - 1], share)
        for i, ref in enumerate(
            (k.outbias_g, k.gain1_g, k.shift1_g, k.downbias_g, k.gain2_g, k.shift2_g)
        ):
            ref[...] = shares[i, :share]
        k.query_g[...] = last[0, :share]
        k.value_g[...] = last[1, :share]
        up_shares, at = early.own_share(first[8:], 4 * share)
        keep = lax.broadcasted_iota(jnp.int32, up_shares.shape, 0) == at
        picked = jnp.sum(jnp.where(keep, up_shares, 0.0), axis=0, keepdims=True)
        k.upbias_g[...] = picked[0, : 4 * share]

    def note(vector, index, values):
        vector.ref[pl.ds(index, 1), :] = jnp.sum(values, axis=0, keepdims=True)

    def flat(ref):
        return ref[...].reshape(1, width)

    def columns_of(third, j):
        return pl.ds(pl.multiple_of(third * width + j * 128, 128), 128)

    def head_state(h):
        return pl.ds(pl.multiple_of(h * 128, 128), 128)

    def both_heads(values):
        nothing = jnp.zeros_like(values)
        return jnp.concatenate(
            [jnp.where(lane < HALF, values, nothing), jnp.where(lane < HALF, nothing, values)],
            axis=0,
        )

    def own_halves(values):
        return jnp.where(lane < HALF, values[:frame_count], values[frame_count:])

    def attend(plane, first):
        at = pl.multiple_of(plane * 4 * frame_count, 128)

        def state(kind, j):
            return k.slope.at[:, pl.ds(pl.multiple_of((kind * HEADS + 2 * j) * 128, 128), 256)]

        def read(kind, j):
            pair_state = state(kind, j)[...]
            return jnp.concatenate([pair_state[:, :128], pair_state[:, 128:]], axis=0)

        def write(kind, j, values):
            state(kind, j)[...] = jnp.concatenate(
                [values[:frame_count], values[frame_count:]], axis=1
            )

        def pair(j, carry):
            query = both_heads(k.projected[mine, :, columns_of(0, j)])
            keys = k.projected[pl.ds(plane * 4, 4), :, columns_of(1, j)].reshape(-1, 128)
            values = k.projected[pl.ds(plane * 4, 4), :, columns_of(2, j)].reshape(-1, 128)
            mask = k.mask[:, pl.ds(at, 4 * frame_count)]
            scores = product(query, keys, CONTRACT_LAST) + jnp.concatenate([mask, mask], axis=0)
            tile = (2 * frame_count, 128)
            peak = jnp.broadcast_to(jnp.max(scores, axis=1, keepdims=True), tile)
            if not first:
                old = read(0, j)
                peak = jnp.maximum(peak, old)
                factor = jnp.exp(old - peak)
            weights = jnp.exp(scores - jnp.concatenate([peak] * 4, axis=1))
            whole = jnp.broadcast_to(jnp.sum(weights, axis=1, keepdims=True), tile)
            if not first:
                whole = whole + read(1, j) * factor
            write(0, j, peak)
            write(1, j, whole)
            both = own_halves(product(weights.astype(low), values, CONTRACT_INNER))
            if not first:
                both = both + k.attended[:, columns_of(0, j)] * own_halves(factor)
            k.attended[:, columns_of(0, j)] = both
            return carry

        lax.fori_loop(0, PAIRS, pair, 0, unroll=UNROLL)

    def own_queries():
        fetch(0).wait()
        own = product(k.frames[...], k.qkv_held[:, pl.ds(0, width)], CONTRACT_INNER)
        k.projected[mine, :, pl.ds(0, width)] = as_query(own)

    def take_plane(plane, present=None):
        def take():
            link.plane_done(plane)
            project(plane)

        if present is None:
            take()
        else:
            pl.when(present)(take)

    def attend_near(plane, present):
        pl.when(present)(lambda: attend(plane, False))

    own_queries()
    qkv_left.share()
    link.line_over()
    take_plane(z)
    link.line_near_over()
    link.cross_near_over()
    link.line_far()
    link.cross_near()
    attend(z, True)
    take_plane(z - 1, has_down)
    take_plane(z + 1, has_up)
    link.cross_far_over()
    link.line_far_over()
    link.cross_far()
    attend_near(z - 1, has_down)
    attend_near(z + 1, has_up)
    take_plane(far)
    attend(far, False)
    logs = jnp.zeros(lane.shape, wide)
    for j in range(PAIRS):
        parts = []
        for h in range(2):
            whole = k.slope[:, head_state(HEADS + 2 * j + h)]
            logs = jnp.where(
                lane == 2 * j + h, k.slope[:, head_state(2 * j + h)] + jnp.log(whole), logs
            )
            parts.append(whole)
        done = k.attended[:, columns_of(0, j)] / jnp.where(lane < HALF, parts[0], parts[1])
        k.attended[:, columns_of(0, j)] = done
        k.context[:, columns_of(0, j)] = done.astype(low)
    k.logs[...] = logs
    out_left.share()

    def normalize(resid):
        centred = resid - jnp.mean(resid, axis=-1, keepdims=True)
        inverse = lax.rsqrt(jnp.mean(centred * centred, axis=-1, keepdims=True) + norm_eps)
        return centred * inverse, inverse

    def normalize_back(upstream, normed, inverse, gain):
        scaled = upstream * gain
        first_mean = jnp.mean(scaled, axis=-1, keepdims=True)
        second_mean = jnp.mean(scaled * normed, axis=-1, keepdims=True)
        return inverse * (scaled - first_mean - normed * second_mean)

    early.ref[...] = jnp.zeros((16, width), wide)
    late.ref[...] = jnp.zeros((8, width), wide)
    fetch(1).wait()
    resid_one = (
        k.frames[...].astype(wide)
        + product(k.context[...], k.out_held[...], CONTRACT_INNER)
        + flat(k.out_bias)
    )
    normed_one, inverse_one = normalize(resid_one)
    k.normed[...] = normed_one
    hidden = normed_one * flat(k.norm1_gain) + flat(k.norm1_shift)
    k.hidden_low[...] = hidden.astype(low)
    up_left.share()
    qkv_left.relay()
    k.running[...] = hidden + flat(k.down_bias)
    fetch(2).wait()
    fetch(3).wait()

    def forward(f, carry):
        columns = pl.ds(pl.multiple_of(f * width, 128), width)
        pre_act = (
            product(k.hidden_low[...], k.up_held[:, columns], CONTRACT_INNER)
            + k.inner_bias[:, columns]
        )
        normal_cdf = 0.5 * (1.0 + lax.erf(pre_act * 0.5**0.5))
        normal_pdf = jnp.exp(-0.5 * pre_act * pre_act) * (2.0 * math.pi) ** (-0.5)
        act = (pre_act * normal_cdf).astype(low)
        k.act[:, columns] = act
        k.slope[:, columns] = normal_cdf + pre_act * normal_pdf
        k.running[...] += product(
            act, k.down_held[pl.ds(pl.multiple_of(f * width, 128), width), :], CONTRACT_INNER
        )
        return carry

    lax.fori_loop(0, inner // width, forward, 0)
    down_left.share()
    normed_two, inverse_two = normalize(k.running[...])
    k.layer_out[...] = (normed_two * flat(k.norm2_gain) + flat(k.norm2_shift)).astype(low)
    upstream = k.cotangent[...].astype(wide)
    second_grad = normalize_back(upstream, normed_two, inverse_two, flat(k.norm2_gain))
    k.second_low[...] = second_grad.astype(low)
    note(early, 3, second_grad)
    note(early, 4, upstream * normed_two)
    note(early, 5, upstream)
    k.running[...] = second_grad

    def backward(p):
        for member in range(4):
            first = member * width + p * STEP
            columns = pl.ds(first, STEP)
            pre_grad = (
                product(k.second_low[...], k.down_held[columns, :], CONTRACT_LAST)
                * k.slope[:, columns]
            )
            early.ref[pl.ds(8 + member, 1), pl.ds(p * STEP, STEP)] = jnp.sum(
                pre_grad, axis=0, keepdims=True
            )
            k.pre_low[:, columns] = pre_grad.astype(low)
            k.running[...] += product(
                k.pre_low[:, columns], k.up_held[:, columns], CONTRACT_LAST
            )

    backward(0)
    ups[0].share()
    up_left.relay()
    backward(1)
    queries_own_far()
    hidden_grad = k.running[...]
    normed_one = k.normed[...]
    first_grad = normalize_back(hidden_grad, normed_one, inverse_one, flat(k.norm1_gain))
    k.first_grad[...] = first_grad
    k.first_low[...] = first_grad.astype(low)
    note(early, 0, first_grad)
    note(early, 1, hidden_grad * normed_one)
    note(early, 2, hidden_grad)
    out_left.relay()
    context_grad = product(k.first_low[...], k.out_held[...], CONTRACT_LAST).astype(low)
    k.grad_block[mine] = context_grad
    delta = jnp.zeros(lane.shape, wide)
    for j in range(PAIRS):
        columns = slice(j * 128, (j + 1) * 128)
        both = context_grad[:, columns].astype(wide) * k.attended[:, columns]
        for h in range(2):
            one = jnp.sum(
                jnp.where((lane < HALF) == (h == 0), both, 0.0), axis=1, keepdims=True
            )
            delta = jnp.where(lane == 2 * j + h, one, delta)
    k.delta[...] = delta
    k.stats[mine, pl.ds(0, 16), :] = k.logs[...].T[:16]
    k.stats[mine, pl.ds(16, 16), :] = delta.T[:16]
    down.share()
    early.step(0)
    back.own()

    @pl.when(jnp.logical_not(middle))
    def _():
        for i in range(4):
            k.projected[lost * 4 + i] = jnp.zeros((frame_count, 3 * width), low)
            k.grad_block[lost * 4 + i] = jnp.zeros((frame_count, width), low)
            k.stats[lost * 4 + i] = jnp.zeros((32, frame_count), wide)
            at = pl.multiple_of((lost * 4 + i) * frame_count, 128)
            k.mask[:, pl.ds(at, frame_count)] = jnp.full(lane.shape, mask_fill, wide)

    def query_pair(j):
        query = k.projected[mine, :, columns_of(0, j)]
        upstream = k.grad_block[mine, :, columns_of(0, j)]
        keys = k.projected[:, :, columns_of(1, j)].reshape(total, 128)
        values = k.projected[:, :, columns_of(2, j)].reshape(total, 128)
        outs = []
        for h in range(2):
            chosen = (lane < HALF) == (h == 0)
            nothing = jnp.zeros_like(query)
            logs = jnp.sum(
                jnp.where(lane == 2 * j + h, k.logs[...], 0.0), axis=1, keepdims=True
            )
            shift = jnp.sum(
                jnp.where(lane == 2 * j + h, k.delta[...], 0.0), axis=1, keepdims=True
            )
            scores = product(jnp.where(chosen, query, nothing), keys, CONTRACT_LAST)
            probs = jnp.exp(scores + k.mask[...] - logs)
            prob_grad = product(jnp.where(chosen, upstream, nothing), values, CONTRACT_LAST)
            score_grad = (probs * (prob_grad - shift)).astype(low)
            outs.append(product(score_grad, keys, CONTRACT_INNER))
        k.proj_grad[:, columns_of(0, j)] = (
            jnp.where(lane < HALF, outs[0], outs[1]) * HEAD_DIM**-0.5
        ).astype(low)

    def key_pair(j):
        key = k.projected[mine, :, columns_of(1, j)]
        value = k.projected[mine, :, columns_of(2, j)]
        queries = k.projected[:, :, columns_of(0, j)].reshape(total, 128)
        upstream = k.grad_block[:, :, columns_of(0, j)].reshape(total, 128)
        key_outs, value_outs = [], []
        for h in range(2):
            chosen = (lane < HALF) == (h == 0)
            nothing = jnp.zeros_like(key)
            logs = jnp.concatenate(
                [k.stats[b, pl.ds(2 * j + h, 1), :] for b in range(BLOCKS)], axis=1
            )
            shift = jnp.concatenate(
                [k.stats[b, pl.ds(16 + 2 * j + h, 1), :] for b in range(BLOCKS)], axis=1
            )
            scores = product(jnp.where(chosen, key, nothing), queries, CONTRACT_LAST)
            probs = jnp.exp(scores + k.mask[...] - logs)
            prob_grad = product(jnp.where(chosen, value, nothing), upstream, CONTRACT_LAST)
            score_grad = (probs * (prob_grad - shift)).astype(low)
            key_outs.append(product(score_grad, queries, CONTRACT_INNER))
            value_outs.append(product(probs.astype(low), upstream, CONTRACT_INNER))
        k.proj_grad[:, columns_of(1, j)] = jnp.where(
            lane < HALF, key_outs[0], key_outs[1]
        ).astype(low)
        k.proj_grad[:, columns_of(2, j)] = jnp.where(
            lane < HALF, value_outs[0], value_outs[1]
        ).astype(low)

    def pairs(one, first, last):
        def body(j, carry):
            one(j)
            return carry

        lax.fori_loop(first, last, body, 0)

    pairs(query_pair, 0, 1)
    early.step(1)
    back.cross_over()
    ups[1].share()
    pairs(query_pair, 1, 2)
    up_left.complete()
    pairs(query_pair, 2, 3)
    back.line_near()
    back.line_over()
    down_left.relay()
    ups[0].multiply()
    pairs(query_pair, 3, 4)
    queries_near()
    back.cross_near_over()
    back.cross_near()
    out_left.complete()
    down_left.complete()
    early.step(2)
    back.line_far()
    ups[1].multiply()
    ups[0].spread()
    down.multiply()
    back.line_near_over()
    early.step(3)
    pairs(query_pair, 4, 5)
    back.cross_far_over()
    pairs(query_pair, 5, 6)
    back.line_far_over()
    ups[0].fold()
    back.cross_far()
    out.share()
    ups[1].spread()
    planes_done()
    qkv_left.complete()
    query.share()
    pairs(key_pair, 0, 1)
    ups[1].fold()
    pairs(key_pair, 1, 2)
    down.spread()
    pairs(key_pair, 2, 3)
    out.multiply()
    keys[0].share()
    pairs(key_pair, 3, 4)
    query.multiply()
    pairs(key_pair, 4, 5)
    down.fold()
    out.spread()
    pairs(key_pair, 5, 6)
    keys[1].share()
    keys[0].multiply()
    late_notes()
    late.step(0)
    late.step(1)
    query.spread()
    query.fold()
    keys[1].multiply()
    out.fold()
    keys[0].spread()
    input_gradient()
    keys[0].fold()
    early.step(4)
    late.step(2)
    ups[0].collect()
    down.collect()
    keys[1].spread()
    keys[1].fold()
    query.collect()
    out.collect()
    keys[0].collect()
    ups[1].collect()
    late.step(3)
    keys[1].collect()
    late.step(4)
    early.step(5)
    late.step(5)
    small_shares()
    for each in [down_left, up_left, out_left, qkv_left, down, out, query] + ups + keys:
        each.finish()
    for each in (back, link, early, late):
        each.finish()


def copy_kernel(*refs):
    count = len(refs) // 2
    for source, target in zip(refs[:count], refs[count:]):
        target[...] = source[...]


def hand_over(results):
    return pl.pallas_call(
        copy_kernel,
        out_shape=tuple(jax.ShapeDtypeStruct(each.shape, each.dtype) for each in results),
        in_specs=[IN_VMEM] * len(results),
        out_specs=(IN_VMEM,) * len(results),
    )(*results)


def layer_step(*args):
    frames = args[0]
    frame_count, width = frames.shape[1:]
    inner = args[9].shape[1]
    low, wide = jnp.bfloat16, jnp.float32
    scratch, held = jax.tree.flatten(layer_scratch(frame_count, width, inner))
    operands = [frames[0]] + list(args[1:-1]) + [args[-1][0]]
    share = width // 32
    shapes = [
        ((frame_count, width), low),
        ((frame_count, width), wide),
        ((share, 3 * width), wide),
        ((share,), wide),
        ((share,), wide),
        ((share, width), wide),
        ((share,), wide),
        ((share,), wide),
        ((share,), wide),
        ((share, inner), wide),
        ((4 * share,), wide),
        ((4 * share, width), wide),
        ((share,), wide),
        ((share,), wide),
        ((share,), wide),
    ]
    results = pl.pallas_call(
        functools.partial(layer_kernel, held),
        out_shape=tuple(jax.ShapeDtypeStruct(shape, kind) for shape, kind in shapes),
        in_specs=[IN_PLACE if each.ndim == 2 and each.shape[0] >= width else IN_VMEM for each in operands],
        out_specs=(IN_VMEM,) * len(shapes),
        scratch_shapes=scratch,
        compiler_params=pltpu.CompilerParams(
            collective_id=0, has_side_effects=True, vmem_limit_bytes=VMEM_BYTES
        ),
    )(*operands)
    results = hand_over(results)
    return (results[0][None], results[1][None]) + tuple(results[2:])


def solution(mesh):
    chosen = layer_step if dict(mesh.shape) == {"rows": 2, "seq": 16} else shards
    in_specs = (
        P("rows", "seq", None),
        P("rows", "seq"),
        P(),
        P(),
        P(),
        P(),
        P(),
        P(),
        P(),
        P(),
        P(),
        P(),
        P(),
        P(),
        P(),
        P("rows", "seq", None),
    )
    out_specs = (
        P("rows", "seq", None),
        P("rows", "seq", None),
        P(("rows", "seq"), None),
        P(("rows", "seq")),
        P(("rows", "seq")),
        P(("rows", "seq"), None),
        P(("rows", "seq")),
        P(("rows", "seq")),
        P(("rows", "seq")),
        P(("rows", "seq"), None),
        P(("rows", "seq")),
        P(("rows", "seq"), None),
        P(("rows", "seq")),
        P(("rows", "seq")),
        P(("rows", "seq")),
    )
    return jax.shard_map(chosen, mesh=mesh, in_specs=in_specs, out_specs=out_specs, check_vma=False)
```

```python
import functools
import math
import typing

import jax
import jax.numpy as jnp
from jax import lax
from jax.experimental import pallas as pl
from jax.experimental.pallas import tpu as pltpu
from jax.sharding import PartitionSpec as P

HEADS = 12
HEAD_DIM = 64


norm_eps = 1e-05
mask_fill = -1e30


def shortened(shard):

    def short(part):
        return part.astype(jnp.bfloat16) if part.dtype == jnp.float32 else part

    return jax.tree.map(short, shard)


def passed_along(value, axis, steps):
    count = lax.axis_size(axis)
    pairs = [(source, (source + steps) % count) for source in range(count)]
    return lax.ppermute(value, axis, pairs)


def layer_norm(resid, gain, shift):
    centred = resid - jnp.mean(resid, axis=-1, keepdims=True)
    inv_std = lax.rsqrt(jnp.mean(centred * centred, axis=-1, keepdims=True) + norm_eps)
    normed = centred * inv_std
    return (normed * gain + shift, normed, inv_std)


def norm_back(upstream, normed, inv_std, gain):
    scaled = upstream * gain
    first_mean = jnp.mean(scaled, axis=-1, keepdims=True)
    second_mean = jnp.mean(scaled * normed, axis=-1, keepdims=True)
    grad_in = inv_std * (scaled - first_mean - normed * second_mean)
    return (grad_in, jnp.sum(upstream * normed, axis=0), jnp.sum(upstream, axis=0))


def gelu_slope(pre_act):
    normal_cdf = 0.5 * (1.0 + lax.erf(pre_act * 0.5**0.5))
    normal_pdf = jnp.exp(-0.5 * pre_act * pre_act) * (2.0 * math.pi) ** (-0.5)
    return normal_cdf + pre_act * normal_pdf


def head_groups(head_count):
    return [(0, head_count, 1)]


def pass_keys(blocks):
    return jax.tree.map(
        lambda part, own: part.astype(own.dtype), passed_along(shortened(blocks), "seq", 1), blocks
    )


def pass_again(blocks):
    return jax.tree.map(
        lambda part, own: part.astype(own.dtype), passed_along(shortened(blocks), "seq", 1), blocks
    )


def pass_grads(blocks):
    return (
        passed_along(blocks[0].astype(jnp.bfloat16), "seq", 1).astype(jnp.float32),
        passed_along(blocks[1].astype(jnp.bfloat16), "seq", 1).astype(jnp.float32),
    )


def block_scores(query_part, key_part, query_ids, key_ids):
    scores = jnp.einsum(
        "qhe,khe->hqk", query_part, key_part, preferred_element_type=jnp.float32
    ) * HEAD_DIM ** (-0.5)
    return jnp.where((query_ids[:, None] == key_ids[None, :])[None], scores, mask_fill)


def attend_block(carried, query_part, key_part, value_part, query_ids, key_ids):
    run_max, run_total, run_acc = carried
    scores = block_scores(query_part, key_part, query_ids, key_ids)
    new_max = jnp.maximum(run_max, jnp.max(scores, axis=-1))
    weights = jnp.exp(scores - new_max[:, :, None])
    factor = jnp.exp(run_max - new_max)
    new_total = run_total * factor + jnp.sum(weights, axis=-1)
    update = jnp.einsum(
        "hqk,khe->qhe", weights.astype(jnp.bfloat16), value_part, preferred_element_type=jnp.float32
    )
    return (new_max, new_total, run_acc * factor.T[:, :, None] + update)


def grad_block(
    carried,
    query_part,
    key_part,
    value_part,
    query_ids,
    key_ids,
    context_part,
    log_part,
    delta_part,
):
    query_acc, key_acc, value_acc = carried
    scores = block_scores(query_part, key_part, query_ids, key_ids)
    probs = jnp.exp(scores - log_part[:, :, None])
    prob_grad = jnp.einsum(
        "qhe,khe->hqk", context_part, value_part, preferred_element_type=jnp.float32
    )
    score_grad = (probs * (prob_grad - delta_part[:, :, None])).astype(jnp.bfloat16)
    scale = HEAD_DIM ** (-0.5)
    query_acc = query_acc + scale * jnp.einsum(
        "hqk,khe->qhe", score_grad, key_part, preferred_element_type=jnp.float32
    )
    key_acc = key_acc + scale * jnp.einsum(
        "hqk,qhe->khe", score_grad, query_part, preferred_element_type=jnp.float32
    )
    value_acc = value_acc + jnp.einsum(
        "hqk,qhe->khe", probs.astype(jnp.bfloat16), context_part, preferred_element_type=jnp.float32
    )
    return (query_acc, key_acc, value_acc)


def forward_cycle(
    query_heads, key_heads, value_heads, local_ids, every_id, cycle_place, cycle_size
):
    frame_count, head_count, head_width = query_heads.shape
    grouping = head_groups(head_count)
    states = []
    blocks = []
    for head_first, head_last, direction in grouping:
        head_span = head_last - head_first
        initial = (
            jnp.full((head_span, frame_count), mask_fill, jnp.float32),
            jnp.zeros((head_span, frame_count), jnp.float32),
            jnp.zeros((frame_count, head_span, head_width), jnp.float32),
        )
        states.append(
            attend_block(initial, query_heads, key_heads, value_heads, local_ids, local_ids)
        )
        blocks.append((key_heads, value_heads))

    def forward_cycle_turn(turn_index, cycle_carry):
        old_states, old_blocks = cycle_carry
        new_states = []
        new_blocks = []
        for group_info, part_state, part_block in zip(grouping, old_states, old_blocks):
            head_first, head_last, direction = group_info
            part_block = pass_keys(part_block)
            source_index = (cycle_place - direction * turn_index) % cycle_size
            key_ids = lax.dynamic_slice_in_dim(every_id, source_index * frame_count, frame_count)
            new_states.append(
                attend_block(
                    part_state, query_heads, part_block[0], part_block[1], local_ids, key_ids
                )
            )
            new_blocks.append(part_block)
        return (new_states, new_blocks)

    states, blocks = lax.fori_loop(1, cycle_size, forward_cycle_turn, (states, blocks))
    maxima = jnp.concatenate([part_state[0] for part_state in states], axis=0)
    totals = jnp.concatenate([part_state[1] for part_state in states], axis=0)
    sums_all = jnp.concatenate([part_state[2] for part_state in states], axis=1)
    attended = sums_all / totals.T[:, :, None]
    return (attended, maxima + jnp.log(totals))


def backward_cycle(
    query_heads,
    key_heads,
    value_heads,
    local_ids,
    every_id,
    context_heads,
    log_total,
    row_delta,
    cycle_place,
    cycle_size,
):
    frame_count, head_count, head_width = query_heads.shape
    grouping = head_groups(head_count)
    initial = []
    for head_first, head_last, direction in grouping:
        zero_part = jnp.zeros((frame_count, head_last - head_first, head_width), jnp.float32)
        initial.append((zero_part, (key_heads, value_heads), (zero_part, zero_part)))

    def backward_cycle_turn(turn_index, cycle_carry):
        new_carry = []
        for group_info, part_carry in zip(grouping, cycle_carry):
            head_first, head_last, direction = group_info
            query_acc, part_block, part_grads = part_carry
            source_index = (cycle_place - direction * turn_index) % cycle_size
            key_ids = lax.dynamic_slice_in_dim(every_id, source_index * frame_count, frame_count)
            query_acc, key_acc, value_acc = grad_block(
                (query_acc, part_grads[0], part_grads[1]),
                query_heads,
                part_block[0],
                part_block[1],
                local_ids,
                key_ids,
                context_heads,
                log_total,
                row_delta,
            )
            part_grads = pass_grads((key_acc, value_acc))
            part_block = pass_again(part_block)
            new_carry.append((query_acc, part_block, part_grads))
        return new_carry

    final = lax.fori_loop(0, cycle_size, backward_cycle_turn, initial)
    query_grad = jnp.concatenate([part_carry[0] for part_carry in final], axis=1)
    key_grad = jnp.concatenate([part_carry[2][0] for part_carry in final], axis=1)
    value_grad = jnp.concatenate([part_carry[2][1] for part_carry in final], axis=1)
    return (query_grad, key_grad, value_grad)


def shards(
    frames,
    segment_ids,
    qkv_weight,
    query_bias,
    value_bias,
    out_weight,
    out_bias,
    norm1_gain,
    norm1_shift,
    up_weight,
    up_bias,
    down_weight,
    down_bias,
    norm2_gain,
    norm2_shift,
    cotangent,
):
    inputs = frames[0]
    local_ids = segment_ids[0]
    frame_count, model_width = inputs.shape
    cycle_size = lax.axis_size("seq")
    cycle_place = lax.axis_index("seq")
    every_id = lax.all_gather(segment_ids, "seq", axis=1, tiled=True)[0]
    head_shape = (frame_count, HEADS, HEAD_DIM)
    projected = jnp.dot(inputs, qkv_weight, preferred_element_type=jnp.float32)
    query_heads = (projected[:, :model_width] + query_bias).astype(jnp.bfloat16).reshape(head_shape)
    key_heads = projected[:, model_width : 2 * model_width].astype(jnp.bfloat16).reshape(head_shape)
    value_heads = (
        (projected[:, 2 * model_width :] + value_bias).astype(jnp.bfloat16).reshape(head_shape)
    )
    attended, log_total = forward_cycle(
        query_heads, key_heads, value_heads, local_ids, every_id, cycle_place, cycle_size
    )
    context = attended.astype(jnp.bfloat16).reshape(frame_count, model_width)
    resid_one = (
        inputs.astype(jnp.float32)
        + jnp.dot(context, out_weight, preferred_element_type=jnp.float32)
        + out_bias
    )
    hidden, normed_one, inverse_one = layer_norm(resid_one, norm1_gain, norm1_shift)
    hidden_low = hidden.astype(jnp.bfloat16)
    pre_act = jnp.dot(hidden_low, up_weight, preferred_element_type=jnp.float32) + up_bias
    act_low = jax.nn.gelu(pre_act, approximate=False).astype(jnp.bfloat16)
    resid_two = (
        hidden + jnp.dot(act_low, down_weight, preferred_element_type=jnp.float32) + down_bias
    )
    output, normed_two, inverse_two = layer_norm(resid_two, norm2_gain, norm2_shift)
    upstream = cotangent[0].astype(jnp.float32)
    second_grad, gain_two_grad, shift_two_grad = norm_back(
        upstream, normed_two, inverse_two, norm2_gain
    )
    second_low = second_grad.astype(jnp.bfloat16)
    down_grad = jnp.einsum("tf,td->fd", act_low, second_low, preferred_element_type=jnp.float32)
    pre_grad = jnp.einsum(
        "td,fd->tf", second_low, down_weight, preferred_element_type=jnp.float32
    ) * gelu_slope(pre_act)
    pre_low = pre_grad.astype(jnp.bfloat16)
    up_grad = jnp.einsum("td,tf->df", hidden_low, pre_low, preferred_element_type=jnp.float32)
    hidden_grad = second_grad + jnp.einsum(
        "tf,df->td", pre_low, up_weight, preferred_element_type=jnp.float32
    )
    first_grad, gain_one_grad, shift_one_grad = norm_back(
        hidden_grad, normed_one, inverse_one, norm1_gain
    )
    first_low = first_grad.astype(jnp.bfloat16)
    out_grad = jnp.einsum("td,te->de", context, first_low, preferred_element_type=jnp.float32)
    context_grad = (
        jnp.einsum("te,de->td", first_low, out_weight, preferred_element_type=jnp.float32)
        .astype(jnp.bfloat16)
        .reshape(head_shape)
    )
    row_delta = jnp.einsum("qhe,qhe->hq", context_grad.astype(jnp.float32), attended)
    query_grad, key_grad, value_grad = backward_cycle(
        query_heads,
        key_heads,
        value_heads,
        local_ids,
        every_id,
        context_grad,
        log_total,
        row_delta,
        cycle_place,
        cycle_size,
    )
    query_low = query_grad.astype(jnp.bfloat16).reshape(frame_count, model_width)
    key_low = key_grad.astype(jnp.bfloat16).reshape(frame_count, model_width)
    value_low = value_grad.astype(jnp.bfloat16).reshape(frame_count, model_width)
    proj_grad = jnp.concatenate([query_low, key_low, value_low], axis=1)
    qkv_grad = jnp.einsum("td,te->de", inputs, proj_grad, preferred_element_type=jnp.float32)
    input_grad = (
        jnp.einsum("te,de->td", proj_grad, qkv_weight, preferred_element_type=jnp.float32)
        + first_grad
    )
    summed = (
        lax.psum_scatter(qkv_grad, ("rows", "seq"), scatter_dimension=0, tiled=True),
        lax.psum_scatter(
            jnp.sum(query_low.astype(jnp.float32), axis=0),
            ("rows", "seq"),
            scatter_dimension=0,
            tiled=True,
        ),
        lax.psum_scatter(
            jnp.sum(value_low.astype(jnp.float32), axis=0),
            ("rows", "seq"),
            scatter_dimension=0,
            tiled=True,
        ),
        lax.psum_scatter(out_grad, ("rows", "seq"), scatter_dimension=0, tiled=True),
        lax.psum_scatter(
            jnp.sum(first_grad, axis=0), ("rows", "seq"), scatter_dimension=0, tiled=True
        ),
        lax.psum_scatter(gain_one_grad, ("rows", "seq"), scatter_dimension=0, tiled=True),
        lax.psum_scatter(shift_one_grad, ("rows", "seq"), scatter_dimension=0, tiled=True),
        lax.psum_scatter(up_grad, ("rows", "seq"), scatter_dimension=0, tiled=True),
        lax.psum_scatter(
            jnp.sum(pre_grad, axis=0), ("rows", "seq"), scatter_dimension=0, tiled=True
        ),
        lax.psum_scatter(down_grad, ("rows", "seq"), scatter_dimension=0, tiled=True),
        lax.psum_scatter(
            jnp.sum(second_grad, axis=0), ("rows", "seq"), scatter_dimension=0, tiled=True
        ),
        lax.psum_scatter(gain_two_grad, ("rows", "seq"), scatter_dimension=0, tiled=True),
        lax.psum_scatter(shift_two_grad, ("rows", "seq"), scatter_dimension=0, tiled=True),
    )
    return (
        output.astype(jnp.bfloat16)[None],
        input_grad[None],
        summed[0],
        summed[1],
        summed[2],
        summed[3],
        summed[4],
        summed[5],
        summed[6],
        summed[7],
        summed[8],
        summed[9],
        summed[10],
        summed[11],
        summed[12],
    )


HALF = HEAD_DIM
PAIRS = HEADS // 2
CONTRACT_LAST = (((1,), (1,)), ((), ()))
CONTRACT_INNER = (((1,), (0,)), ((), ()))
CONTRACT_FIRST = (((0,), (0,)), ((), ()))
IN_VMEM = pl.BlockSpec(memory_space=pltpu.VMEM)
IN_PLACE = pl.BlockSpec(memory_space=pl.ANY)
MESH_ID = pl.DeviceIdType.MESH
VMEM_BYTES = 60 << 20
BLOCKS = 16
PLANES = 4


def product(left, right, dims):
    return lax.dot_general(left, right, dims, preferred_element_type=jnp.float32)


def where_am_i():
    row = lax.axis_index("rows")
    place = lax.axis_index("seq")
    return row, place // 4, place // 2 % 2, place % 2


def meet(partners, count):
    barrier = pltpu.get_barrier_semaphore()
    for present, target in partners:

        def signal(target=target):
            pl.semaphore_signal(barrier, inc=1, device_id=target, device_id_type=MESH_ID)

        if present is None:
            signal()
        else:
            pl.when(present)(signal)
    pl.semaphore_wait(barrier, count)


class RowGather:
    UP, DOWN, ACROSS, BESIDE = range(4)

    def __init__(self, parts, line, crossing, sems):
        self.parts, self.line, self.crossing = parts, line, crossing
        self.recv_sem, self.beside_sem, self.line_sem, self.out_sem = sems
        self.row, self.z, self.x, self.c = where_am_i()
        self.has_up, self.has_down = self.z < PLANES - 1, self.z > 0
        self.far = (self.z + 2) % PLANES
        self.buffers = []
        for ref, _, _ in parts:
            if not any(ref is known for known in self.buffers):
                self.buffers.append(ref)

    def group(self, part):
        return [self.parts[part][0] is ref for ref in self.buffers].index(True)

    def device(self, z, x, c):
        return (self.row, z * 4 + x * 2 + c)

    def target(self, way):
        return (
            self.device(self.z + 1, self.x, self.c),
            self.device(self.z - 1, self.x, self.c),
            self.device(self.z, 1 - self.x, self.c),
            self.device(self.z, self.x, 1 - self.c),
        )[way]

    def copy(self, part, z, x, way):
        ref, first, rows = self.parts[part]
        piece = ref.at[z * 4 + x * 2 + self.c, pl.ds(first, rows)]
        beside = way == self.BESIDE
        return pltpu.make_async_remote_copy(
            src_ref=piece,
            dst_ref=piece,
            send_sem=self.out_sem.at[self.group(part)] if beside else self.line_sem.at[part, way],
            recv_sem=(
                self.beside_sem.at[self.group(part), z]
                if beside
                else self.recv_sem.at[part, z * 2 + x]
            ),
            device_id=self.target(way),
            device_id_type=MESH_ID,
        )

    def send(self, part, z, x, way):
        present = {self.UP: self.has_up, self.DOWN: self.has_down}.get(way)
        if present is None:
            self.copy(part, z, x, way).start()
        else:
            pl.when(present)(lambda: self.copy(part, z, x, way).start())

    def relay(self, part, z, x, ways, present=None):
        def both():
            self.copy(part, z, x, self.ACROSS).wait_recv()
            for way in ways:
                self.send(part, z, x, way)

        if present is None:
            both()
        else:
            pl.when(present)(both)

    def own(self):
        z, x = self.z, self.x
        for part in self.crossing:
            self.send(part, z, x, self.ACROSS)
        for part in self.line + self.crossing:
            self.send(part, z, x, self.UP)
            self.send(part, z, x, self.DOWN)
        for part in self.line:
            self.send(part, z, x, self.ACROSS)
        for part in self.crossing + self.line:
            self.send(part, z, x, self.BESIDE)

    def line_near(self):
        for part in self.line:
            self.relay(part, self.z - 1, self.x, (self.UP, self.ACROSS, self.BESIDE), self.has_down)
            self.relay(part, self.z + 1, self.x, (self.DOWN, self.ACROSS, self.BESIDE), self.has_up)

    def cross_over(self):
        for part in self.crossing:
            self.relay(part, self.z, 1 - self.x, (self.UP, self.DOWN, self.BESIDE))

    def cross_from(self, x):
        for part in self.crossing:
            self.relay(part, self.z - 1, x, (self.UP, self.BESIDE), self.has_down)
            self.relay(part, self.z + 1, x, (self.DOWN, self.BESIDE), self.has_up)

    def cross_near(self):
        self.cross_from(self.x)

    def cross_near_over(self):
        self.cross_from(1 - self.x)

    def line_over(self):
        for part in self.line:
            self.relay(part, self.z, 1 - self.x, (self.BESIDE,))

    def line_near_over(self):
        for part in self.line:
            self.relay(part, self.z - 1, 1 - self.x, (self.BESIDE,), self.has_down)
            self.relay(part, self.z + 1, 1 - self.x, (self.BESIDE,), self.has_up)

    def line_far(self):
        for part in self.line:
            self.relay(part, self.far, self.x, (self.ACROSS, self.BESIDE))

    def cross_far(self):
        for part in self.crossing:
            self.relay(part, self.far, self.x, (self.BESIDE,))

    def line_far_over(self):
        for part in self.line:
            self.relay(part, self.far, 1 - self.x, (self.BESIDE,))

    def cross_far_over(self):
        for part in self.crossing:
            self.relay(part, self.far, 1 - self.x, (self.BESIDE,))

    def plane_done(self, z, present=None):
        def wait():
            for i, ref in enumerate(self.buffers):
                both = ref.at[pl.ds(0, 2)]
                pltpu.make_async_remote_copy(
                    src_ref=both,
                    dst_ref=both,
                    send_sem=self.out_sem.at[i],
                    recv_sem=self.beside_sem.at[i, z],
                    device_id=self.target(self.BESIDE),
                    device_id_type=MESH_ID,
                ).wait_recv()

        if present is None:
            wait()
        else:
            pl.when(present)(wait)

    def left(self, sem, ref, count, first, rows):
        sent = ref.at[pl.ds(0, count), pl.ds(first, rows)]
        pltpu.make_async_remote_copy(
            src_ref=sent,
            dst_ref=sent,
            send_sem=sem,
            recv_sem=self.beside_sem.at[0, 0],
            device_id=self.target(self.BESIDE),
            device_id_type=MESH_ID,
        ).wait_send()

    def finish(self):
        def settle(ways, hops, planes):
            for part, (ref, first, rows) in enumerate(self.parts):
                wide = 1 if part in self.line else 2
                for way in ways:
                    self.left(self.line_sem.at[part, way], ref, wide * hops, first, rows)
                across = planes if part in self.line else 1
                self.left(self.line_sem.at[part, self.ACROSS], ref, across, first, rows)
            for i, ref in enumerate(self.buffers):
                self.left(self.out_sem.at[i], ref, 2 * planes, 0, ref.shape[1])

        pl.when(self.has_up & self.has_down)(lambda: settle((self.UP, self.DOWN), 2, 4))
        pl.when(jnp.logical_not(self.has_down))(lambda: settle((self.UP,), 1, 3))
        pl.when(jnp.logical_not(self.has_up))(lambda: settle((self.DOWN,), 1, 3))


def gather_sems(parts, groups):
    dma = pltpu.SemaphoreType.DMA
    return [dma((parts, 2 * PLANES)), dma((groups, PLANES)), dma((parts, 3)), dma((groups,))]


class VectorSum:
    STAGES = 5

    def __init__(self, ref, partial, arrived, send_sem, recv_sem):
        self.ref, self.partial, self.arrived = ref, partial, arrived
        self.send_sem, self.recv_sem = send_sem, recv_sem
        self.y, self.z, self.x, self.c = where_am_i()

    def copy(self, stage):
        y, z, x, c = self.y, self.z, self.x, self.c
        core, row, across, near, far = (
            (y, z, x, 1 - c),
            (1 - y, z, x, c),
            (y, z, 1 - x, c),
            (y, z + 1 - 2 * (z % 2), x, c),
            (y, (z + 2) % PLANES, x, c),
        )
        y, z, x, c = (core, row, across, near, far)[stage]
        return pltpu.make_async_remote_copy(
            src_ref=self.ref if stage == 0 else self.partial.at[stage - 1],
            dst_ref=self.arrived.at[stage],
            send_sem=self.send_sem.at[stage],
            recv_sem=self.recv_sem.at[stage],
            device_id=(y, z * 4 + x * 2 + c),
            device_id_type=MESH_ID,
        )

    def step(self, stage):
        if stage > 0:
            self.copy(stage - 1).wait_recv()
            before = self.ref[...] if stage == 1 else self.partial[stage - 2]
            self.partial[stage - 1] = before + self.arrived[stage - 1]
        if stage < self.STAGES:
            self.copy(stage).start()

    def finish(self):
        for stage in range(self.STAGES):
            self.copy(stage).wait_send()

    def own_share(self, rows, share):
        width = self.ref.shape[1]
        place = self.y * 16 + self.z * 4 + self.x * 2 + self.c
        per_row = width // share
        offset = place % per_row * share
        row_index = lax.broadcasted_iota(jnp.int32, (width, 128), 0)
        column_index = lax.broadcasted_iota(jnp.int32, (width, 128), 1)
        picked = jnp.where(
            (row_index == column_index + offset) & (column_index < share), 1.0, 0.0
        ).astype(jnp.bfloat16)
        rest = rows
        total = jnp.zeros((rows.shape[0], 128), jnp.float32)
        for _ in range(3):
            piece = rest.astype(jnp.bfloat16)
            total = total + product(piece, picked, CONTRACT_INNER)
            rest = rest - piece.astype(jnp.float32)
        return total, place // per_row


STEP = 384
KEY_STEPS = (384, 256, 128)
UNROLL = 6


class CubeSum:
    STAGES = 3

    def __init__(self, partial, cube, line, send_sem, recv_sem):
        self.partial, self.cube, self.line = partial, cube, line
        self.send_sem, self.recv_sem = send_sem, recv_sem
        self.y, self.z, self.x, self.c = where_am_i()
        self.member = self.y * 4 + self.x * 2 + self.c

    def link(self, source, target, stage, device):
        return pltpu.make_async_remote_copy(
            src_ref=source,
            dst_ref=target,
            send_sem=self.send_sem.at[stage],
            recv_sem=self.recv_sem.at[stage],
            device_id=device,
            device_id_type=MESH_ID,
        )

    def others(self):
        for step in range(1, 8):
            other = (self.member + step) % 8
            yield (other // 4, self.z * 4 + other % 4)

    def copy(self, stage):
        beside = self.z + 1 - 2 * (self.z % 2) if stage == 1 else (self.z + 2) % PLANES
        return self.link(
            self.partial.at[stage - 1], self.line.at[stage - 1], stage,
            (self.y, beside * 4 + self.x * 2 + self.c),
        )

    def seven(self):
        seven = self.cube.at[pl.ds(0, 7)]
        return self.link(seven, seven, 0, (self.y, self.z * 4 + self.x * 2 + 1 - self.c))

    def step(self, stage):
        if stage == 0:
            own = self.cube.at[self.member]
            for device in self.others():
                self.link(own, own, 0, device).start()
            return
        if stage == 1:
            self.seven().wait_recv()
            self.partial[0] = jnp.sum(self.cube[...], axis=0)
        else:
            self.copy(stage - 1).wait_recv()
            self.partial[stage - 1] = self.partial[stage - 2] + self.line[stage - 2]
        if stage < self.STAGES:
            self.copy(stage).start()

    def finish(self):
        self.seven().wait_send()
        for stage in range(1, self.STAGES):
            self.copy(stage).wait_send()


class Quad:
    def __init__(self, by_x):
        self.by_x = by_x
        self.y, self.z, self.x, self.c = where_am_i()
        self.a, self.b = (self.x, self.y) if by_x else (self.y, self.x)
        self.mine = self.a * 2 + self.c
        self.peer = (1 - self.a) * 2 + self.c
        self.beside = self.a * 2 + 1 - self.c
        self.corner = (1 - self.a) * 2 + 1 - self.c

    def device(self, a, b, z, c):
        y, x = (b, a) if self.by_x else (a, b)
        return (y, z * 4 + x * 2 + c)

    def at_peer(self):
        return self.device(1 - self.a, self.b, self.z, self.c)

    def at_beside(self):
        return self.device(self.a, self.b, self.z, 1 - self.c)

    def at_corner(self):
        return self.device(1 - self.a, self.b, self.z, 1 - self.c)

    def link(self, source, target, send_sem, recv_sem, device):
        return pltpu.make_async_remote_copy(
            src_ref=source,
            dst_ref=target,
            send_sem=send_sem,
            recv_sem=recv_sem,
            device_id=device,
            device_id_type=MESH_ID,
        )

    def count(self, ref, send_sem, recv_sem):
        return self.link(ref, ref, send_sem, recv_sem, self.at_beside())


class Shared:
    def __init__(self, left, by_x, buffers):
        self.left = left
        self.held, self.send_sem, self.recv_sem = buffers
        self.quad = Quad(by_x)
        self.width = self.held.shape[2]

    def part(self, a):
        if self.quad.by_x:
            return self.left
        return self.left.at[:, pl.ds(pl.multiple_of(a * self.width, 128), self.width)]

    def share(self):
        q = self.quad
        slot = self.held.at[q.mine]
        send = self.send_sem.at[0]
        q.link(self.part(1 - q.a), slot, send, self.recv_sem.at[0], q.at_peer()).start()
        q.link(self.part(q.a), slot, send, self.recv_sem.at[1], q.at_beside()).start()
        self.held[q.mine] = self.part(q.a)[...]

    def relay(self):
        q = self.quad
        slot = self.held.at[q.peer]
        q.count(slot, self.send_sem.at[0], self.recv_sem.at[0]).wait_recv()
        q.link(slot, slot, self.send_sem.at[0], self.recv_sem.at[1], q.at_beside()).start()

    def complete(self):
        two = self.held.at[pl.ds(0, 2)]
        self.quad.count(two, self.send_sem.at[0], self.recv_sem.at[1]).wait_recv()

    def finish(self):
        three = self.held.at[pl.ds(0, 3)]
        self.quad.count(three, self.send_sem.at[0], self.recv_sem.at[1]).wait_send()


class Piece:
    def __init__(self, shared, right, base, stride, out, buffers):
        self.shared, self.right, self.base, self.stride, self.out = shared, right, base, stride, out
        self.rights, self.whole, self.b_in, self.z_in, self.last, self.send_sem, self.recv_sem = buffers
        self.wide = self.rights.shape[2]
        self.quad = shared.quad
        self.share_rows = out.shape[0]

    def columns(self, member):
        place = member if self.quad.by_x else member % 2
        return pl.ds(pl.multiple_of(self.base + place * self.stride, 128), self.wide)

    def give(self, member, device):
        self.quad.link(
            self.right.at[:, self.columns(member)], self.rights.at[self.quad.mine],
            self.send_sem.at[0], self.recv_sem.at[0], device,
        ).start()

    def share(self):
        q = self.quad
        self.give(q.peer, q.at_peer())
        self.give(q.corner, q.at_corner())
        self.give(q.beside, q.at_beside())
        self.rights[q.mine] = self.right[:, self.columns(q.mine)]

    def slab(self, b):
        return self.whole.at[b] if self.quad.by_x else self.whole.at[:, b]

    def cell(self, z):
        b = self.quad.b
        return self.whole.at[b, z] if self.quad.by_x else self.whole.at[z, b]

    def multiply(self):
        q = self.quad
        three = self.rights.at[pl.ds(0, 3)]
        q.count(three, self.send_sem.at[0], self.recv_sem.at[0]).wait_recv()
        held = self.shared.held
        tokens = held.shape[0] * held.shape[1]
        right = self.rights[...].reshape(tokens, self.wide)
        if self.shared.width > STEP:

            def one(i, carry):
                left = held[:, :, pl.ds(pl.multiple_of(i * STEP, 128), STEP)]
                part = product(left.reshape(tokens, STEP), right, CONTRACT_FIRST)
                self.whole[i] = part.astype(jnp.bfloat16).reshape(self.whole.shape[1:])
                return carry

            lax.fori_loop(0, self.shared.width // STEP, one, 0)
        else:
            part = product(held[...].reshape(tokens, STEP), right, CONTRACT_FIRST)
            self.whole[...] = part.astype(jnp.bfloat16).reshape(self.whole.shape)
        q.link(
            self.slab(1 - q.b), self.b_in, self.send_sem.at[1], self.recv_sem.at[1],
            q.device(q.a, 1 - q.b, q.z, q.c),
        ).start()

    def spread(self):
        q = self.quad
        q.count(self.b_in, self.send_sem.at[1], self.recv_sem.at[1]).wait_recv()
        slab = self.slab(q.b)
        slab[...] = (slab[...].astype(jnp.float32) + self.b_in[...].astype(jnp.float32)).astype(
            jnp.bfloat16
        )
        q.count(self.rights.at[pl.ds(0, 3)], self.send_sem.at[0], self.recv_sem.at[0]).wait_send()
        inner = self.inner()

        @pl.when(inner)
        def _():
            self.to_plane(self.cell(self.end()), 0, 1, self.end())

        @pl.when(jnp.logical_not(inner))
        def _():
            first = 1 - q.z // (PLANES - 1)
            three = pl.ds(first, 3)
            cells = self.whole.at[q.b, three] if q.by_x else self.whole.at[three, q.b]
            self.to_plane(cells, pl.ds(0, 3), 0, 1 + q.z // 2)

    def inner(self):
        return (self.quad.z > 0) & (self.quad.z < PLANES - 1)

    def end(self):
        return self.quad.z // 2 * (PLANES - 1)

    def to_plane(self, source, slot, which, z):
        q = self.quad
        q.link(
            source, self.z_in.at[slot], self.send_sem.at[0], self.recv_sem.at[2 + which],
            q.device(q.a, q.b, z, q.c),
        ).start()

    def fold(self):
        q = self.quad

        @pl.when(self.inner())
        def _():
            three = self.z_in.at[pl.ds(0, 3)]
            q.count(three, self.send_sem.at[0], self.recv_sem.at[2]).wait_recv()
            first = 2 - q.z
            for target in (PLANES - 1 - self.end(), PLANES - 1 - q.z):
                cell = self.cell(target)
                cell[...] = (
                    cell[...].astype(jnp.float32) + self.z_in[target - first].astype(jnp.float32)
                ).astype(jnp.bfloat16)
                self.to_plane(cell, 3, 1, target)

    def rows_of(self, member):
        place = member if self.quad.by_x else member % 2
        return self.last.at[pl.ds(pl.multiple_of(place * self.share_rows, 8), self.share_rows)]

    def collect(self):
        q = self.quad
        inner = self.inner()

        def arrived(count):
            some = self.z_in.at[pl.ds(0, count)]
            q.count(some, self.send_sem.at[0], self.recv_sem.at[3]).wait_recv()

        pl.when(inner)(lambda: arrived(1))
        pl.when(jnp.logical_not(inner))(lambda: arrived(2))
        beside = q.z // 2 * 2 * (1 - q.z // (PLANES - 1))
        self.last[...] = (
            self.cell(q.z)[...].astype(jnp.float32)
            + self.z_in[beside].astype(jnp.float32)
            + self.z_in[3].astype(jnp.float32)
        )
        q.count(self.b_in, self.send_sem.at[1], self.recv_sem.at[1]).wait_send()
        columns = self.out.at[:, self.columns(q.mine)]
        partners = [(q.beside, q.at_beside())]
        if q.by_x:
            partners = [(q.peer, q.at_peer()), (q.corner, q.at_corner())] + partners
        for member, device in partners:
            q.link(
                self.rows_of(member), columns, self.send_sem.at[1], self.recv_sem.at[4], device
            ).start()
        columns[...] = self.rows_of(q.mine)[...]

    def finish(self):
        q = self.quad
        others = self.last.at[pl.ds(0, (3 if q.by_x else 1) * self.share_rows)]
        q.count(others, self.send_sem.at[1], self.recv_sem.at[4]).wait()
        three = self.z_in.at[pl.ds(0, 3)]
        q.count(three, self.send_sem.at[0], self.recv_sem.at[2]).wait_send()


def shared_scratch(frame_count, left_width, by_x):
    return [
        pltpu.VMEM((4, frame_count, left_width if by_x else left_width // 2), jnp.bfloat16),
        pltpu.SemaphoreType.DMA((1,)),
        pltpu.SemaphoreType.DMA((2,)),
    ]


def piece_scratch(frame_count, left_width, by_x, wide=STEP):
    rows = left_width // (2 * PLANES) if by_x else left_width // (4 * PLANES)
    low = jnp.bfloat16
    return [
        pltpu.VMEM((4, frame_count, wide), low),
        pltpu.VMEM((2, PLANES, rows, wide) if by_x else (PLANES, 2, rows, wide), low),
        pltpu.VMEM((PLANES, rows, wide), low),
        pltpu.VMEM((PLANES, rows, wide), low),
        pltpu.VMEM((rows, wide), jnp.float32),
        pltpu.SemaphoreType.DMA((2,)),
        pltpu.SemaphoreType.DMA((5,)),
    ]


def cube_scratch(width):
    return [
        pltpu.VMEM((CubeSum.STAGES, 1, width), jnp.float32),
        pltpu.VMEM((8, 1, width), jnp.float32),
        pltpu.VMEM((CubeSum.STAGES - 1, 1, width), jnp.float32),
        pltpu.SemaphoreType.DMA((CubeSum.STAGES,)),
        pltpu.SemaphoreType.DMA((CubeSum.STAGES,)),
    ]


def vector_scratch(rows, width):
    wide = jnp.float32
    return [
        pltpu.VMEM((rows, width), wide),
        pltpu.VMEM((VectorSum.STAGES, rows, width), wide),
        pltpu.VMEM((VectorSum.STAGES, rows, width), wide),
        pltpu.SemaphoreType.DMA((VectorSum.STAGES,)),
        pltpu.SemaphoreType.DMA((VectorSum.STAGES,)),
    ]


def layer_scratch(frame_count, width, inner):
    low, wide = jnp.bfloat16, jnp.float32
    dma = pltpu.SemaphoreType.DMA
    return dict(
        qkv_held=pltpu.VMEM((width, 3 * width), low),
        out_held=pltpu.VMEM((width, width), low),
        up_held=pltpu.VMEM((width, inner), low),
        down_held=pltpu.VMEM((inner, width), low),
        weight_sem=dma((4,)),
        block=pltpu.VMEM((BLOCKS, frame_count + 16, width), low),
        block_sems=gather_sems(2, 1),
        grad_block=pltpu.VMEM((BLOCKS, frame_count, width), low),
        stats=pltpu.VMEM((BLOCKS, 32, frame_count), wide),
        grad_sems=gather_sems(3, 2),
        projected=pltpu.VMEM((BLOCKS, frame_count, 3 * width), low),
        mask=pltpu.VMEM((frame_count, BLOCKS * frame_count), wide),
        attended=pltpu.VMEM((frame_count, width), wide),
        slope=pltpu.VMEM((frame_count, inner), wide),
        logs=pltpu.VMEM((frame_count, 128), wide),
        delta=pltpu.VMEM((frame_count, 128), wide),
        inner_bias=pltpu.VMEM((1, inner), wide),
        act=pltpu.VMEM((frame_count, inner), low),
        pre_low=pltpu.VMEM((frame_count, inner), low),
        context=pltpu.VMEM((frame_count, width), low),
        hidden_low=pltpu.VMEM((frame_count, width), low),
        second_low=pltpu.VMEM((frame_count, width), low),
        first_low=pltpu.VMEM((frame_count, width), low),
        normed=pltpu.VMEM((frame_count, width), wide),
        running=pltpu.VMEM((frame_count, width), wide),
        first_grad=pltpu.VMEM((frame_count, width), wide),
        proj_grad=pltpu.VMEM((frame_count, 3 * width), low),
        early=vector_scratch(16, width),
        late=cube_scratch(width),
        down_left=shared_scratch(frame_count, inner, False),
        up_left=shared_scratch(frame_count, width, True),
        out_left=shared_scratch(frame_count, width, False),
        qkv_left=shared_scratch(frame_count, width, False),
        down_piece=piece_scratch(frame_count, inner, False),
        up_pieces=[piece_scratch(frame_count, width, True) for _ in range(2)],
        out_piece=piece_scratch(frame_count, width, False),
        query_piece=piece_scratch(frame_count, width, False),
        key_pieces=[
            piece_scratch(frame_count, width, False, step) for step in KEY_STEPS
        ],
    )


class Inputs(typing.NamedTuple):
    frames: typing.Any
    segment_ids: typing.Any
    qkv_weight: typing.Any
    query_bias: typing.Any
    value_bias: typing.Any
    out_weight: typing.Any
    out_bias: typing.Any
    norm1_gain: typing.Any
    norm1_shift: typing.Any
    up_weight: typing.Any
    up_bias: typing.Any
    down_weight: typing.Any
    down_bias: typing.Any
    norm2_gain: typing.Any
    norm2_shift: typing.Any
    cotangent: typing.Any


class Outputs(typing.NamedTuple):
    layer_out: typing.Any
    input_grad: typing.Any
    qkv_g: typing.Any
    query_g: typing.Any
    value_g: typing.Any
    out_g: typing.Any
    outbias_g: typing.Any
    gain1_g: typing.Any
    shift1_g: typing.Any
    up_g: typing.Any
    upbias_g: typing.Any
    down_g: typing.Any
    downbias_g: typing.Any
    gain2_g: typing.Any
    shift2_g: typing.Any


class Refs:
    def __init__(self, *groups):
        for group in groups:
            for name, ref in group.items():
                setattr(self, name, ref)


def layer_kernel(held, *refs):
    inputs, outputs = len(Inputs._fields), len(Outputs._fields)
    scratch = jax.tree.unflatten(held, refs[inputs + outputs :])
    k = Refs(dict(zip(Inputs._fields + Outputs._fields, refs)), scratch)
    frame_count, width = k.frames.shape
    inner = k.inner_bias.shape[1]
    low, wide = jnp.bfloat16, jnp.float32
    total = BLOCKS * frame_count
    row, z, x, c = where_am_i()
    mine = z * 4 + x * 2 + c
    has_up, has_down = z < PLANES - 1, z > 0
    far = (z + 2) % PLANES
    lost = PLANES - 1 - z
    lane = lax.broadcasted_iota(jnp.int32, (frame_count, 128), 1)

    def fetch(i):
        source, target = (
            (k.qkv_weight, k.qkv_held),
            (k.out_weight, k.out_held),
            (k.up_weight, k.up_held),
            (k.down_weight, k.down_held),
        )[i]
        return pltpu.make_async_copy(source, target, k.weight_sem.at[i])

    for i in range(4):
        fetch(i).start()

    line_rows = frame_count * 80 // 128
    back_rows = frame_count * 64 // 128
    link = RowGather(
        [
            (k.block, 0, line_rows),
            (k.block, line_rows, k.block.shape[1] - line_rows),
        ],
        (0,),
        (1,),
        k.block_sems,
    )
    back = RowGather(
        [
            (k.grad_block, 0, back_rows),
            (k.grad_block, back_rows, frame_count - back_rows),
            (k.stats, 0, 32),
        ],
        (2, 0),
        (1,),
        k.grad_sems,
    )
    down_left = Shared(k.act, False, k.down_left)
    up_left = Shared(k.hidden_low, True, k.up_left)
    out_left = Shared(k.context, False, k.out_left)
    qkv_left = Shared(k.frames, False, k.qkv_left)
    half_width = width // 2
    down = Piece(down_left, k.second_low, 0, half_width, k.down_g, k.down_piece)
    ups = [
        Piece(up_left, k.pre_low, p * STEP, width, k.up_g, k.up_pieces[p]) for p in range(2)
    ]
    out = Piece(out_left, k.first_low, 0, half_width, k.out_g, k.out_piece)
    query = Piece(qkv_left, k.proj_grad, 0, half_width, k.qkv_g, k.query_piece)
    keys = [
        Piece(qkv_left, k.proj_grad, width + sum(KEY_STEPS[:i]), width, k.qkv_g, buffers)
        for i, buffers in enumerate(k.key_pieces)
    ]
    early, late = VectorSum(*k.early), CubeSum(*k.late)

    places = [(row, z, x, 1 - c), (1 - row, z, x, c), (1 - row, z, x, 1 - c)]
    places += [(row, z, 1 - x, c), (row, z, 1 - x, 1 - c)]
    places += [(1 - row, z, 1 - x, c), (1 - row, z, 1 - x, 1 - c)]
    places += [(row, (z + 2) % PLANES, x, c), (row, z + 1 - 2 * (z % 2), x, c)]
    partners = [(None, (y, at * 4 + across * 2 + core)) for y, at, across, core in places]
    middle = has_up & has_down
    partners.append((middle, (row, (PLANES - 1 - z) * 4 + x * 2 + c)))
    meet(partners, len(places) + middle.astype(jnp.int32))

    own_ids = jnp.broadcast_to(k.segment_ids[...], (frame_count, frame_count)).astype(wide)
    ids_column = own_ids.T
    k.block[mine, pl.ds(0, frame_count), :] = k.frames[...]
    k.block[mine, pl.ds(frame_count, 16), pl.ds(0, frame_count)] = own_ids[:16].astype(low)
    link.own()
    link.cross_over()
    link.line_near()
    k.inner_bias[...] = k.up_bias[...].reshape(1, inner)
    query_bias = k.query_bias[...].reshape(1, width)
    value_bias = k.value_bias[...].reshape(1, width)

    def plane_rows(plane):
        return jnp.concatenate(
            [k.block[plane * 4 + i, pl.ds(0, frame_count), :] for i in range(4)], axis=0
        )

    def store_rows(plane, third, part):
        for i in range(4):
            k.projected[plane * 4 + i, :, pl.ds(third * width, width)] = part[
                i * frame_count : (i + 1) * frame_count
            ]

    def as_query(part):
        return (part + query_bias).astype(low) * HEAD_DIM**-0.5

    def project(plane):
        rows = plane_rows(plane)
        keys = product(rows, k.qkv_held[:, pl.ds(width, width)], CONTRACT_INNER)
        store_rows(plane, 1, keys.astype(low))
        values = product(rows, k.qkv_held[:, pl.ds(2 * width, width)], CONTRACT_INNER)
        store_rows(plane, 2, (values + value_bias).astype(low))
        for i in range(4):
            ids = k.block[plane * 4 + i, pl.ds(frame_count, 8), pl.ds(0, frame_count)]
            same = jnp.broadcast_to(ids.astype(wide)[:1], own_ids.shape) == ids_column
            at = pl.multiple_of((plane * 4 + i) * frame_count, 128)
            k.mask[:, pl.ds(at, frame_count)] = jnp.where(same, 0.0, mask_fill)

    def project_queries(plane):
        queries = product(plane_rows(plane), k.qkv_held[:, pl.ds(0, width)], CONTRACT_INNER)
        store_rows(plane, 0, as_query(queries))

    def queries_own_far():
        project_queries(z)
        project_queries(far)

    def queries_near():
        pl.when(has_down)(lambda: project_queries(z - 1))
        pl.when(has_up)(lambda: project_queries(z + 1))

    def planes_done():
        back.plane_done(z)
        back.plane_done(z - 1, has_down)
        back.plane_done(z + 1, has_up)
        back.plane_done(far)

    def input_gradient():
        k.input_grad[...] = k.first_grad[...] + product(
            k.proj_grad[...], k.qkv_held[...], CONTRACT_LAST
        )

    def query_note():
        note(early, 6, k.proj_grad[:, pl.ds(0, width)].astype(wide))

    def late_notes():
        values = k.proj_grad[:, pl.ds(2 * width, width)].astype(wide)
        late.cube[late.member] = jnp.sum(values, axis=0, keepdims=True)

    def small_shares():
        share = k.query_g.shape[0]
        first = early.partial[VectorSum.STAGES - 1]
        shares, _ = early.own_share(first[:8], share)
        k.query_g[...] = shares[6, :share]
        last = jnp.broadcast_to(late.partial[CubeSum.STAGES - 1], (8, width))
        k.value_g[...] = early.own_share(last, share)[0][0, :share]
        for i, ref in enumerate(
            (k.outbias_g, k.gain1_g, k.shift1_g, k.downbias_g, k.gain2_g, k.shift2_g)
        ):
            ref[...] = shares[i, :share]
        up_shares, at = early.own_share(first[8:], 4 * share)
        keep = lax.broadcasted_iota(jnp.int32, up_shares.shape, 0) == at
        picked = jnp.sum(jnp.where(keep, up_shares, 0.0), axis=0, keepdims=True)
        k.upbias_g[...] = picked[0, : 4 * share]

    def note(vector, index, values):
        vector.ref[pl.ds(index, 1), :] = jnp.sum(values, axis=0, keepdims=True)

    def flat(ref):
        return ref[...].reshape(1, width)

    def columns_of(third, j):
        return pl.ds(pl.multiple_of(third * width + j * 128, 128), 128)

    def head_state(h):
        return pl.ds(pl.multiple_of(h * 128, 128), 128)

    def both_heads(values):
        nothing = jnp.zeros_like(values)
        return jnp.concatenate(
            [jnp.where(lane < HALF, values, nothing), jnp.where(lane < HALF, nothing, values)],
            axis=0,
        )

    def own_halves(values):
        return jnp.where(lane < HALF, values[:frame_count], values[frame_count:])

    def attend(plane, first):
        at = pl.multiple_of(plane * 4 * frame_count, 128)

        def state(kind, j):
            return k.slope.at[:, pl.ds(pl.multiple_of((kind * HEADS + 2 * j) * 128, 128), 256)]

        def read(kind, j):
            pair_state = state(kind, j)[...]
            return jnp.concatenate([pair_state[:, :128], pair_state[:, 128:]], axis=0)

        def write(kind, j, values):
            state(kind, j)[...] = jnp.concatenate(
                [values[:frame_count], values[frame_count:]], axis=1
            )

        def pair(j, carry):
            query = both_heads(k.projected[mine, :, columns_of(0, j)])
            keys = k.projected[pl.ds(plane * 4, 4), :, columns_of(1, j)].reshape(-1, 128)
            values = k.projected[pl.ds(plane * 4, 4), :, columns_of(2, j)].reshape(-1, 128)
            mask = k.mask[:, pl.ds(at, 4 * frame_count)]
            scores = product(query, keys, CONTRACT_LAST) + jnp.concatenate([mask, mask], axis=0)
            tile = (2 * frame_count, 128)
            peak = jnp.broadcast_to(jnp.max(scores, axis=1, keepdims=True), tile)
            if not first:
                old = read(0, j)
                peak = jnp.maximum(peak, old)
                factor = jnp.exp(old - peak)
            weights = jnp.exp(scores - jnp.concatenate([peak] * 4, axis=1))
            whole = jnp.broadcast_to(jnp.sum(weights, axis=1, keepdims=True), tile)
            if not first:
                whole = whole + read(1, j) * factor
            write(0, j, peak)
            write(1, j, whole)
            both = own_halves(product(weights.astype(low), values, CONTRACT_INNER))
            if not first:
                both = both + k.attended[:, columns_of(0, j)] * own_halves(factor)
            k.attended[:, columns_of(0, j)] = both
            return carry

        lax.fori_loop(0, PAIRS, pair, 0, unroll=UNROLL)

    def own_queries():
        fetch(0).wait()
        own = product(k.frames[...], k.qkv_held[:, pl.ds(0, width)], CONTRACT_INNER)
        k.projected[mine, :, pl.ds(0, width)] = as_query(own)

    def take_plane(plane, present=None):
        def take():
            link.plane_done(plane)
            project(plane)

        if present is None:
            take()
        else:
            pl.when(present)(take)

    def attend_near(plane, present):
        pl.when(present)(lambda: attend(plane, False))

    own_queries()
    link.line_over()
    take_plane(z)
    link.cross_near_over()
    link.cross_near()
    link.line_near_over()
    link.line_far()
    qkv_left.share()
    attend(z, True)
    take_plane(z - 1, has_down)
    take_plane(z + 1, has_up)
    link.line_far_over()
    link.cross_far()
    link.cross_far_over()
    attend_near(z + 1, has_up)
    attend_near(z - 1, has_down)
    take_plane(far)
    attend(far, False)
    logs = jnp.zeros(lane.shape, wide)
    for j in range(PAIRS):
        parts = []
        for h in range(2):
            whole = k.slope[:, head_state(HEADS + 2 * j + h)]
            logs = jnp.where(
                lane == 2 * j + h, k.slope[:, head_state(2 * j + h)] + jnp.log(whole), logs
            )
            parts.append(whole)
        done = k.attended[:, columns_of(0, j)] / jnp.where(lane < HALF, parts[0], parts[1])
        k.attended[:, columns_of(0, j)] = done
        k.context[:, columns_of(0, j)] = done.astype(low)
    k.logs[...] = logs

    def normalize(resid):
        centred = resid - jnp.mean(resid, axis=-1, keepdims=True)
        inverse = lax.rsqrt(jnp.mean(centred * centred, axis=-1, keepdims=True) + norm_eps)
        return centred * inverse, inverse

    def normalize_back(upstream, normed, inverse, gain):
        scaled = upstream * gain
        first_mean = jnp.mean(scaled, axis=-1, keepdims=True)
        second_mean = jnp.mean(scaled * normed, axis=-1, keepdims=True)
        return inverse * (scaled - first_mean - normed * second_mean)

    early.ref[...] = jnp.zeros((16, width), wide)
    fetch(1).wait()
    resid_one = (
        k.frames[...].astype(wide)
        + product(k.context[...], k.out_held[...], CONTRACT_INNER)
        + flat(k.out_bias)
    )
    normed_one, inverse_one = normalize(resid_one)
    k.normed[...] = normed_one
    hidden = normed_one * flat(k.norm1_gain) + flat(k.norm1_shift)
    k.hidden_low[...] = hidden.astype(low)
    up_left.share()
    k.running[...] = hidden + flat(k.down_bias)
    fetch(2).wait()
    fetch(3).wait()

    def forward(f, carry):
        columns = pl.ds(pl.multiple_of(f * width, 128), width)
        pre_act = (
            product(k.hidden_low[...], k.up_held[:, columns], CONTRACT_INNER)
            + k.inner_bias[:, columns]
        )
        normal_cdf = 0.5 * (1.0 + lax.erf(pre_act * 0.5**0.5))
        normal_pdf = jnp.exp(-0.5 * pre_act * pre_act) * (2.0 * math.pi) ** (-0.5)
        act = (pre_act * normal_cdf).astype(low)
        k.act[:, columns] = act
        k.slope[:, columns] = normal_cdf + pre_act * normal_pdf
        k.running[...] += product(
            act, k.down_held[pl.ds(pl.multiple_of(f * width, 128), width), :], CONTRACT_INNER
        )
        return carry

    lax.fori_loop(0, inner // width, forward, 0)
    down_left.share()
    out_left.share()
    normed_two, inverse_two = normalize(k.running[...])
    k.layer_out[...] = (normed_two * flat(k.norm2_gain) + flat(k.norm2_shift)).astype(low)
    upstream = k.cotangent[...].astype(wide)
    second_grad = normalize_back(upstream, normed_two, inverse_two, flat(k.norm2_gain))
    k.second_low[...] = second_grad.astype(low)
    note(early, 3, second_grad)
    note(early, 4, upstream * normed_two)
    note(early, 5, upstream)
    k.running[...] = second_grad

    def backward(p):
        for member in range(4):
            first = member * width + p * STEP
            columns = pl.ds(first, STEP)
            pre_grad = (
                product(k.second_low[...], k.down_held[columns, :], CONTRACT_LAST)
                * k.slope[:, columns]
            )
            early.ref[pl.ds(8 + member, 1), pl.ds(p * STEP, STEP)] = jnp.sum(
                pre_grad, axis=0, keepdims=True
            )
            k.pre_low[:, columns] = pre_grad.astype(low)
            k.running[...] += product(
                k.pre_low[:, columns], k.up_held[:, columns], CONTRACT_LAST
            )

    backward(0)
    ups[0].share()
    up_left.relay()
    backward(1)
    hidden_grad = k.running[...]
    normed_one = k.normed[...]
    first_grad = normalize_back(hidden_grad, normed_one, inverse_one, flat(k.norm1_gain))
    k.first_grad[...] = first_grad
    k.first_low[...] = first_grad.astype(low)
    note(early, 0, first_grad)
    note(early, 1, hidden_grad * normed_one)
    note(early, 2, hidden_grad)
    context_grad = product(k.first_low[...], k.out_held[...], CONTRACT_LAST).astype(low)
    k.grad_block[mine] = context_grad
    delta = jnp.zeros(lane.shape, wide)
    for j in range(PAIRS):
        columns = slice(j * 128, (j + 1) * 128)
        both = context_grad[:, columns].astype(wide) * k.attended[:, columns]
        for h in range(2):
            one = jnp.sum(
                jnp.where((lane < HALF) == (h == 0), both, 0.0), axis=1, keepdims=True
            )
            delta = jnp.where(lane == 2 * j + h, one, delta)
    k.delta[...] = delta
    k.stats[mine, pl.ds(0, 16), :] = k.logs[...].T[:16]
    k.stats[mine, pl.ds(16, 16), :] = delta.T[:16]
    down.share()
    back.own()

    @pl.when(jnp.logical_not(middle))
    def _():
        for i in range(4):
            k.projected[lost * 4 + i] = jnp.zeros((frame_count, 3 * width), low)
            k.grad_block[lost * 4 + i] = jnp.zeros((frame_count, width), low)
            k.stats[lost * 4 + i] = jnp.zeros((32, frame_count), wide)
            at = pl.multiple_of((lost * 4 + i) * frame_count, 128)
            k.mask[:, pl.ds(at, frame_count)] = jnp.full(lane.shape, mask_fill, wide)

    def query_pair(j):
        query = k.projected[mine, :, columns_of(0, j)]
        upstream = k.grad_block[mine, :, columns_of(0, j)]
        keys = k.projected[:, :, columns_of(1, j)].reshape(total, 128)
        values = k.projected[:, :, columns_of(2, j)].reshape(total, 128)
        outs = []
        for h in range(2):
            chosen = (lane < HALF) == (h == 0)
            nothing = jnp.zeros_like(query)
            logs = jnp.sum(
                jnp.where(lane == 2 * j + h, k.logs[...], 0.0), axis=1, keepdims=True
            )
            shift = jnp.sum(
                jnp.where(lane == 2 * j + h, k.delta[...], 0.0), axis=1, keepdims=True
            )
            scores = product(jnp.where(chosen, query, nothing), keys, CONTRACT_LAST)
            probs = jnp.exp(scores + k.mask[...] - logs)
            prob_grad = product(jnp.where(chosen, upstream, nothing), values, CONTRACT_LAST)
            score_grad = (probs * (prob_grad - shift)).astype(low)
            outs.append(product(score_grad, keys, CONTRACT_INNER))
        k.proj_grad[:, columns_of(0, j)] = (
            jnp.where(lane < HALF, outs[0], outs[1]) * HEAD_DIM**-0.5
        ).astype(low)

    def key_pair(j):
        key = k.projected[mine, :, columns_of(1, j)]
        value = k.projected[mine, :, columns_of(2, j)]
        queries = k.projected[:, :, columns_of(0, j)].reshape(total, 128)
        upstream = k.grad_block[:, :, columns_of(0, j)].reshape(total, 128)
        key_outs, value_outs = [], []
        for h in range(2):
            chosen = (lane < HALF) == (h == 0)
            nothing = jnp.zeros_like(key)
            logs = jnp.concatenate(
                [k.stats[b, pl.ds(2 * j + h, 1), :] for b in range(BLOCKS)], axis=1
            )
            shift = jnp.concatenate(
                [k.stats[b, pl.ds(16 + 2 * j + h, 1), :] for b in range(BLOCKS)], axis=1
            )
            scores = product(jnp.where(chosen, key, nothing), queries, CONTRACT_LAST)
            probs = jnp.exp(scores + k.mask[...] - logs)
            prob_grad = product(jnp.where(chosen, value, nothing), upstream, CONTRACT_LAST)
            score_grad = (probs * (prob_grad - shift)).astype(low)
            key_outs.append(product(score_grad, queries, CONTRACT_INNER))
            value_outs.append(product(probs.astype(low), upstream, CONTRACT_INNER))
        k.proj_grad[:, columns_of(1, j)] = jnp.where(
            lane < HALF, key_outs[0], key_outs[1]
        ).astype(low)
        k.proj_grad[:, columns_of(2, j)] = jnp.where(
            lane < HALF, value_outs[0], value_outs[1]
        ).astype(low)

    def pairs(one, first, last):
        def body(j, carry):
            one(j)
            return carry

        lax.fori_loop(first, last, body, 0)

    pairs(query_pair, 0, 3)
    back.cross_over()
    ups[1].share()
    pairs(query_pair, 3, 4)
    up_left.complete()
    back.line_near()
    down_left.relay()
    back.cross_near()
    pairs(query_pair, 4, 5)
    ups[0].multiply()
    back.line_far()
    down_left.complete()
    queries_own_far()
    back.cross_near_over()
    back.cross_far()
    back.line_near_over()
    ups[1].multiply()
    down.multiply()
    out_left.relay()
    queries_near()
    out.share()
    back.line_over()
    back.line_far_over()
    back.cross_far_over()
    ups[0].spread()
    pairs(query_pair, 5, 6)
    out_left.complete()
    planes_done()
    query_note()
    early.step(0)
    pairs(key_pair, 0, 1)
    qkv_left.relay()
    ups[1].spread()
    early.step(1)
    query.share()
    pairs(key_pair, 1, 2)
    qkv_left.complete()
    pairs(key_pair, 2, 3)
    ups[1].fold()
    ups[0].fold()
    pairs(key_pair, 3, 4)
    down.spread()
    out.multiply()
    early.step(2)
    pairs(key_pair, 4, 5)
    keys[0].share()
    pairs(key_pair, 5, 6)
    query.multiply()
    early.step(3)
    down.fold()
    keys[2].share()
    keys[1].share()
    out.spread()
    late_notes()
    late.step(0)
    input_gradient()
    keys[0].multiply()
    query.spread()
    out.fold()
    keys[2].multiply()
    early.step(4)
    keys[1].multiply()
    late.step(1)
    ups[0].collect()
    query.fold()
    down.collect()
    keys[0].spread()
    keys[0].fold()
    keys[2].spread()
    keys[1].spread()
    late.step(2)
    keys[2].fold()
    keys[1].fold()
    ups[1].collect()
    late.step(3)
    query.collect()
    keys[0].collect()
    early.step(5)
    out.collect()
    small_shares()
    keys[2].collect()
    keys[1].collect()
    for each in [down_left, up_left, out_left, qkv_left, down, out, query] + ups + keys:
        each.finish()
    for each in (back, link, early, late):
        each.finish()


def copy_kernel(*refs):
    count = len(refs) // 2
    for source, target in zip(refs[:count], refs[count:]):
        target[...] = source[...]


def hand_over(results):
    return pl.pallas_call(
        copy_kernel,
        out_shape=tuple(jax.ShapeDtypeStruct(each.shape, each.dtype) for each in results),
        in_specs=[IN_VMEM] * len(results),
        out_specs=(IN_VMEM,) * len(results),
    )(*results)


def layer_step(*args):
    frames = args[0]
    frame_count, width = frames.shape[1:]
    inner = args[9].shape[1]
    low, wide = jnp.bfloat16, jnp.float32
    scratch, held = jax.tree.flatten(layer_scratch(frame_count, width, inner))
    operands = [frames[0]] + list(args[1:-1]) + [args[-1][0]]
    share = width // 32
    shapes = [
        ((frame_count, width), low),
        ((frame_count, width), wide),
        ((share, 3 * width), wide),
        ((share,), wide),
        ((share,), wide),
        ((share, width), wide),
        ((share,), wide),
        ((share,), wide),
        ((share,), wide),
        ((share, inner), wide),
        ((4 * share,), wide),
        ((4 * share, width), wide),
        ((share,), wide),
        ((share,), wide),
        ((share,), wide),
    ]
    results = pl.pallas_call(
        functools.partial(layer_kernel, held),
        out_shape=tuple(jax.ShapeDtypeStruct(shape, kind) for shape, kind in shapes),
        in_specs=[IN_PLACE if each.ndim == 2 and each.shape[0] >= width else IN_VMEM for each in operands],
        out_specs=(IN_VMEM,) * len(shapes),
        scratch_shapes=scratch,
        compiler_params=pltpu.CompilerParams(
            collective_id=0, has_side_effects=True, vmem_limit_bytes=VMEM_BYTES
        ),
    )(*operands)
    results = hand_over(results)
    return (results[0][None], results[1][None]) + tuple(results[2:])


def solution(mesh):
    chosen = layer_step if dict(mesh.shape) == {"rows": 2, "seq": 16} else shards
    in_specs = (
        P("rows", "seq", None),
        P("rows", "seq"),
        P(),
        P(),
        P(),
        P(),
        P(),
        P(),
        P(),
        P(),
        P(),
        P(),
        P(),
        P(),
        P(),
        P("rows", "seq", None),
    )
    out_specs = (
        P("rows", "seq", None),
        P("rows", "seq", None),
        P(("rows", "seq"), None),
        P(("rows", "seq")),
        P(("rows", "seq")),
        P(("rows", "seq"), None),
        P(("rows", "seq")),
        P(("rows", "seq")),
        P(("rows", "seq")),
        P(("rows", "seq"), None),
        P(("rows", "seq")),
        P(("rows", "seq"), None),
        P(("rows", "seq")),
        P(("rows", "seq")),
        P(("rows", "seq")),
    )
    return jax.shard_map(chosen, mesh=mesh, in_specs=in_specs, out_specs=out_specs, check_vma=False)
```

```python
import functools
import math
import typing

import jax
import jax.numpy as jnp
from jax import lax
from jax.experimental import pallas as pl
from jax.experimental.pallas import tpu as pltpu
from jax.sharding import PartitionSpec as P

HEADS = 12
HEAD_DIM = 64


norm_eps = 1e-05
mask_fill = -1e30


def shortened(shard):

    def short(part):
        return part.astype(jnp.bfloat16) if part.dtype == jnp.float32 else part

    return jax.tree.map(short, shard)


def passed_along(value, axis, steps):
    count = lax.axis_size(axis)
    pairs = [(source, (source + steps) % count) for source in range(count)]
    return lax.ppermute(value, axis, pairs)


def layer_norm(resid, gain, shift):
    centred = resid - jnp.mean(resid, axis=-1, keepdims=True)
    inv_std = lax.rsqrt(jnp.mean(centred * centred, axis=-1, keepdims=True) + norm_eps)
    normed = centred * inv_std
    return (normed * gain + shift, normed, inv_std)


def norm_back(upstream, normed, inv_std, gain):
    scaled = upstream * gain
    first_mean = jnp.mean(scaled, axis=-1, keepdims=True)
    second_mean = jnp.mean(scaled * normed, axis=-1, keepdims=True)
    grad_in = inv_std * (scaled - first_mean - normed * second_mean)
    return (grad_in, jnp.sum(upstream * normed, axis=0), jnp.sum(upstream, axis=0))


def gelu_slope(pre_act):
    normal_cdf = 0.5 * (1.0 + lax.erf(pre_act * 0.5**0.5))
    normal_pdf = jnp.exp(-0.5 * pre_act * pre_act) * (2.0 * math.pi) ** (-0.5)
    return normal_cdf + pre_act * normal_pdf


def head_groups(head_count):
    return [(0, head_count, 1)]


def pass_keys(blocks):
    return jax.tree.map(
        lambda part, own: part.astype(own.dtype), passed_along(shortened(blocks), "seq", 1), blocks
    )


def pass_again(blocks):
    return jax.tree.map(
        lambda part, own: part.astype(own.dtype), passed_along(shortened(blocks), "seq", 1), blocks
    )


def pass_grads(blocks):
    return (
        passed_along(blocks[0].astype(jnp.bfloat16), "seq", 1).astype(jnp.float32),
        passed_along(blocks[1].astype(jnp.bfloat16), "seq", 1).astype(jnp.float32),
    )


def block_scores(query_part, key_part, query_ids, key_ids):
    scores = jnp.einsum(
        "qhe,khe->hqk", query_part, key_part, preferred_element_type=jnp.float32
    ) * HEAD_DIM ** (-0.5)
    return jnp.where((query_ids[:, None] == key_ids[None, :])[None], scores, mask_fill)


def attend_block(carried, query_part, key_part, value_part, query_ids, key_ids):
    run_max, run_total, run_acc = carried
    scores = block_scores(query_part, key_part, query_ids, key_ids)
    new_max = jnp.maximum(run_max, jnp.max(scores, axis=-1))
    weights = jnp.exp(scores - new_max[:, :, None])
    factor = jnp.exp(run_max - new_max)
    new_total = run_total * factor + jnp.sum(weights, axis=-1)
    update = jnp.einsum(
        "hqk,khe->qhe", weights.astype(jnp.bfloat16), value_part, preferred_element_type=jnp.float32
    )
    return (new_max, new_total, run_acc * factor.T[:, :, None] + update)


def grad_block(
    carried,
    query_part,
    key_part,
    value_part,
    query_ids,
    key_ids,
    context_part,
    log_part,
    delta_part,
):
    query_acc, key_acc, value_acc = carried
    scores = block_scores(query_part, key_part, query_ids, key_ids)
    probs = jnp.exp(scores - log_part[:, :, None])
    prob_grad = jnp.einsum(
        "qhe,khe->hqk", context_part, value_part, preferred_element_type=jnp.float32
    )
    score_grad = (probs * (prob_grad - delta_part[:, :, None])).astype(jnp.bfloat16)
    scale = HEAD_DIM ** (-0.5)
    query_acc = query_acc + scale * jnp.einsum(
        "hqk,khe->qhe", score_grad, key_part, preferred_element_type=jnp.float32
    )
    key_acc = key_acc + scale * jnp.einsum(
        "hqk,qhe->khe", score_grad, query_part, preferred_element_type=jnp.float32
    )
    value_acc = value_acc + jnp.einsum(
        "hqk,qhe->khe", probs.astype(jnp.bfloat16), context_part, preferred_element_type=jnp.float32
    )
    return (query_acc, key_acc, value_acc)


def forward_cycle(
    query_heads, key_heads, value_heads, local_ids, every_id, cycle_place, cycle_size
):
    frame_count, head_count, head_width = query_heads.shape
    grouping = head_groups(head_count)
    states = []
    blocks = []
    for head_first, head_last, direction in grouping:
        head_span = head_last - head_first
        initial = (
            jnp.full((head_span, frame_count), mask_fill, jnp.float32),
            jnp.zeros((head_span, frame_count), jnp.float32),
            jnp.zeros((frame_count, head_span, head_width), jnp.float32),
        )
        states.append(
            attend_block(initial, query_heads, key_heads, value_heads, local_ids, local_ids)
        )
        blocks.append((key_heads, value_heads))

    def forward_cycle_turn(turn_index, cycle_carry):
        old_states, old_blocks = cycle_carry
        new_states = []
        new_blocks = []
        for group_info, part_state, part_block in zip(grouping, old_states, old_blocks):
            head_first, head_last, direction = group_info
            part_block = pass_keys(part_block)
            source_index = (cycle_place - direction * turn_index) % cycle_size
            key_ids = lax.dynamic_slice_in_dim(every_id, source_index * frame_count, frame_count)
            new_states.append(
                attend_block(
                    part_state, query_heads, part_block[0], part_block[1], local_ids, key_ids
                )
            )
            new_blocks.append(part_block)
        return (new_states, new_blocks)

    states, blocks = lax.fori_loop(1, cycle_size, forward_cycle_turn, (states, blocks))
    maxima = jnp.concatenate([part_state[0] for part_state in states], axis=0)
    totals = jnp.concatenate([part_state[1] for part_state in states], axis=0)
    sums_all = jnp.concatenate([part_state[2] for part_state in states], axis=1)
    attended = sums_all / totals.T[:, :, None]
    return (attended, maxima + jnp.log(totals))


def backward_cycle(
    query_heads,
    key_heads,
    value_heads,
    local_ids,
    every_id,
    context_heads,
    log_total,
    row_delta,
    cycle_place,
    cycle_size,
):
    frame_count, head_count, head_width = query_heads.shape
    grouping = head_groups(head_count)
    initial = []
    for head_first, head_last, direction in grouping:
        zero_part = jnp.zeros((frame_count, head_last - head_first, head_width), jnp.float32)
        initial.append((zero_part, (key_heads, value_heads), (zero_part, zero_part)))

    def backward_cycle_turn(turn_index, cycle_carry):
        new_carry = []
        for group_info, part_carry in zip(grouping, cycle_carry):
            head_first, head_last, direction = group_info
            query_acc, part_block, part_grads = part_carry
            source_index = (cycle_place - direction * turn_index) % cycle_size
            key_ids = lax.dynamic_slice_in_dim(every_id, source_index * frame_count, frame_count)
            query_acc, key_acc, value_acc = grad_block(
                (query_acc, part_grads[0], part_grads[1]),
                query_heads,
                part_block[0],
                part_block[1],
                local_ids,
                key_ids,
                context_heads,
                log_total,
                row_delta,
            )
            part_grads = pass_grads((key_acc, value_acc))
            part_block = pass_again(part_block)
            new_carry.append((query_acc, part_block, part_grads))
        return new_carry

    final = lax.fori_loop(0, cycle_size, backward_cycle_turn, initial)
    query_grad = jnp.concatenate([part_carry[0] for part_carry in final], axis=1)
    key_grad = jnp.concatenate([part_carry[2][0] for part_carry in final], axis=1)
    value_grad = jnp.concatenate([part_carry[2][1] for part_carry in final], axis=1)
    return (query_grad, key_grad, value_grad)


def shards(
    frames,
    segment_ids,
    qkv_weight,
    query_bias,
    value_bias,
    out_weight,
    out_bias,
    norm1_gain,
    norm1_shift,
    up_weight,
    up_bias,
    down_weight,
    down_bias,
    norm2_gain,
    norm2_shift,
    cotangent,
):
    inputs = frames[0]
    local_ids = segment_ids[0]
    frame_count, model_width = inputs.shape
    cycle_size = lax.axis_size("seq")
    cycle_place = lax.axis_index("seq")
    every_id = lax.all_gather(segment_ids, "seq", axis=1, tiled=True)[0]
    head_shape = (frame_count, HEADS, HEAD_DIM)
    projected = jnp.dot(inputs, qkv_weight, preferred_element_type=jnp.float32)
    query_heads = (projected[:, :model_width] + query_bias).astype(jnp.bfloat16).reshape(head_shape)
    key_heads = projected[:, model_width : 2 * model_width].astype(jnp.bfloat16).reshape(head_shape)
    value_heads = (
        (projected[:, 2 * model_width :] + value_bias).astype(jnp.bfloat16).reshape(head_shape)
    )
    attended, log_total = forward_cycle(
        query_heads, key_heads, value_heads, local_ids, every_id, cycle_place, cycle_size
    )
    context = attended.astype(jnp.bfloat16).reshape(frame_count, model_width)
    resid_one = (
        inputs.astype(jnp.float32)
        + jnp.dot(context, out_weight, preferred_element_type=jnp.float32)
        + out_bias
    )
    hidden, normed_one, inverse_one = layer_norm(resid_one, norm1_gain, norm1_shift)
    hidden_low = hidden.astype(jnp.bfloat16)
    pre_act = jnp.dot(hidden_low, up_weight, preferred_element_type=jnp.float32) + up_bias
    act_low = jax.nn.gelu(pre_act, approximate=False).astype(jnp.bfloat16)
    resid_two = (
        hidden + jnp.dot(act_low, down_weight, preferred_element_type=jnp.float32) + down_bias
    )
    output, normed_two, inverse_two = layer_norm(resid_two, norm2_gain, norm2_shift)
    upstream = cotangent[0].astype(jnp.float32)
    second_grad, gain_two_grad, shift_two_grad = norm_back(
        upstream, normed_two, inverse_two, norm2_gain
    )
    second_low = second_grad.astype(jnp.bfloat16)
    down_grad = jnp.einsum("tf,td->fd", act_low, second_low, preferred_element_type=jnp.float32)
    pre_grad = jnp.einsum(
        "td,fd->tf", second_low, down_weight, preferred_element_type=jnp.float32
    ) * gelu_slope(pre_act)
    pre_low = pre_grad.astype(jnp.bfloat16)
    up_grad = jnp.einsum("td,tf->df", hidden_low, pre_low, preferred_element_type=jnp.float32)
    hidden_grad = second_grad + jnp.einsum(
        "tf,df->td", pre_low, up_weight, preferred_element_type=jnp.float32
    )
    first_grad, gain_one_grad, shift_one_grad = norm_back(
        hidden_grad, normed_one, inverse_one, norm1_gain
    )
    first_low = first_grad.astype(jnp.bfloat16)
    out_grad = jnp.einsum("td,te->de", context, first_low, preferred_element_type=jnp.float32)
    context_grad = (
        jnp.einsum("te,de->td", first_low, out_weight, preferred_element_type=jnp.float32)
        .astype(jnp.bfloat16)
        .reshape(head_shape)
    )
    row_delta = jnp.einsum("qhe,qhe->hq", context_grad.astype(jnp.float32), attended)
    query_grad, key_grad, value_grad = backward_cycle(
        query_heads,
        key_heads,
        value_heads,
        local_ids,
        every_id,
        context_grad,
        log_total,
        row_delta,
        cycle_place,
        cycle_size,
    )
    query_low = query_grad.astype(jnp.bfloat16).reshape(frame_count, model_width)
    key_low = key_grad.astype(jnp.bfloat16).reshape(frame_count, model_width)
    value_low = value_grad.astype(jnp.bfloat16).reshape(frame_count, model_width)
    proj_grad = jnp.concatenate([query_low, key_low, value_low], axis=1)
    qkv_grad = jnp.einsum("td,te->de", inputs, proj_grad, preferred_element_type=jnp.float32)
    input_grad = (
        jnp.einsum("te,de->td", proj_grad, qkv_weight, preferred_element_type=jnp.float32)
        + first_grad
    )
    summed = (
        lax.psum_scatter(qkv_grad, ("rows", "seq"), scatter_dimension=0, tiled=True),
        lax.psum_scatter(
            jnp.sum(query_low.astype(jnp.float32), axis=0),
            ("rows", "seq"),
            scatter_dimension=0,
            tiled=True,
        ),
        lax.psum_scatter(
            jnp.sum(value_low.astype(jnp.float32), axis=0),
            ("rows", "seq"),
            scatter_dimension=0,
            tiled=True,
        ),
        lax.psum_scatter(out_grad, ("rows", "seq"), scatter_dimension=0, tiled=True),
        lax.psum_scatter(
            jnp.sum(first_grad, axis=0), ("rows", "seq"), scatter_dimension=0, tiled=True
        ),
        lax.psum_scatter(gain_one_grad, ("rows", "seq"), scatter_dimension=0, tiled=True),
        lax.psum_scatter(shift_one_grad, ("rows", "seq"), scatter_dimension=0, tiled=True),
        lax.psum_scatter(up_grad, ("rows", "seq"), scatter_dimension=0, tiled=True),
        lax.psum_scatter(
            jnp.sum(pre_grad, axis=0), ("rows", "seq"), scatter_dimension=0, tiled=True
        ),
        lax.psum_scatter(down_grad, ("rows", "seq"), scatter_dimension=0, tiled=True),
        lax.psum_scatter(
            jnp.sum(second_grad, axis=0), ("rows", "seq"), scatter_dimension=0, tiled=True
        ),
        lax.psum_scatter(gain_two_grad, ("rows", "seq"), scatter_dimension=0, tiled=True),
        lax.psum_scatter(shift_two_grad, ("rows", "seq"), scatter_dimension=0, tiled=True),
    )
    return (
        output.astype(jnp.bfloat16)[None],
        input_grad[None],
        summed[0],
        summed[1],
        summed[2],
        summed[3],
        summed[4],
        summed[5],
        summed[6],
        summed[7],
        summed[8],
        summed[9],
        summed[10],
        summed[11],
        summed[12],
    )


HALF = HEAD_DIM
PAIRS = HEADS // 2
CONTRACT_LAST = (((1,), (1,)), ((), ()))
CONTRACT_INNER = (((1,), (0,)), ((), ()))
CONTRACT_FIRST = (((0,), (0,)), ((), ()))
IN_VMEM = pl.BlockSpec(memory_space=pltpu.VMEM)
IN_PLACE = pl.BlockSpec(memory_space=pl.ANY)
MESH_ID = pl.DeviceIdType.MESH
VMEM_BYTES = 60 << 20
BLOCKS = 16
PLANES = 4


def product(left, right, dims):
    return lax.dot_general(left, right, dims, preferred_element_type=jnp.float32)


def where_am_i():
    row = lax.axis_index("rows")
    place = lax.axis_index("seq")
    return row, place // 4, place // 2 % 2, place % 2


def meet(partners, count):
    barrier = pltpu.get_barrier_semaphore()
    for present, target in partners:

        def signal(target=target):
            pl.semaphore_signal(barrier, inc=1, device_id=target, device_id_type=MESH_ID)

        if present is None:
            signal()
        else:
            pl.when(present)(signal)
    pl.semaphore_wait(barrier, count)


class RowGather:
    UP, DOWN, ACROSS, BESIDE = range(4)

    def __init__(self, parts, line, crossing, sems):
        self.parts, self.line, self.crossing = parts, line, crossing
        self.recv_sem, self.beside_sem, self.line_sem, self.out_sem = sems
        self.row, self.z, self.x, self.c = where_am_i()
        self.has_up, self.has_down = self.z < PLANES - 1, self.z > 0
        self.far = (self.z + 2) % PLANES
        self.buffers = []
        for ref, _, _ in parts:
            if not any(ref is known for known in self.buffers):
                self.buffers.append(ref)

    def group(self, part):
        return [self.parts[part][0] is ref for ref in self.buffers].index(True)

    def device(self, z, x, c):
        return (self.row, z * 4 + x * 2 + c)

    def target(self, way):
        return (
            self.device(self.z + 1, self.x, self.c),
            self.device(self.z - 1, self.x, self.c),
            self.device(self.z, 1 - self.x, self.c),
            self.device(self.z, self.x, 1 - self.c),
        )[way]

    def copy(self, part, z, x, way):
        ref, first, rows = self.parts[part]
        piece = ref.at[z * 4 + x * 2 + self.c, pl.ds(first, rows)]
        beside = way == self.BESIDE
        return pltpu.make_async_remote_copy(
            src_ref=piece,
            dst_ref=piece,
            send_sem=self.out_sem.at[self.group(part)] if beside else self.line_sem.at[part, way],
            recv_sem=(
                self.beside_sem.at[self.group(part), z]
                if beside
                else self.recv_sem.at[part, z * 2 + x]
            ),
            device_id=self.target(way),
            device_id_type=MESH_ID,
        )

    def send(self, part, z, x, way):
        present = {self.UP: self.has_up, self.DOWN: self.has_down}.get(way)
        if present is None:
            self.copy(part, z, x, way).start()
        else:
            pl.when(present)(lambda: self.copy(part, z, x, way).start())

    def relay(self, part, z, x, ways, present=None):
        def both():
            self.copy(part, z, x, self.ACROSS).wait_recv()
            for way in ways:
                self.send(part, z, x, way)

        if present is None:
            both()
        else:
            pl.when(present)(both)

    def own(self):
        z, x = self.z, self.x
        for part in self.crossing:
            self.send(part, z, x, self.ACROSS)
        for part in self.line + self.crossing:
            self.send(part, z, x, self.UP)
            self.send(part, z, x, self.DOWN)
        for part in self.line:
            self.send(part, z, x, self.ACROSS)
        for part in self.crossing + self.line:
            self.send(part, z, x, self.BESIDE)

    def line_near(self):
        for part in self.line:
            self.relay(part, self.z - 1, self.x, (self.UP, self.ACROSS, self.BESIDE), self.has_down)
            self.relay(part, self.z + 1, self.x, (self.DOWN, self.ACROSS, self.BESIDE), self.has_up)

    def cross_over(self):
        for part in self.crossing:
            self.relay(part, self.z, 1 - self.x, (self.UP, self.DOWN, self.BESIDE))

    def cross_from(self, x):
        for part in self.crossing:
            self.relay(part, self.z - 1, x, (self.UP, self.BESIDE), self.has_down)
            self.relay(part, self.z + 1, x, (self.DOWN, self.BESIDE), self.has_up)

    def cross_near(self):
        self.cross_from(self.x)

    def cross_near_over(self):
        self.cross_from(1 - self.x)

    def line_over(self):
        for part in self.line:
            self.relay(part, self.z, 1 - self.x, (self.BESIDE,))

    def line_near_over(self):
        for part in self.line:
            self.relay(part, self.z - 1, 1 - self.x, (self.BESIDE,), self.has_down)
            self.relay(part, self.z + 1, 1 - self.x, (self.BESIDE,), self.has_up)

    def line_far(self):
        for part in self.line:
            self.relay(part, self.far, self.x, (self.ACROSS, self.BESIDE))

    def cross_far(self):
        for part in self.crossing:
            self.relay(part, self.far, self.x, (self.BESIDE,))

    def line_far_over(self):
        for part in self.line:
            self.relay(part, self.far, 1 - self.x, (self.BESIDE,))

    def cross_far_over(self):
        for part in self.crossing:
            self.relay(part, self.far, 1 - self.x, (self.BESIDE,))

    def plane_done(self, z, present=None):
        def wait():
            for i, ref in enumerate(self.buffers):
                both = ref.at[pl.ds(0, 2)]
                pltpu.make_async_remote_copy(
                    src_ref=both,
                    dst_ref=both,
                    send_sem=self.out_sem.at[i],
                    recv_sem=self.beside_sem.at[i, z],
                    device_id=self.target(self.BESIDE),
                    device_id_type=MESH_ID,
                ).wait_recv()

        if present is None:
            wait()
        else:
            pl.when(present)(wait)

    def left(self, sem, ref, count, first, rows):
        sent = ref.at[pl.ds(0, count), pl.ds(first, rows)]
        pltpu.make_async_remote_copy(
            src_ref=sent,
            dst_ref=sent,
            send_sem=sem,
            recv_sem=self.beside_sem.at[0, 0],
            device_id=self.target(self.BESIDE),
            device_id_type=MESH_ID,
        ).wait_send()

    def finish(self):
        def settle(ways, hops, planes):
            for part, (ref, first, rows) in enumerate(self.parts):
                wide = 1 if part in self.line else 2
                for way in ways:
                    self.left(self.line_sem.at[part, way], ref, wide * hops, first, rows)
                across = planes if part in self.line else 1
                self.left(self.line_sem.at[part, self.ACROSS], ref, across, first, rows)
            for i, ref in enumerate(self.buffers):
                self.left(self.out_sem.at[i], ref, 2 * planes, 0, ref.shape[1])

        pl.when(self.has_up & self.has_down)(lambda: settle((self.UP, self.DOWN), 2, 4))
        pl.when(jnp.logical_not(self.has_down))(lambda: settle((self.UP,), 1, 3))
        pl.when(jnp.logical_not(self.has_up))(lambda: settle((self.DOWN,), 1, 3))


def gather_sems(parts, groups):
    dma = pltpu.SemaphoreType.DMA
    return [dma((parts, 2 * PLANES)), dma((groups, PLANES)), dma((parts, 3)), dma((groups,))]


class VectorSum:
    STAGES = 5

    def __init__(self, ref, partial, arrived, send_sem, recv_sem):
        self.ref, self.partial, self.arrived = ref, partial, arrived
        self.send_sem, self.recv_sem = send_sem, recv_sem
        self.y, self.z, self.x, self.c = where_am_i()

    def copy(self, stage):
        y, z, x, c = self.y, self.z, self.x, self.c
        core, row, across, near, far = (
            (y, z, x, 1 - c),
            (1 - y, z, x, c),
            (y, z, 1 - x, c),
            (y, z + 1 - 2 * (z % 2), x, c),
            (y, (z + 2) % PLANES, x, c),
        )
        y, z, x, c = (core, row, across, near, far)[stage]
        return pltpu.make_async_remote_copy(
            src_ref=self.ref if stage == 0 else self.partial.at[stage - 1],
            dst_ref=self.arrived.at[stage],
            send_sem=self.send_sem.at[stage],
            recv_sem=self.recv_sem.at[stage],
            device_id=(y, z * 4 + x * 2 + c),
            device_id_type=MESH_ID,
        )

    def step(self, stage):
        if stage > 0:
            self.copy(stage - 1).wait_recv()
            before = self.ref[...] if stage == 1 else self.partial[stage - 2]
            self.partial[stage - 1] = before + self.arrived[stage - 1]
        if stage < self.STAGES:
            self.copy(stage).start()

    def finish(self):
        for stage in range(self.STAGES):
            self.copy(stage).wait_send()

    def own_share(self, rows, share):
        width = self.ref.shape[1]
        place = self.y * 16 + self.z * 4 + self.x * 2 + self.c
        per_row = width // share
        offset = place % per_row * share
        row_index = lax.broadcasted_iota(jnp.int32, (width, 128), 0)
        column_index = lax.broadcasted_iota(jnp.int32, (width, 128), 1)
        picked = jnp.where(
            (row_index == column_index + offset) & (column_index < share), 1.0, 0.0
        ).astype(jnp.bfloat16)
        rest = rows
        total = jnp.zeros((rows.shape[0], 128), jnp.float32)
        for _ in range(3):
            piece = rest.astype(jnp.bfloat16)
            total = total + product(piece, picked, CONTRACT_INNER)
            rest = rest - piece.astype(jnp.float32)
        return total, place // per_row


STEP = 384
KEY_STEPS = (384, 256, 128)
UNROLL = 6
CHUNK = 768


class CubeSum:
    STAGES = 3

    def __init__(self, partial, cube, line, send_sem, recv_sem):
        self.partial, self.cube, self.line = partial, cube, line
        self.send_sem, self.recv_sem = send_sem, recv_sem
        self.y, self.z, self.x, self.c = where_am_i()
        self.member = self.y * 4 + self.x * 2 + self.c

    def link(self, source, target, stage, device):
        return pltpu.make_async_remote_copy(
            src_ref=source,
            dst_ref=target,
            send_sem=self.send_sem.at[stage],
            recv_sem=self.recv_sem.at[stage],
            device_id=device,
            device_id_type=MESH_ID,
        )

    def others(self):
        for step in range(1, 8):
            other = (self.member + step) % 8
            yield (other // 4, self.z * 4 + other % 4)

    def copy(self, stage):
        beside = self.z + 1 - 2 * (self.z % 2) if stage == 1 else (self.z + 2) % PLANES
        return self.link(
            self.partial.at[stage - 1], self.line.at[stage - 1], stage,
            (self.y, beside * 4 + self.x * 2 + self.c),
        )

    def seven(self):
        seven = self.cube.at[pl.ds(0, 7)]
        return self.link(seven, seven, 0, (self.y, self.z * 4 + self.x * 2 + 1 - self.c))

    def step(self, stage):
        if stage == 0:
            own = self.cube.at[self.member]
            for device in self.others():
                self.link(own, own, 0, device).start()
            return
        if stage == 1:
            self.seven().wait_recv()
            self.partial[0] = jnp.sum(self.cube[...], axis=0)
        else:
            self.copy(stage - 1).wait_recv()
            self.partial[stage - 1] = self.partial[stage - 2] + self.line[stage - 2]
        if stage < self.STAGES:
            self.copy(stage).start()

    def finish(self):
        self.seven().wait_send()
        for stage in range(1, self.STAGES):
            self.copy(stage).wait_send()


class Quad:
    def __init__(self, by_x):
        self.by_x = by_x
        self.y, self.z, self.x, self.c = where_am_i()
        self.a, self.b = (self.x, self.y) if by_x else (self.y, self.x)
        self.mine = self.a * 2 + self.c
        self.peer = (1 - self.a) * 2 + self.c
        self.beside = self.a * 2 + 1 - self.c
        self.corner = (1 - self.a) * 2 + 1 - self.c

    def device(self, a, b, z, c):
        y, x = (b, a) if self.by_x else (a, b)
        return (y, z * 4 + x * 2 + c)

    def at_peer(self):
        return self.device(1 - self.a, self.b, self.z, self.c)

    def at_beside(self):
        return self.device(self.a, self.b, self.z, 1 - self.c)

    def at_corner(self):
        return self.device(1 - self.a, self.b, self.z, 1 - self.c)

    def link(self, source, target, send_sem, recv_sem, device):
        return pltpu.make_async_remote_copy(
            src_ref=source,
            dst_ref=target,
            send_sem=send_sem,
            recv_sem=recv_sem,
            device_id=device,
            device_id_type=MESH_ID,
        )

    def count(self, ref, send_sem, recv_sem):
        return self.link(ref, ref, send_sem, recv_sem, self.at_beside())


class Shared:
    def __init__(self, left, by_x, buffers):
        self.left = left
        self.held, self.send_sem, self.recv_sem = buffers
        self.quad = Quad(by_x)
        self.width = self.held.shape[2]

    def part(self, a):
        if self.quad.by_x:
            return self.left
        return self.left.at[:, pl.ds(pl.multiple_of(a * self.width, 128), self.width)]

    def share(self):
        q = self.quad
        slot = self.held.at[q.mine]
        send = self.send_sem.at[0]
        q.link(self.part(1 - q.a), slot, send, self.recv_sem.at[0], q.at_peer()).start()
        q.link(self.part(q.a), slot, send, self.recv_sem.at[1], q.at_beside()).start()
        self.held[q.mine] = self.part(q.a)[...]

    def relay(self):
        q = self.quad
        slot = self.held.at[q.peer]
        q.count(slot, self.send_sem.at[0], self.recv_sem.at[0]).wait_recv()
        q.link(slot, slot, self.send_sem.at[0], self.recv_sem.at[1], q.at_beside()).start()

    def complete(self):
        two = self.held.at[pl.ds(0, 2)]
        self.quad.count(two, self.send_sem.at[0], self.recv_sem.at[1]).wait_recv()

    def finish(self):
        three = self.held.at[pl.ds(0, 3)]
        self.quad.count(three, self.send_sem.at[0], self.recv_sem.at[1]).wait_send()


class Piece:
    def __init__(self, shared, right, base, stride, out, buffers):
        self.shared, self.right, self.base, self.stride, self.out = shared, right, base, stride, out
        self.rights, self.whole, self.b_in, self.z_in, self.last, self.send_sem, self.recv_sem = buffers
        self.wide = self.rights.shape[2]
        self.quad = shared.quad
        self.share_rows = out.shape[0]

    def columns(self, member):
        place = member if self.quad.by_x else member % 2
        return pl.ds(pl.multiple_of(self.base + place * self.stride, 128), self.wide)

    def give(self, member, device):
        self.quad.link(
            self.right.at[:, self.columns(member)], self.rights.at[self.quad.mine],
            self.send_sem.at[0], self.recv_sem.at[0], device,
        ).start()

    def share(self):
        q = self.quad
        self.give(q.peer, q.at_peer())
        self.give(q.corner, q.at_corner())
        self.give(q.beside, q.at_beside())
        self.rights[q.mine] = self.right[:, self.columns(q.mine)]

    def slab(self, b):
        return self.whole.at[b] if self.quad.by_x else self.whole.at[:, b]

    def cell(self, z):
        b = self.quad.b
        return self.whole.at[b, z] if self.quad.by_x else self.whole.at[z, b]

    def multiply(self):
        q = self.quad
        three = self.rights.at[pl.ds(0, 3)]
        q.count(three, self.send_sem.at[0], self.recv_sem.at[0]).wait_recv()
        held = self.shared.held
        tokens = held.shape[0] * held.shape[1]
        right = self.rights[...].reshape(tokens, self.wide)
        if self.shared.width > STEP:

            def one(i, carry):
                left = held[:, :, pl.ds(pl.multiple_of(i * STEP, 128), STEP)]
                part = product(left.reshape(tokens, STEP), right, CONTRACT_FIRST)
                self.whole[i] = part.astype(jnp.bfloat16).reshape(self.whole.shape[1:])
                return carry

            lax.fori_loop(0, self.shared.width // STEP, one, 0)
        else:
            part = product(held[...].reshape(tokens, STEP), right, CONTRACT_FIRST)
            self.whole[...] = part.astype(jnp.bfloat16).reshape(self.whole.shape)
        q.link(
            self.slab(1 - q.b), self.b_in, self.send_sem.at[1], self.recv_sem.at[1],
            q.device(q.a, 1 - q.b, q.z, q.c),
        ).start()

    def spread(self):
        q = self.quad
        q.count(self.b_in, self.send_sem.at[1], self.recv_sem.at[1]).wait_recv()
        slab = self.slab(q.b)
        slab[...] = (slab[...].astype(jnp.float32) + self.b_in[...].astype(jnp.float32)).astype(
            jnp.bfloat16
        )
        q.count(self.rights.at[pl.ds(0, 3)], self.send_sem.at[0], self.recv_sem.at[0]).wait_send()
        inner = self.inner()

        @pl.when(inner)
        def _():
            self.to_plane(self.cell(self.end()), 0, 1, self.end())

        @pl.when(jnp.logical_not(inner))
        def _():
            first = 1 - q.z // (PLANES - 1)
            three = pl.ds(first, 3)
            cells = self.whole.at[q.b, three] if q.by_x else self.whole.at[three, q.b]
            self.to_plane(cells, pl.ds(0, 3), 0, 1 + q.z // 2)

    def inner(self):
        return (self.quad.z > 0) & (self.quad.z < PLANES - 1)

    def end(self):
        return self.quad.z // 2 * (PLANES - 1)

    def to_plane(self, source, slot, which, z):
        q = self.quad
        q.link(
            source, self.z_in.at[slot], self.send_sem.at[0], self.recv_sem.at[2 + which],
            q.device(q.a, q.b, z, q.c),
        ).start()

    def fold(self):
        q = self.quad

        @pl.when(self.inner())
        def _():
            three = self.z_in.at[pl.ds(0, 3)]
            q.count(three, self.send_sem.at[0], self.recv_sem.at[2]).wait_recv()
            first = 2 - q.z
            for target in (PLANES - 1 - self.end(), PLANES - 1 - q.z):
                cell = self.cell(target)
                cell[...] = (
                    cell[...].astype(jnp.float32) + self.z_in[target - first].astype(jnp.float32)
                ).astype(jnp.bfloat16)
                self.to_plane(cell, 3, 1, target)

    def rows_of(self, member):
        place = member if self.quad.by_x else member % 2
        return self.last.at[pl.ds(pl.multiple_of(place * self.share_rows, 8), self.share_rows)]

    def collect(self):
        q = self.quad
        inner = self.inner()

        def arrived(count):
            some = self.z_in.at[pl.ds(0, count)]
            q.count(some, self.send_sem.at[0], self.recv_sem.at[3]).wait_recv()

        pl.when(inner)(lambda: arrived(1))
        pl.when(jnp.logical_not(inner))(lambda: arrived(2))
        beside = q.z // 2 * 2 * (1 - q.z // (PLANES - 1))
        self.last[...] = (
            self.cell(q.z)[...].astype(jnp.float32)
            + self.z_in[beside].astype(jnp.float32)
            + self.z_in[3].astype(jnp.float32)
        )
        q.count(self.b_in, self.send_sem.at[1], self.recv_sem.at[1]).wait_send()
        columns = self.out.at[:, self.columns(q.mine)]
        partners = [(q.beside, q.at_beside())]
        if q.by_x:
            partners = [(q.peer, q.at_peer()), (q.corner, q.at_corner())] + partners
        for member, device in partners:
            q.link(
                self.rows_of(member), columns, self.send_sem.at[1], self.recv_sem.at[4], device
            ).start()
        columns[...] = self.rows_of(q.mine)[...]

    def finish(self):
        q = self.quad
        others = self.last.at[pl.ds(0, (3 if q.by_x else 1) * self.share_rows)]
        q.count(others, self.send_sem.at[1], self.recv_sem.at[4]).wait()
        three = self.z_in.at[pl.ds(0, 3)]
        q.count(three, self.send_sem.at[0], self.recv_sem.at[2]).wait_send()


def shared_scratch(frame_count, left_width, by_x):
    return [
        pltpu.VMEM((4, frame_count, left_width if by_x else left_width // 2), jnp.bfloat16),
        pltpu.SemaphoreType.DMA((1,)),
        pltpu.SemaphoreType.DMA((2,)),
    ]


def piece_scratch(frame_count, left_width, by_x, wide=STEP):
    rows = left_width // (2 * PLANES) if by_x else left_width // (4 * PLANES)
    low = jnp.bfloat16
    return [
        pltpu.VMEM((4, frame_count, wide), low),
        pltpu.VMEM((2, PLANES, rows, wide) if by_x else (PLANES, 2, rows, wide), low),
        pltpu.VMEM((PLANES, rows, wide), low),
        pltpu.VMEM((PLANES, rows, wide), low),
        pltpu.VMEM((rows, wide), jnp.float32),
        pltpu.SemaphoreType.DMA((2,)),
        pltpu.SemaphoreType.DMA((5,)),
    ]


def cube_scratch(width):
    return [
        pltpu.VMEM((CubeSum.STAGES, 1, width), jnp.float32),
        pltpu.VMEM((8, 1, width), jnp.float32),
        pltpu.VMEM((CubeSum.STAGES - 1, 1, width), jnp.float32),
        pltpu.SemaphoreType.DMA((CubeSum.STAGES,)),
        pltpu.SemaphoreType.DMA((CubeSum.STAGES,)),
    ]


def vector_scratch(rows, width):
    wide = jnp.float32
    return [
        pltpu.VMEM((rows, width), wide),
        pltpu.VMEM((VectorSum.STAGES, rows, width), wide),
        pltpu.VMEM((VectorSum.STAGES, rows, width), wide),
        pltpu.SemaphoreType.DMA((VectorSum.STAGES,)),
        pltpu.SemaphoreType.DMA((VectorSum.STAGES,)),
    ]


def layer_scratch(frame_count, width, inner):
    low, wide = jnp.bfloat16, jnp.float32
    dma = pltpu.SemaphoreType.DMA
    return dict(
        qkv_held=pltpu.VMEM((width, 3 * width), low),
        out_held=pltpu.VMEM((width, width), low),
        up_held=pltpu.VMEM((width, inner), low),
        down_held=pltpu.VMEM((inner, width), low),
        weight_sem=dma((4,)),
        block=pltpu.VMEM((BLOCKS, frame_count + 16, width), low),
        block_sems=gather_sems(2, 1),
        grad_block=pltpu.VMEM((BLOCKS, frame_count, width), low),
        stats=pltpu.VMEM((BLOCKS, 32, frame_count), wide),
        grad_sems=gather_sems(3, 2),
        projected=pltpu.VMEM((BLOCKS, frame_count, 3 * width), low),
        mask=pltpu.VMEM((frame_count, BLOCKS * frame_count), wide),
        attended=pltpu.VMEM((frame_count, width), wide),
        slope=pltpu.VMEM((frame_count, inner), wide),
        logs=pltpu.VMEM((frame_count, 128), wide),
        delta=pltpu.VMEM((frame_count, 128), wide),
        inner_bias=pltpu.VMEM((1, inner), wide),
        proj_bias=pltpu.VMEM((1, 3 * width), wide),
        act=pltpu.VMEM((frame_count, inner), low),
        pre_low=pltpu.VMEM((frame_count, inner), low),
        context=pltpu.VMEM((frame_count, width), low),
        hidden_low=pltpu.VMEM((frame_count, width), low),
        second_low=pltpu.VMEM((frame_count, width), low),
        first_low=pltpu.VMEM((frame_count, width), low),
        normed=pltpu.VMEM((frame_count, width), wide),
        running=pltpu.VMEM((frame_count, width), wide),
        first_grad=pltpu.VMEM((frame_count, width), wide),
        proj_grad=pltpu.VMEM((frame_count, 3 * width), low),
        early=vector_scratch(16, width),
        late=cube_scratch(width),
        down_left=shared_scratch(frame_count, inner, False),
        up_left=shared_scratch(frame_count, width, True),
        out_left=shared_scratch(frame_count, width, False),
        qkv_left=shared_scratch(frame_count, width, False),
        down_piece=piece_scratch(frame_count, inner, False),
        up_pieces=[piece_scratch(frame_count, width, True) for _ in range(2)],
        out_piece=piece_scratch(frame_count, width, False),
        query_piece=piece_scratch(frame_count, width, False),
        key_pieces=[
            piece_scratch(frame_count, width, False, step) for step in KEY_STEPS
        ],
    )


class Inputs(typing.NamedTuple):
    frames: typing.Any
    segment_ids: typing.Any
    qkv_weight: typing.Any
    query_bias: typing.Any
    value_bias: typing.Any
    out_weight: typing.Any
    out_bias: typing.Any
    norm1_gain: typing.Any
    norm1_shift: typing.Any
    up_weight: typing.Any
    up_bias: typing.Any
    down_weight: typing.Any
    down_bias: typing.Any
    norm2_gain: typing.Any
    norm2_shift: typing.Any
    cotangent: typing.Any


class Outputs(typing.NamedTuple):
    layer_out: typing.Any
    input_grad: typing.Any
    qkv_g: typing.Any
    query_g: typing.Any
    value_g: typing.Any
    out_g: typing.Any
    outbias_g: typing.Any
    gain1_g: typing.Any
    shift1_g: typing.Any
    up_g: typing.Any
    upbias_g: typing.Any
    down_g: typing.Any
    downbias_g: typing.Any
    gain2_g: typing.Any
    shift2_g: typing.Any


class Refs:
    def __init__(self, *groups):
        for group in groups:
            for name, ref in group.items():
                setattr(self, name, ref)


def layer_kernel(held, *refs):
    inputs, outputs = len(Inputs._fields), len(Outputs._fields)
    scratch = jax.tree.unflatten(held, refs[inputs + outputs :])
    k = Refs(dict(zip(Inputs._fields + Outputs._fields, refs)), scratch)
    frame_count, width = k.frames.shape
    inner = k.inner_bias.shape[1]
    low, wide = jnp.bfloat16, jnp.float32
    total = BLOCKS * frame_count
    row, z, x, c = where_am_i()
    mine = z * 4 + x * 2 + c
    has_up, has_down = z < PLANES - 1, z > 0
    far = (z + 2) % PLANES
    lost = PLANES - 1 - z
    lane = lax.broadcasted_iota(jnp.int32, (frame_count, 128), 1)

    def fetch(i):
        source, target = (
            (k.qkv_weight, k.qkv_held),
            (k.out_weight, k.out_held),
            (k.up_weight, k.up_held),
            (k.down_weight, k.down_held),
        )[i]
        return pltpu.make_async_copy(source, target, k.weight_sem.at[i])

    for i in range(4):
        fetch(i).start()

    line_rows = frame_count * 80 // 128
    back_rows = frame_count * 64 // 128
    link = RowGather(
        [
            (k.block, 0, line_rows),
            (k.block, line_rows, k.block.shape[1] - line_rows),
        ],
        (0,),
        (1,),
        k.block_sems,
    )
    back = RowGather(
        [
            (k.grad_block, 0, back_rows),
            (k.grad_block, back_rows, frame_count - back_rows),
            (k.stats, 0, 32),
        ],
        (2, 0),
        (1,),
        k.grad_sems,
    )
    down_left = Shared(k.act, False, k.down_left)
    up_left = Shared(k.hidden_low, True, k.up_left)
    out_left = Shared(k.context, False, k.out_left)
    qkv_left = Shared(k.frames, False, k.qkv_left)
    half_width = width // 2
    down = Piece(down_left, k.second_low, 0, half_width, k.down_g, k.down_piece)
    ups = [
        Piece(up_left, k.pre_low, p * STEP, width, k.up_g, k.up_pieces[p]) for p in range(2)
    ]
    out = Piece(out_left, k.first_low, 0, half_width, k.out_g, k.out_piece)
    query = Piece(qkv_left, k.proj_grad, 0, half_width, k.qkv_g, k.query_piece)
    keys = [
        Piece(qkv_left, k.proj_grad, width + sum(KEY_STEPS[:i]), width, k.qkv_g, buffers)
        for i, buffers in enumerate(k.key_pieces)
    ]
    early, late = VectorSum(*k.early), CubeSum(*k.late)

    places = [(row, z, x, 1 - c), (1 - row, z, x, c), (1 - row, z, x, 1 - c)]
    places += [(row, z, 1 - x, c), (row, z, 1 - x, 1 - c)]
    places += [(1 - row, z, 1 - x, c), (1 - row, z, 1 - x, 1 - c)]
    places += [(row, (z + 2) % PLANES, x, c), (row, z + 1 - 2 * (z % 2), x, c)]
    partners = [(None, (y, at * 4 + across * 2 + core)) for y, at, across, core in places]
    middle = has_up & has_down
    partners.append((middle, (row, (PLANES - 1 - z) * 4 + x * 2 + c)))
    meet(partners, len(places) + middle.astype(jnp.int32))

    own_ids = jnp.broadcast_to(k.segment_ids[...], (frame_count, frame_count)).astype(wide)
    ids_column = own_ids.T
    k.block[mine, pl.ds(0, frame_count), :] = k.frames[...]
    k.block[mine, pl.ds(frame_count, 16), pl.ds(0, frame_count)] = own_ids[:16].astype(low)
    link.own()
    link.cross_over()
    link.line_near()
    k.inner_bias[...] = k.up_bias[...].reshape(1, inner)
    query_bias = k.query_bias[...].reshape(1, width)
    k.proj_bias[...] = jnp.concatenate(
        [query_bias, jnp.zeros((1, width), wide), k.value_bias[...].reshape(1, width)], axis=1
    )

    def plane_rows(plane):
        return jnp.concatenate(
            [k.block[plane * 4 + i, pl.ds(0, frame_count), :] for i in range(4)], axis=0
        )

    def project_columns(plane, first, count):
        def some(i, carry):
            columns = pl.ds(pl.multiple_of(first + i * CHUNK, 128), CHUNK)
            part = product(plane_rows(plane), k.qkv_held[:, columns], CONTRACT_INNER)
            part = (part + k.proj_bias[:, columns]).astype(low)
            if first == 0:
                part = part * HEAD_DIM**-0.5
            for b in range(4):
                k.projected[plane * 4 + b, :, columns] = part[
                    b * frame_count : (b + 1) * frame_count
                ]
            return carry

        lax.fori_loop(0, count // CHUNK, some, 0)

    def as_query(part):
        return (part + query_bias).astype(low) * HEAD_DIM**-0.5

    def project(plane):
        project_columns(plane, width, 2 * width)
        for i in range(4):
            ids = k.block[plane * 4 + i, pl.ds(frame_count, 8), pl.ds(0, frame_count)]
            same = jnp.broadcast_to(ids.astype(wide)[:1], own_ids.shape) == ids_column
            at = pl.multiple_of((plane * 4 + i) * frame_count, 128)
            k.mask[:, pl.ds(at, frame_count)] = jnp.where(same, 0.0, mask_fill)

    def project_queries(plane):
        project_columns(plane, 0, width)

    def queries_own_far():
        project_queries(z)
        project_queries(far)

    def queries_near():
        pl.when(has_down)(lambda: project_queries(z - 1))
        pl.when(has_up)(lambda: project_queries(z + 1))

    def planes_done():
        back.plane_done(z)
        back.plane_done(z - 1, has_down)
        back.plane_done(z + 1, has_up)
        back.plane_done(far)

    def input_gradient():
        k.input_grad[...] = k.first_grad[...] + product(
            k.proj_grad[...], k.qkv_held[...], CONTRACT_LAST
        )

    def query_note():
        note(early, 6, k.proj_grad[:, pl.ds(0, width)].astype(wide))

    def late_notes():
        values = k.proj_grad[:, pl.ds(2 * width, width)].astype(wide)
        late.cube[late.member] = jnp.sum(values, axis=0, keepdims=True)

    def small_shares():
        share = k.query_g.shape[0]
        first = early.partial[VectorSum.STAGES - 1]
        shares, _ = early.own_share(first[:8], share)
        k.query_g[...] = shares[6, :share]
        last = jnp.broadcast_to(late.partial[CubeSum.STAGES - 1], (8, width))
        k.value_g[...] = early.own_share(last, share)[0][0, :share]
        for i, ref in enumerate(
            (k.outbias_g, k.gain1_g, k.shift1_g, k.downbias_g, k.gain2_g, k.shift2_g)
        ):
            ref[...] = shares[i, :share]
        up_shares, at = early.own_share(first[8:], 4 * share)
        keep = lax.broadcasted_iota(jnp.int32, up_shares.shape, 0) == at
        picked = jnp.sum(jnp.where(keep, up_shares, 0.0), axis=0, keepdims=True)
        k.upbias_g[...] = picked[0, : 4 * share]

    def note(vector, index, values):
        vector.ref[pl.ds(index, 1), :] = jnp.sum(values, axis=0, keepdims=True)

    def flat(ref):
        return ref[...].reshape(1, width)

    def columns_of(third, j):
        return pl.ds(pl.multiple_of(third * width + j * 128, 128), 128)

    def head_state(h):
        return pl.ds(pl.multiple_of(h * 128, 128), 128)

    def both_heads(values):
        nothing = jnp.zeros_like(values)
        return jnp.concatenate(
            [jnp.where(lane < HALF, values, nothing), jnp.where(lane < HALF, nothing, values)],
            axis=0,
        )

    def own_halves(values):
        return jnp.where(lane < HALF, values[:frame_count], values[frame_count:])

    def attend(plane, first):
        at = pl.multiple_of(plane * 4 * frame_count, 128)

        def state(kind, j):
            return k.slope.at[:, pl.ds(pl.multiple_of((kind * HEADS + 2 * j) * 128, 128), 256)]

        def read(kind, j):
            pair_state = state(kind, j)[...]
            return jnp.concatenate([pair_state[:, :128], pair_state[:, 128:]], axis=0)

        def write(kind, j, values):
            state(kind, j)[...] = jnp.concatenate(
                [values[:frame_count], values[frame_count:]], axis=1
            )

        def pair(j, carry):
            query = both_heads(k.projected[mine, :, columns_of(0, j)])
            keys = k.projected[pl.ds(plane * 4, 4), :, columns_of(1, j)].reshape(-1, 128)
            values = k.projected[pl.ds(plane * 4, 4), :, columns_of(2, j)].reshape(-1, 128)
            mask = k.mask[:, pl.ds(at, 4 * frame_count)]
            scores = product(query, keys, CONTRACT_LAST) + jnp.concatenate([mask, mask], axis=0)
            tile = (2 * frame_count, 128)
            peak = jnp.broadcast_to(jnp.max(scores, axis=1, keepdims=True), tile)
            if not first:
                old = read(0, j)
                peak = jnp.maximum(peak, old)
                factor = jnp.exp(old - peak)
            weights = jnp.exp(scores - jnp.concatenate([peak] * 4, axis=1))
            whole = jnp.broadcast_to(jnp.sum(weights, axis=1, keepdims=True), tile)
            if not first:
                whole = whole + read(1, j) * factor
            write(0, j, peak)
            write(1, j, whole)
            both = own_halves(product(weights.astype(low), values, CONTRACT_INNER))
            if not first:
                both = both + k.attended[:, columns_of(0, j)] * own_halves(factor)
            k.attended[:, columns_of(0, j)] = both
            return carry

        lax.fori_loop(0, PAIRS, pair, 0, unroll=2 if first else UNROLL)

    def own_queries():
        fetch(0).wait()
        own = product(k.frames[...], k.qkv_held[:, pl.ds(0, width)], CONTRACT_INNER)
        k.projected[mine, :, pl.ds(0, width)] = as_query(own)

    def take_plane(plane, present=None):
        def take():
            link.plane_done(plane)
            project(plane)

        if present is None:
            take()
        else:
            pl.when(present)(take)

    def attend_near(plane, present):
        pl.when(present)(lambda: attend(plane, False))

    own_queries()
    link.line_over()
    take_plane(z)
    link.cross_near_over()
    link.cross_near()
    link.line_near_over()
    link.line_far()
    qkv_left.share()
    attend(z, True)
    take_plane(z - 1, has_down)
    take_plane(z + 1, has_up)
    link.line_far_over()
    link.cross_far()
    link.cross_far_over()
    attend_near(z + 1, has_up)
    attend_near(z - 1, has_down)
    take_plane(far)
    attend(far, False)
    logs = jnp.zeros(lane.shape, wide)
    for j in range(PAIRS):
        parts = []
        for h in range(2):
            whole = k.slope[:, head_state(HEADS + 2 * j + h)]
            logs = jnp.where(
                lane == 2 * j + h, k.slope[:, head_state(2 * j + h)] + jnp.log(whole), logs
            )
            parts.append(whole)
        done = k.attended[:, columns_of(0, j)] / jnp.where(lane < HALF, parts[0], parts[1])
        k.attended[:, columns_of(0, j)] = done
        k.context[:, columns_of(0, j)] = done.astype(low)
    k.logs[...] = logs

    def normalize(resid):
        centred = resid - jnp.mean(resid, axis=-1, keepdims=True)
        inverse = lax.rsqrt(jnp.mean(centred * centred, axis=-1, keepdims=True) + norm_eps)
        return centred * inverse, inverse

    def normalize_back(upstream, normed, inverse, gain):
        scaled = upstream * gain
        first_mean = jnp.mean(scaled, axis=-1, keepdims=True)
        second_mean = jnp.mean(scaled * normed, axis=-1, keepdims=True)
        return inverse * (scaled - first_mean - normed * second_mean)

    early.ref[...] = jnp.zeros((16, width), wide)
    fetch(1).wait()
    resid_one = (
        k.frames[...].astype(wide)
        + product(k.context[...], k.out_held[...], CONTRACT_INNER)
        + flat(k.out_bias)
    )
    normed_one, inverse_one = normalize(resid_one)
    k.normed[...] = normed_one
    hidden = normed_one * flat(k.norm1_gain) + flat(k.norm1_shift)
    k.hidden_low[...] = hidden.astype(low)
    up_left.share()
    k.running[...] = hidden + flat(k.down_bias)
    fetch(2).wait()
    fetch(3).wait()

    def forward(f, carry):
        columns = pl.ds(pl.multiple_of(f * width, 128), width)
        pre_act = (
            product(k.hidden_low[...], k.up_held[:, columns], CONTRACT_INNER)
            + k.inner_bias[:, columns]
        )
        normal_cdf = 0.5 * (1.0 + lax.erf(pre_act * 0.5**0.5))
        normal_pdf = jnp.exp(-0.5 * pre_act * pre_act) * (2.0 * math.pi) ** (-0.5)
        act = (pre_act * normal_cdf).astype(low)
        k.act[:, columns] = act
        k.slope[:, columns] = normal_cdf + pre_act * normal_pdf
        k.running[...] += product(
            act, k.down_held[pl.ds(pl.multiple_of(f * width, 128), width), :], CONTRACT_INNER
        )
        return carry

    lax.fori_loop(0, inner // width, forward, 0)
    down_left.share()
    out_left.share()
    normed_two, inverse_two = normalize(k.running[...])
    k.layer_out[...] = (normed_two * flat(k.norm2_gain) + flat(k.norm2_shift)).astype(low)
    upstream = k.cotangent[...].astype(wide)
    second_grad = normalize_back(upstream, normed_two, inverse_two, flat(k.norm2_gain))
    k.second_low[...] = second_grad.astype(low)
    note(early, 3, second_grad)
    note(early, 4, upstream * normed_two)
    note(early, 5, upstream)
    k.running[...] = second_grad

    def backward(p):
        for member in range(4):
            first = member * width + p * STEP
            columns = pl.ds(first, STEP)
            pre_grad = (
                product(k.second_low[...], k.down_held[columns, :], CONTRACT_LAST)
                * k.slope[:, columns]
            )
            early.ref[pl.ds(8 + member, 1), pl.ds(p * STEP, STEP)] = jnp.sum(
                pre_grad, axis=0, keepdims=True
            )
            k.pre_low[:, columns] = pre_grad.astype(low)
            k.running[...] += product(
                k.pre_low[:, columns], k.up_held[:, columns], CONTRACT_LAST
            )

    backward(0)
    ups[0].share()
    up_left.relay()
    backward(1)
    hidden_grad = k.running[...]
    normed_one = k.normed[...]
    first_grad = normalize_back(hidden_grad, normed_one, inverse_one, flat(k.norm1_gain))
    k.first_grad[...] = first_grad
    k.first_low[...] = first_grad.astype(low)
    note(early, 0, first_grad)
    note(early, 1, hidden_grad * normed_one)
    note(early, 2, hidden_grad)
    context_grad = product(k.first_low[...], k.out_held[...], CONTRACT_LAST).astype(low)
    k.grad_block[mine] = context_grad
    delta = jnp.zeros(lane.shape, wide)
    for j in range(PAIRS):
        columns = slice(j * 128, (j + 1) * 128)
        both = context_grad[:, columns].astype(wide) * k.attended[:, columns]
        for h in range(2):
            one = jnp.sum(
                jnp.where((lane < HALF) == (h == 0), both, 0.0), axis=1, keepdims=True
            )
            delta = jnp.where(lane == 2 * j + h, one, delta)
    k.delta[...] = delta
    k.stats[mine, pl.ds(0, 16), :] = k.logs[...].T[:16]
    k.stats[mine, pl.ds(16, 16), :] = delta.T[:16]
    down.share()
    back.own()

    @pl.when(jnp.logical_not(middle))
    def _():
        for i in range(4):
            k.projected[lost * 4 + i] = jnp.zeros((frame_count, 3 * width), low)
            k.grad_block[lost * 4 + i] = jnp.zeros((frame_count, width), low)
            k.stats[lost * 4 + i] = jnp.zeros((32, frame_count), wide)
            at = pl.multiple_of((lost * 4 + i) * frame_count, 128)
            k.mask[:, pl.ds(at, frame_count)] = jnp.full(lane.shape, mask_fill, wide)

    def query_pair(j):
        query = k.projected[mine, :, columns_of(0, j)]
        upstream = k.grad_block[mine, :, columns_of(0, j)]
        keys = k.projected[:, :, columns_of(1, j)].reshape(total, 128)
        values = k.projected[:, :, columns_of(2, j)].reshape(total, 128)
        outs = []
        for h in range(2):
            chosen = (lane < HALF) == (h == 0)
            nothing = jnp.zeros_like(query)
            logs = jnp.sum(
                jnp.where(lane == 2 * j + h, k.logs[...], 0.0), axis=1, keepdims=True
            )
            shift = jnp.sum(
                jnp.where(lane == 2 * j + h, k.delta[...], 0.0), axis=1, keepdims=True
            )
            scores = product(jnp.where(chosen, query, nothing), keys, CONTRACT_LAST)
            probs = jnp.exp(scores + k.mask[...] - logs)
            prob_grad = product(jnp.where(chosen, upstream, nothing), values, CONTRACT_LAST)
            score_grad = (probs * (prob_grad - shift)).astype(low)
            outs.append(product(score_grad, keys, CONTRACT_INNER))
        k.proj_grad[:, columns_of(0, j)] = (
            jnp.where(lane < HALF, outs[0], outs[1]) * HEAD_DIM**-0.5
        ).astype(low)

    def key_pair(j):
        key = k.projected[mine, :, columns_of(1, j)]
        value = k.projected[mine, :, columns_of(2, j)]
        queries = k.projected[:, :, columns_of(0, j)].reshape(total, 128)
        upstream = k.grad_block[:, :, columns_of(0, j)].reshape(total, 128)
        key_outs, value_outs = [], []
        for h in range(2):
            chosen = (lane < HALF) == (h == 0)
            nothing = jnp.zeros_like(key)
            logs = jnp.concatenate(
                [k.stats[b, pl.ds(2 * j + h, 1), :] for b in range(BLOCKS)], axis=1
            )
            shift = jnp.concatenate(
                [k.stats[b, pl.ds(16 + 2 * j + h, 1), :] for b in range(BLOCKS)], axis=1
            )
            scores = product(jnp.where(chosen, key, nothing), queries, CONTRACT_LAST)
            probs = jnp.exp(scores + k.mask[...] - logs)
            prob_grad = product(jnp.where(chosen, value, nothing), upstream, CONTRACT_LAST)
            score_grad = (probs * (prob_grad - shift)).astype(low)
            key_outs.append(product(score_grad, queries, CONTRACT_INNER))
            value_outs.append(product(probs.astype(low), upstream, CONTRACT_INNER))
        k.proj_grad[:, columns_of(1, j)] = jnp.where(
            lane < HALF, key_outs[0], key_outs[1]
        ).astype(low)
        k.proj_grad[:, columns_of(2, j)] = jnp.where(
            lane < HALF, value_outs[0], value_outs[1]
        ).astype(low)

    def pairs(one, first, last):
        def body(j, carry):
            one(j)
            return carry

        lax.fori_loop(first, last, body, 0)

    pairs(query_pair, 0, 3)
    back.cross_over()
    ups[1].share()
    pairs(query_pair, 3, 4)
    up_left.complete()
    back.line_near()
    down_left.relay()
    back.cross_near()
    pairs(query_pair, 4, 5)
    ups[0].multiply()
    back.line_far()
    down_left.complete()
    queries_own_far()
    back.cross_near_over()
    back.cross_far()
    back.line_near_over()
    ups[1].multiply()
    down.multiply()
    out_left.relay()
    queries_near()
    out.share()
    back.line_over()
    back.line_far_over()
    back.cross_far_over()
    ups[0].spread()
    pairs(query_pair, 5, 6)
    out_left.complete()
    planes_done()
    query_note()
    early.step(0)
    pairs(key_pair, 0, 1)
    qkv_left.relay()
    ups[1].spread()
    early.step(1)
    query.share()
    pairs(key_pair, 1, 2)
    qkv_left.complete()
    pairs(key_pair, 2, 3)
    ups[1].fold()
    ups[0].fold()
    pairs(key_pair, 3, 4)
    down.spread()
    out.multiply()
    early.step(2)
    pairs(key_pair, 4, 5)
    keys[0].share()
    pairs(key_pair, 5, 6)
    query.multiply()
    early.step(3)
    down.fold()
    keys[2].share()
    keys[1].share()
    out.spread()
    late_notes()
    late.step(0)
    input_gradient()
    keys[0].multiply()
    query.spread()
    out.fold()
    keys[2].multiply()
    early.step(4)
    keys[1].multiply()
    late.step(1)
    ups[0].collect()
    query.fold()
    down.collect()
    keys[0].spread()
    keys[0].fold()
    keys[2].spread()
    keys[1].spread()
    late.step(2)
    keys[2].fold()
    keys[1].fold()
    ups[1].collect()
    late.step(3)
    query.collect()
    keys[0].collect()
    early.step(5)
    out.collect()
    small_shares()
    keys[2].collect()
    keys[1].collect()
    for each in [down_left, up_left, out_left, qkv_left, down, out, query] + ups + keys:
        each.finish()
    for each in (back, link, early, late):
        each.finish()


def copy_kernel(*refs):
    count = len(refs) // 2
    for source, target in zip(refs[:count], refs[count:]):
        target[...] = source[...]


def hand_over(results):
    return pl.pallas_call(
        copy_kernel,
        out_shape=tuple(jax.ShapeDtypeStruct(each.shape, each.dtype) for each in results),
        in_specs=[IN_VMEM] * len(results),
        out_specs=(IN_VMEM,) * len(results),
    )(*results)


def layer_step(*args):
    frames = args[0]
    frame_count, width = frames.shape[1:]
    inner = args[9].shape[1]
    low, wide = jnp.bfloat16, jnp.float32
    scratch, held = jax.tree.flatten(layer_scratch(frame_count, width, inner))
    operands = [frames[0]] + list(args[1:-1]) + [args[-1][0]]
    share = width // 32
    shapes = [
        ((frame_count, width), low),
        ((frame_count, width), wide),
        ((share, 3 * width), wide),
        ((share,), wide),
        ((share,), wide),
        ((share, width), wide),
        ((share,), wide),
        ((share,), wide),
        ((share,), wide),
        ((share, inner), wide),
        ((4 * share,), wide),
        ((4 * share, width), wide),
        ((share,), wide),
        ((share,), wide),
        ((share,), wide),
    ]
    results = pl.pallas_call(
        functools.partial(layer_kernel, held),
        out_shape=tuple(jax.ShapeDtypeStruct(shape, kind) for shape, kind in shapes),
        in_specs=[IN_PLACE if each.ndim == 2 and each.shape[0] >= width else IN_VMEM for each in operands],
        out_specs=(IN_VMEM,) * len(shapes),
        scratch_shapes=scratch,
        compiler_params=pltpu.CompilerParams(
            collective_id=0, has_side_effects=True, vmem_limit_bytes=VMEM_BYTES
        ),
    )(*operands)
    results = hand_over(results)
    return (results[0][None], results[1][None]) + tuple(results[2:])


def solution(mesh):
    chosen = layer_step if dict(mesh.shape) == {"rows": 2, "seq": 16} else shards
    in_specs = (
        P("rows", "seq", None),
        P("rows", "seq"),
        P(),
        P(),
        P(),
        P(),
        P(),
        P(),
        P(),
        P(),
        P(),
        P(),
        P(),
        P(),
        P(),
        P("rows", "seq", None),
    )
    out_specs = (
        P("rows", "seq", None),
        P("rows", "seq", None),
        P(("rows", "seq"), None),
        P(("rows", "seq")),
        P(("rows", "seq")),
        P(("rows", "seq"), None),
        P(("rows", "seq")),
        P(("rows", "seq")),
        P(("rows", "seq")),
        P(("rows", "seq"), None),
        P(("rows", "seq")),
        P(("rows", "seq"), None),
        P(("rows", "seq")),
        P(("rows", "seq")),
        P(("rows", "seq")),
    )
    return jax.shard_map(chosen, mesh=mesh, in_specs=in_specs, out_specs=out_specs, check_vma=False)
```

```python
import functools
import math
import typing

import jax
import jax.numpy as jnp
from jax import lax
from jax.experimental import pallas as pl
from jax.experimental.pallas import tpu as pltpu
from jax.sharding import PartitionSpec as P

HEADS = 12
HEAD_DIM = 64


norm_eps = 1e-05
mask_fill = -1e30


def shortened(shard):

    def short(part):
        return part.astype(jnp.bfloat16) if part.dtype == jnp.float32 else part

    return jax.tree.map(short, shard)


def passed_along(value, axis, steps):
    count = lax.axis_size(axis)
    pairs = [(source, (source + steps) % count) for source in range(count)]
    return lax.ppermute(value, axis, pairs)


def layer_norm(resid, gain, shift):
    centred = resid - jnp.mean(resid, axis=-1, keepdims=True)
    inv_std = lax.rsqrt(jnp.mean(centred * centred, axis=-1, keepdims=True) + norm_eps)
    normed = centred * inv_std
    return (normed * gain + shift, normed, inv_std)


def norm_back(upstream, normed, inv_std, gain):
    scaled = upstream * gain
    first_mean = jnp.mean(scaled, axis=-1, keepdims=True)
    second_mean = jnp.mean(scaled * normed, axis=-1, keepdims=True)
    grad_in = inv_std * (scaled - first_mean - normed * second_mean)
    return (grad_in, jnp.sum(upstream * normed, axis=0), jnp.sum(upstream, axis=0))


def gelu_slope(pre_act):
    normal_cdf = 0.5 * (1.0 + lax.erf(pre_act * 0.5**0.5))
    normal_pdf = jnp.exp(-0.5 * pre_act * pre_act) * (2.0 * math.pi) ** (-0.5)
    return normal_cdf + pre_act * normal_pdf


def head_groups(head_count):
    return [(0, head_count, 1)]


def pass_keys(blocks):
    return jax.tree.map(
        lambda part, own: part.astype(own.dtype), passed_along(shortened(blocks), "seq", 1), blocks
    )


def pass_again(blocks):
    return jax.tree.map(
        lambda part, own: part.astype(own.dtype), passed_along(shortened(blocks), "seq", 1), blocks
    )


def pass_grads(blocks):
    return (
        passed_along(blocks[0].astype(jnp.bfloat16), "seq", 1).astype(jnp.float32),
        passed_along(blocks[1].astype(jnp.bfloat16), "seq", 1).astype(jnp.float32),
    )


def block_scores(query_part, key_part, query_ids, key_ids):
    scores = jnp.einsum(
        "qhe,khe->hqk", query_part, key_part, preferred_element_type=jnp.float32
    ) * HEAD_DIM ** (-0.5)
    return jnp.where((query_ids[:, None] == key_ids[None, :])[None], scores, mask_fill)


def attend_block(carried, query_part, key_part, value_part, query_ids, key_ids):
    run_max, run_total, run_acc = carried
    scores = block_scores(query_part, key_part, query_ids, key_ids)
    new_max = jnp.maximum(run_max, jnp.max(scores, axis=-1))
    weights = jnp.exp(scores - new_max[:, :, None])
    factor = jnp.exp(run_max - new_max)
    new_total = run_total * factor + jnp.sum(weights, axis=-1)
    update = jnp.einsum(
        "hqk,khe->qhe", weights.astype(jnp.bfloat16), value_part, preferred_element_type=jnp.float32
    )
    return (new_max, new_total, run_acc * factor.T[:, :, None] + update)


def grad_block(
    carried,
    query_part,
    key_part,
    value_part,
    query_ids,
    key_ids,
    context_part,
    log_part,
    delta_part,
):
    query_acc, key_acc, value_acc = carried
    scores = block_scores(query_part, key_part, query_ids, key_ids)
    probs = jnp.exp(scores - log_part[:, :, None])
    prob_grad = jnp.einsum(
        "qhe,khe->hqk", context_part, value_part, preferred_element_type=jnp.float32
    )
    score_grad = (probs * (prob_grad - delta_part[:, :, None])).astype(jnp.bfloat16)
    scale = HEAD_DIM ** (-0.5)
    query_acc = query_acc + scale * jnp.einsum(
        "hqk,khe->qhe", score_grad, key_part, preferred_element_type=jnp.float32
    )
    key_acc = key_acc + scale * jnp.einsum(
        "hqk,qhe->khe", score_grad, query_part, preferred_element_type=jnp.float32
    )
    value_acc = value_acc + jnp.einsum(
        "hqk,qhe->khe", probs.astype(jnp.bfloat16), context_part, preferred_element_type=jnp.float32
    )
    return (query_acc, key_acc, value_acc)


def forward_cycle(
    query_heads, key_heads, value_heads, local_ids, every_id, cycle_place, cycle_size
):
    frame_count, head_count, head_width = query_heads.shape
    grouping = head_groups(head_count)
    states = []
    blocks = []
    for head_first, head_last, direction in grouping:
        head_span = head_last - head_first
        initial = (
            jnp.full((head_span, frame_count), mask_fill, jnp.float32),
            jnp.zeros((head_span, frame_count), jnp.float32),
            jnp.zeros((frame_count, head_span, head_width), jnp.float32),
        )
        states.append(
            attend_block(initial, query_heads, key_heads, value_heads, local_ids, local_ids)
        )
        blocks.append((key_heads, value_heads))

    def forward_cycle_turn(turn_index, cycle_carry):
        old_states, old_blocks = cycle_carry
        new_states = []
        new_blocks = []
        for group_info, part_state, part_block in zip(grouping, old_states, old_blocks):
            head_first, head_last, direction = group_info
            part_block = pass_keys(part_block)
            source_index = (cycle_place - direction * turn_index) % cycle_size
            key_ids = lax.dynamic_slice_in_dim(every_id, source_index * frame_count, frame_count)
            new_states.append(
                attend_block(
                    part_state, query_heads, part_block[0], part_block[1], local_ids, key_ids
                )
            )
            new_blocks.append(part_block)
        return (new_states, new_blocks)

    states, blocks = lax.fori_loop(1, cycle_size, forward_cycle_turn, (states, blocks))
    maxima = jnp.concatenate([part_state[0] for part_state in states], axis=0)
    totals = jnp.concatenate([part_state[1] for part_state in states], axis=0)
    sums_all = jnp.concatenate([part_state[2] for part_state in states], axis=1)
    attended = sums_all / totals.T[:, :, None]
    return (attended, maxima + jnp.log(totals))


def backward_cycle(
    query_heads,
    key_heads,
    value_heads,
    local_ids,
    every_id,
    context_heads,
    log_total,
    row_delta,
    cycle_place,
    cycle_size,
):
    frame_count, head_count, head_width = query_heads.shape
    grouping = head_groups(head_count)
    initial = []
    for head_first, head_last, direction in grouping:
        zero_part = jnp.zeros((frame_count, head_last - head_first, head_width), jnp.float32)
        initial.append((zero_part, (key_heads, value_heads), (zero_part, zero_part)))

    def backward_cycle_turn(turn_index, cycle_carry):
        new_carry = []
        for group_info, part_carry in zip(grouping, cycle_carry):
            head_first, head_last, direction = group_info
            query_acc, part_block, part_grads = part_carry
            source_index = (cycle_place - direction * turn_index) % cycle_size
            key_ids = lax.dynamic_slice_in_dim(every_id, source_index * frame_count, frame_count)
            query_acc, key_acc, value_acc = grad_block(
                (query_acc, part_grads[0], part_grads[1]),
                query_heads,
                part_block[0],
                part_block[1],
                local_ids,
                key_ids,
                context_heads,
                log_total,
                row_delta,
            )
            part_grads = pass_grads((key_acc, value_acc))
            part_block = pass_again(part_block)
            new_carry.append((query_acc, part_block, part_grads))
        return new_carry

    final = lax.fori_loop(0, cycle_size, backward_cycle_turn, initial)
    query_grad = jnp.concatenate([part_carry[0] for part_carry in final], axis=1)
    key_grad = jnp.concatenate([part_carry[2][0] for part_carry in final], axis=1)
    value_grad = jnp.concatenate([part_carry[2][1] for part_carry in final], axis=1)
    return (query_grad, key_grad, value_grad)


def shards(
    frames,
    segment_ids,
    qkv_weight,
    query_bias,
    value_bias,
    out_weight,
    out_bias,
    norm1_gain,
    norm1_shift,
    up_weight,
    up_bias,
    down_weight,
    down_bias,
    norm2_gain,
    norm2_shift,
    cotangent,
):
    inputs = frames[0]
    local_ids = segment_ids[0]
    frame_count, model_width = inputs.shape
    cycle_size = lax.axis_size("seq")
    cycle_place = lax.axis_index("seq")
    every_id = lax.all_gather(segment_ids, "seq", axis=1, tiled=True)[0]
    head_shape = (frame_count, HEADS, HEAD_DIM)
    projected = jnp.dot(inputs, qkv_weight, preferred_element_type=jnp.float32)
    query_heads = (projected[:, :model_width] + query_bias).astype(jnp.bfloat16).reshape(head_shape)
    key_heads = projected[:, model_width : 2 * model_width].astype(jnp.bfloat16).reshape(head_shape)
    value_heads = (
        (projected[:, 2 * model_width :] + value_bias).astype(jnp.bfloat16).reshape(head_shape)
    )
    attended, log_total = forward_cycle(
        query_heads, key_heads, value_heads, local_ids, every_id, cycle_place, cycle_size
    )
    context = attended.astype(jnp.bfloat16).reshape(frame_count, model_width)
    resid_one = (
        inputs.astype(jnp.float32)
        + jnp.dot(context, out_weight, preferred_element_type=jnp.float32)
        + out_bias
    )
    hidden, normed_one, inverse_one = layer_norm(resid_one, norm1_gain, norm1_shift)
    hidden_low = hidden.astype(jnp.bfloat16)
    pre_act = jnp.dot(hidden_low, up_weight, preferred_element_type=jnp.float32) + up_bias
    act_low = jax.nn.gelu(pre_act, approximate=False).astype(jnp.bfloat16)
    resid_two = (
        hidden + jnp.dot(act_low, down_weight, preferred_element_type=jnp.float32) + down_bias
    )
    output, normed_two, inverse_two = layer_norm(resid_two, norm2_gain, norm2_shift)
    upstream = cotangent[0].astype(jnp.float32)
    second_grad, gain_two_grad, shift_two_grad = norm_back(
        upstream, normed_two, inverse_two, norm2_gain
    )
    second_low = second_grad.astype(jnp.bfloat16)
    down_grad = jnp.einsum("tf,td->fd", act_low, second_low, preferred_element_type=jnp.float32)
    pre_grad = jnp.einsum(
        "td,fd->tf", second_low, down_weight, preferred_element_type=jnp.float32
    ) * gelu_slope(pre_act)
    pre_low = pre_grad.astype(jnp.bfloat16)
    up_grad = jnp.einsum("td,tf->df", hidden_low, pre_low, preferred_element_type=jnp.float32)
    hidden_grad = second_grad + jnp.einsum(
        "tf,df->td", pre_low, up_weight, preferred_element_type=jnp.float32
    )
    first_grad, gain_one_grad, shift_one_grad = norm_back(
        hidden_grad, normed_one, inverse_one, norm1_gain
    )
    first_low = first_grad.astype(jnp.bfloat16)
    out_grad = jnp.einsum("td,te->de", context, first_low, preferred_element_type=jnp.float32)
    context_grad = (
        jnp.einsum("te,de->td", first_low, out_weight, preferred_element_type=jnp.float32)
        .astype(jnp.bfloat16)
        .reshape(head_shape)
    )
    row_delta = jnp.einsum("qhe,qhe->hq", context_grad.astype(jnp.float32), attended)
    query_grad, key_grad, value_grad = backward_cycle(
        query_heads,
        key_heads,
        value_heads,
        local_ids,
        every_id,
        context_grad,
        log_total,
        row_delta,
        cycle_place,
        cycle_size,
    )
    query_low = query_grad.astype(jnp.bfloat16).reshape(frame_count, model_width)
    key_low = key_grad.astype(jnp.bfloat16).reshape(frame_count, model_width)
    value_low = value_grad.astype(jnp.bfloat16).reshape(frame_count, model_width)
    proj_grad = jnp.concatenate([query_low, key_low, value_low], axis=1)
    qkv_grad = jnp.einsum("td,te->de", inputs, proj_grad, preferred_element_type=jnp.float32)
    input_grad = (
        jnp.einsum("te,de->td", proj_grad, qkv_weight, preferred_element_type=jnp.float32)
        + first_grad
    )
    summed = (
        lax.psum_scatter(qkv_grad, ("rows", "seq"), scatter_dimension=0, tiled=True),
        lax.psum_scatter(
            jnp.sum(query_low.astype(jnp.float32), axis=0),
            ("rows", "seq"),
            scatter_dimension=0,
            tiled=True,
        ),
        lax.psum_scatter(
            jnp.sum(value_low.astype(jnp.float32), axis=0),
            ("rows", "seq"),
            scatter_dimension=0,
            tiled=True,
        ),
        lax.psum_scatter(out_grad, ("rows", "seq"), scatter_dimension=0, tiled=True),
        lax.psum_scatter(
            jnp.sum(first_grad, axis=0), ("rows", "seq"), scatter_dimension=0, tiled=True
        ),
        lax.psum_scatter(gain_one_grad, ("rows", "seq"), scatter_dimension=0, tiled=True),
        lax.psum_scatter(shift_one_grad, ("rows", "seq"), scatter_dimension=0, tiled=True),
        lax.psum_scatter(up_grad, ("rows", "seq"), scatter_dimension=0, tiled=True),
        lax.psum_scatter(
            jnp.sum(pre_grad, axis=0), ("rows", "seq"), scatter_dimension=0, tiled=True
        ),
        lax.psum_scatter(down_grad, ("rows", "seq"), scatter_dimension=0, tiled=True),
        lax.psum_scatter(
            jnp.sum(second_grad, axis=0), ("rows", "seq"), scatter_dimension=0, tiled=True
        ),
        lax.psum_scatter(gain_two_grad, ("rows", "seq"), scatter_dimension=0, tiled=True),
        lax.psum_scatter(shift_two_grad, ("rows", "seq"), scatter_dimension=0, tiled=True),
    )
    return (
        output.astype(jnp.bfloat16)[None],
        input_grad[None],
        summed[0],
        summed[1],
        summed[2],
        summed[3],
        summed[4],
        summed[5],
        summed[6],
        summed[7],
        summed[8],
        summed[9],
        summed[10],
        summed[11],
        summed[12],
    )


HALF = HEAD_DIM
PAIRS = HEADS // 2
CONTRACT_LAST = (((1,), (1,)), ((), ()))
CONTRACT_INNER = (((1,), (0,)), ((), ()))
CONTRACT_FIRST = (((0,), (0,)), ((), ()))
IN_VMEM = pl.BlockSpec(memory_space=pltpu.VMEM)
IN_PLACE = pl.BlockSpec(memory_space=pl.ANY)
MESH_ID = pl.DeviceIdType.MESH
VMEM_BYTES = 60 << 20
BLOCKS = 16
PLANES = 4


def product(left, right, dims):
    return lax.dot_general(left, right, dims, preferred_element_type=jnp.float32)


def where_am_i():
    row = lax.axis_index("rows")
    place = lax.axis_index("seq")
    return row, place // 4, place // 2 % 2, place % 2


def meet(partners, count):
    barrier = pltpu.get_barrier_semaphore()
    for present, target in partners:

        def signal(target=target):
            pl.semaphore_signal(barrier, inc=1, device_id=target, device_id_type=MESH_ID)

        if present is None:
            signal()
        else:
            pl.when(present)(signal)
    pl.semaphore_wait(barrier, count)


class RowGather:
    UP, DOWN, ACROSS, BESIDE = range(4)

    def __init__(self, parts, line, crossing, sems):
        self.parts, self.line, self.crossing = parts, line, crossing
        self.recv_sem, self.beside_sem, self.line_sem, self.out_sem = sems
        self.row, self.z, self.x, self.c = where_am_i()
        self.has_up, self.has_down = self.z < PLANES - 1, self.z > 0
        self.far = (self.z + 2) % PLANES
        self.buffers = []
        for ref, _, _ in parts:
            if not any(ref is known for known in self.buffers):
                self.buffers.append(ref)

    def group(self, part):
        return [self.parts[part][0] is ref for ref in self.buffers].index(True)

    def device(self, z, x, c):
        return (self.row, z * 4 + x * 2 + c)

    def target(self, way):
        return (
            self.device(self.z + 1, self.x, self.c),
            self.device(self.z - 1, self.x, self.c),
            self.device(self.z, 1 - self.x, self.c),
            self.device(self.z, self.x, 1 - self.c),
        )[way]

    def copy(self, part, z, x, way):
        ref, first, rows = self.parts[part]
        piece = ref.at[z * 4 + x * 2 + self.c, pl.ds(first, rows)]
        beside = way == self.BESIDE
        return pltpu.make_async_remote_copy(
            src_ref=piece,
            dst_ref=piece,
            send_sem=self.out_sem.at[self.group(part)] if beside else self.line_sem.at[part, way],
            recv_sem=(
                self.beside_sem.at[self.group(part), z]
                if beside
                else self.recv_sem.at[part, z * 2 + x]
            ),
            device_id=self.target(way),
            device_id_type=MESH_ID,
        )

    def send(self, part, z, x, way):
        present = {self.UP: self.has_up, self.DOWN: self.has_down}.get(way)
        if present is None:
            self.copy(part, z, x, way).start()
        else:
            pl.when(present)(lambda: self.copy(part, z, x, way).start())

    def relay(self, part, z, x, ways, present=None):
        def both():
            self.copy(part, z, x, self.ACROSS).wait_recv()
            for way in ways:
                self.send(part, z, x, way)

        if present is None:
            both()
        else:
            pl.when(present)(both)

    def own(self):
        z, x = self.z, self.x
        for part in self.crossing:
            self.send(part, z, x, self.ACROSS)
        for part in self.line + self.crossing:
            self.send(part, z, x, self.UP)
            self.send(part, z, x, self.DOWN)
        for part in self.line:
            self.send(part, z, x, self.ACROSS)
        for part in self.crossing + self.line:
            self.send(part, z, x, self.BESIDE)

    def line_near(self):
        for part in self.line:
            self.relay(part, self.z - 1, self.x, (self.UP, self.ACROSS, self.BESIDE), self.has_down)
            self.relay(part, self.z + 1, self.x, (self.DOWN, self.ACROSS, self.BESIDE), self.has_up)

    def cross_over(self):
        for part in self.crossing:
            self.relay(part, self.z, 1 - self.x, (self.UP, self.DOWN, self.BESIDE))

    def cross_from(self, x):
        for part in self.crossing:
            self.relay(part, self.z - 1, x, (self.UP, self.BESIDE), self.has_down)
            self.relay(part, self.z + 1, x, (self.DOWN, self.BESIDE), self.has_up)

    def cross_near(self):
        self.cross_from(self.x)

    def cross_near_over(self):
        self.cross_from(1 - self.x)

    def line_over(self):
        for part in self.line:
            self.relay(part, self.z, 1 - self.x, (self.BESIDE,))

    def line_near_over(self):
        for part in self.line:
            self.relay(part, self.z - 1, 1 - self.x, (self.BESIDE,), self.has_down)
            self.relay(part, self.z + 1, 1 - self.x, (self.BESIDE,), self.has_up)

    def line_far(self):
        for part in self.line:
            self.relay(part, self.far, self.x, (self.ACROSS, self.BESIDE))

    def cross_far(self):
        for part in self.crossing:
            self.relay(part, self.far, self.x, (self.BESIDE,))

    def line_far_over(self):
        for part in self.line:
            self.relay(part, self.far, 1 - self.x, (self.BESIDE,))

    def cross_far_over(self):
        for part in self.crossing:
            self.relay(part, self.far, 1 - self.x, (self.BESIDE,))

    def plane_done(self, z, present=None):
        def wait():
            for i, ref in enumerate(self.buffers):
                both = ref.at[pl.ds(0, 2)]
                pltpu.make_async_remote_copy(
                    src_ref=both,
                    dst_ref=both,
                    send_sem=self.out_sem.at[i],
                    recv_sem=self.beside_sem.at[i, z],
                    device_id=self.target(self.BESIDE),
                    device_id_type=MESH_ID,
                ).wait_recv()

        if present is None:
            wait()
        else:
            pl.when(present)(wait)

    def left(self, sem, ref, count, first, rows):
        sent = ref.at[pl.ds(0, count), pl.ds(first, rows)]
        pltpu.make_async_remote_copy(
            src_ref=sent,
            dst_ref=sent,
            send_sem=sem,
            recv_sem=self.beside_sem.at[0, 0],
            device_id=self.target(self.BESIDE),
            device_id_type=MESH_ID,
        ).wait_send()

    def finish(self):
        def settle(ways, hops, planes):
            for part, (ref, first, rows) in enumerate(self.parts):
                wide = 1 if part in self.line else 2
                for way in ways:
                    self.left(self.line_sem.at[part, way], ref, wide * hops, first, rows)
                across = planes if part in self.line else 1
                self.left(self.line_sem.at[part, self.ACROSS], ref, across, first, rows)
            for i, ref in enumerate(self.buffers):
                self.left(self.out_sem.at[i], ref, 2 * planes, 0, ref.shape[1])

        pl.when(self.has_up & self.has_down)(lambda: settle((self.UP, self.DOWN), 2, 4))
        pl.when(jnp.logical_not(self.has_down))(lambda: settle((self.UP,), 1, 3))
        pl.when(jnp.logical_not(self.has_up))(lambda: settle((self.DOWN,), 1, 3))


def gather_sems(parts, groups):
    dma = pltpu.SemaphoreType.DMA
    return [dma((parts, 2 * PLANES)), dma((groups, PLANES)), dma((parts, 3)), dma((groups,))]


class VectorSum:
    STAGES = 5

    def __init__(self, ref, partial, arrived, send_sem, recv_sem):
        self.ref, self.partial, self.arrived = ref, partial, arrived
        self.send_sem, self.recv_sem = send_sem, recv_sem
        self.y, self.z, self.x, self.c = where_am_i()

    def copy(self, stage):
        y, z, x, c = self.y, self.z, self.x, self.c
        core, row, across, near, far = (
            (y, z, x, 1 - c),
            (1 - y, z, x, c),
            (y, z, 1 - x, c),
            (y, z + 1 - 2 * (z % 2), x, c),
            (y, (z + 2) % PLANES, x, c),
        )
        y, z, x, c = (core, row, across, near, far)[stage]
        return pltpu.make_async_remote_copy(
            src_ref=self.ref if stage == 0 else self.partial.at[stage - 1],
            dst_ref=self.arrived.at[stage],
            send_sem=self.send_sem.at[stage],
            recv_sem=self.recv_sem.at[stage],
            device_id=(y, z * 4 + x * 2 + c),
            device_id_type=MESH_ID,
        )

    def step(self, stage):
        if stage > 0:
            self.copy(stage - 1).wait_recv()
            before = self.ref[...] if stage == 1 else self.partial[stage - 2]
            self.partial[stage - 1] = before + self.arrived[stage - 1]
        if stage < self.STAGES:
            self.copy(stage).start()

    def finish(self):
        for stage in range(self.STAGES):
            self.copy(stage).wait_send()

    def own_share(self, rows, share):
        width = self.ref.shape[1]
        place = self.y * 16 + self.z * 4 + self.x * 2 + self.c
        per_row = width // share
        offset = place % per_row * share
        row_index = lax.broadcasted_iota(jnp.int32, (width, 128), 0)
        column_index = lax.broadcasted_iota(jnp.int32, (width, 128), 1)
        picked = jnp.where(
            (row_index == column_index + offset) & (column_index < share), 1.0, 0.0
        ).astype(jnp.bfloat16)
        rest = rows
        total = jnp.zeros((rows.shape[0], 128), jnp.float32)
        for _ in range(3):
            piece = rest.astype(jnp.bfloat16)
            total = total + product(piece, picked, CONTRACT_INNER)
            rest = rest - piece.astype(jnp.float32)
        return total, place // per_row


STEP = 384
KEY_STEPS = (384, 256, 128)
UNROLL = 6
CHUNK = 768


class CubeSum:
    STAGES = 3

    def __init__(self, partial, cube, line, send_sem, recv_sem):
        self.partial, self.cube, self.line = partial, cube, line
        self.send_sem, self.recv_sem = send_sem, recv_sem
        self.y, self.z, self.x, self.c = where_am_i()
        self.member = self.y * 4 + self.x * 2 + self.c

    def link(self, source, target, stage, device):
        return pltpu.make_async_remote_copy(
            src_ref=source,
            dst_ref=target,
            send_sem=self.send_sem.at[stage],
            recv_sem=self.recv_sem.at[stage],
            device_id=device,
            device_id_type=MESH_ID,
        )

    def others(self):
        for step in range(1, 8):
            other = (self.member + step) % 8
            yield (other // 4, self.z * 4 + other % 4)

    def copy(self, stage):
        beside = self.z + 1 - 2 * (self.z % 2) if stage == 1 else (self.z + 2) % PLANES
        return self.link(
            self.partial.at[stage - 1], self.line.at[stage - 1], stage,
            (self.y, beside * 4 + self.x * 2 + self.c),
        )

    def seven(self):
        seven = self.cube.at[pl.ds(0, 7)]
        return self.link(seven, seven, 0, (self.y, self.z * 4 + self.x * 2 + 1 - self.c))

    def step(self, stage):
        if stage == 0:
            own = self.cube.at[self.member]
            for device in self.others():
                self.link(own, own, 0, device).start()
            return
        if stage == 1:
            self.seven().wait_recv()
            self.partial[0] = jnp.sum(self.cube[...], axis=0)
        else:
            self.copy(stage - 1).wait_recv()
            self.partial[stage - 1] = self.partial[stage - 2] + self.line[stage - 2]
        if stage < self.STAGES:
            self.copy(stage).start()

    def finish(self):
        self.seven().wait_send()
        for stage in range(1, self.STAGES):
            self.copy(stage).wait_send()


class Quad:
    def __init__(self, by_x):
        self.by_x = by_x
        self.y, self.z, self.x, self.c = where_am_i()
        self.a, self.b = (self.x, self.y) if by_x else (self.y, self.x)
        self.mine = self.a * 2 + self.c
        self.peer = (1 - self.a) * 2 + self.c
        self.beside = self.a * 2 + 1 - self.c
        self.corner = (1 - self.a) * 2 + 1 - self.c

    def device(self, a, b, z, c):
        y, x = (b, a) if self.by_x else (a, b)
        return (y, z * 4 + x * 2 + c)

    def at_peer(self):
        return self.device(1 - self.a, self.b, self.z, self.c)

    def at_beside(self):
        return self.device(self.a, self.b, self.z, 1 - self.c)

    def at_corner(self):
        return self.device(1 - self.a, self.b, self.z, 1 - self.c)

    def link(self, source, target, send_sem, recv_sem, device):
        return pltpu.make_async_remote_copy(
            src_ref=source,
            dst_ref=target,
            send_sem=send_sem,
            recv_sem=recv_sem,
            device_id=device,
            device_id_type=MESH_ID,
        )

    def count(self, ref, send_sem, recv_sem):
        return self.link(ref, ref, send_sem, recv_sem, self.at_beside())


class Shared:
    def __init__(self, left, by_x, buffers):
        self.left = left
        self.held, self.send_sem, self.recv_sem = buffers
        self.quad = Quad(by_x)
        self.width = self.held.shape[2]

    def part(self, a):
        if self.quad.by_x:
            return self.left
        return self.left.at[:, pl.ds(pl.multiple_of(a * self.width, 128), self.width)]

    def share(self):
        q = self.quad
        slot = self.held.at[q.mine]
        send = self.send_sem.at[0]
        q.link(self.part(1 - q.a), slot, send, self.recv_sem.at[0], q.at_peer()).start()
        q.link(self.part(q.a), slot, send, self.recv_sem.at[1], q.at_beside()).start()
        self.held[q.mine] = self.part(q.a)[...]

    def relay(self):
        q = self.quad
        slot = self.held.at[q.peer]
        q.count(slot, self.send_sem.at[0], self.recv_sem.at[0]).wait_recv()
        q.link(slot, slot, self.send_sem.at[0], self.recv_sem.at[1], q.at_beside()).start()

    def complete(self):
        two = self.held.at[pl.ds(0, 2)]
        self.quad.count(two, self.send_sem.at[0], self.recv_sem.at[1]).wait_recv()

    def finish(self):
        three = self.held.at[pl.ds(0, 3)]
        self.quad.count(three, self.send_sem.at[0], self.recv_sem.at[1]).wait_send()


class Piece:
    def __init__(self, shared, right, base, stride, out, buffers):
        self.shared, self.right, self.base, self.stride, self.out = shared, right, base, stride, out
        self.rights, self.whole, self.b_in, self.z_in, self.last, self.send_sem, self.recv_sem = buffers
        self.wide = self.rights.shape[2]
        self.quad = shared.quad
        self.share_rows = out.shape[0]

    def columns(self, member):
        place = member if self.quad.by_x else member % 2
        return pl.ds(pl.multiple_of(self.base + place * self.stride, 128), self.wide)

    def give(self, member, device):
        self.quad.link(
            self.right.at[:, self.columns(member)], self.rights.at[self.quad.mine],
            self.send_sem.at[0], self.recv_sem.at[0], device,
        ).start()

    def share(self):
        q = self.quad
        self.give(q.peer, q.at_peer())
        self.give(q.corner, q.at_corner())
        self.give(q.beside, q.at_beside())
        self.rights[q.mine] = self.right[:, self.columns(q.mine)]

    def slab(self, b):
        return self.whole.at[b] if self.quad.by_x else self.whole.at[:, b]

    def cell(self, z):
        b = self.quad.b
        return self.whole.at[b, z] if self.quad.by_x else self.whole.at[z, b]

    def multiply(self):
        q = self.quad
        three = self.rights.at[pl.ds(0, 3)]
        q.count(three, self.send_sem.at[0], self.recv_sem.at[0]).wait_recv()
        held = self.shared.held
        tokens = held.shape[0] * held.shape[1]
        right = self.rights[...].reshape(tokens, self.wide)
        if self.shared.width > STEP:

            def one(i, carry):
                left = held[:, :, pl.ds(pl.multiple_of(i * STEP, 128), STEP)]
                part = product(left.reshape(tokens, STEP), right, CONTRACT_FIRST)
                self.whole[i] = part.astype(jnp.bfloat16).reshape(self.whole.shape[1:])
                return carry

            lax.fori_loop(0, self.shared.width // STEP, one, 0)
        else:
            part = product(held[...].reshape(tokens, STEP), right, CONTRACT_FIRST)
            self.whole[...] = part.astype(jnp.bfloat16).reshape(self.whole.shape)
        q.link(
            self.slab(1 - q.b), self.b_in, self.send_sem.at[1], self.recv_sem.at[1],
            q.device(q.a, 1 - q.b, q.z, q.c),
        ).start()

    def spread(self):
        q = self.quad
        q.count(self.b_in, self.send_sem.at[1], self.recv_sem.at[1]).wait_recv()
        slab = self.slab(q.b)
        slab[...] = (slab[...].astype(jnp.float32) + self.b_in[...].astype(jnp.float32)).astype(
            jnp.bfloat16
        )
        q.count(self.rights.at[pl.ds(0, 3)], self.send_sem.at[0], self.recv_sem.at[0]).wait_send()
        inner = self.inner()

        @pl.when(inner)
        def _():
            self.to_plane(self.cell(self.end()), 0, 1, self.end())

        @pl.when(jnp.logical_not(inner))
        def _():
            first = 1 - q.z // (PLANES - 1)
            three = pl.ds(first, 3)
            cells = self.whole.at[q.b, three] if q.by_x else self.whole.at[three, q.b]
            self.to_plane(cells, pl.ds(0, 3), 0, 1 + q.z // 2)

    def inner(self):
        return (self.quad.z > 0) & (self.quad.z < PLANES - 1)

    def end(self):
        return self.quad.z // 2 * (PLANES - 1)

    def to_plane(self, source, slot, which, z):
        q = self.quad
        q.link(
            source, self.z_in.at[slot], self.send_sem.at[0], self.recv_sem.at[2 + which],
            q.device(q.a, q.b, z, q.c),
        ).start()

    def fold(self):
        q = self.quad

        @pl.when(self.inner())
        def _():
            three = self.z_in.at[pl.ds(0, 3)]
            q.count(three, self.send_sem.at[0], self.recv_sem.at[2]).wait_recv()
            first = 2 - q.z
            for target in (PLANES - 1 - self.end(), PLANES - 1 - q.z):
                cell = self.cell(target)
                cell[...] = (
                    cell[...].astype(jnp.float32) + self.z_in[target - first].astype(jnp.float32)
                ).astype(jnp.bfloat16)
                self.to_plane(cell, 3, 1, target)

    def rows_of(self, member):
        place = member if self.quad.by_x else member % 2
        return self.last.at[pl.ds(pl.multiple_of(place * self.share_rows, 8), self.share_rows)]

    def collect(self):
        q = self.quad
        inner = self.inner()

        def arrived(count):
            some = self.z_in.at[pl.ds(0, count)]
            q.count(some, self.send_sem.at[0], self.recv_sem.at[3]).wait_recv()

        pl.when(inner)(lambda: arrived(1))
        pl.when(jnp.logical_not(inner))(lambda: arrived(2))
        beside = q.z // 2 * 2 * (1 - q.z // (PLANES - 1))
        self.last[...] = (
            self.cell(q.z)[...].astype(jnp.float32)
            + self.z_in[beside].astype(jnp.float32)
            + self.z_in[3].astype(jnp.float32)
        )
        q.count(self.b_in, self.send_sem.at[1], self.recv_sem.at[1]).wait_send()
        columns = self.out.at[:, self.columns(q.mine)]
        partners = [(q.beside, q.at_beside())]
        if q.by_x:
            partners = [(q.peer, q.at_peer()), (q.corner, q.at_corner())] + partners
        for member, device in partners:
            q.link(
                self.rows_of(member), columns, self.send_sem.at[1], self.recv_sem.at[4], device
            ).start()
        columns[...] = self.rows_of(q.mine)[...]

    def finish(self):
        q = self.quad
        others = self.last.at[pl.ds(0, (3 if q.by_x else 1) * self.share_rows)]
        q.count(others, self.send_sem.at[1], self.recv_sem.at[4]).wait()
        three = self.z_in.at[pl.ds(0, 3)]
        q.count(three, self.send_sem.at[0], self.recv_sem.at[2]).wait_send()


def shared_scratch(frame_count, left_width, by_x):
    return [
        pltpu.VMEM((4, frame_count, left_width if by_x else left_width // 2), jnp.bfloat16),
        pltpu.SemaphoreType.DMA((1,)),
        pltpu.SemaphoreType.DMA((2,)),
    ]


def piece_scratch(frame_count, left_width, by_x, wide=STEP):
    rows = left_width // (2 * PLANES) if by_x else left_width // (4 * PLANES)
    low = jnp.bfloat16
    return [
        pltpu.VMEM((4, frame_count, wide), low),
        pltpu.VMEM((2, PLANES, rows, wide) if by_x else (PLANES, 2, rows, wide), low),
        pltpu.VMEM((PLANES, rows, wide), low),
        pltpu.VMEM((PLANES, rows, wide), low),
        pltpu.VMEM((rows, wide), jnp.float32),
        pltpu.SemaphoreType.DMA((2,)),
        pltpu.SemaphoreType.DMA((5,)),
    ]


def cube_scratch(width):
    return [
        pltpu.VMEM((CubeSum.STAGES, 1, width), jnp.float32),
        pltpu.VMEM((8, 1, width), jnp.float32),
        pltpu.VMEM((CubeSum.STAGES - 1, 1, width), jnp.float32),
        pltpu.SemaphoreType.DMA((CubeSum.STAGES,)),
        pltpu.SemaphoreType.DMA((CubeSum.STAGES,)),
    ]


def vector_scratch(rows, width):
    wide = jnp.float32
    return [
        pltpu.VMEM((rows, width), wide),
        pltpu.VMEM((VectorSum.STAGES, rows, width), wide),
        pltpu.VMEM((VectorSum.STAGES, rows, width), wide),
        pltpu.SemaphoreType.DMA((VectorSum.STAGES,)),
        pltpu.SemaphoreType.DMA((VectorSum.STAGES,)),
    ]


def layer_scratch(frame_count, width, inner):
    low, wide = jnp.bfloat16, jnp.float32
    dma = pltpu.SemaphoreType.DMA
    return dict(
        qkv_held=pltpu.VMEM((width, 3 * width), low),
        out_held=pltpu.VMEM((width, width), low),
        up_held=pltpu.VMEM((width, inner), low),
        down_held=pltpu.VMEM((inner, width), low),
        weight_sem=dma((4,)),
        ready=pltpu.SemaphoreType.REGULAR,
        block=pltpu.VMEM((BLOCKS, frame_count + 16, width), low),
        block_sems=gather_sems(2, 1),
        grad_block=pltpu.VMEM((BLOCKS, frame_count, width), low),
        stats=pltpu.VMEM((BLOCKS, 32, frame_count), wide),
        grad_sems=gather_sems(3, 2),
        projected=pltpu.VMEM((BLOCKS, frame_count, 3 * width), low),
        mask=pltpu.VMEM((frame_count, BLOCKS * frame_count), wide),
        attended=pltpu.VMEM((frame_count, width), wide),
        slope=pltpu.VMEM((frame_count, inner), wide),
        logs=pltpu.VMEM((frame_count, 128), wide),
        delta=pltpu.VMEM((frame_count, 128), wide),
        inner_bias=pltpu.VMEM((1, inner), wide),
        proj_bias=pltpu.VMEM((1, 3 * width), wide),
        act=pltpu.VMEM((frame_count, inner), low),
        pre_low=pltpu.VMEM((frame_count, inner), low),
        context=pltpu.VMEM((frame_count, width), low),
        hidden_low=pltpu.VMEM((frame_count, width), low),
        second_low=pltpu.VMEM((frame_count, width), low),
        first_low=pltpu.VMEM((frame_count, width), low),
        normed=pltpu.VMEM((frame_count, width), wide),
        running=pltpu.VMEM((frame_count, width), wide),
        first_grad=pltpu.VMEM((frame_count, width), wide),
        proj_grad=pltpu.VMEM((frame_count, 3 * width), low),
        early=vector_scratch(16, width),
        late=cube_scratch(width),
        down_left=shared_scratch(frame_count, inner, False),
        up_left=shared_scratch(frame_count, width, True),
        out_left=shared_scratch(frame_count, width, False),
        qkv_left=shared_scratch(frame_count, width, False),
        down_piece=piece_scratch(frame_count, inner, False),
        up_pieces=[piece_scratch(frame_count, width, True) for _ in range(2)],
        out_piece=piece_scratch(frame_count, width, False),
        query_piece=piece_scratch(frame_count, width, False),
        key_pieces=[
            piece_scratch(frame_count, width, False, step) for step in KEY_STEPS
        ],
    )


class Inputs(typing.NamedTuple):
    frames: typing.Any
    segment_ids: typing.Any
    qkv_weight: typing.Any
    query_bias: typing.Any
    value_bias: typing.Any
    out_weight: typing.Any
    out_bias: typing.Any
    norm1_gain: typing.Any
    norm1_shift: typing.Any
    up_weight: typing.Any
    up_bias: typing.Any
    down_weight: typing.Any
    down_bias: typing.Any
    norm2_gain: typing.Any
    norm2_shift: typing.Any
    cotangent: typing.Any


class Outputs(typing.NamedTuple):
    layer_out: typing.Any
    input_grad: typing.Any
    qkv_g: typing.Any
    query_g: typing.Any
    value_g: typing.Any
    out_g: typing.Any
    outbias_g: typing.Any
    gain1_g: typing.Any
    shift1_g: typing.Any
    up_g: typing.Any
    upbias_g: typing.Any
    down_g: typing.Any
    downbias_g: typing.Any
    gain2_g: typing.Any
    shift2_g: typing.Any


class Refs:
    def __init__(self, *groups):
        for group in groups:
            for name, ref in group.items():
                setattr(self, name, ref)


def layer_kernel(held, *refs):
    inputs, outputs = len(Inputs._fields), len(Outputs._fields)
    scratch = jax.tree.unflatten(held, refs[inputs + outputs :])
    k = Refs(dict(zip(Inputs._fields + Outputs._fields, refs)), scratch)
    frame_count, width = k.frames.shape
    inner = k.inner_bias.shape[1]
    low, wide = jnp.bfloat16, jnp.float32
    total = BLOCKS * frame_count
    row, z, x, c = where_am_i()
    mine = z * 4 + x * 2 + c
    has_up, has_down = z < PLANES - 1, z > 0
    far = (z + 2) % PLANES
    lost = PLANES - 1 - z
    lane = lax.broadcasted_iota(jnp.int32, (frame_count, 128), 1)

    def fetch(i):
        source, target = (
            (k.qkv_weight, k.qkv_held),
            (k.out_weight, k.out_held),
            (k.up_weight, k.up_held),
            (k.down_weight, k.down_held),
        )[i]
        return pltpu.make_async_copy(source, target, k.weight_sem.at[i])

    for i in range(4):
        fetch(i).start()

    line_rows = frame_count * 80 // 128
    back_rows = frame_count * 64 // 128
    link = RowGather(
        [
            (k.block, 0, line_rows),
            (k.block, line_rows, k.block.shape[1] - line_rows),
        ],
        (0,),
        (1,),
        k.block_sems,
    )
    back = RowGather(
        [
            (k.grad_block, 0, back_rows),
            (k.grad_block, back_rows, frame_count - back_rows),
            (k.stats, 0, 32),
        ],
        (2, 0),
        (1,),
        k.grad_sems,
    )
    down_left = Shared(k.act, False, k.down_left)
    up_left = Shared(k.hidden_low, True, k.up_left)
    out_left = Shared(k.context, False, k.out_left)
    qkv_left = Shared(k.frames, False, k.qkv_left)
    half_width = width // 2
    down = Piece(down_left, k.second_low, 0, half_width, k.down_g, k.down_piece)
    ups = [
        Piece(up_left, k.pre_low, p * STEP, width, k.up_g, k.up_pieces[p]) for p in range(2)
    ]
    out = Piece(out_left, k.first_low, 0, half_width, k.out_g, k.out_piece)
    query = Piece(qkv_left, k.proj_grad, 0, half_width, k.qkv_g, k.query_piece)
    keys = [
        Piece(qkv_left, k.proj_grad, width + sum(KEY_STEPS[:i]), width, k.qkv_g, buffers)
        for i, buffers in enumerate(k.key_pieces)
    ]
    early, late = VectorSum(*k.early), CubeSum(*k.late)

    middle = has_up & has_down
    places = [(row, z, x, 1 - c), (1 - row, z, x, c), (1 - row, z, x, 1 - c)]
    places += [(row, z, 1 - x, c), (row, z, 1 - x, 1 - c)]
    partners = [(None, (y, at * 4 + across * 2 + core)) for y, at, across, core in places]
    partners += [
        (has_up, (row, (z + 1) * 4 + x * 2 + c)),
        (has_down, (row, (z - 1) * 4 + x * 2 + c)),
    ]
    meet(partners, len(places) + has_up.astype(jnp.int32) + has_down.astype(jnp.int32))

    def tell(device):
        pl.semaphore_signal(k.ready, inc=1, device_id=device, device_id_type=MESH_ID)

    tell((row, z * 4 + (1 - x) * 2 + c))

    @pl.when(middle)
    def _():
        tell((row, (z + 1) * 4 + x * 2 + c))
        tell((row, (z - 1) * 4 + x * 2 + c))

    own_ids = jnp.broadcast_to(k.segment_ids[...], (frame_count, frame_count)).astype(wide)
    ids_column = own_ids.T
    k.block[mine, pl.ds(0, frame_count), :] = k.frames[...]
    k.block[mine, pl.ds(frame_count, 16), pl.ds(0, frame_count)] = own_ids[:16].astype(low)
    link.own()
    link.cross_over()
    link.line_near()
    k.inner_bias[...] = k.up_bias[...].reshape(1, inner)
    query_bias = k.query_bias[...].reshape(1, width)
    k.proj_bias[...] = jnp.concatenate(
        [query_bias, jnp.zeros((1, width), wide), k.value_bias[...].reshape(1, width)], axis=1
    )

    def plane_rows(plane):
        return jnp.concatenate(
            [k.block[plane * 4 + i, pl.ds(0, frame_count), :] for i in range(4)], axis=0
        )

    def project_columns(plane, first, count):
        def some(i, carry):
            columns = pl.ds(pl.multiple_of(first + i * CHUNK, 128), CHUNK)
            part = product(plane_rows(plane), k.qkv_held[:, columns], CONTRACT_INNER)
            part = (part + k.proj_bias[:, columns]).astype(low)
            if first == 0:
                part = part * HEAD_DIM**-0.5
            for b in range(4):
                k.projected[plane * 4 + b, :, columns] = part[
                    b * frame_count : (b + 1) * frame_count
                ]
            return carry

        lax.fori_loop(0, count // CHUNK, some, 0)

    def as_query(part):
        return (part + query_bias).astype(low) * HEAD_DIM**-0.5

    def project(plane):
        project_columns(plane, width, 2 * width)
        for i in range(4):
            ids = k.block[plane * 4 + i, pl.ds(frame_count, 8), pl.ds(0, frame_count)]
            same = jnp.broadcast_to(ids.astype(wide)[:1], own_ids.shape) == ids_column
            at = pl.multiple_of((plane * 4 + i) * frame_count, 128)
            k.mask[:, pl.ds(at, frame_count)] = jnp.where(same, 0.0, mask_fill)

    def project_queries(plane):
        project_columns(plane, 0, width)

    def queries_own_far():
        project_queries(z)
        project_queries(far)

    def queries_near():
        pl.when(has_down)(lambda: project_queries(z - 1))
        pl.when(has_up)(lambda: project_queries(z + 1))

    def planes_done():
        back.plane_done(z)
        back.plane_done(z - 1, has_down)
        back.plane_done(z + 1, has_up)
        back.plane_done(far)

    def input_gradient():
        k.input_grad[...] = k.first_grad[...] + product(
            k.proj_grad[...], k.qkv_held[...], CONTRACT_LAST
        )

    def query_note():
        note(early, 6, k.proj_grad[:, pl.ds(0, width)].astype(wide))

    def late_notes():
        values = k.proj_grad[:, pl.ds(2 * width, width)].astype(wide)
        late.cube[late.member] = jnp.sum(values, axis=0, keepdims=True)

    def small_shares():
        share = k.query_g.shape[0]
        first = early.partial[VectorSum.STAGES - 1]
        shares, _ = early.own_share(first[:8], share)
        k.query_g[...] = shares[6, :share]
        last = jnp.broadcast_to(late.partial[CubeSum.STAGES - 1], (8, width))
        k.value_g[...] = early.own_share(last, share)[0][0, :share]
        for i, ref in enumerate(
            (k.outbias_g, k.gain1_g, k.shift1_g, k.downbias_g, k.gain2_g, k.shift2_g)
        ):
            ref[...] = shares[i, :share]
        up_shares, at = early.own_share(first[8:], 4 * share)
        keep = lax.broadcasted_iota(jnp.int32, up_shares.shape, 0) == at
        picked = jnp.sum(jnp.where(keep, up_shares, 0.0), axis=0, keepdims=True)
        k.upbias_g[...] = picked[0, : 4 * share]

    def note(vector, index, values):
        vector.ref[pl.ds(index, 1), :] = jnp.sum(values, axis=0, keepdims=True)

    def flat(ref):
        return ref[...].reshape(1, width)

    def columns_of(third, j):
        return pl.ds(pl.multiple_of(third * width + j * 128, 128), 128)

    def head_state(h):
        return pl.ds(pl.multiple_of(h * 128, 128), 128)

    def both_heads(values):
        nothing = jnp.zeros_like(values)
        return jnp.concatenate(
            [jnp.where(lane < HALF, values, nothing), jnp.where(lane < HALF, nothing, values)],
            axis=0,
        )

    def own_halves(values):
        return jnp.where(lane < HALF, values[:frame_count], values[frame_count:])

    def attend(plane, first):
        at = pl.multiple_of(plane * 4 * frame_count, 128)

        def state(kind, j):
            return k.slope.at[:, pl.ds(pl.multiple_of((kind * HEADS + 2 * j) * 128, 128), 256)]

        def read(kind, j):
            pair_state = state(kind, j)[...]
            return jnp.concatenate([pair_state[:, :128], pair_state[:, 128:]], axis=0)

        def write(kind, j, values):
            state(kind, j)[...] = jnp.concatenate(
                [values[:frame_count], values[frame_count:]], axis=1
            )

        def pair(j, carry):
            query = both_heads(k.projected[mine, :, columns_of(0, j)])
            keys = k.projected[pl.ds(plane * 4, 4), :, columns_of(1, j)].reshape(-1, 128)
            values = k.projected[pl.ds(plane * 4, 4), :, columns_of(2, j)].reshape(-1, 128)
            mask = k.mask[:, pl.ds(at, 4 * frame_count)]
            scores = product(query, keys, CONTRACT_LAST) + jnp.concatenate([mask, mask], axis=0)
            tile = (2 * frame_count, 128)
            peak = jnp.broadcast_to(jnp.max(scores, axis=1, keepdims=True), tile)
            if not first:
                old = read(0, j)
                peak = jnp.maximum(peak, old)
                factor = jnp.exp(old - peak)
            weights = jnp.exp(scores - jnp.concatenate([peak] * 4, axis=1))
            whole = jnp.broadcast_to(jnp.sum(weights, axis=1, keepdims=True), tile)
            if not first:
                whole = whole + read(1, j) * factor
            write(0, j, peak)
            write(1, j, whole)
            both = own_halves(product(weights.astype(low), values, CONTRACT_INNER))
            if not first:
                both = both + k.attended[:, columns_of(0, j)] * own_halves(factor)
            k.attended[:, columns_of(0, j)] = both
            return carry

        lax.fori_loop(0, PAIRS, pair, 0, unroll=2 if first else UNROLL)

    def own_queries():
        fetch(0).wait()
        own = product(k.frames[...], k.qkv_held[:, pl.ds(0, width)], CONTRACT_INNER)
        k.projected[mine, :, pl.ds(0, width)] = as_query(own)

    def take_plane(plane, present=None):
        def take():
            link.plane_done(plane)
            project(plane)

        if present is None:
            take()
        else:
            pl.when(present)(take)

    def attend_near(plane, present):
        pl.when(present)(lambda: attend(plane, False))

    own_queries()
    link.line_over()
    take_plane(z)
    link.cross_near_over()
    link.cross_near()
    link.line_near_over()
    link.line_far()
    qkv_left.share()
    attend(z, True)
    take_plane(z - 1, has_down)
    take_plane(z + 1, has_up)
    link.line_far_over()
    link.cross_far()
    link.cross_far_over()
    attend_near(z + 1, has_up)
    attend_near(z - 1, has_down)
    take_plane(far)
    attend(far, False)
    logs = jnp.zeros(lane.shape, wide)
    for j in range(PAIRS):
        parts = []
        for h in range(2):
            whole = k.slope[:, head_state(HEADS + 2 * j + h)]
            logs = jnp.where(
                lane == 2 * j + h, k.slope[:, head_state(2 * j + h)] + jnp.log(whole), logs
            )
            parts.append(whole)
        done = k.attended[:, columns_of(0, j)] / jnp.where(lane < HALF, parts[0], parts[1])
        k.attended[:, columns_of(0, j)] = done
        k.context[:, columns_of(0, j)] = done.astype(low)
    k.logs[...] = logs

    def normalize(resid):
        centred = resid - jnp.mean(resid, axis=-1, keepdims=True)
        inverse = lax.rsqrt(jnp.mean(centred * centred, axis=-1, keepdims=True) + norm_eps)
        return centred * inverse, inverse

    def normalize_back(upstream, normed, inverse, gain):
        scaled = upstream * gain
        first_mean = jnp.mean(scaled, axis=-1, keepdims=True)
        second_mean = jnp.mean(scaled * normed, axis=-1, keepdims=True)
        return inverse * (scaled - first_mean - normed * second_mean)

    early.ref[...] = jnp.zeros((16, width), wide)
    fetch(1).wait()
    resid_one = (
        k.frames[...].astype(wide)
        + product(k.context[...], k.out_held[...], CONTRACT_INNER)
        + flat(k.out_bias)
    )
    normed_one, inverse_one = normalize(resid_one)
    k.normed[...] = normed_one
    hidden = normed_one * flat(k.norm1_gain) + flat(k.norm1_shift)
    k.hidden_low[...] = hidden.astype(low)
    up_left.share()
    k.running[...] = hidden + flat(k.down_bias)
    fetch(2).wait()
    fetch(3).wait()

    def forward(f, carry):
        columns = pl.ds(pl.multiple_of(f * width, 128), width)
        pre_act = (
            product(k.hidden_low[...], k.up_held[:, columns], CONTRACT_INNER)
            + k.inner_bias[:, columns]
        )
        normal_cdf = 0.5 * (1.0 + lax.erf(pre_act * 0.5**0.5))
        normal_pdf = jnp.exp(-0.5 * pre_act * pre_act) * (2.0 * math.pi) ** (-0.5)
        act = (pre_act * normal_cdf).astype(low)
        k.act[:, columns] = act
        k.slope[:, columns] = normal_cdf + pre_act * normal_pdf
        k.running[...] += product(
            act, k.down_held[pl.ds(pl.multiple_of(f * width, 128), width), :], CONTRACT_INNER
        )
        return carry

    lax.fori_loop(0, inner // width, forward, 0)
    down_left.share()
    out_left.share()
    normed_two, inverse_two = normalize(k.running[...])
    k.layer_out[...] = (normed_two * flat(k.norm2_gain) + flat(k.norm2_shift)).astype(low)
    upstream = k.cotangent[...].astype(wide)
    second_grad = normalize_back(upstream, normed_two, inverse_two, flat(k.norm2_gain))
    k.second_low[...] = second_grad.astype(low)
    note(early, 3, second_grad)
    note(early, 4, upstream * normed_two)
    note(early, 5, upstream)
    k.running[...] = second_grad

    def backward(p):
        for member in range(4):
            first = member * width + p * STEP
            columns = pl.ds(first, STEP)
            pre_grad = (
                product(k.second_low[...], k.down_held[columns, :], CONTRACT_LAST)
                * k.slope[:, columns]
            )
            early.ref[pl.ds(8 + member, 1), pl.ds(p * STEP, STEP)] = jnp.sum(
                pre_grad, axis=0, keepdims=True
            )
            k.pre_low[:, columns] = pre_grad.astype(low)
            k.running[...] += product(
                k.pre_low[:, columns], k.up_held[:, columns], CONTRACT_LAST
            )

    backward(0)
    ups[0].share()
    up_left.relay()
    backward(1)
    hidden_grad = k.running[...]
    normed_one = k.normed[...]
    first_grad = normalize_back(hidden_grad, normed_one, inverse_one, flat(k.norm1_gain))
    k.first_grad[...] = first_grad
    k.first_low[...] = first_grad.astype(low)
    note(early, 0, first_grad)
    note(early, 1, hidden_grad * normed_one)
    note(early, 2, hidden_grad)
    context_grad = product(k.first_low[...], k.out_held[...], CONTRACT_LAST).astype(low)
    k.grad_block[mine] = context_grad
    delta = jnp.zeros(lane.shape, wide)
    for j in range(PAIRS):
        columns = slice(j * 128, (j + 1) * 128)
        both = context_grad[:, columns].astype(wide) * k.attended[:, columns]
        for h in range(2):
            one = jnp.sum(
                jnp.where((lane < HALF) == (h == 0), both, 0.0), axis=1, keepdims=True
            )
            delta = jnp.where(lane == 2 * j + h, one, delta)
    k.delta[...] = delta
    k.stats[mine, pl.ds(0, 16), :] = k.logs[...].T[:16]
    k.stats[mine, pl.ds(16, 16), :] = delta.T[:16]
    down.share()
    back.own()
    pl.semaphore_wait(k.ready, 2)

    @pl.when(jnp.logical_not(middle))
    def _():
        for i in range(4):
            k.projected[lost * 4 + i] = jnp.zeros((frame_count, 3 * width), low)
            k.grad_block[lost * 4 + i] = jnp.zeros((frame_count, width), low)
            k.stats[lost * 4 + i] = jnp.zeros((32, frame_count), wide)
            at = pl.multiple_of((lost * 4 + i) * frame_count, 128)
            k.mask[:, pl.ds(at, frame_count)] = jnp.full(lane.shape, mask_fill, wide)

    def query_pair(j):
        query = k.projected[mine, :, columns_of(0, j)]
        upstream = k.grad_block[mine, :, columns_of(0, j)]
        keys = k.projected[:, :, columns_of(1, j)].reshape(total, 128)
        values = k.projected[:, :, columns_of(2, j)].reshape(total, 128)
        outs = []
        for h in range(2):
            chosen = (lane < HALF) == (h == 0)
            nothing = jnp.zeros_like(query)
            logs = jnp.sum(
                jnp.where(lane == 2 * j + h, k.logs[...], 0.0), axis=1, keepdims=True
            )
            shift = jnp.sum(
                jnp.where(lane == 2 * j + h, k.delta[...], 0.0), axis=1, keepdims=True
            )
            scores = product(jnp.where(chosen, query, nothing), keys, CONTRACT_LAST)
            probs = jnp.exp(scores + k.mask[...] - logs)
            prob_grad = product(jnp.where(chosen, upstream, nothing), values, CONTRACT_LAST)
            score_grad = (probs * (prob_grad - shift)).astype(low)
            outs.append(product(score_grad, keys, CONTRACT_INNER))
        k.proj_grad[:, columns_of(0, j)] = (
            jnp.where(lane < HALF, outs[0], outs[1]) * HEAD_DIM**-0.5
        ).astype(low)

    def key_pair(j):
        key = k.projected[mine, :, columns_of(1, j)]
        value = k.projected[mine, :, columns_of(2, j)]
        queries = k.projected[:, :, columns_of(0, j)].reshape(total, 128)
        upstream = k.grad_block[:, :, columns_of(0, j)].reshape(total, 128)
        key_outs, value_outs = [], []
        for h in range(2):
            chosen = (lane < HALF) == (h == 0)
            nothing = jnp.zeros_like(key)
            logs = jnp.concatenate(
                [k.stats[b, pl.ds(2 * j + h, 1), :] for b in range(BLOCKS)], axis=1
            )
            shift = jnp.concatenate(
                [k.stats[b, pl.ds(16 + 2 * j + h, 1), :] for b in range(BLOCKS)], axis=1
            )
            scores = product(jnp.where(chosen, key, nothing), queries, CONTRACT_LAST)
            probs = jnp.exp(scores + k.mask[...] - logs)
            prob_grad = product(jnp.where(chosen, value, nothing), upstream, CONTRACT_LAST)
            score_grad = (probs * (prob_grad - shift)).astype(low)
            key_outs.append(product(score_grad, queries, CONTRACT_INNER))
            value_outs.append(product(probs.astype(low), upstream, CONTRACT_INNER))
        k.proj_grad[:, columns_of(1, j)] = jnp.where(
            lane < HALF, key_outs[0], key_outs[1]
        ).astype(low)
        k.proj_grad[:, columns_of(2, j)] = jnp.where(
            lane < HALF, value_outs[0], value_outs[1]
        ).astype(low)

    def pairs(one, first, last):
        def body(j, carry):
            one(j)
            return carry

        lax.fori_loop(first, last, body, 0)

    pairs(query_pair, 0, 3)
    back.cross_over()
    ups[1].share()
    pairs(query_pair, 3, 4)
    up_left.complete()
    back.line_near()
    down_left.relay()
    back.cross_near()
    pairs(query_pair, 4, 5)
    ups[0].multiply()
    back.line_far()
    down_left.complete()
    queries_own_far()
    back.cross_near_over()
    back.cross_far()
    back.line_near_over()
    ups[1].multiply()
    down.multiply()
    out_left.relay()
    queries_near()
    out.share()
    back.line_over()
    back.line_far_over()
    back.cross_far_over()
    ups[0].spread()
    pairs(query_pair, 5, 6)
    out_left.complete()
    planes_done()
    query_note()
    early.step(0)
    pairs(key_pair, 0, 1)
    qkv_left.relay()
    ups[1].spread()
    early.step(1)
    query.share()
    pairs(key_pair, 1, 2)
    qkv_left.complete()
    pairs(key_pair, 2, 3)
    ups[1].fold()
    ups[0].fold()
    pairs(key_pair, 3, 4)
    down.spread()
    out.multiply()
    early.step(2)
    pairs(key_pair, 4, 5)
    keys[0].share()
    pairs(key_pair, 5, 6)
    query.multiply()
    early.step(3)
    down.fold()
    keys[2].share()
    keys[1].share()
    out.spread()
    late_notes()
    late.step(0)
    input_gradient()
    keys[0].multiply()
    query.spread()
    out.fold()
    keys[2].multiply()
    early.step(4)
    keys[1].multiply()
    late.step(1)
    ups[0].collect()
    query.fold()
    down.collect()
    keys[0].spread()
    keys[0].fold()
    keys[2].spread()
    keys[1].spread()
    late.step(2)
    keys[2].fold()
    keys[1].fold()
    ups[1].collect()
    late.step(3)
    query.collect()
    keys[0].collect()
    early.step(5)
    out.collect()
    small_shares()
    keys[2].collect()
    keys[1].collect()
    for each in [down_left, up_left, out_left, qkv_left, down, out, query] + ups + keys:
        each.finish()
    for each in (back, link, early, late):
        each.finish()


def copy_kernel(*refs):
    count = len(refs) // 2
    for source, target in zip(refs[:count], refs[count:]):
        target[...] = source[...]


def hand_over(results):
    return pl.pallas_call(
        copy_kernel,
        out_shape=tuple(jax.ShapeDtypeStruct(each.shape, each.dtype) for each in results),
        in_specs=[IN_VMEM] * len(results),
        out_specs=(IN_VMEM,) * len(results),
    )(*results)


def layer_step(*args):
    frames = args[0]
    frame_count, width = frames.shape[1:]
    inner = args[9].shape[1]
    low, wide = jnp.bfloat16, jnp.float32
    scratch, held = jax.tree.flatten(layer_scratch(frame_count, width, inner))
    operands = [frames[0]] + list(args[1:-1]) + [args[-1][0]]
    share = width // 32
    shapes = [
        ((frame_count, width), low),
        ((frame_count, width), wide),
        ((share, 3 * width), wide),
        ((share,), wide),
        ((share,), wide),
        ((share, width), wide),
        ((share,), wide),
        ((share,), wide),
        ((share,), wide),
        ((share, inner), wide),
        ((4 * share,), wide),
        ((4 * share, width), wide),
        ((share,), wide),
        ((share,), wide),
        ((share,), wide),
    ]
    results = pl.pallas_call(
        functools.partial(layer_kernel, held),
        out_shape=tuple(jax.ShapeDtypeStruct(shape, kind) for shape, kind in shapes),
        in_specs=[IN_PLACE if each.ndim == 2 and each.shape[0] >= width else IN_VMEM for each in operands],
        out_specs=(IN_VMEM,) * len(shapes),
        scratch_shapes=scratch,
        compiler_params=pltpu.CompilerParams(
            collective_id=0, has_side_effects=True, vmem_limit_bytes=VMEM_BYTES
        ),
    )(*operands)
    results = hand_over(results)
    return (results[0][None], results[1][None]) + tuple(results[2:])


def solution(mesh):
    chosen = layer_step if dict(mesh.shape) == {"rows": 2, "seq": 16} else shards
    in_specs = (
        P("rows", "seq", None),
        P("rows", "seq"),
        P(),
        P(),
        P(),
        P(),
        P(),
        P(),
        P(),
        P(),
        P(),
        P(),
        P(),
        P(),
        P(),
        P("rows", "seq", None),
    )
    out_specs = (
        P("rows", "seq", None),
        P("rows", "seq", None),
        P(("rows", "seq"), None),
        P(("rows", "seq")),
        P(("rows", "seq")),
        P(("rows", "seq"), None),
        P(("rows", "seq")),
        P(("rows", "seq")),
        P(("rows", "seq")),
        P(("rows", "seq"), None),
        P(("rows", "seq")),
        P(("rows", "seq"), None),
        P(("rows", "seq")),
        P(("rows", "seq")),
        P(("rows", "seq")),
    )
    return jax.shard_map(chosen, mesh=mesh, in_specs=in_specs, out_specs=out_specs, check_vma=False)
```
